32 devices in a mesh: ctx: 16 (over z, x, core), fsdp: 2 (over y).
Axes of the slice: x: 2, y: 2, z: 4, core: 2. Of those that a mesh axis runs over, the one named last changes fastest.
Arguments:
- tokens: bfloat16 [4, 2048, 768], P('fsdp', 'ctx'), may hold values from -6 to 6
- cotangent: bfloat16 [4, 2048, 768], P('fsdp', 'ctx'), may hold values from -6 to 6
- doc_lengths: int32 [4, 4], P('fsdp'), may hold values from 1 to 1280, 2048 in all within a row
- w_qkv: bfloat16 [768, 2304], P('fsdp'), may hold values from -0.21875 to 0.21875
- w_out: bfloat16 [768, 768], P('fsdp'), may hold values from -6 to 6
- w_in: bfloat16 [768, 3072], P('fsdp'), may hold values from -0.21875 to 0.21875
- w_back: bfloat16 [3072, 768], P('fsdp'), may hold values from -0.109375 to 0.109375
- b_query: bfloat16 [768], P('fsdp'), may hold values from -4 to 4
- b_value: bfloat16 [768], P('fsdp'), may hold values from -0.3125 to 0.3125
- b_out: bfloat16 [768], P('fsdp'), may hold values from -4 to 4
- b_in: bfloat16 [3072], P('fsdp'), may hold values from -4 to 4
- b_back: bfloat16 [768], P('fsdp'), may hold values from -4 to 4
- gain_one: bfloat16 [768], P('fsdp'), may hold values from 0.5 to 1.5
- shift_one: bfloat16 [768], P('fsdp'), may hold values from -3 to 3
- gain_two: bfloat16 [768], P('fsdp'), may hold values from 0.5 to 1.5
- shift_two: bfloat16 [768], P('fsdp'), may hold values from -3 to 3
Outputs:
- output: bfloat16 [4, 2048, 768], P('fsdp', 'ctx')
- input_grad: float32 [4, 2048, 768], P('fsdp', 'ctx')
- w_qkv_grad: float32 [768, 2304], P('fsdp')
- w_out_grad: float32 [768, 768], P('fsdp')
- w_in_grad: float32 [768, 3072], P('fsdp')
- w_back_grad: float32 [3072, 768], P('fsdp')
- b_query_grad: float32 [768], P('fsdp')
- b_value_grad: float32 [768], P('fsdp')
- b_out_grad: float32 [768], P('fsdp')
- b_in_grad: float32 [3072], P('fsdp')
- b_back_grad: float32 [768], P('fsdp')
- gain_one_grad: float32 [768], P('fsdp')
- shift_one_grad: float32 [768], P('fsdp')
- gain_two_grad: float32 [768], P('fsdp')
- shift_two_grad: float32 [768], P('fsdp')
The draws below stay inside these ranges and needn't reach their ends.
Inputs may be any that keep to these rules, and one draw needn't show every extreme that they name: `doc_lengths`: row s holds the lengths of the 4 documents of stream s in order; they sum to 2048, and in every stream the longest is 1280.
All inputs are finite; a program needn't handle non-finite values.
Results may differ from the reference program's by a relative error of at most 0.02.
Values may be sent and summed in bfloat16 or wider, within the bound.
A program may use at most 256 MiB of HBM per device.

```python
import math
import jax
import jax.numpy as jnp
import numpy as np
from jax import lax

D = 768
HEADS = 12
HEAD = 64
FF = 3072
DOCS = 4
KEYBLK = 512
STREAM = 2048
DOC_MOST = 1280
STREAMS = 4


def levels(stream_key, shape, pieces, low, largest):
    gain, own = 1.0, jax.random.fold_in(stream_key, 6)
    for position, blocks in pieces:
        draws = jnp.exp(jax.random.uniform(jax.random.fold_in(own, position), (blocks,), jnp.float32, low / len(pieces), largest / len(pieces)))
        gain = gain * jnp.repeat(draws, shape[position] // blocks).reshape([-1 if axis == position else 1 for axis in range(len(shape))])
    return gain


def length_profile(count, total, bound, skew):
    portions = [(1 << 20) // math.isqrt(standing ** skew) + 1 for standing in range(2, count + 1)]
    spare, holding = total - bound - (count - 1), [1] * (count - 1)
    while spare > 0:
        movable = [i for i in range(count - 1) if holding[i] < bound]
        pool, budget = sum([portions[i] for i in movable]), spare
        for i in movable:
            addition = min(bound - holding[i], max(1, budget * portions[i] // pool), spare)
            holding[i] = holding[i] + addition
            spare = spare - addition
    return np.array([bound] + holding)


def uneven_parts(key, number_of, total, reach, lean):
    if number_of == 2:
        one = jax.random.randint(key, (), max(1, total - reach), min(reach, total - 1) + 1)
        return jnp.stack([one, total - one])
    sizes = jnp.asarray(length_profile(number_of, total, reach, lean), jnp.int32)
    twos = (number_of - 1) // 2
    donor, taker = sizes[1:1 + 2 * twos:2], sizes[2:2 + 2 * twos:2]
    slack = jnp.minimum(donor - 1, reach - taker)
    moved = jax.random.randint(jax.random.fold_in(key, 1), (twos,), 0, 1 << 20) % (slack + 1)
    sizes = sizes.at[1:1 + 2 * twos:2].set(donor - moved).at[2:2 + 2 * twos:2].set(taker + moved)
    return sizes[jax.random.permutation(jax.random.fold_in(key, 2), number_of)]


def gaussian(key, shape, width, bound, cuts=(), kind=jnp.bfloat16):
    drawn = jax.random.normal(key, shape, jnp.float32) * width
    if len(cuts) > 0:
        drawn = levels(key, shape, cuts, -0.22, 0.18) * drawn
    return jnp.clip(drawn, min=-bound, max=bound).astype(kind)


def setup_inputs(seed: int = 0) -> dict:
    splits = jax.random.split(jax.random.key(seed), 17)
    return {
        "tokens": gaussian(splits[0], (STREAMS, STREAM, D), 1.0, 6.0, ((0, 2), (1, 16))),
        "cotangent": gaussian(splits[1], (STREAMS, STREAM, D), 1.0, 6.0, ((0, 2), (1, 16))),
        "doc_lengths": jax.vmap(lambda own: uneven_parts(own, DOCS, STREAM, DOC_MOST, 2))(jax.random.split(splits[2], STREAMS)).reshape((STREAMS, DOCS)).astype(jnp.int32),
        "w_qkv": gaussian(splits[3], (D, 3 * D), D ** -0.5, 0.21875, ((0, 2),)),
        "w_out": gaussian(splits[4], (D, D), 1 ** -0.5, 6.0, ((0, 2),)),
        "w_in": gaussian(splits[5], (D, FF), D ** -0.5, 0.21875, ((0, 2),)),
        "w_back": gaussian(splits[6], (FF, D), FF ** -0.5, 0.109375, ((0, 2),)),
        "b_query": gaussian(splits[7], (D,), 0.3, 4.0, ((0, 2),)),
        "b_value": gaussian(splits[8], (D,), 0.02, 0.3125, ((0, 2),)),
        "b_out": gaussian(splits[9], (D,), 0.3, 4.0, ((0, 2),)),
        "b_in": gaussian(splits[10], (FF,), 0.3, 4.0, ((0, 2),)),
        "b_back": gaussian(splits[11], (D,), 0.3, 4.0, ((0, 2),)),
        "gain_one": jnp.clip(1.0 + 0.1 * jax.random.normal(splits[12], (D,), jnp.float32), 0.5, 1.5).astype(jnp.bfloat16),
        "shift_one": gaussian(splits[13], (D,), 0.2, 3.0, ((0, 2),)),
        "gain_two": jnp.clip(1.0 + 0.1 * jax.random.normal(splits[14], (D,), jnp.float32), 0.5, 1.5).astype(jnp.bfloat16),
        "shift_two": gaussian(splits[15], (D,), 0.2, 3.0, ((0, 2),)),
    }


@jax.custom_vjp
def low(v):
    return lax.optimization_barrier(v.astype(jnp.bfloat16)).astype(jnp.float32)

@jax.custom_vjp
def low_back(v):
    return v

def low_keep(v):
    return (low(v), None)

def low_pass(kept, grad):
    return (grad,)

def back_keep(v):
    return (v, None)

def back_low(kept, grad):
    return (low(grad),)
low.defvjp(low_keep, low_pass)
low_back.defvjp(back_keep, back_low)
EPSILON = 1e-12
NEGATIVE = -1e+30
HIGHEST_MODE = lax.Precision.HIGHEST

def product(left_side, right_side):
    return jnp.dot(left_side, right_side, precision=HIGHEST_MODE)

def layer_norm(values, gain_row, shift_row):
    average = lax.optimization_barrier(jnp.mean(values, axis=-1, keepdims=True))
    centered = values - average
    variance = lax.optimization_barrier(jnp.mean(centered * centered, axis=-1, keepdims=True))
    return centered * lax.rsqrt(variance + EPSILON) * gain_row + shift_row

def document_ids(stream_lengths):
    boundary = jnp.cumsum(stream_lengths)
    positions = jnp.arange(STREAM, dtype=jnp.int32)
    return lax.optimization_barrier(jnp.sum((positions[:, None] >= boundary[None, :]).astype(jnp.int32), axis=1))

def attend(queries, keys, values, doc_ids):
    block_count = STREAM // KEYBLK
    head_queries = queries.reshape(block_count, KEYBLK, HEADS, HEAD)
    block_docs = doc_ids.reshape(block_count, KEYBLK)
    head_keys = keys.reshape(STREAM, HEADS, HEAD)
    head_values = values.reshape(STREAM, HEADS, HEAD)

    def one_block(block_args):
        query_block, query_docs = block_args
        raw_scores = jnp.einsum('qhd,khd->hqk', query_block, head_keys, precision=HIGHEST_MODE) * 0.125
        scores = low_back(raw_scores)
        allowed = (query_docs[:, None] == doc_ids[None, :])[None]
        scores = jnp.where(allowed, scores, NEGATIVE)
        log_total = jax.nn.logsumexp(scores, axis=-1, keepdims=True)
        weights = low(jnp.exp(scores - log_total))
        return jnp.einsum('hqk,khd->qhd', weights, head_values, precision=HIGHEST_MODE)
    mixed_blocks = lax.map(jax.checkpoint(one_block), (head_queries, block_docs))
    return mixed_blocks.reshape(STREAM, D)

def forward_layer(stream_in, doc_ids, params):
    w_qkv, w_out, w_in, w_back, b_query, b_value, b_out, b_in, b_back, gain_one, shift_one, gain_two, shift_two = params
    joined = product(stream_in, w_qkv)
    queries = low(low_back(joined[:, :D] + b_query))
    keys = low(low_back(joined[:, D:2 * D]))
    values = low(low_back(joined[:, 2 * D:] + b_value))
    attended = low(low_back(attend(queries, keys, values, doc_ids)))
    branch = low_back(product(attended, w_out) + b_out)
    normed = layer_norm(stream_in + branch, gain_one, shift_one)
    hidden = low_back(product(low(normed), w_in) + b_in)
    activated = low(jax.nn.gelu(hidden, approximate=False))
    second = low_back(product(activated, w_back) + b_back)
    return layer_norm(normed + second, gain_two, shift_two)

def reference(tokens, cotangent, doc_lengths, w_qkv, w_out, w_in, w_back, b_query, b_value, b_out, b_in, b_back, gain_one, shift_one, gain_two, shift_two):
    params = tuple((member.astype(jnp.float32) for member in (w_qkv, w_out, w_in, w_back, b_query, b_value, b_out, b_in, b_back, gain_one, shift_one, gain_two, shift_two)))

    def stream_step(grad_sums, stream_args):
        stream_in, stream_cot, stream_lengths = stream_args
        doc_ids = document_ids(stream_lengths)

        def forward_fixed(inputs, weights_all):
            return forward_layer(inputs, doc_ids, weights_all)
        result, pullback = jax.vjp(forward_fixed, stream_in, params)
        grad_in, grad_params = pullback(stream_cot)
        grad_sums = jax.tree.map(jnp.add, grad_sums, grad_params)
        return (grad_sums, (result.astype(jnp.bfloat16), grad_in))
    start_sums = jax.tree.map(jnp.zeros_like, params)
    grad_sums, (output, input_grad) = lax.scan(stream_step, start_sums, (tokens.astype(jnp.float32), cotangent.astype(jnp.float32), doc_lengths))
    return (output, input_grad, grad_sums[0], grad_sums[1], grad_sums[2], grad_sums[3], grad_sums[4], grad_sums[5], grad_sums[6], grad_sums[7], grad_sums[8], grad_sums[9], grad_sums[10], grad_sums[11], grad_sums[12])
```

```python
import functools

import jax
import jax.numpy as jnp
from jax import lax
from jax.experimental import pallas as pl
from jax.experimental.pallas import tpu as pltpu
from jax.sharding import PartitionSpec as P

MESH = pl.DeviceIdType.MESH
DMA = pltpu.SemaphoreType.DMA
F32, BF16 = jnp.float32, jnp.bfloat16
EPSILON = 1e-12

def place(cols):
    index = lax.axis_index("ctx")
    return index // (2 * cols), lax.rem(index // 2, cols), lax.rem(index, 2), lax.axis_index("fsdp")

def device(a, b, c, f, cols):
    return {"ctx": (a * cols + b) * 2 + c, "fsdp": f}

def meet(peers):
    barrier = pltpu.get_barrier_semaphore()
    for peer in peers:
        pl.semaphore_signal(barrier, inc=1, device_id=peer, device_id_type=MESH)
    pl.semaphore_wait(barrier, len(peers))

def remote(source, target, send, recv, peer):
    return pltpu.make_async_remote_copy(
        src_ref=source, dst_ref=target, send_sem=send, recv_sem=recv, device_id=peer, device_id_type=MESH)

def gather_kernel(nf, cols, count, *refs):
    shards, tiny, fulls, tiny_out = refs[:count], refs[count], refs[count+1:2*count+1], refs[2*count+1]
    local_sem, s1, r1, s2, r2, s3, r3, st, rt = refs[2*count+2:]
    a, b, c, f = place(cols)
    other = 1 - c
    fpeers = [device(a, b, c, lax.rem(f + j, nf), cols) for j in range(1, nf)]
    bpeers = [device(a, lax.rem(b + k, cols), c, f, cols) for k in range(1, cols)]
    sibling = device(a, b, other, f, cols)
    meet(fpeers + bpeers + [sibling])

    def view(w, owner, bb, cc, base=0):
        rows, wide = shards[w].shape
        part, half = rows // cols, wide // 2
        return fulls[w].at[pl.ds(pl.multiple_of(owner * rows + bb * part, 8), part), pl.ds(pl.multiple_of(cc * half, 128), half)]

    waits = []
    for j in range(1, nf):
        cp = remote(tiny, tiny_out.at[f], st.at[j - 1], rt.at[j - 1], fpeers[j - 1])
        cp.start()
        waits.append(cp)
    locals_ = [pltpu.make_async_copy(tiny, tiny_out.at[f], local_sem.at[count])]
    locals_[0].start()
    first = {}
    for w in range(count):
        rows, wide = shards[w].shape
        part, half = rows // cols, wide // 2
        mine = shards[w].at[pl.ds(pl.multiple_of(b * part, 8), part), pl.ds(pl.multiple_of(c * half, 128), half)]
        for j in range(1, nf):
            cp = remote(mine, view(w, f, b, c), s1.at[w, j - 1], r1.at[w, j - 1], fpeers[j - 1])
            cp.start()
            first[w, j] = cp
    for w in range(count):
        rows = shards[w].shape[0]
        cp = pltpu.make_async_copy(shards[w], fulls[w].at[pl.ds(pl.multiple_of(f * rows, 8), rows)], local_sem.at[w])
        cp.start()
        locals_.append(cp)
    second, third = {}, []
    for w in range(count):
        for j in range(1, nf):
            owner = lax.rem(f + nf - j, nf)
            first[w, j].wait_recv()
            piece = view(w, owner, b, c)
            for k in range(1, cols):
                slot = (j - 1) * (cols - 1) + k - 1
                cp = remote(piece, piece, s2.at[w, slot], r2.at[w, slot], bpeers[k - 1])
                cp.start()
                second[w, j, k] = cp
            cp = remote(piece, piece, s3.at[w, (j - 1) * cols], r3.at[w, (j - 1) * cols], sibling)
            cp.start()
            third.append(cp)
    for w in range(count):
        for j in range(1, nf):
            owner = lax.rem(f + nf - j, nf)
            for k in range(1, cols):
                second[w, j, k].wait_recv()
                piece = view(w, owner, lax.rem(b + cols - k, cols), c)
                cp = remote(piece, piece, s3.at[w, (j - 1) * cols + k], r3.at[w, (j - 1) * cols + k], sibling)
                cp.start()
                third.append(cp)
    for cp in third:
        cp.wait_recv()
    for cp in waits:
        cp.wait()
    for cp in list(first.values()) + list(second.values()) + third:
        cp.wait_send()
    for cp in locals_:
        cp.wait()

def gather_weights(shards, tiny, nf, cols):
    count = len(shards)
    any_spec = pl.BlockSpec(memory_space=pl.ANY)
    dma = pltpu.SemaphoreType.DMA
    return pl.pallas_call(
        functools.partial(gather_kernel, nf, cols, count),
        out_shape=[jax.ShapeDtypeStruct((s.shape[0] * nf, s.shape[1]), s.dtype) for s in shards]
        + [jax.ShapeDtypeStruct((nf,) + tiny.shape, tiny.dtype)],
        in_specs=[pl.BlockSpec(memory_space=pltpu.VMEM)] * (count + 1),
        out_specs=[any_spec] * (count + 1),
        scratch_shapes=[dma((count + 1,)), dma((count, nf - 1)), dma((count, nf - 1)),
                        dma((count, (nf - 1) * (cols - 1))), dma((count, (nf - 1) * (cols - 1))),
                        dma((count, (nf - 1) * cols)), dma((count, (nf - 1) * cols)),
                        dma((nf - 1,)), dma((nf - 1,))],
        compiler_params=pltpu.CompilerParams(collective_id=1, has_side_effects=True, vmem_limit_bytes=32 << 20),
        name="gather_weights",
    )(*shards, tiny)

def octet(a, b, c, f, cols):
    me = a * 2 + c
    out = []
    for k in range(1, 8):
        other = lax.rem(me + k, 8)
        out.append((other, device(other // 2, b, lax.rem(other, 2), f, cols)))
    return me, out

def swap_kernel(cols, count, *refs):
    sources, targets = refs[:count], refs[count:2 * count]
    send, recv, here = refs[2 * count:]
    a, b, c, f = place(cols)
    me, peers = octet(a, b, c, f, cols)
    meet([p for _, p in peers])
    copies = []
    for k, (other, peer) in enumerate(peers):
        for i in range(count):
            cp = remote(sources[i].at[other], targets[i].at[me], send.at[i, k], recv.at[i, k], peer)
            cp.start()
            copies.append(cp)
    for i in range(count):
        cp = pltpu.make_async_copy(sources[i].at[me], targets[i].at[me], here.at[i])
        cp.start()
        copies.append(cp)
    for cp in copies:
        cp.wait()

def swap(arrays, cols, ident):
    count = len(arrays)
    return pl.pallas_call(
        functools.partial(swap_kernel, cols, count),
        out_shape=[jax.ShapeDtypeStruct(x.shape, x.dtype) for x in arrays],
        in_specs=[vmem()] * count, out_specs=[vmem()] * count,
        scratch_shapes=[DMA((count, 7)), DMA((count, 7)), DMA((count,))],
        compiler_params=pltpu.CompilerParams(collective_id=ident, has_side_effects=True, vmem_limit_bytes=16 << 20),
        name="swap",
    )(*arrays)

def spread_kernel(cols, q, kv, qg, full, sq, rq, sk, rk, s2, r2, here):
    a, b, c, f = place(cols)
    me, peers = octet(a, b, c, f, cols)
    bpeers = [device(a, lax.rem(b + k, cols), c, f, cols) for k in range(1, cols)]
    meet([p for _, p in peers] + bpeers)

    def slot(block, bb):
        return (block // 2 * cols + bb) * 2 + lax.rem(block, 2)

    first = []
    for k, (other, peer) in enumerate(peers):
        cp = remote(kv.at[other], full.at[slot(me, b)], sk.at[k], rk.at[k], peer)
        cp.start()
        first.append(cp)
    own = pltpu.make_async_copy(kv.at[me], full.at[slot(me, b)], here.at[0])
    own.start()
    ownq = pltpu.make_async_copy(q.at[me], qg.at[me], here.at[1])
    ownq.start()
    second = []
    for k, peer in enumerate(bpeers):
        cp = remote(kv.at[me], full.at[slot(me, b)], s2.at[7, k], r2.at[7, k], peer)
        cp.start()
        second.append(cp)
    third = []
    for k, (other, peer) in enumerate(peers):
        cp = remote(q.at[other], qg.at[me], sq.at[k], rq.at[k], peer)
        cp.start()
        third.append(cp)
    for k in range(7):
        first[k].wait_recv()
        source = lax.rem(me + 8 - (k + 1), 8)
        piece = full.at[slot(source, b)]
        for m, peer in enumerate(bpeers):
            cp = remote(piece, piece, s2.at[k, m], r2.at[k, m], peer)
            cp.start()
            second.append(cp)
    for cp in first:
        cp.wait_send()
    for cp in second + third:
        cp.wait()
    own.wait()
    ownq.wait()

def spread(q, kv, cols, ident):
    return pl.pallas_call(
        functools.partial(spread_kernel, cols),
        out_shape=[jax.ShapeDtypeStruct(q.shape, q.dtype), jax.ShapeDtypeStruct((8 * cols,) + kv.shape[1:], kv.dtype)],
        in_specs=[vmem()] * 2, out_specs=[vmem()] * 2,
        scratch_shapes=[DMA((7,))] * 4 + [DMA((8, max(cols - 1, 1)))] * 2 + [DMA((2,))],
        compiler_params=pltpu.CompilerParams(collective_id=ident, has_side_effects=True, vmem_limit_bytes=16 << 20),
        name="spread",
    )(q, kv)

def collect_kernel(cols, dq, dkv, dqo, dkvo, rbuf, total, sq, rq, sk, rk, s2, r2, here):
    a, b, c, f = place(cols)
    me, peers = octet(a, b, c, f, cols)
    bpeers = [(lax.rem(b + k, cols), device(a, lax.rem(b + k, cols), c, f, cols)) for k in range(1, cols)]
    meet([p for _, p in peers] + [p for _, p in bpeers])

    def slot(block, bb):
        return (block // 2 * cols + bb) * 2 + lax.rem(block, 2)

    order = [other for other, _ in peers] + [me]
    first = {}
    for n, block in enumerate(order):
        for k, (bb, peer) in enumerate(bpeers):
            cp = remote(dkv.at[slot(block, bb)], rbuf.at[k, n], s2.at[k, n], r2.at[k, n], peer)
            cp.start()
            first[k, n] = cp
    rest = []
    for k, (other, peer) in enumerate(peers):
        cp = remote(dq.at[other], dqo.at[me], sq.at[k], rq.at[k], peer)
        cp.start()
        rest.append(cp)
    own = pltpu.make_async_copy(dq.at[me], dqo.at[me], here.at[0])
    own.start()
    for n, block in enumerate(order):
        value = dkv[slot(block, b)].astype(F32)
        for k in range(cols - 1):
            first[k, n].wait_recv()
            value = value + rbuf[k, n].astype(F32)
        if n < 7:
            total[n] = value.astype(BF16)
            cp = remote(total.at[n], dkvo.at[me], sk.at[n], rk.at[n], peers[n][1])
            cp.start()
            rest.append(cp)
        else:
            dkvo[me] = value.astype(BF16)
    for cp in first.values():
        cp.wait_send()
    for cp in rest:
        cp.wait()
    own.wait()

def collect(dq, dkv, cols, ident):
    block = dkv.shape[1:]
    return pl.pallas_call(
        functools.partial(collect_kernel, cols),
        out_shape=[jax.ShapeDtypeStruct(dq.shape, dq.dtype), jax.ShapeDtypeStruct((8,) + block, dkv.dtype)],
        in_specs=[vmem()] * 2, out_specs=[vmem()] * 2,
        scratch_shapes=[pltpu.VMEM((max(cols - 1, 1), 8) + block, BF16), pltpu.VMEM((7,) + block, BF16)]
        + [DMA((7,))] * 4 + [DMA((max(cols - 1, 1), 8))] * 2 + [DMA((1,))],
        compiler_params=pltpu.CompilerParams(collective_id=ident, has_side_effects=True, vmem_limit_bytes=24 << 20),
        name="collect",
    )(dq, dkv)

def reduce_kernel(nf, cols, parts, grads, small, out, small_out, *refs):
    own, core_in, f_in, b_in, f_in2, b_in2, a_in, v_core, v_sum, v_f, v_b, v_a = refs[:12]
    load, sc, rc, s1, r1, s2, r2, s3, r3, s4, r4, s5, r5, s6, r6, sv, rv = refs[12:]
    a, b, c, f = place(cols)
    rows = grads.shape[5]
    fpeers = [(lax.rem(f + j, nf), device(a, b, c, lax.rem(f + j, nf), cols)) for j in range(1, nf)]
    bpeers = [(lax.rem(b + k, cols), device(a, lax.rem(b + k, cols), c, f, cols)) for k in range(1, cols)]
    apeers = [(lax.rem(a + k, 4), device(lax.rem(a + k, 4), b, c, f, cols)) for k in range(1, 4)]
    sibling = device(a, b, 1 - c, f, cols)
    meet([p for _, p in fpeers + bpeers + apeers] + [sibling])
    vector = remote(small, v_core, sv.at[0], rv.at[0], sibling)
    vector.start()
    order = [2, 1, 3, 0]
    dest = {k: lax.rem(a + k, 4) for k in range(4)}
    by_f = {k: k in (1, 2) for k in range(4)}
    loads, cores = {}, {}
    for k in order:
        for i in range(parts):
            cp = pltpu.make_async_copy(grads.at[c, dest[k], i], own.at[k, i], load.at[k, i])
            cp.start()
            loads[k, i] = cp
            cp = remote(grads.at[1 - c, dest[k], i], core_in.at[k, i], sc.at[k, i], rc.at[k, i], sibling)
            cp.start()
            cores[k, i] = cp
    one, two, three = {}, {}, {}
    vec = {}
    vector.wait_recv()
    v_sum[...] = small[...] + v_core[...]
    for j, (ff, peer) in enumerate(fpeers):
        vec[0, j] = remote(v_sum.at[ff], v_f.at[j], sv.at[1 + j], rv.at[1 + j], peer)
        vec[0, j].start()
    for k in order:
        for i in range(parts):
            loads[k, i].wait()
            cores[k, i].wait_recv()

            @pl.loop(0, nf * cols)
            def _(n):
                ff, bb = n // cols, lax.rem(n, cols)
                own[k, i, ff, bb] = (own[k, i, ff, bb].astype(F32) + core_in[k, i, ff, bb].astype(F32)).astype(BF16)

            if by_f[k]:
                for j, (ff, peer) in enumerate(fpeers):
                    cp = remote(own.at[k, i, ff], f_in.at[k, i, j], s1.at[k, i, j], r1.at[k, i, j], peer)
                    cp.start()
                    one[k, i, j] = cp
            else:
                for m, (bb, peer) in enumerate(bpeers):
                    for ff in range(nf):
                        cp = remote(own.at[k, i, ff, bb], b_in.at[k, i, m, ff], s1.at[k, i, m * nf + ff], r1.at[k, i, m * nf + ff], peer)
                        cp.start()
                        one[k, i, m * nf + ff] = cp
    value = v_sum[f]
    for j in range(nf - 1):
        vec[0, j].wait_recv()
        value = value + v_f[j]
    v_b[b] = value
    for m, (bb, peer) in enumerate(bpeers):
        vec[1, m] = remote(v_b.at[b], v_b.at[b], sv.at[nf + m], rv.at[nf + m], peer)
        vec[1, m].start()
    for k in order:
        for i in range(parts):
            if by_f[k]:
                for j in range(nf - 1):
                    one[k, i, j].wait_recv()

                @pl.loop(0, cols)
                def _(bb):
                    value = own[k, i, f, bb].astype(F32)
                    for j in range(nf - 1):
                        value = value + f_in[k, i, j, bb].astype(F32)
                    own[k, i, f, bb] = value.astype(BF16)

                for m, (bb, peer) in enumerate(bpeers):
                    cp = remote(own.at[k, i, f, bb], b_in2.at[k, i, m], s2.at[k, i, m], r2.at[k, i, m], peer)
                    cp.start()
                    two[k, i, m] = cp
            else:
                for m in range(cols - 1):
                    for ff in range(nf):
                        one[k, i, m * nf + ff].wait_recv()

                @pl.loop(0, nf)
                def _(ff):
                    value = own[k, i, ff, b].astype(F32)
                    for m in range(cols - 1):
                        value = value + b_in[k, i, m, ff].astype(F32)
                    own[k, i, ff, b] = value.astype(BF16)

                for j, (ff, peer) in enumerate(fpeers):
                    cp = remote(own.at[k, i, ff, b], f_in2.at[k, i, j], s2.at[k, i, j], r2.at[k, i, j], peer)
                    cp.start()
                    two[k, i, j] = cp
    for m in range(cols - 1):
        vec[1, m].wait_recv()
    value = v_b[0]
    for m in range(1, cols):
        value = value + v_b[m]
    v_a[a] = value
    for k in range(1, 4):
        vec[2, k] = remote(v_a.at[a], v_a.at[a], sv.at[nf + cols + k - 2], rv.at[nf + cols + k - 2], apeers[k - 1][1])
        vec[2, k].start()
    for k in order:
        for i in range(parts):
            value = own[k, i, f, b].astype(F32)
            if by_f[k]:
                for m in range(cols - 1):
                    two[k, i, m].wait_recv()
                    value = value + b_in2[k, i, m].astype(F32)
            else:
                for j in range(nf - 1):
                    two[k, i, j].wait_recv()
                    value = value + f_in2[k, i, j].astype(F32)
            if k != 0:
                own[k, i, f, b] = value.astype(BF16)
                cp = remote(own.at[k, i, f, b], a_in.at[k - 1, i], s3.at[k - 1, i], r3.at[k - 1, i], apeers[k - 1][1])
                cp.start()
                three[k, i] = cp
            else:
                own[k, i, f, b] = value.astype(BF16)
    for k in range(1, 4):
        vec[2, k].wait_recv()
    small_out[...] = v_a[0] + v_a[1] + v_a[2] + v_a[3]
    four, five, six = {}, {}, {}

    def piece(aa, bb, cc, i):
        return out.at[cc, aa, bb, i]

    pending = []
    for i in range(parts):
        value = own[0, i, f, b].astype(F32)
        for k in range(1, 4):
            three[k, i].wait_recv()
            value = value + a_in[k - 1, i].astype(F32)
        out[c, a, b, i] = value.astype(BF16)
        mine = piece(a, b, c, i)
        for k in (2, 1, 3):
            cp = remote(mine, mine, s4.at[k - 1, i], r4.at[k - 1, i], apeers[k - 1][1])
            cp.start()
            four[k, i] = cp
        for m, (bb, peer) in enumerate(bpeers):
            cp = remote(mine, mine, s5.at[0, i, m], r5.at[0, i, m], peer)
            cp.start()
            five[0, i, m] = cp
        cp = remote(mine, mine, s6.at[0, i, 0], r6.at[0, i, 0], sibling)
        cp.start()
        six[0, i, 0] = cp
    for i in range(parts):
        for k in (1, 3, 2):
            four[k, i].wait_recv()
            got = piece(lax.rem(a + 4 - k, 4), b, c, i)
            for m, (bb, peer) in enumerate(bpeers):
                cp = remote(got, got, s5.at[k, i, m], r5.at[k, i, m], peer)
                cp.start()
                five[k, i, m] = cp
            cp = remote(got, got, s6.at[k, i, 0], r6.at[k, i, 0], sibling)
            cp.start()
            six[k, i, 0] = cp
    for i in range(parts):
        for k in (0, 1, 3, 2):
            for m in range(cols - 1):
                five[k, i, m].wait_recv()
                got = piece(lax.rem(a + 4 - k, 4), lax.rem(b + cols - (m + 1), cols), c, i)
                cp = remote(got, got, s6.at[k, i, m + 1], r6.at[k, i, m + 1], sibling)
                cp.start()
                six[k, i, m + 1] = cp
    for cp in six.values():
        cp.wait_recv()
    vector.wait_send()
    for group in (cores, one, two, three, four, five, six, vec):
        for cp in group.values():
            cp.wait_send()

def reduce_grads(grads, small, nf, cols, ident):
    _, _, parts, _, _, rows, width = grads.shape
    block = (rows, width)
    m = max(cols - 1, 1)
    n = max((cols - 1) * nf, nf - 1)
    return pl.pallas_call(
        functools.partial(reduce_kernel, nf, cols, parts),
        out_shape=[jax.ShapeDtypeStruct((2, 4, cols, parts) + block, BF16), jax.ShapeDtypeStruct(small.shape[1:], F32)],
        in_specs=[pl.BlockSpec(memory_space=pl.ANY), vmem()], out_specs=[vmem()] * 2,
        scratch_shapes=[pltpu.VMEM((4, parts, nf, cols) + block, BF16), pltpu.VMEM((4, parts, nf, cols) + block, BF16),
                        pltpu.VMEM((4, parts, nf - 1, cols) + block, BF16), pltpu.VMEM((4, parts, m, nf) + block, BF16),
                        pltpu.VMEM((4, parts, nf - 1) + block, BF16), pltpu.VMEM((4, parts, m) + block, BF16),
                        pltpu.VMEM((3, parts) + block, BF16),
                        pltpu.VMEM(small.shape, F32), pltpu.VMEM(small.shape, F32), pltpu.VMEM((nf - 1,) + small.shape[1:], F32),
                        pltpu.VMEM((cols,) + small.shape[1:], F32), pltpu.VMEM((4,) + small.shape[1:], F32),
                        DMA((4, parts)), DMA((4, parts)), DMA((4, parts)), DMA((4, parts, n)), DMA((4, parts, n)),
                        DMA((4, parts, max(m, nf - 1))), DMA((4, parts, max(m, nf - 1))),
                        DMA((3, parts)), DMA((3, parts)), DMA((3, parts)), DMA((3, parts)),
                        DMA((4, parts, m)), DMA((4, parts, m)), DMA((4, parts, cols)), DMA((4, parts, cols)),
                        DMA((nf + cols + 2,)), DMA((nf + cols + 2,))],
        compiler_params=pltpu.CompilerParams(collective_id=ident, has_side_effects=True, vmem_limit_bytes=56 << 20),
        name="reduce_grads",
    )(grads, small)
KB = 256
SPAN = 256
MASKED = -1e30

def dot(x, y, dims):
    return lax.dot_general(x, y, (dims, ((), ())), preferred_element_type=F32)

NT = ((1,), (1,))
NN = ((1,), (0,))
TN = ((0,), (0,))

def bounds(lens, stream):
    ends, total = [], 0
    for j in range(4):
        total = total + lens[stream, j]
        ends.append(total)
    return ends

def doc_range(pos, ends):
    start = jnp.where(pos >= ends[0], ends[0], 0)
    stop = jnp.where(pos < ends[0], ends[0], ends[3])
    for j in (1, 2):
        start = jnp.where(pos >= ends[j], ends[j], start)
    for j in (2, 1, 0):
        stop = jnp.where(pos < ends[j], ends[j], stop)
    return start, stop

def block_range(base, ends):
    low, _ = doc_range(base, ends)
    _, high = doc_range(base + (SPAN - 1), ends)
    return low // KB, (high + (KB - 1)) // KB

def lane_head(shape, shift):
    lane = lax.broadcasted_iota(jnp.int32, shape, 1)
    return (lane - shift) // 64

def forward_kernel(cols, lens, q_ref, kv_ref, o_ref, ot_ref, lse_ref, qm, vt, acc):
    index = lax.axis_index("ctx")
    b, c = lax.rem(index // 2, cols), lax.rem(index, 2)
    ends = bounds(lens, c)
    total = kv_ref.shape[0]

    @pl.loop(0, total // KB)
    def _(n):
        rows = pl.ds(pl.multiple_of(n * KB, KB), KB)
        vt[:, rows] = kv_ref[rows, 128:384].astype(F32).T.astype(BF16)

    @pl.loop(0, 4)
    def _(stripe):
        base = SPAN * (stripe * cols + b)
        rows = pl.ds(pl.multiple_of(stripe * SPAN, SPAN), SPAN)
        head = lane_head((SPAN, 256), 0)
        q = q_ref[rows].astype(F32) * 0.125
        for h in range(3):
            qm[h] = jnp.where(head == h, q, 0.0).astype(BF16)
        qpos = base + lax.broadcasted_iota(jnp.int32, (1, SPAN), 1)
        start, stop = doc_range(qpos, ends)
        low, high = block_range(base, ends)
        acc[...] = jnp.zeros_like(acc)

        def step(n, state):
            krows = pl.ds(pl.multiple_of(n * KB, KB), KB)
            keys = kv_ref[krows, 0:256]
            kpos = n * KB + lax.broadcasted_iota(jnp.int32, (KB, 1), 0)
            allowed = (kpos >= start) & (kpos < stop)
            out = []
            for h in range(3):
                top, tot = state[h]
                s = jnp.where(allowed, dot(keys, qm[h], NT), MASKED)
                new = jnp.maximum(top, jnp.max(s, axis=0, keepdims=True))
                p = jnp.exp(s - new)
                scale = jnp.exp(top - new)
                hrows = pl.ds(64 * (h + 1), 64)
                acc[hrows] = acc[hrows] * scale + dot(vt[hrows, krows], p.astype(BF16), NN)
                out.append((new, tot * scale + jnp.sum(p, axis=0, keepdims=True)))
            return tuple(out)

        first = tuple((jnp.full((1, SPAN), MASKED, F32), jnp.zeros((1, SPAN), F32)) for _ in range(3))
        final = lax.fori_loop(low, high, step, first)
        for h in range(3):
            top, tot = final[h]
            hrows = pl.ds(64 * (h + 1), 64)
            acc[hrows] = acc[hrows] * (1.0 / tot)
            lse_ref[stripe, pl.ds(h, 1)] = top + jnp.log(tot)
        ot_ref[stripe] = acc[...]
        o_ref[rows] = acc[...].T.astype(BF16)

def vmem():
    return pl.BlockSpec(memory_space=pltpu.VMEM)

def attend_forward(lens, q, kv, cols):
    total = kv.shape[0]
    return pl.pallas_call(
        functools.partial(forward_kernel, cols),
        out_shape=[jax.ShapeDtypeStruct(q.shape, BF16), jax.ShapeDtypeStruct((4, 256, SPAN), F32),
                   jax.ShapeDtypeStruct((4, 8, SPAN), F32)],
        in_specs=[pl.BlockSpec(memory_space=pltpu.SMEM), vmem(), vmem()],
        out_specs=[vmem()] * 3,
        scratch_shapes=[pltpu.VMEM((3, SPAN, 256), BF16), pltpu.VMEM((256, total), BF16), pltpu.VMEM((256, SPAN), F32)],
        compiler_params=pltpu.CompilerParams(vmem_limit_bytes=32 << 20),
        name="attend_forward",
    )(lens, q, kv)

def backward_kernel(cols, lens, q_ref, kv_ref, do_ref, ot_ref, lse_ref, dq_ref, dkv_ref, qm, dm, kt, dk, dv, acc):
    index = lax.axis_index("ctx")
    b, c = lax.rem(index // 2, cols), lax.rem(index, 2)
    ends = bounds(lens, c)
    total = kv_ref.shape[0]

    @pl.loop(0, total // KB)
    def _(n):
        rows = pl.ds(pl.multiple_of(n * KB, KB), KB)
        kt[:, rows] = kv_ref[rows, 0:256].astype(F32).T.astype(BF16)
        dk[rows] = jnp.zeros((KB, 256), F32)
        dv[rows] = jnp.zeros((KB, 256), F32)

    @pl.loop(0, 4)
    def _(stripe):
        base = SPAN * (stripe * cols + b)
        rows = pl.ds(pl.multiple_of(stripe * SPAN, SPAN), SPAN)
        head = lane_head((SPAN, 256), 0)
        headv = lane_head((SPAN, 256), 64)
        q = q_ref[rows].astype(F32) * 0.125
        grad = do_ref[rows].astype(F32)
        for h in range(3):
            qm[h] = jnp.where(head == h, q, 0.0).astype(BF16)
            dm[h] = jnp.where(headv == h, grad, 0.0).astype(BF16)
        prod = grad.T * ot_ref[stripe]
        deltas = [jnp.sum(prod[64 * (h + 1):64 * (h + 2)], axis=0, keepdims=True) for h in range(3)]
        lses = [lse_ref[stripe, pl.ds(h, 1)] for h in range(3)]
        qpos = base + lax.broadcasted_iota(jnp.int32, (1, SPAN), 1)
        start, stop = doc_range(qpos, ends)
        low, high = block_range(base, ends)
        acc[...] = jnp.zeros_like(acc)

        @pl.loop(low, high)
        def _(n):
            krows = pl.ds(pl.multiple_of(n * KB, KB), KB)
            keys = kv_ref[krows, 0:256]
            vals = kv_ref[krows, 128:384]
            kpos = n * KB + lax.broadcasted_iota(jnp.int32, (KB, 1), 0)
            allowed = (kpos >= start) & (kpos < stop)
            newk, newv = dk[krows], dv[krows]
            for h in range(3):
                s = jnp.where(allowed, dot(keys, qm[h], NT), MASKED)
                p = jnp.exp(s - lses[h])
                gp = dot(vals, dm[h], NT)
                ds = (p * (gp - deltas[h])).astype(BF16)
                newv = newv + dot(p.astype(BF16), dm[h], NN)
                newk = newk + dot(ds, qm[h], NN)
                hrows = pl.ds(64 * h, 64)
                acc[hrows] = acc[hrows] + dot(kt[hrows, krows], ds, NN)
            dk[krows] = newk
            dv[krows] = newv

        dq_ref[rows] = (acc[...] * 0.125).T.astype(BF16)

    @pl.loop(0, total // KB)
    def _(n):
        rows = pl.ds(pl.multiple_of(n * KB, KB), KB)
        dkv_ref[rows, 0:128] = dk[rows, 0:128].astype(BF16)
        dkv_ref[rows, 128:256] = (dk[rows, 128:256] + dv[rows, 0:128]).astype(BF16)
        dkv_ref[rows, 256:384] = dv[rows, 128:256].astype(BF16)

def attend_backward(lens, q, kv, do, ot, lse, cols):
    total = kv.shape[0]
    return pl.pallas_call(
        functools.partial(backward_kernel, cols),
        out_shape=[jax.ShapeDtypeStruct(q.shape, BF16), jax.ShapeDtypeStruct(kv.shape, BF16)],
        in_specs=[pl.BlockSpec(memory_space=pltpu.SMEM)] + [vmem()] * 5,
        out_specs=[vmem()] * 2,
        scratch_shapes=[pltpu.VMEM((3, SPAN, 256), BF16), pltpu.VMEM((3, SPAN, 256), BF16), pltpu.VMEM((256, total), BF16),
                        pltpu.VMEM((total, 256), F32), pltpu.VMEM((total, 256), F32), pltpu.VMEM((256, SPAN), F32)],
        compiler_params=pltpu.CompilerParams(vmem_limit_bytes=40 << 20),
        name="attend_backward",
    )(lens, q, kv, do, ot, lse)


def layer_norm(values, gain_row, shift_row):
    average = jnp.mean(values, axis=-1, keepdims=True)
    centered = values - average
    variance = jnp.mean(centered * centered, axis=-1, keepdims=True)
    return centered * lax.rsqrt(variance + EPSILON) * gain_row + shift_row


def exact_gelu(values):
    return jax.nn.gelu(values, approximate=False)


def by_group(rows, micro, front, back):
    parts = rows.reshape(micro, -1, 4, 192).transpose(2, 0, 1, 3)
    parts = jnp.pad(parts, ((0, 0), (0, 0), (0, 0), (front, back)))
    return parts.reshape((-1,) + parts.shape[2:])


def from_group(blocks, micro, front):
    rows = blocks.shape[1]
    parts = blocks.reshape(4, micro, rows, -1)[..., front:front + 192]
    return parts.transpose(1, 2, 0, 3).reshape(micro * rows, 768)


def shards(tokens, cotangent, doc_lengths, w_qkv, w_out, w_in, w_back, *vectors):
    micro, per, width = tokens.shape
    nf, cols = lax.axis_size("fsdp"), lax.axis_size("ctx") // 8
    share = width // nf
    tiny = jnp.concatenate(vectors).reshape(8, -1)
    full_qkv, full_out, full_in, full_back, tinies = gather_weights((w_qkv, w_out, w_in, w_back), tiny, nf, cols)
    tinies = tinies.reshape(nf, -1).astype(F32)
    named, at = [], 0
    for vector in vectors:
        size = vector.shape[0]
        named.append(tinies[:, at:at + size].reshape(-1))
        at += size
    b_query, b_value, b_out, b_in, b_back, gain_one, shift_one, gain_two, shift_two = named
    inputs = tokens.reshape(micro * per, width)
    joined = jnp.dot(inputs, full_qkv, preferred_element_type=F32)
    bias = jnp.concatenate([b_query, jnp.zeros_like(b_query), b_value])
    joined = (joined + bias).astype(BF16)
    q_sent = by_group(joined[:, :width], micro, 0, 64)
    kv_sent = jnp.concatenate([by_group(joined[:, width:2 * width], micro, 0, 0), by_group(joined[:, 2 * width:], micro, 0, 0)], axis=2)
    q_held, kv_held = spread(q_sent, kv_sent, cols, 2)
    q_held = q_held.reshape(8 * per, 256)
    kv_held = kv_held.reshape(-1, 384)
    mixed, mixed_t, log_total = attend_forward(doc_lengths, q_held, kv_held, cols)
    (back,) = swap([mixed.reshape(8, per, 256)], cols, 3)
    attended = from_group(back, micro, 64)
    first_sum = inputs.astype(F32) + (jnp.dot(attended, full_out, preferred_element_type=F32) + b_out)
    normed = layer_norm(first_sum, gain_one, shift_one)
    normed_low = normed.astype(BF16)
    hidden = jnp.dot(normed_low, full_in, preferred_element_type=F32) + b_in
    activated = exact_gelu(hidden).astype(BF16)
    final_sum = normed + (jnp.dot(activated, full_back, preferred_element_type=F32) + b_back)
    output = layer_norm(final_sum, gain_two, shift_two).astype(BF16)

    upstream = cotangent.reshape(micro * per, width).astype(F32)
    grad_final, g_gain_two, g_shift_two = jax.vjp(layer_norm, final_sum, gain_two, shift_two)[1](upstream)
    grad_second = grad_final.astype(BF16)
    g_back_bias = jnp.sum(grad_second.astype(F32), axis=0)
    grad_activated = jnp.einsum("rm,km->rk", grad_second, full_back, preferred_element_type=F32)
    grad_hidden = jax.vjp(exact_gelu, hidden)[1](grad_activated)[0].astype(BF16)
    g_in_bias = jnp.sum(grad_hidden.astype(F32), axis=0)
    grad_normed = grad_final + jnp.einsum("rf,mf->rm", grad_hidden, full_in, preferred_element_type=F32)
    grad_first, g_gain_one, g_shift_one = jax.vjp(layer_norm, first_sum, gain_one, shift_one)[1](grad_normed)
    grad_branch = grad_first.astype(BF16)
    g_out_bias = jnp.sum(grad_branch.astype(F32), axis=0)
    grad_attended = jnp.einsum("rm,km->rk", grad_branch, full_out, preferred_element_type=F32).astype(BF16)
    (do_held,) = swap([by_group(grad_attended, micro, 64, 0)], cols, 4)
    dq, dkv = attend_backward(doc_lengths, q_held, kv_held, do_held.reshape(8 * per, 256), mixed_t, log_total, cols)
    dq_own, dkv_own = collect(dq.reshape(8, per, 256), dkv.reshape(8 * cols, per, 384), cols, 5)
    grad_joined = jnp.concatenate(
        [from_group(dq_own, micro, 0), from_group(dkv_own, micro, 0), from_group(dkv_own, micro, 192)], axis=1)
    g_query_bias = jnp.sum(grad_joined[:, :width].astype(F32), axis=0)
    g_value_bias = jnp.sum(grad_joined[:, 2 * width:].astype(F32), axis=0)
    input_grad = grad_first + jnp.einsum("rc,mc->rm", grad_joined, full_qkv, preferred_element_type=F32)

    def halves(left, right):
        blocks = right.shape[1] // 384
        return jnp.einsum("rm,rhc->hmc", left, right.reshape(-1, blocks, 384), preferred_element_type=F32).astype(BF16)

    back_grads = jnp.einsum("rk,rm->km", activated, grad_second, preferred_element_type=F32).astype(BF16)
    back_grads = back_grads.reshape(nf, 4, share, 2, 384).transpose(1, 3, 0, 2, 4).reshape(8, width, 384)
    grads = jnp.concatenate(
        [halves(inputs, grad_joined), halves(attended, grad_branch), halves(normed_low, grad_hidden), back_grads])
    grads = grads.reshape(2, 4, 3, nf, cols, share // cols, 384)
    small = (g_query_bias, g_value_bias, g_out_bias, g_in_bias, g_back_bias, g_gain_one, g_shift_one, g_gain_two, g_shift_two)
    small = jnp.concatenate([x.reshape(nf, -1) for x in small], axis=1).reshape(nf, 8, -1)
    owned, small_owned = reduce_grads(grads, small, nf, cols, 6)
    owned = owned.transpose(0, 1, 3, 2, 4, 5).reshape(24, share, 384)

    def columns(first, last):
        return owned[first:last].transpose(1, 0, 2).reshape(share, -1).astype(F32)

    g_back = owned[16:].reshape(4, 2, share, 384).transpose(0, 2, 1, 3).reshape(4 * share, width).astype(F32)
    small_owned = small_owned.reshape(-1)
    small_grads, at = [], 0
    for vector in vectors:
        small_grads.append(small_owned[at:at + vector.shape[0]])
        at += vector.shape[0]
    return (output.reshape(tokens.shape), input_grad.reshape(tokens.shape), columns(0, 6), columns(6, 8), columns(8, 16), g_back) + tuple(small_grads)


def solution(mesh):
    rows, flat = P("fsdp", "ctx", None), P("fsdp", None)
    return jax.shard_map(
        shards,
        mesh=mesh,
        in_specs=(rows, rows, flat) + (flat,) * 4 + (P("fsdp"),) * 9,
        out_specs=(rows, rows) + (flat,) * 4 + (P("fsdp"),) * 9,
        check_vma=False,
    )
```

```python
import functools

import jax
import jax.numpy as jnp
from jax import lax
from jax.experimental import pallas as pl
from jax.experimental.pallas import tpu as pltpu
from jax.sharding import PartitionSpec as P

MESH = pl.DeviceIdType.MESH
DMA = pltpu.SemaphoreType.DMA
F32, BF16 = jnp.float32, jnp.bfloat16
EPSILON = 1e-12

def place(cols):
    index = lax.axis_index("ctx")
    return index // (2 * cols), lax.rem(index // 2, cols), lax.rem(index, 2), lax.axis_index("fsdp")

def device(a, b, c, f, cols):
    return {"ctx": (a * cols + b) * 2 + c, "fsdp": f}

def meet(peers):
    barrier = pltpu.get_barrier_semaphore()
    for peer in peers:
        pl.semaphore_signal(barrier, inc=1, device_id=peer, device_id_type=MESH)
    pl.semaphore_wait(barrier, len(peers))

def remote(source, target, send, recv, peer):
    return pltpu.make_async_remote_copy(
        src_ref=source, dst_ref=target, send_sem=send, recv_sem=recv, device_id=peer, device_id_type=MESH)

def gather_kernel(nf, cols, count, *refs):
    shards, tiny, fulls, tiny_out = refs[:count], refs[count], refs[count+1:2*count+1], refs[2*count+1]
    local_sem, s1, r1, s2, r2, s3, r3, st, rt = refs[2*count+2:]
    a, b, c, f = place(cols)
    other = 1 - c
    fpeers = [device(a, b, c, lax.rem(f + j, nf), cols) for j in range(1, nf)]
    bpeers = [device(a, lax.rem(b + k, cols), c, f, cols) for k in range(1, cols)]
    sibling = device(a, b, other, f, cols)
    meet(fpeers + bpeers + [sibling])

    def view(w, owner, bb, cc, base=0):
        rows, wide = shards[w].shape
        part, half = rows // cols, wide // 2
        return fulls[w].at[pl.ds(pl.multiple_of(owner * rows + bb * part, 8), part), pl.ds(pl.multiple_of(cc * half, 128), half)]

    waits = []
    for j in range(1, nf):
        cp = remote(tiny, tiny_out.at[f], st.at[j - 1], rt.at[j - 1], fpeers[j - 1])
        cp.start()
        waits.append(cp)
    locals_ = [pltpu.make_async_copy(tiny, tiny_out.at[f], local_sem.at[count])]
    locals_[0].start()
    first = {}
    for w in range(count):
        rows, wide = shards[w].shape
        part, half = rows // cols, wide // 2
        mine = shards[w].at[pl.ds(pl.multiple_of(b * part, 8), part), pl.ds(pl.multiple_of(c * half, 128), half)]
        for j in range(1, nf):
            cp = remote(mine, view(w, f, b, c), s1.at[w, j - 1], r1.at[w, j - 1], fpeers[j - 1])
            cp.start()
            first[w, j] = cp
    for w in range(count):
        rows = shards[w].shape[0]
        cp = pltpu.make_async_copy(shards[w], fulls[w].at[pl.ds(pl.multiple_of(f * rows, 8), rows)], local_sem.at[w])
        cp.start()
        locals_.append(cp)
    second, third = {}, []
    for w in range(count):
        for j in range(1, nf):
            owner = lax.rem(f + nf - j, nf)
            first[w, j].wait_recv()
            piece = view(w, owner, b, c)
            for k in range(1, cols):
                slot = (j - 1) * (cols - 1) + k - 1
                cp = remote(piece, piece, s2.at[w, slot], r2.at[w, slot], bpeers[k - 1])
                cp.start()
                second[w, j, k] = cp
            cp = remote(piece, piece, s3.at[w, (j - 1) * cols], r3.at[w, (j - 1) * cols], sibling)
            cp.start()
            third.append(cp)
    for w in range(count):
        for j in range(1, nf):
            owner = lax.rem(f + nf - j, nf)
            for k in range(1, cols):
                second[w, j, k].wait_recv()
                piece = view(w, owner, lax.rem(b + cols - k, cols), c)
                cp = remote(piece, piece, s3.at[w, (j - 1) * cols + k], r3.at[w, (j - 1) * cols + k], sibling)
                cp.start()
                third.append(cp)
    for cp in third:
        cp.wait_recv()
    for cp in waits:
        cp.wait()
    for cp in list(first.values()) + list(second.values()) + third:
        cp.wait_send()
    for cp in locals_:
        cp.wait()

def gather_weights(shards, tiny, nf, cols):
    count = len(shards)
    any_spec = pl.BlockSpec(memory_space=pl.ANY)
    dma = pltpu.SemaphoreType.DMA
    return pl.pallas_call(
        functools.partial(gather_kernel, nf, cols, count),
        out_shape=[jax.ShapeDtypeStruct((s.shape[0] * nf, s.shape[1]), s.dtype) for s in shards]
        + [jax.ShapeDtypeStruct((nf,) + tiny.shape, tiny.dtype)],
        in_specs=[pl.BlockSpec(memory_space=pltpu.VMEM)] * (count + 1),
        out_specs=[any_spec] * (count + 1),
        scratch_shapes=[dma((count + 1,)), dma((count, nf - 1)), dma((count, nf - 1)),
                        dma((count, (nf - 1) * (cols - 1))), dma((count, (nf - 1) * (cols - 1))),
                        dma((count, (nf - 1) * cols)), dma((count, (nf - 1) * cols)),
                        dma((nf - 1,)), dma((nf - 1,))],
        compiler_params=pltpu.CompilerParams(collective_id=1, has_side_effects=True, vmem_limit_bytes=32 << 20),
        name="gather_weights",
    )(*shards, tiny)

def octet(a, b, c, f, cols):
    me = a * 2 + c
    out = []
    for k in range(1, 8):
        other = lax.rem(me + k, 8)
        out.append((other, device(other // 2, b, lax.rem(other, 2), f, cols)))
    return me, out

def swap_kernel(cols, count, *refs):
    sources, targets = refs[:count], refs[count:2 * count]
    send, recv, here = refs[2 * count:]
    a, b, c, f = place(cols)
    me, peers = octet(a, b, c, f, cols)
    meet([p for _, p in peers])
    copies = []
    for k, (other, peer) in enumerate(peers):
        for i in range(count):
            cp = remote(sources[i].at[other], targets[i].at[me], send.at[i, k], recv.at[i, k], peer)
            cp.start()
            copies.append(cp)
    for i in range(count):
        cp = pltpu.make_async_copy(sources[i].at[me], targets[i].at[me], here.at[i])
        cp.start()
        copies.append(cp)
    for cp in copies:
        cp.wait()

def swap(arrays, cols, ident):
    count = len(arrays)
    return pl.pallas_call(
        functools.partial(swap_kernel, cols, count),
        out_shape=[jax.ShapeDtypeStruct(x.shape, x.dtype) for x in arrays],
        in_specs=[vmem()] * count, out_specs=[vmem()] * count,
        scratch_shapes=[DMA((count, 7)), DMA((count, 7)), DMA((count,))],
        compiler_params=pltpu.CompilerParams(collective_id=ident, has_side_effects=True, vmem_limit_bytes=16 << 20),
        name="swap",
    )(*arrays)

def spread_kernel(cols, q, kv, qg, full, sq, rq, sk, rk, s2, r2, here):
    a, b, c, f = place(cols)
    me, peers = octet(a, b, c, f, cols)
    bpeers = [device(a, lax.rem(b + k, cols), c, f, cols) for k in range(1, cols)]
    meet([p for _, p in peers] + bpeers)

    def slot(block, bb):
        return (block // 2 * cols + bb) * 2 + lax.rem(block, 2)

    first = []
    for k, (other, peer) in enumerate(peers):
        cp = remote(kv.at[other], full.at[slot(me, b)], sk.at[k], rk.at[k], peer)
        cp.start()
        first.append(cp)
    own = pltpu.make_async_copy(kv.at[me], full.at[slot(me, b)], here.at[0])
    own.start()
    ownq = pltpu.make_async_copy(q.at[me], qg.at[me], here.at[1])
    ownq.start()
    second = []
    for k, peer in enumerate(bpeers):
        cp = remote(kv.at[me], full.at[slot(me, b)], s2.at[7, k], r2.at[7, k], peer)
        cp.start()
        second.append(cp)
    third = []
    for k, (other, peer) in enumerate(peers):
        cp = remote(q.at[other], qg.at[me], sq.at[k], rq.at[k], peer)
        cp.start()
        third.append(cp)
    for k in range(7):
        first[k].wait_recv()
        source = lax.rem(me + 8 - (k + 1), 8)
        piece = full.at[slot(source, b)]
        for m, peer in enumerate(bpeers):
            cp = remote(piece, piece, s2.at[k, m], r2.at[k, m], peer)
            cp.start()
            second.append(cp)
    for cp in first:
        cp.wait_send()
    for cp in second + third:
        cp.wait()
    own.wait()
    ownq.wait()

def spread(q, kv, cols, ident):
    return pl.pallas_call(
        functools.partial(spread_kernel, cols),
        out_shape=[jax.ShapeDtypeStruct(q.shape, q.dtype), jax.ShapeDtypeStruct((8 * cols,) + kv.shape[1:], kv.dtype)],
        in_specs=[vmem()] * 2, out_specs=[vmem()] * 2,
        scratch_shapes=[DMA((7,))] * 4 + [DMA((8, max(cols - 1, 1)))] * 2 + [DMA((2,))],
        compiler_params=pltpu.CompilerParams(collective_id=ident, has_side_effects=True, vmem_limit_bytes=16 << 20),
        name="spread",
    )(q, kv)

def collect_kernel(cols, dq, dkv, dqo, dkvo, rbuf, total, sq, rq, sk, rk, s2, r2, here):
    a, b, c, f = place(cols)
    me, peers = octet(a, b, c, f, cols)
    bpeers = [(lax.rem(b + k, cols), device(a, lax.rem(b + k, cols), c, f, cols)) for k in range(1, cols)]
    meet([p for _, p in peers] + [p for _, p in bpeers])

    def slot(block, bb):
        return (block // 2 * cols + bb) * 2 + lax.rem(block, 2)

    order = [other for other, _ in peers] + [me]
    first = {}
    for n, block in enumerate(order):
        for k, (bb, peer) in enumerate(bpeers):
            cp = remote(dkv.at[slot(block, bb)], rbuf.at[k, n], s2.at[k, n], r2.at[k, n], peer)
            cp.start()
            first[k, n] = cp
    rest = []
    for k, (other, peer) in enumerate(peers):
        cp = remote(dq.at[other], dqo.at[me], sq.at[k], rq.at[k], peer)
        cp.start()
        rest.append(cp)
    own = pltpu.make_async_copy(dq.at[me], dqo.at[me], here.at[0])
    own.start()
    for n, block in enumerate(order):
        value = dkv[slot(block, b)].astype(F32)
        for k in range(cols - 1):
            first[k, n].wait_recv()
            value = value + rbuf[k, n].astype(F32)
        if n < 7:
            total[n] = value.astype(BF16)
            cp = remote(total.at[n], dkvo.at[me], sk.at[n], rk.at[n], peers[n][1])
            cp.start()
            rest.append(cp)
        else:
            dkvo[me] = value.astype(BF16)
    for cp in first.values():
        cp.wait_send()
    for cp in rest:
        cp.wait()
    own.wait()

def collect(dq, dkv, cols, ident):
    block = dkv.shape[1:]
    return pl.pallas_call(
        functools.partial(collect_kernel, cols),
        out_shape=[jax.ShapeDtypeStruct(dq.shape, dq.dtype), jax.ShapeDtypeStruct((8,) + block, dkv.dtype)],
        in_specs=[vmem()] * 2, out_specs=[vmem()] * 2,
        scratch_shapes=[pltpu.VMEM((max(cols - 1, 1), 8) + block, BF16), pltpu.VMEM((7,) + block, BF16)]
        + [DMA((7,))] * 4 + [DMA((max(cols - 1, 1), 8))] * 2 + [DMA((1,))],
        compiler_params=pltpu.CompilerParams(collective_id=ident, has_side_effects=True, vmem_limit_bytes=24 << 20),
        name="collect",
    )(dq, dkv)

def reduce_kernel(nf, cols, parts, grads, small, out, small_out, *refs):
    own, core_in, f_in, b_in, f_in2, b_in2, a_in, v_core, v_sum, v_f, v_b, v_a = refs[:12]
    load, sc, rc, s1, r1, s2, r2, s3, r3, s4, r4, s5, r5, s6, r6, sv, rv = refs[12:]
    a, b, c, f = place(cols)
    rows = grads.shape[5]
    fpeers = [(lax.rem(f + j, nf), device(a, b, c, lax.rem(f + j, nf), cols)) for j in range(1, nf)]
    bpeers = [(lax.rem(b + k, cols), device(a, lax.rem(b + k, cols), c, f, cols)) for k in range(1, cols)]
    apeers = [(lax.rem(a + k, 4), device(lax.rem(a + k, 4), b, c, f, cols)) for k in range(1, 4)]
    sibling = device(a, b, 1 - c, f, cols)
    meet([p for _, p in fpeers + bpeers + apeers] + [sibling])
    vector = remote(small, v_core, sv.at[0], rv.at[0], sibling)
    vector.start()
    order = [2, 1, 3, 0]
    dest = {k: lax.rem(a + k, 4) for k in range(4)}
    by_f = {k: k in (1, 2) for k in range(4)}
    loads, cores = {}, {}
    for k in order:
        for i in range(parts):
            cp = pltpu.make_async_copy(grads.at[c, dest[k], i], own.at[k, i], load.at[k, i])
            cp.start()
            loads[k, i] = cp
            cp = remote(grads.at[1 - c, dest[k], i], core_in.at[k, i], sc.at[k, i], rc.at[k, i], sibling)
            cp.start()
            cores[k, i] = cp
    one, two, three = {}, {}, {}
    vec = {}
    vector.wait_recv()
    v_sum[...] = small[...] + v_core[...]
    for j, (ff, peer) in enumerate(fpeers):
        vec[0, j] = remote(v_sum.at[ff], v_f.at[j], sv.at[1 + j], rv.at[1 + j], peer)
        vec[0, j].start()
    for k in order:
        for i in range(parts):
            loads[k, i].wait()
            cores[k, i].wait_recv()

            @pl.loop(0, nf * cols)
            def _(n):
                ff, bb = n // cols, lax.rem(n, cols)
                own[k, i, ff, bb] = (own[k, i, ff, bb].astype(F32) + core_in[k, i, ff, bb].astype(F32)).astype(BF16)

            if by_f[k]:
                for j, (ff, peer) in enumerate(fpeers):
                    cp = remote(own.at[k, i, ff], f_in.at[k, i, j], s1.at[k, i, j], r1.at[k, i, j], peer)
                    cp.start()
                    one[k, i, j] = cp
            else:
                for m, (bb, peer) in enumerate(bpeers):
                    for ff in range(nf):
                        cp = remote(own.at[k, i, ff, bb], b_in.at[k, i, m, ff], s1.at[k, i, m * nf + ff], r1.at[k, i, m * nf + ff], peer)
                        cp.start()
                        one[k, i, m * nf + ff] = cp
    value = v_sum[f]
    for j in range(nf - 1):
        vec[0, j].wait_recv()
        value = value + v_f[j]
    v_b[b] = value
    for m, (bb, peer) in enumerate(bpeers):
        vec[1, m] = remote(v_b.at[b], v_b.at[b], sv.at[nf + m], rv.at[nf + m], peer)
        vec[1, m].start()
    for k in order:
        for i in range(parts):
            if by_f[k]:
                for j in range(nf - 1):
                    one[k, i, j].wait_recv()

                @pl.loop(0, cols)
                def _(bb):
                    value = own[k, i, f, bb].astype(F32)
                    for j in range(nf - 1):
                        value = value + f_in[k, i, j, bb].astype(F32)
                    own[k, i, f, bb] = value.astype(BF16)

                for m, (bb, peer) in enumerate(bpeers):
                    cp = remote(own.at[k, i, f, bb], b_in2.at[k, i, m], s2.at[k, i, m], r2.at[k, i, m], peer)
                    cp.start()
                    two[k, i, m] = cp
            else:
                for m in range(cols - 1):
                    for ff in range(nf):
                        one[k, i, m * nf + ff].wait_recv()

                @pl.loop(0, nf)
                def _(ff):
                    value = own[k, i, ff, b].astype(F32)
                    for m in range(cols - 1):
                        value = value + b_in[k, i, m, ff].astype(F32)
                    own[k, i, ff, b] = value.astype(BF16)

                for j, (ff, peer) in enumerate(fpeers):
                    cp = remote(own.at[k, i, ff, b], f_in2.at[k, i, j], s2.at[k, i, j], r2.at[k, i, j], peer)
                    cp.start()
                    two[k, i, j] = cp
    for m in range(cols - 1):
        vec[1, m].wait_recv()
    value = v_b[0]
    for m in range(1, cols):
        value = value + v_b[m]
    v_a[a] = value
    for k in range(1, 4):
        vec[2, k] = remote(v_a.at[a], v_a.at[a], sv.at[nf + cols + k - 2], rv.at[nf + cols + k - 2], apeers[k - 1][1])
        vec[2, k].start()
    for k in order:
        for i in range(parts):
            value = own[k, i, f, b].astype(F32)
            if by_f[k]:
                for m in range(cols - 1):
                    two[k, i, m].wait_recv()
                    value = value + b_in2[k, i, m].astype(F32)
            else:
                for j in range(nf - 1):
                    two[k, i, j].wait_recv()
                    value = value + f_in2[k, i, j].astype(F32)
            if k != 0:
                own[k, i, f, b] = value.astype(BF16)
                cp = remote(own.at[k, i, f, b], a_in.at[k - 1, i], s3.at[k - 1, i], r3.at[k - 1, i], apeers[k - 1][1])
                cp.start()
                three[k, i] = cp
            else:
                own[k, i, f, b] = value.astype(BF16)
    for k in range(1, 4):
        vec[2, k].wait_recv()
    small_out[...] = v_a[0] + v_a[1] + v_a[2] + v_a[3]
    four, five, six = {}, {}, {}

    def piece(aa, bb, cc, i):
        return out.at[cc, aa, bb, i]

    pending = []
    for i in range(parts):
        value = own[0, i, f, b].astype(F32)
        for k in range(1, 4):
            three[k, i].wait_recv()
            value = value + a_in[k - 1, i].astype(F32)
        out[c, a, b, i] = value.astype(BF16)
        mine = piece(a, b, c, i)
        for k in (2, 1, 3):
            cp = remote(mine, mine, s4.at[k - 1, i], r4.at[k - 1, i], apeers[k - 1][1])
            cp.start()
            four[k, i] = cp
        for m, (bb, peer) in enumerate(bpeers):
            cp = remote(mine, mine, s5.at[0, i, m], r5.at[0, i, m], peer)
            cp.start()
            five[0, i, m] = cp
        cp = remote(mine, mine, s6.at[0, i, 0], r6.at[0, i, 0], sibling)
        cp.start()
        six[0, i, 0] = cp
    for i in range(parts):
        for k in (1, 3, 2):
            four[k, i].wait_recv()
            got = piece(lax.rem(a + 4 - k, 4), b, c, i)
            for m, (bb, peer) in enumerate(bpeers):
                cp = remote(got, got, s5.at[k, i, m], r5.at[k, i, m], peer)
                cp.start()
                five[k, i, m] = cp
            cp = remote(got, got, s6.at[k, i, 0], r6.at[k, i, 0], sibling)
            cp.start()
            six[k, i, 0] = cp
    for i in range(parts):
        for k in (0, 1, 3, 2):
            for m in range(cols - 1):
                five[k, i, m].wait_recv()
                got = piece(lax.rem(a + 4 - k, 4), lax.rem(b + cols - (m + 1), cols), c, i)
                cp = remote(got, got, s6.at[k, i, m + 1], r6.at[k, i, m + 1], sibling)
                cp.start()
                six[k, i, m + 1] = cp
    for cp in six.values():
        cp.wait_recv()
    vector.wait_send()
    for group in (cores, one, two, three, four, five, six, vec):
        for cp in group.values():
            cp.wait_send()

def reduce_grads(grads, small, nf, cols, ident):
    _, _, parts, _, _, rows, width = grads.shape
    block = (rows, width)
    m = max(cols - 1, 1)
    n = max((cols - 1) * nf, nf - 1)
    return pl.pallas_call(
        functools.partial(reduce_kernel, nf, cols, parts),
        out_shape=[jax.ShapeDtypeStruct((2, 4, cols, parts) + block, BF16), jax.ShapeDtypeStruct(small.shape[1:], F32)],
        in_specs=[pl.BlockSpec(memory_space=pl.ANY), vmem()], out_specs=[vmem()] * 2,
        scratch_shapes=[pltpu.VMEM((4, parts, nf, cols) + block, BF16), pltpu.VMEM((4, parts, nf, cols) + block, BF16),
                        pltpu.VMEM((4, parts, nf - 1, cols) + block, BF16), pltpu.VMEM((4, parts, m, nf) + block, BF16),
                        pltpu.VMEM((4, parts, nf - 1) + block, BF16), pltpu.VMEM((4, parts, m) + block, BF16),
                        pltpu.VMEM((3, parts) + block, BF16),
                        pltpu.VMEM(small.shape, F32), pltpu.VMEM(small.shape, F32), pltpu.VMEM((nf - 1,) + small.shape[1:], F32),
                        pltpu.VMEM((cols,) + small.shape[1:], F32), pltpu.VMEM((4,) + small.shape[1:], F32),
                        DMA((4, parts)), DMA((4, parts)), DMA((4, parts)), DMA((4, parts, n)), DMA((4, parts, n)),
                        DMA((4, parts, max(m, nf - 1))), DMA((4, parts, max(m, nf - 1))),
                        DMA((3, parts)), DMA((3, parts)), DMA((3, parts)), DMA((3, parts)),
                        DMA((4, parts, m)), DMA((4, parts, m)), DMA((4, parts, cols)), DMA((4, parts, cols)),
                        DMA((nf + cols + 2,)), DMA((nf + cols + 2,))],
        compiler_params=pltpu.CompilerParams(collective_id=ident, has_side_effects=True, vmem_limit_bytes=56 << 20),
        name="reduce_grads",
    )(grads, small)
KB = 256
SPAN = 256
MASKED = -1e30

def dot(x, y, dims):
    return lax.dot_general(x, y, (dims, ((), ())), preferred_element_type=F32)

NT = ((1,), (1,))
NN = ((1,), (0,))
TN = ((0,), (0,))

def bounds(lens, stream):
    ends, total = [], 0
    for j in range(4):
        total = total + lens[stream, j]
        ends.append(total)
    return ends

def doc_range(pos, ends):
    start = jnp.where(pos >= ends[0], ends[0], 0)
    stop = jnp.where(pos < ends[0], ends[0], ends[3])
    for j in (1, 2):
        start = jnp.where(pos >= ends[j], ends[j], start)
    for j in (2, 1, 0):
        stop = jnp.where(pos < ends[j], ends[j], stop)
    return start, stop

def block_range(base, ends):
    low, _ = doc_range(base, ends)
    _, high = doc_range(base + (SPAN - 1), ends)
    return low // KB, (high + (KB - 1)) // KB

def lane_head(shape, shift):
    lane = lax.broadcasted_iota(jnp.int32, shape, 1)
    return (lane - shift) // 64

def forward_kernel(cols, lens, q_ref, kv_ref, o_ref, ot_ref, lse_ref, qm, vt, acc):
    index = lax.axis_index("ctx")
    b, c = lax.rem(index // 2, cols), lax.rem(index, 2)
    ends = bounds(lens, c)
    total = kv_ref.shape[0]

    @pl.loop(0, total // KB)
    def _(n):
        rows = pl.ds(pl.multiple_of(n * KB, KB), KB)
        vt[:, rows] = kv_ref[rows, 128:384].astype(F32).T.astype(BF16)

    @pl.loop(0, 4)
    def _(stripe):
        base = SPAN * (stripe * cols + b)
        rows = pl.ds(pl.multiple_of(stripe * SPAN, SPAN), SPAN)
        head = lane_head((SPAN, 256), 0)
        q = q_ref[rows].astype(F32) * 0.125
        for h in range(3):
            qm[h] = jnp.where(head == h, q, 0.0).astype(BF16)
        qpos = base + lax.broadcasted_iota(jnp.int32, (1, SPAN), 1)
        start, stop = doc_range(qpos, ends)
        low, high = block_range(base, ends)
        acc[...] = jnp.zeros_like(acc)

        def step(n, state):
            krows = pl.ds(pl.multiple_of(n * KB, KB), KB)
            keys = kv_ref[krows, 0:256]
            kpos = n * KB + lax.broadcasted_iota(jnp.int32, (KB, 1), 0)
            allowed = (kpos >= start) & (kpos < stop)
            out = []
            for h in range(3):
                top, tot = state[h]
                s = jnp.where(allowed, dot(keys, qm[h], NT), MASKED)
                new = jnp.maximum(top, jnp.max(s, axis=0, keepdims=True))
                p = jnp.exp(s - new)
                scale = jnp.exp(top - new)
                hrows = pl.ds(64 * (h + 1), 64)
                acc[hrows] = acc[hrows] * scale + dot(vt[hrows, krows], p.astype(BF16), NN)
                out.append((new, tot * scale + jnp.sum(p, axis=0, keepdims=True)))
            return tuple(out)

        first = tuple((jnp.full((1, SPAN), MASKED, F32), jnp.zeros((1, SPAN), F32)) for _ in range(3))
        final = lax.fori_loop(low, high, step, first)
        for h in range(3):
            top, tot = final[h]
            hrows = pl.ds(64 * (h + 1), 64)
            acc[hrows] = acc[hrows] * (1.0 / tot)
            lse_ref[stripe, pl.ds(h, 1)] = top + jnp.log(tot)
        ot_ref[stripe] = acc[...]
        o_ref[rows] = acc[...].T.astype(BF16)

def vmem():
    return pl.BlockSpec(memory_space=pltpu.VMEM)

def attend_forward(lens, q, kv, cols):
    total = kv.shape[0]
    return pl.pallas_call(
        functools.partial(forward_kernel, cols),
        out_shape=[jax.ShapeDtypeStruct(q.shape, BF16), jax.ShapeDtypeStruct((4, 256, SPAN), F32),
                   jax.ShapeDtypeStruct((4, 8, SPAN), F32)],
        in_specs=[pl.BlockSpec(memory_space=pltpu.SMEM), vmem(), vmem()],
        out_specs=[vmem()] * 3,
        scratch_shapes=[pltpu.VMEM((3, SPAN, 256), BF16), pltpu.VMEM((256, total), BF16), pltpu.VMEM((256, SPAN), F32)],
        compiler_params=pltpu.CompilerParams(vmem_limit_bytes=32 << 20),
        name="attend_forward",
    )(lens, q, kv)

def backward_kernel(cols, lens, q_ref, kv_ref, do_ref, ot_ref, lse_ref, dq_ref, dkv_ref, qm, dm, kt, dk, dv, acc):
    index = lax.axis_index("ctx")
    b, c = lax.rem(index // 2, cols), lax.rem(index, 2)
    ends = bounds(lens, c)
    total = kv_ref.shape[0]

    @pl.loop(0, total // KB)
    def _(n):
        rows = pl.ds(pl.multiple_of(n * KB, KB), KB)
        kt[:, rows] = kv_ref[rows, 0:256].astype(F32).T.astype(BF16)
        dk[rows] = jnp.zeros((KB, 256), F32)
        dv[rows] = jnp.zeros((KB, 256), F32)

    @pl.loop(0, 4)
    def _(stripe):
        base = SPAN * (stripe * cols + b)
        rows = pl.ds(pl.multiple_of(stripe * SPAN, SPAN), SPAN)
        head = lane_head((SPAN, 256), 0)
        headv = lane_head((SPAN, 256), 64)
        q = q_ref[rows].astype(F32) * 0.125
        grad = do_ref[rows].astype(F32)
        for h in range(3):
            qm[h] = jnp.where(head == h, q, 0.0).astype(BF16)
            dm[h] = jnp.where(headv == h, grad, 0.0).astype(BF16)
        prod = grad.T * ot_ref[stripe]
        deltas = [jnp.sum(prod[64 * (h + 1):64 * (h + 2)], axis=0, keepdims=True) for h in range(3)]
        lses = [lse_ref[stripe, pl.ds(h, 1)] for h in range(3)]
        qpos = base + lax.broadcasted_iota(jnp.int32, (1, SPAN), 1)
        start, stop = doc_range(qpos, ends)
        low, high = block_range(base, ends)
        acc[...] = jnp.zeros_like(acc)

        @pl.loop(low, high)
        def _(n):
            krows = pl.ds(pl.multiple_of(n * KB, KB), KB)
            keys = kv_ref[krows, 0:256]
            vals = kv_ref[krows, 128:384]
            kpos = n * KB + lax.broadcasted_iota(jnp.int32, (KB, 1), 0)
            allowed = (kpos >= start) & (kpos < stop)
            newk, newv = dk[krows], dv[krows]
            for h in range(3):
                s = jnp.where(allowed, dot(keys, qm[h], NT), MASKED)
                p = jnp.exp(s - lses[h])
                gp = dot(vals, dm[h], NT)
                ds = (p * (gp - deltas[h])).astype(BF16)
                newv = newv + dot(p.astype(BF16), dm[h], NN)
                newk = newk + dot(ds, qm[h], NN)
                hrows = pl.ds(64 * h, 64)
                acc[hrows] = acc[hrows] + dot(kt[hrows, krows], ds, NN)
            dk[krows] = newk
            dv[krows] = newv

        dq_ref[rows] = (acc[...] * 0.125).T.astype(BF16)

    @pl.loop(0, total // KB)
    def _(n):
        rows = pl.ds(pl.multiple_of(n * KB, KB), KB)
        dkv_ref[rows, 0:128] = dk[rows, 0:128].astype(BF16)
        dkv_ref[rows, 128:256] = (dk[rows, 128:256] + dv[rows, 0:128]).astype(BF16)
        dkv_ref[rows, 256:384] = dv[rows, 128:256].astype(BF16)

def attend_backward(lens, q, kv, do, ot, lse, cols):
    total = kv.shape[0]
    return pl.pallas_call(
        functools.partial(backward_kernel, cols),
        out_shape=[jax.ShapeDtypeStruct(q.shape, BF16), jax.ShapeDtypeStruct(kv.shape, BF16)],
        in_specs=[pl.BlockSpec(memory_space=pltpu.SMEM)] + [vmem()] * 5,
        out_specs=[vmem()] * 2,
        scratch_shapes=[pltpu.VMEM((3, SPAN, 256), BF16), pltpu.VMEM((3, SPAN, 256), BF16), pltpu.VMEM((256, total), BF16),
                        pltpu.VMEM((total, 256), F32), pltpu.VMEM((total, 256), F32), pltpu.VMEM((256, SPAN), F32)],
        compiler_params=pltpu.CompilerParams(vmem_limit_bytes=40 << 20),
        name="attend_backward",
    )(lens, q, kv, do, ot, lse)


class Wires:
    def __init__(self, send, recv):
        self.send, self.recv, self.made = send, recv, []

    def go(self, source, target, peer):
        n = len(self.made)
        cp = remote(source, target, self.send.at[n], self.recv.at[n], peer)
        cp.start()
        self.made.append(cp)
        return cp


def transpose_into(target, source, base):
    width = source.shape[1]

    @pl.loop(0, width // 128)
    def _(n):
        at = pl.multiple_of(n * 128, 128)
        target[pl.ds(base + at, 128)] = source[:, pl.ds(at, 128)].astype(F32).T.astype(BF16)


def pair_columns(even, odd, lane, second):
    if second:
        return jnp.where(lane < 192, pltpu.roll(even, 192, 1), odd)
    return jnp.where(lane < 192, even, pltpu.roll(odd, 192, 1))


BLK = 48
Z1, X1, Y1, Z2, Y2, X2 = (0, 1152), (1152, 1920), (1920, 3456), (3456, 3840), (3840, 4224), (4224, 4608)


def gradient_kernel(tok, att, low, act, gbr, ghid, gsec, gfirst, wqkv, small, dq, dkv,
                    out, igrad, small_out,
                    xt, joined, mine, sib, cin, dqo, dkvo, rbuf, total,
                    y8, y4, x8, x4, z4, z1r, zyb, zxb, v_own, v_core, v_f, v_b, v_a, send, recv, here):
    a, b, c, f = place(2)
    me, peers = octet(a, b, c, f, 2)
    xp, yp, sp = device(a, 1 - b, c, f, 2), device(a, b, c, 1 - f, 2), device(a, b, 1 - c, f, 2)
    up, down = lax.rem(a + 1, 4), lax.rem(a + 3, 4)
    upp, downp = device(up, b, c, f, 2), device(down, b, c, f, 2)
    meet([p for _, p in peers] + [xp, yp])
    wires = Wires(send, recv)
    go = wires.go

    order = [other for other, _ in peers] + [me]

    def slot(block, bb):
        return (block // 2 * 2 + bb) * 2 + lax.rem(block, 2)

    crossed = [go(dkv.at[slot(block, 1 - b)], rbuf.at[n], xp) for n, block in enumerate(order)]
    swapped = [go(dq.at[other], dqo.at[me], peer) for other, peer in peers]
    own_q = pltpu.make_async_copy(dq.at[me], dqo.at[me], here.at[0])
    own_q.start()

    transpose_into(xt, att, 0)
    transpose_into(xt, low, 768)
    transpose_into(xt, act, 1536)
    transpose_into(xt, tok, 4608)

    def produce(kind, first, count, part, finish):
        @pl.loop(0, 2 * count)
        def _(n):
            ff, j = lax.rem(n, 2), first + n // 2
            if kind == "out":
                left, right = xt[pl.ds(pl.multiple_of(ff * 384, 128), 384)], gbr[:, pl.ds(pl.multiple_of(part * 384, 128), 384)]
                col = 0
            elif kind == "in":
                left = xt[pl.ds(pl.multiple_of(768 + ff * 384, 128), 384)]
                right = ghid[:, pl.ds(pl.multiple_of(part * 1536 + j * 384, 128), 384)]
                col = pl.multiple_of(384 + j * 384, 128)
            elif kind == "back":
                left = xt[pl.ds(pl.multiple_of(1536 + ff * 1536 + j * 384, 128), 384)]
                right = gsec[:, pl.ds(pl.multiple_of(part * 384, 128), 384)]
                col = pl.multiple_of(1920 + j * 384, 128)
            else:
                left = xt[pl.ds(pl.multiple_of(4608 + ff * 384, 128), 384)]
                right = joined[:, pl.ds(pl.multiple_of(part * 1152 + j * 384, 128), 384)]
                col = pl.multiple_of(3456 + j * 384, 128)
            finish(pl.ds(ff * 2, 2), pl.ds(col, 384), dot(left, right, NN).reshape(2, 4, BLK, 384))

    def keep(rows, cols, value):
        sib[rows, :, :, cols] = value.astype(BF16)

    def join(rows, cols, value):
        mine[rows, :, :, cols] = (value + cin[rows, :, :, cols].astype(F32)).astype(BF16)

    core = {}

    def share(span):
        cols = slice(span[0], span[1])
        core[span] = go(sib.at[:, :, :, cols], cin.at[:, :, :, cols], sp)

    def inside(span, group):
        base = 0
        for member in group:
            if member == span:
                return slice(base, base + span[1] - span[0])
            base += member[1] - member[0]

    YS, XS, ZS, RS = (Y1, Y2), (X1, X2), (Z1, Z2), (Y1, X1, Y2, X2)

    def add(target, source):
        def step(n):
            t, s = target(n), source(n)
            t[...] = (t[...].astype(F32) + s[...].astype(F32)).astype(BF16)
        return step

    def accumulate(target, source, count):
        pl.loop(0, count)(add(target, source))

    def start_y(span):
        cols, own = slice(span[0], span[1]), inside(span, YS)
        return go(mine.at[pl.ds((1 - f) * 2, 2), :, :, cols], y8.at[:, :, :, own], yp)

    def start_x(span):
        cols, own = slice(span[0], span[1]), inside(span, XS)
        return [go(mine.at[ff * 2 + 1 - b, :, :, cols], x8.at[ff, :, :, own], xp) for ff in range(2)]

    def next_y(span, cp):
        cols, own = slice(span[0], span[1]), inside(span, YS)
        cp.wait_recv()
        accumulate(lambda n: mine.at[f * 2 + n // 4, lax.rem(n, 4), :, cols], lambda n: y8.at[n // 4, lax.rem(n, 4), :, own], 8)
        return go(mine.at[f * 2 + 1 - b, :, :, cols], x4.at[:, :, own], xp)

    def next_x(span, cps):
        cols, own = slice(span[0], span[1]), inside(span, XS)
        for cp in cps:
            cp.wait_recv()
        accumulate(lambda n: mine.at[n // 4 * 2 + b, lax.rem(n, 4), :, cols], lambda n: x8.at[n // 4, lax.rem(n, 4), :, own], 8)
        return go(mine.at[(1 - f) * 2 + b, :, :, cols], y4.at[:, :, own], yp)

    def last_y(span, cp):
        cols, own = slice(span[0], span[1]), inside(span, YS)
        cp.wait_recv()
        accumulate(lambda n: mine.at[f * 2 + b, n, :, cols], lambda n: x4.at[n, :, own], 4)

    def last_x(span, cp):
        cols, own = slice(span[0], span[1]), inside(span, XS)
        cp.wait_recv()
        accumulate(lambda n: mine.at[f * 2 + b, n, :, cols], lambda n: y4.at[n, :, own], 4)

    def halves(span):
        tiles = (span[1] - span[0]) // 128
        mid = span[0] + tiles // 2 * 128
        return (span[0], mid), (mid, span[1])

    def landing(span, step, part, small_ring):
        base = inside(span, RS if small_ring else ZS).start - span[0]
        cols = slice(base + part[0], base + part[1])
        return z1r.at[step, :, cols] if small_ring else z4.at[step, :, :, cols]

    def ring_source(aa, part, small_ring):
        cols = slice(part[0], part[1])
        return mine.at[f * 2 + b, aa, :, cols] if small_ring else mine.at[:, aa, :, cols]

    def ring_send(span, step, small_ring):
        lo, hi = halves(span)
        ud, dd = lax.rem(a + 3 - step, 4), lax.rem(a + 1 + step, 4)
        return (go(ring_source(ud, lo, small_ring), landing(span, step, lo, small_ring), upp),
                go(ring_source(dd, hi, small_ring), landing(span, step, hi, small_ring), downp))

    def ring_add(span, step, small_ring, cps):
        lo, hi = halves(span)
        ud, dd = lax.rem(a + 6 - step, 4), lax.rem(a + 2 + step, 4)
        for cp, part, aa in zip(cps, (lo, hi), (ud, dd)):
            cp.wait_recv()
            got = landing(span, step, part, small_ring)
            if small_ring:
                add(lambda n: ring_source(aa, part, True), lambda n: got)(0)
            else:
                cols = slice(part[0], part[1])
                accumulate(lambda n: mine.at[n, aa, :, cols], lambda n: got.at[n], 4)

    def tail_z_y(span):
        cols, own = slice(span[0], span[1]), inside(span, ZS)
        return go(mine.at[pl.ds((1 - f) * 2, 2), a, :, cols], zyb.at[:, :, own], yp)

    def tail_z_x(span, cp):
        cols, own = slice(span[0], span[1]), inside(span, ZS)
        cp.wait_recv()
        accumulate(lambda n: mine.at[f * 2 + n, a, :, cols], lambda n: zyb.at[n, :, own], 2)
        return go(mine.at[f * 2 + 1 - b, a, :, cols], zxb.at[:, own], xp)

    def tail_z_end(span, cp):
        cols, own = slice(span[0], span[1]), inside(span, ZS)
        cp.wait_recv()
        add(lambda n: mine.at[f * 2 + b, a, :, cols], lambda n: zxb.at[:, own])(0)

    produce("out", 0, 1, 1 - c, keep)
    produce("in", 0, 2, 1 - c, keep)
    share(Z1)
    produce("back", 0, 4, 1 - c, keep)
    share(Y1)
    produce("in", 2, 2, 1 - c, keep)
    share(X1)
    core[Z1].wait_recv()
    produce("out", 0, 1, c, join)
    produce("in", 0, 2, c, join)
    z1 = ring_send(Z1, 0, False)
    core[Y1].wait_recv()
    produce("back", 0, 4, c, join)
    y1 = start_y(Y1)
    core[X1].wait_recv()
    produce("in", 2, 2, c, join)

    for n, block in enumerate(order):
        crossed[n].wait_recv()
        value = (dkv[slot(block, b)].astype(F32) + rbuf[n].astype(F32)).astype(BF16)
        if n < 7:
            total[n] = value
            swapped.append(go(total.at[n], dkvo.at[me], peers[n][1]))
        else:
            dkvo[me] = value
    x1 = start_x(X1)

    ring_add(Z1, 0, False, z1)
    z1 = ring_send(Z1, 1, False)
    y1 = next_y(Y1, y1)
    ring_add(Z1, 1, False, z1)
    z1 = ring_send(Z1, 2, False)
    x1 = next_x(X1, x1)

    own_q.wait()
    for cp in swapped:
        cp.wait_recv()
    lane = lax.broadcasted_iota(jnp.int32, (128, 384), 1)
    for s in range(2):
        rows = slice(s * 128, s * 128 + 128)
        for p in range(2):
            even, odd = 4 * p + s, 4 * p + 2 + s
            blank = jnp.zeros((128, 128), F32)
            qe = jnp.concatenate([dqo[even].astype(F32), blank], axis=1)
            qo = jnp.concatenate([dqo[odd].astype(F32), blank], axis=1)
            joined[rows, 384 * p:384 * p + 384] = pair_columns(qe, qo, lane, False).astype(BF16)
            ke, ko = dkvo[even].astype(F32), dkvo[odd].astype(F32)
            joined[rows, 768 + 384 * p:1152 + 384 * p] = pair_columns(ke, ko, lane, False).astype(BF16)
            joined[rows, 1536 + 384 * p:1920 + 384 * p] = pair_columns(ke, ko, lane, True).astype(BF16)
    produce("qkv", 0, 3, 1 - c, keep)
    for span in (Z2, Y2, X2):
        share(span)
    v_own[...] = small[...]
    v_own[0:1] = jnp.sum(joined[:, 0:768].astype(F32), axis=0, keepdims=True)
    v_own[1:2] = jnp.sum(joined[:, 1536:2304].astype(F32), axis=0, keepdims=True)
    vec = go(v_own, v_core, sp)
    for span in (Z2, Y2, X2):
        core[span].wait_recv()
    produce("qkv", 0, 3, c, join)
    z2 = ring_send(Z2, 0, False)
    y2 = start_y(Y2)
    x2 = start_x(X2)

    ring_add(Z1, 2, False, z1)
    z1 = tail_z_y(Z1)
    last_y(Y1, y1)
    y1 = ring_send(Y1, 0, True)
    last_x(X1, x1)
    x1 = ring_send(X1, 0, True)

    @pl.loop(0, 3)
    def _(n):
        rows = pl.ds(pl.multiple_of(n * 256, 256), 256)
        igrad[:, rows] = gfirst[:, rows] + dot(joined[...], wqkv[rows], NT)

    vec.wait_recv()
    v_own2 = v_own[...] + v_core[...]
    v_core[...] = v_own2
    vec = go(v_core.at[:, pl.ds(pl.multiple_of((1 - f) * 384, 128), 384)], v_f, yp)

    z1 = tail_z_x(Z1, z1)
    ring_add(Y1, 0, True, y1)
    y1 = ring_send(Y1, 1, True)
    ring_add(X1, 0, True, x1)
    x1 = ring_send(X1, 1, True)
    ring_add(Z2, 0, False, z2)
    z2 = ring_send(Z2, 1, False)
    y2 = next_y(Y2, y2)
    x2 = next_x(X2, x2)
    vec.wait_recv()
    v_b[b] = v_core[:, pl.ds(pl.multiple_of(f * 384, 128), 384)] + v_f[...]
    vec = go(v_b.at[b], v_b.at[b], xp)
    ring_add(Y1, 1, True, y1)
    y1 = ring_send(Y1, 2, True)
    ring_add(X1, 1, True, x1)
    x1 = ring_send(X1, 2, True)
    ring_add(Z2, 1, False, z2)
    z2 = ring_send(Z2, 2, False)
    tail_z_end(Z1, z1)
    vec.wait_recv()
    v_a[a] = v_b[0] + v_b[1]
    vec = [go(v_a.at[a], v_a.at[a], device(lax.rem(a + k, 4), b, c, f, 2)) for k in range(1, 4)]

    pending = []

    def piece(cc, bb, aa, span):
        return out.at[cc, bb * 4 + aa, :, span[0]:span[1]]

    class Gather:
        def __init__(self, span, first):
            self.span, self.first = span, first
            out[c, b * 4 + a, :, span[0]:span[1]] = mine[f * 2 + b, a, :, span[0]:span[1]]
            self.spread(b, a, span)
            self.ring = self.around(b)
            self.cross = go(piece(c, b, a, span), piece(c, b, a, span), xp)

        def spread(self, bb, aa, span):
            pending.append(go(piece(c, bb, aa, span), piece(c, bb, aa, span), sp))

        def around(self, bb):
            p = piece(c, bb, a, self.span)
            return go(p, p, upp), go(p, p, downp)

        def passed(self, bb, ring):
            lo, hi = halves(self.span)
            ring[0].wait_recv()
            p = piece(c, bb, down, lo)
            first = go(p, p, upp)
            ring[1].wait_recv()
            p = piece(c, bb, up, hi)
            second = go(p, p, downp)
            for aa in (down, up):
                self.spread(bb, aa, self.span)
            return first, second

        def arrived(self, bb, ring):
            for cp in ring:
                cp.wait_recv()
            self.spread(bb, lax.rem(a + 2, 4), self.span)

        def second(self):
            self.ring2 = self.passed(b, self.ring)
            if self.first == "b":
                self.cross.wait_recv()
                self.spread(1 - b, a, self.span)
                self.other = self.around(1 - b)
            else:
                self.more = [go(piece(c, b, aa, self.span), piece(c, b, aa, self.span), xp) for aa in (down, up)]

        def third(self):
            self.arrived(b, self.ring2)
            if self.first == "b":
                self.other2 = self.passed(1 - b, self.other)
            else:
                p = piece(c, b, lax.rem(a + 2, 4), self.span)
                self.more.append(go(p, p, xp))
                self.cross.wait_recv()
                self.spread(1 - b, a, self.span)

        def fourth(self):
            if self.first == "b":
                self.arrived(1 - b, self.other2)
            else:
                for cp, aa in zip(self.more, (down, up, lax.rem(a + 2, 4))):
                    cp.wait_recv()
                    self.spread(1 - b, aa, self.span)

    g_z1 = Gather(Z1, "a")
    ring_add(Y1, 2, True, y1)
    g_y1 = Gather(Y1, "b")
    ring_add(X1, 2, True, x1)
    g_x1 = Gather(X1, "b")
    ring_add(Z2, 2, False, z2)
    z2 = tail_z_y(Z2)
    last_y(Y2, y2)
    y2 = ring_send(Y2, 0, True)
    last_x(X2, x2)
    x2 = ring_send(X2, 0, True)
    g_z1.second()
    z2 = tail_z_x(Z2, z2)
    ring_add(Y2, 0, True, y2)
    y2 = ring_send(Y2, 1, True)
    ring_add(X2, 0, True, x2)
    x2 = ring_send(X2, 1, True)
    g_y1.second()
    g_x1.second()
    tail_z_end(Z2, z2)
    g_z2 = Gather(Z2, "a")
    ring_add(Y2, 1, True, y2)
    y2 = ring_send(Y2, 2, True)
    ring_add(X2, 1, True, x2)
    x2 = ring_send(X2, 2, True)
    g_z1.third()
    ring_add(Y2, 2, True, y2)
    g_y2 = Gather(Y2, "b")
    ring_add(X2, 2, True, x2)
    g_x2 = Gather(X2, "b")
    g_y1.third()
    g_x1.third()
    g_z1.fourth()
    g_z2.second()
    g_y2.second()
    g_x2.second()
    g_y1.fourth()
    g_x1.fourth()
    g_z2.third()
    g_y2.third()
    g_x2.third()
    g_z2.fourth()
    g_y2.fourth()
    g_x2.fourth()
    for cp in vec + pending:
        cp.wait_recv()
    small_out[...] = v_a[0] + v_a[1] + v_a[2] + v_a[3]
    for cp in wires.made:
        cp.wait_send()


def reduce_all(tok, att, low, act, gbr, ghid, gsec, gfirst, wqkv, small, dq, dkv, ident):
    block = (BLK,)
    wires = 192
    return pl.pallas_call(
        gradient_kernel,
        out_shape=[jax.ShapeDtypeStruct((2, 8, BLK, 4608), BF16), jax.ShapeDtypeStruct(gfirst.shape, F32), jax.ShapeDtypeStruct((16, 384), F32)],
        in_specs=[vmem()] * 12, out_specs=[vmem()] * 3,
        scratch_shapes=[
            pltpu.VMEM((5376, 256), BF16), pltpu.VMEM((256, 2304), BF16),
            pltpu.VMEM((4, 4, BLK, 4608), BF16), pltpu.VMEM((4, 4, BLK, 4608), BF16), pltpu.VMEM((4, 4, BLK, 4608), BF16),
            pltpu.VMEM(dq.shape, BF16), pltpu.VMEM((8,) + dkv.shape[1:], BF16),
            pltpu.VMEM((8,) + dkv.shape[1:], BF16), pltpu.VMEM((7,) + dkv.shape[1:], BF16),
            pltpu.VMEM((2, 4, BLK, 1920), BF16), pltpu.VMEM((4, BLK, 1152), BF16),
            pltpu.VMEM((2, 4, BLK, 1152), BF16), pltpu.VMEM((4, BLK, 1920), BF16),
            pltpu.VMEM((3, 4, BLK, 1536), BF16), pltpu.VMEM((3, BLK, 3072), BF16),
            pltpu.VMEM((2, BLK, 1536), BF16), pltpu.VMEM((BLK, 1536), BF16),
            pltpu.VMEM((16, 768), F32), pltpu.VMEM((16, 768), F32), pltpu.VMEM((16, 384), F32),
            pltpu.VMEM((2, 16, 384), F32), pltpu.VMEM((4, 16, 384), F32),
            DMA((wires,)), DMA((wires,)), DMA((1,))],
        compiler_params=pltpu.CompilerParams(collective_id=ident, has_side_effects=True, vmem_limit_bytes=62 << 20),
        name="reduce_all",
    )(tok, att, low, act, gbr, ghid, gsec, gfirst, wqkv, small, dq, dkv)


def widen_kernel(grads, g_qkv, g_out, g_in, g_back):
    for core in range(2):
        part = grads.at[core]
        g_out[:, core * 384:core * 384 + 384] = part[:, 0:384].astype(F32)
        g_in[:, core * 1536:core * 1536 + 1536] = part[:, 384:1920].astype(F32)
        for j in range(4):
            g_back[j, :, core * 384:core * 384 + 384] = part[:, 1920 + 384 * j:2304 + 384 * j].astype(F32)
        g_qkv[:, core * 1152:core * 1152 + 1152] = part[:, 3456:4608].astype(F32)


def widen(grads):
    rows, step = 384, 48
    spec = lambda wide: pl.BlockSpec((step, wide), lambda n: (n, 0))
    return pl.pallas_call(
        widen_kernel,
        grid=(rows // step,),
        out_shape=[jax.ShapeDtypeStruct((rows, 2304), F32), jax.ShapeDtypeStruct((rows, 768), F32),
                   jax.ShapeDtypeStruct((rows, 3072), F32), jax.ShapeDtypeStruct((4, rows, 768), F32)],
        in_specs=[pl.BlockSpec((2, step, 4608), lambda n: (0, n, 0))],
        out_specs=[spec(2304), spec(768), spec(3072), pl.BlockSpec((4, step, 768), lambda n: (0, n, 0))],
        name="widen",
    )(grads)


def layer_norm(values, gain_row, shift_row):
    average = jnp.mean(values, axis=-1, keepdims=True)
    centered = values - average
    variance = jnp.mean(centered * centered, axis=-1, keepdims=True)
    return centered * lax.rsqrt(variance + EPSILON) * gain_row + shift_row


def exact_gelu(values):
    return jax.nn.gelu(values, approximate=False)


def by_group(rows, micro, front, back):
    parts = rows.reshape(micro, -1, 4, 192).transpose(2, 0, 1, 3)
    parts = jnp.pad(parts, ((0, 0), (0, 0), (0, 0), (front, back)))
    return parts.reshape((-1,) + parts.shape[2:])


def from_group(blocks, micro, front):
    rows = blocks.shape[1]
    parts = blocks.reshape(4, micro, rows, -1)[..., front:front + 192]
    return parts.transpose(1, 2, 0, 3).reshape(micro * rows, 768)


def shards(tokens, cotangent, doc_lengths, w_qkv, w_out, w_in, w_back, *vectors):
    micro, per, width = tokens.shape
    nf, cols = lax.axis_size("fsdp"), lax.axis_size("ctx") // 8
    share = width // nf
    tiny = jnp.concatenate(vectors).reshape(8, -1)
    full_qkv, full_out, full_in, full_back, tinies = gather_weights((w_qkv, w_out, w_in, w_back), tiny, nf, cols)
    tinies = tinies.reshape(nf, -1).astype(F32)
    named, at = [], 0
    for vector in vectors:
        size = vector.shape[0]
        named.append(tinies[:, at:at + size].reshape(-1))
        at += size
    b_query, b_value, b_out, b_in, b_back, gain_one, shift_one, gain_two, shift_two = named
    inputs = tokens.reshape(micro * per, width)
    joined = jnp.dot(inputs, full_qkv, preferred_element_type=F32)
    bias = jnp.concatenate([b_query, jnp.zeros_like(b_query), b_value])
    joined = (joined + bias).astype(BF16)
    q_sent = by_group(joined[:, :width], micro, 0, 64)
    kv_sent = jnp.concatenate([by_group(joined[:, width:2 * width], micro, 0, 0), by_group(joined[:, 2 * width:], micro, 0, 0)], axis=2)
    q_held, kv_held = spread(q_sent, kv_sent, cols, 2)
    q_held = q_held.reshape(8 * per, 256)
    kv_held = kv_held.reshape(-1, 384)
    mixed, mixed_t, log_total = attend_forward(doc_lengths, q_held, kv_held, cols)
    (back,) = swap([mixed.reshape(8, per, 256)], cols, 3)
    attended = from_group(back, micro, 64)
    first_sum = inputs.astype(F32) + (jnp.dot(attended, full_out, preferred_element_type=F32) + b_out)
    normed = layer_norm(first_sum, gain_one, shift_one)
    normed_low = normed.astype(BF16)
    hidden = jnp.dot(normed_low, full_in, preferred_element_type=F32) + b_in
    activated = exact_gelu(hidden).astype(BF16)
    final_sum = normed + (jnp.dot(activated, full_back, preferred_element_type=F32) + b_back)
    output = layer_norm(final_sum, gain_two, shift_two).astype(BF16)

    upstream = cotangent.reshape(micro * per, width).astype(F32)
    grad_final, g_gain_two, g_shift_two = jax.vjp(layer_norm, final_sum, gain_two, shift_two)[1](upstream)
    grad_second = grad_final.astype(BF16)
    g_back_bias = jnp.sum(grad_second.astype(F32), axis=0)
    grad_activated = jnp.einsum("rm,km->rk", grad_second, full_back, preferred_element_type=F32)
    grad_hidden = jax.vjp(exact_gelu, hidden)[1](grad_activated)[0].astype(BF16)
    g_in_bias = jnp.sum(grad_hidden.astype(F32), axis=0)
    grad_normed = grad_final + jnp.einsum("rf,mf->rm", grad_hidden, full_in, preferred_element_type=F32)
    grad_first, g_gain_one, g_shift_one = jax.vjp(layer_norm, first_sum, gain_one, shift_one)[1](grad_normed)
    grad_branch = grad_first.astype(BF16)
    g_out_bias = jnp.sum(grad_branch.astype(F32), axis=0)
    grad_attended = jnp.einsum("rm,km->rk", grad_branch, full_out, preferred_element_type=F32).astype(BF16)
    (do_held,) = swap([by_group(grad_attended, micro, 64, 0)], cols, 4)
    if nf == 2 and cols == 2:
        small = [jnp.zeros((2, width), F32)] + [x[None] for x in (g_out_bias, g_back_bias, g_gain_one, g_shift_one, g_gain_two, g_shift_two)]
        small += [g_in_bias.reshape(2, 4, share).transpose(1, 0, 2).reshape(4, width), jnp.zeros((4, width), F32)]
    dq, dkv = attend_backward(doc_lengths, q_held, kv_held, do_held.reshape(8 * per, 256), mixed_t, log_total, cols)
    if nf == 2 and cols == 2:
        grads, input_grad, sums = reduce_all(
            inputs, attended, normed_low, activated, grad_branch, grad_hidden, grad_second, grad_first, full_qkv,
            jnp.concatenate(small), dq.reshape(8, per, 256), dkv.reshape(8 * cols, per, 384), 5)
        g_qkv, g_out, g_in, g_back = widen(grads.reshape(2, share, 4608))
        rows = [sums[0], sums[1], sums[2], sums[8:12].reshape(-1), sums[3], sums[4], sums[5], sums[6], sums[7]]
        return (output.reshape(tokens.shape), input_grad.reshape(tokens.shape), g_qkv, g_out, g_in, g_back.reshape(4 * share, width)) + tuple(rows)
    dq_own, dkv_own = collect(dq.reshape(8, per, 256), dkv.reshape(8 * cols, per, 384), cols, 5)
    grad_joined = jnp.concatenate(
        [from_group(dq_own, micro, 0), from_group(dkv_own, micro, 0), from_group(dkv_own, micro, 192)], axis=1)
    g_query_bias = jnp.sum(grad_joined[:, :width].astype(F32), axis=0)
    g_value_bias = jnp.sum(grad_joined[:, 2 * width:].astype(F32), axis=0)
    input_grad = grad_first + jnp.einsum("rc,mc->rm", grad_joined, full_qkv, preferred_element_type=F32)

    def halves(left, right):
        blocks = right.shape[1] // 384
        return jnp.einsum("rm,rhc->hmc", left, right.reshape(-1, blocks, 384), preferred_element_type=F32).astype(BF16)

    back_grads = jnp.einsum("rk,rm->km", activated, grad_second, preferred_element_type=F32).astype(BF16)
    back_grads = back_grads.reshape(nf, 4, share, 2, 384).transpose(1, 3, 0, 2, 4).reshape(8, width, 384)
    grads = jnp.concatenate(
        [halves(inputs, grad_joined), halves(attended, grad_branch), halves(normed_low, grad_hidden), back_grads])
    grads = grads.reshape(2, 4, 3, nf, cols, share // cols, 384)
    small = (g_query_bias, g_value_bias, g_out_bias, g_in_bias, g_back_bias, g_gain_one, g_shift_one, g_gain_two, g_shift_two)
    small = jnp.concatenate([x.reshape(nf, -1) for x in small], axis=1).reshape(nf, 8, -1)
    owned, small_owned = reduce_grads(grads, small, nf, cols, 6)
    owned = owned.transpose(0, 1, 3, 2, 4, 5).reshape(24, share, 384)

    def columns(first, last):
        return owned[first:last].transpose(1, 0, 2).reshape(share, -1).astype(F32)

    g_back = owned[16:].reshape(4, 2, share, 384).transpose(0, 2, 1, 3).reshape(4 * share, width).astype(F32)
    small_owned = small_owned.reshape(-1)
    small_grads, at = [], 0
    for vector in vectors:
        small_grads.append(small_owned[at:at + vector.shape[0]])
        at += vector.shape[0]
    return (output.reshape(tokens.shape), input_grad.reshape(tokens.shape), columns(0, 6), columns(6, 8), columns(8, 16), g_back) + tuple(small_grads)


def solution(mesh):
    rows, flat = P("fsdp", "ctx", None), P("fsdp", None)
    return jax.shard_map(
        shards,
        mesh=mesh,
        in_specs=(rows, rows, flat) + (flat,) * 4 + (P("fsdp"),) * 9,
        out_specs=(rows, rows) + (flat,) * 4 + (P("fsdp"),) * 9,
        check_vma=False,
    )
```

```python
import functools

import jax
import jax.numpy as jnp
from jax import lax
from jax.experimental import pallas as pl
from jax.experimental.pallas import tpu as pltpu
from jax.sharding import PartitionSpec as P

MESH = pl.DeviceIdType.MESH
DMA = pltpu.SemaphoreType.DMA
F32, BF16 = jnp.float32, jnp.bfloat16
EPSILON = 1e-12

def place(cols):
    index = lax.axis_index("ctx")
    return index // (2 * cols), lax.rem(index // 2, cols), lax.rem(index, 2), lax.axis_index("fsdp")

def device(a, b, c, f, cols):
    return {"ctx": (a * cols + b) * 2 + c, "fsdp": f}

def meet(peers):
    barrier = pltpu.get_barrier_semaphore()
    for peer in peers:
        pl.semaphore_signal(barrier, inc=1, device_id=peer, device_id_type=MESH)
    pl.semaphore_wait(barrier, len(peers))

def remote(source, target, send, recv, peer):
    return pltpu.make_async_remote_copy(
        src_ref=source, dst_ref=target, send_sem=send, recv_sem=recv, device_id=peer, device_id_type=MESH)

def gather_kernel(nf, cols, count, *refs):
    shards, tiny, fulls, tiny_out = refs[:count], refs[count], refs[count+1:2*count+1], refs[2*count+1]
    local_sem, s1, r1, s2, r2, s3, r3, st, rt = refs[2*count+2:]
    a, b, c, f = place(cols)
    other = 1 - c
    fpeers = [device(a, b, c, lax.rem(f + j, nf), cols) for j in range(1, nf)]
    bpeers = [device(a, lax.rem(b + k, cols), c, f, cols) for k in range(1, cols)]
    sibling = device(a, b, other, f, cols)
    meet(fpeers + bpeers + [sibling])

    def view(w, owner, bb, cc, base=0):
        rows, wide = shards[w].shape
        part, half = rows // cols, wide // 2
        return fulls[w].at[pl.ds(pl.multiple_of(owner * rows + bb * part, 8), part), pl.ds(pl.multiple_of(cc * half, 128), half)]

    waits = []
    for j in range(1, nf):
        cp = remote(tiny, tiny_out.at[f], st.at[j - 1], rt.at[j - 1], fpeers[j - 1])
        cp.start()
        waits.append(cp)
    locals_ = [pltpu.make_async_copy(tiny, tiny_out.at[f], local_sem.at[count])]
    locals_[0].start()
    first = {}
    for w in range(count):
        rows, wide = shards[w].shape
        part, half = rows // cols, wide // 2
        mine = shards[w].at[pl.ds(pl.multiple_of(b * part, 8), part), pl.ds(pl.multiple_of(c * half, 128), half)]
        for j in range(1, nf):
            cp = remote(mine, view(w, f, b, c), s1.at[w, j - 1], r1.at[w, j - 1], fpeers[j - 1])
            cp.start()
            first[w, j] = cp
    for w in range(count):
        rows = shards[w].shape[0]
        cp = pltpu.make_async_copy(shards[w], fulls[w].at[pl.ds(pl.multiple_of(f * rows, 8), rows)], local_sem.at[w])
        cp.start()
        locals_.append(cp)
    second, third = {}, []
    for w in range(count):
        for j in range(1, nf):
            owner = lax.rem(f + nf - j, nf)
            first[w, j].wait_recv()
            piece = view(w, owner, b, c)
            for k in range(1, cols):
                slot = (j - 1) * (cols - 1) + k - 1
                cp = remote(piece, piece, s2.at[w, slot], r2.at[w, slot], bpeers[k - 1])
                cp.start()
                second[w, j, k] = cp
            cp = remote(piece, piece, s3.at[w, (j - 1) * cols], r3.at[w, (j - 1) * cols], sibling)
            cp.start()
            third.append(cp)
    for w in range(count):
        for j in range(1, nf):
            owner = lax.rem(f + nf - j, nf)
            for k in range(1, cols):
                second[w, j, k].wait_recv()
                piece = view(w, owner, lax.rem(b + cols - k, cols), c)
                cp = remote(piece, piece, s3.at[w, (j - 1) * cols + k], r3.at[w, (j - 1) * cols + k], sibling)
                cp.start()
                third.append(cp)
    for cp in third:
        cp.wait_recv()
    for cp in waits:
        cp.wait()
    for cp in list(first.values()) + list(second.values()) + third:
        cp.wait_send()
    for cp in locals_:
        cp.wait()

def gather_weights(shards, tiny, nf, cols):
    count = len(shards)
    any_spec = pl.BlockSpec(memory_space=pl.ANY)
    dma = pltpu.SemaphoreType.DMA
    return pl.pallas_call(
        functools.partial(gather_kernel, nf, cols, count),
        out_shape=[jax.ShapeDtypeStruct((s.shape[0] * nf, s.shape[1]), s.dtype) for s in shards]
        + [jax.ShapeDtypeStruct((nf,) + tiny.shape, tiny.dtype)],
        in_specs=[pl.BlockSpec(memory_space=pltpu.VMEM)] * (count + 1),
        out_specs=[any_spec] * (count + 1),
        scratch_shapes=[dma((count + 1,)), dma((count, nf - 1)), dma((count, nf - 1)),
                        dma((count, (nf - 1) * (cols - 1))), dma((count, (nf - 1) * (cols - 1))),
                        dma((count, (nf - 1) * cols)), dma((count, (nf - 1) * cols)),
                        dma((nf - 1,)), dma((nf - 1,))],
        compiler_params=pltpu.CompilerParams(collective_id=1, has_side_effects=True, vmem_limit_bytes=32 << 20),
        name="gather_weights",
    )(*shards, tiny)

def octet(a, b, c, f, cols):
    me = a * 2 + c
    out = []
    for k in range(1, 8):
        other = lax.rem(me + k, 8)
        out.append((other, device(other // 2, b, lax.rem(other, 2), f, cols)))
    return me, out

def swap_kernel(cols, count, *refs):
    sources, targets = refs[:count], refs[count:2 * count]
    send, recv, here = refs[2 * count:]
    a, b, c, f = place(cols)
    me, peers = octet(a, b, c, f, cols)
    meet([p for _, p in peers])
    copies = []
    for k, (other, peer) in enumerate(peers):
        for i in range(count):
            cp = remote(sources[i].at[other], targets[i].at[me], send.at[i, k], recv.at[i, k], peer)
            cp.start()
            copies.append(cp)
    for i in range(count):
        cp = pltpu.make_async_copy(sources[i].at[me], targets[i].at[me], here.at[i])
        cp.start()
        copies.append(cp)
    for cp in copies:
        cp.wait()

def swap(arrays, cols, ident):
    count = len(arrays)
    return pl.pallas_call(
        functools.partial(swap_kernel, cols, count),
        out_shape=[jax.ShapeDtypeStruct(x.shape, x.dtype) for x in arrays],
        in_specs=[vmem()] * count, out_specs=[vmem()] * count,
        scratch_shapes=[DMA((count, 7)), DMA((count, 7)), DMA((count,))],
        compiler_params=pltpu.CompilerParams(collective_id=ident, has_side_effects=True, vmem_limit_bytes=16 << 20),
        name="swap",
    )(*arrays)

def spread_kernel(cols, q, kv, qg, full, sq, rq, sk, rk, s2, r2, here):
    a, b, c, f = place(cols)
    me, peers = octet(a, b, c, f, cols)
    bpeers = [device(a, lax.rem(b + k, cols), c, f, cols) for k in range(1, cols)]
    meet([p for _, p in peers] + bpeers)

    def slot(block, bb):
        return (block // 2 * cols + bb) * 2 + lax.rem(block, 2)

    first = []
    for k, (other, peer) in enumerate(peers):
        cp = remote(kv.at[other], full.at[slot(me, b)], sk.at[k], rk.at[k], peer)
        cp.start()
        first.append(cp)
    own = pltpu.make_async_copy(kv.at[me], full.at[slot(me, b)], here.at[0])
    own.start()
    ownq = pltpu.make_async_copy(q.at[me], qg.at[me], here.at[1])
    ownq.start()
    second = []
    for k, peer in enumerate(bpeers):
        cp = remote(kv.at[me], full.at[slot(me, b)], s2.at[7, k], r2.at[7, k], peer)
        cp.start()
        second.append(cp)
    third = []
    for k, (other, peer) in enumerate(peers):
        cp = remote(q.at[other], qg.at[me], sq.at[k], rq.at[k], peer)
        cp.start()
        third.append(cp)
    for k in range(7):
        first[k].wait_recv()
        source = lax.rem(me + 8 - (k + 1), 8)
        piece = full.at[slot(source, b)]
        for m, peer in enumerate(bpeers):
            cp = remote(piece, piece, s2.at[k, m], r2.at[k, m], peer)
            cp.start()
            second.append(cp)
    for cp in first:
        cp.wait_send()
    for cp in second + third:
        cp.wait()
    own.wait()
    ownq.wait()

def spread(q, kv, cols, ident):
    return pl.pallas_call(
        functools.partial(spread_kernel, cols),
        out_shape=[jax.ShapeDtypeStruct(q.shape, q.dtype), jax.ShapeDtypeStruct((8 * cols,) + kv.shape[1:], kv.dtype)],
        in_specs=[vmem()] * 2, out_specs=[vmem()] * 2,
        scratch_shapes=[DMA((7,))] * 4 + [DMA((8, max(cols - 1, 1)))] * 2 + [DMA((2,))],
        compiler_params=pltpu.CompilerParams(collective_id=ident, has_side_effects=True, vmem_limit_bytes=16 << 20),
        name="spread",
    )(q, kv)

def collect_kernel(cols, dq, dkv, dqo, dkvo, rbuf, total, sq, rq, sk, rk, s2, r2, here):
    a, b, c, f = place(cols)
    me, peers = octet(a, b, c, f, cols)
    bpeers = [(lax.rem(b + k, cols), device(a, lax.rem(b + k, cols), c, f, cols)) for k in range(1, cols)]
    meet([p for _, p in peers] + [p for _, p in bpeers])

    def slot(block, bb):
        return (block // 2 * cols + bb) * 2 + lax.rem(block, 2)

    order = [other for other, _ in peers] + [me]
    first = {}
    for n, block in enumerate(order):
        for k, (bb, peer) in enumerate(bpeers):
            cp = remote(dkv.at[slot(block, bb)], rbuf.at[k, n], s2.at[k, n], r2.at[k, n], peer)
            cp.start()
            first[k, n] = cp
    rest = []
    for k, (other, peer) in enumerate(peers):
        cp = remote(dq.at[other], dqo.at[me], sq.at[k], rq.at[k], peer)
        cp.start()
        rest.append(cp)
    own = pltpu.make_async_copy(dq.at[me], dqo.at[me], here.at[0])
    own.start()
    for n, block in enumerate(order):
        value = dkv[slot(block, b)].astype(F32)
        for k in range(cols - 1):
            first[k, n].wait_recv()
            value = value + rbuf[k, n].astype(F32)
        if n < 7:
            total[n] = value.astype(BF16)
            cp = remote(total.at[n], dkvo.at[me], sk.at[n], rk.at[n], peers[n][1])
            cp.start()
            rest.append(cp)
        else:
            dkvo[me] = value.astype(BF16)
    for cp in first.values():
        cp.wait_send()
    for cp in rest:
        cp.wait()
    own.wait()

def collect(dq, dkv, cols, ident):
    block = dkv.shape[1:]
    return pl.pallas_call(
        functools.partial(collect_kernel, cols),
        out_shape=[jax.ShapeDtypeStruct(dq.shape, dq.dtype), jax.ShapeDtypeStruct((8,) + block, dkv.dtype)],
        in_specs=[vmem()] * 2, out_specs=[vmem()] * 2,
        scratch_shapes=[pltpu.VMEM((max(cols - 1, 1), 8) + block, BF16), pltpu.VMEM((7,) + block, BF16)]
        + [DMA((7,))] * 4 + [DMA((max(cols - 1, 1), 8))] * 2 + [DMA((1,))],
        compiler_params=pltpu.CompilerParams(collective_id=ident, has_side_effects=True, vmem_limit_bytes=24 << 20),
        name="collect",
    )(dq, dkv)

def reduce_kernel(nf, cols, parts, grads, small, out, small_out, *refs):
    own, core_in, f_in, b_in, f_in2, b_in2, a_in, v_core, v_sum, v_f, v_b, v_a = refs[:12]
    load, sc, rc, s1, r1, s2, r2, s3, r3, s4, r4, s5, r5, s6, r6, sv, rv = refs[12:]
    a, b, c, f = place(cols)
    rows = grads.shape[5]
    fpeers = [(lax.rem(f + j, nf), device(a, b, c, lax.rem(f + j, nf), cols)) for j in range(1, nf)]
    bpeers = [(lax.rem(b + k, cols), device(a, lax.rem(b + k, cols), c, f, cols)) for k in range(1, cols)]
    apeers = [(lax.rem(a + k, 4), device(lax.rem(a + k, 4), b, c, f, cols)) for k in range(1, 4)]
    sibling = device(a, b, 1 - c, f, cols)
    meet([p for _, p in fpeers + bpeers + apeers] + [sibling])
    vector = remote(small, v_core, sv.at[0], rv.at[0], sibling)
    vector.start()
    order = [2, 1, 3, 0]
    dest = {k: lax.rem(a + k, 4) for k in range(4)}
    by_f = {k: k in (1, 2) for k in range(4)}
    loads, cores = {}, {}
    for k in order:
        for i in range(parts):
            cp = pltpu.make_async_copy(grads.at[c, dest[k], i], own.at[k, i], load.at[k, i])
            cp.start()
            loads[k, i] = cp
            cp = remote(grads.at[1 - c, dest[k], i], core_in.at[k, i], sc.at[k, i], rc.at[k, i], sibling)
            cp.start()
            cores[k, i] = cp
    one, two, three = {}, {}, {}
    vec = {}
    vector.wait_recv()
    v_sum[...] = small[...] + v_core[...]
    for j, (ff, peer) in enumerate(fpeers):
        vec[0, j] = remote(v_sum.at[ff], v_f.at[j], sv.at[1 + j], rv.at[1 + j], peer)
        vec[0, j].start()
    for k in order:
        for i in range(parts):
            loads[k, i].wait()
            cores[k, i].wait_recv()

            @pl.loop(0, nf * cols)
            def _(n):
                ff, bb = n // cols, lax.rem(n, cols)
                own[k, i, ff, bb] = (own[k, i, ff, bb].astype(F32) + core_in[k, i, ff, bb].astype(F32)).astype(BF16)

            if by_f[k]:
                for j, (ff, peer) in enumerate(fpeers):
                    cp = remote(own.at[k, i, ff], f_in.at[k, i, j], s1.at[k, i, j], r1.at[k, i, j], peer)
                    cp.start()
                    one[k, i, j] = cp
            else:
                for m, (bb, peer) in enumerate(bpeers):
                    for ff in range(nf):
                        cp = remote(own.at[k, i, ff, bb], b_in.at[k, i, m, ff], s1.at[k, i, m * nf + ff], r1.at[k, i, m * nf + ff], peer)
                        cp.start()
                        one[k, i, m * nf + ff] = cp
    value = v_sum[f]
    for j in range(nf - 1):
        vec[0, j].wait_recv()
        value = value + v_f[j]
    v_b[b] = value
    for m, (bb, peer) in enumerate(bpeers):
        vec[1, m] = remote(v_b.at[b], v_b.at[b], sv.at[nf + m], rv.at[nf + m], peer)
        vec[1, m].start()
    for k in order:
        for i in range(parts):
            if by_f[k]:
                for j in range(nf - 1):
                    one[k, i, j].wait_recv()

                @pl.loop(0, cols)
                def _(bb):
                    value = own[k, i, f, bb].astype(F32)
                    for j in range(nf - 1):
                        value = value + f_in[k, i, j, bb].astype(F32)
                    own[k, i, f, bb] = value.astype(BF16)

                for m, (bb, peer) in enumerate(bpeers):
                    cp = remote(own.at[k, i, f, bb], b_in2.at[k, i, m], s2.at[k, i, m], r2.at[k, i, m], peer)
                    cp.start()
                    two[k, i, m] = cp
            else:
                for m in range(cols - 1):
                    for ff in range(nf):
                        one[k, i, m * nf + ff].wait_recv()

                @pl.loop(0, nf)
                def _(ff):
                    value = own[k, i, ff, b].astype(F32)
                    for m in range(cols - 1):
                        value = value + b_in[k, i, m, ff].astype(F32)
                    own[k, i, ff, b] = value.astype(BF16)

                for j, (ff, peer) in enumerate(fpeers):
                    cp = remote(own.at[k, i, ff, b], f_in2.at[k, i, j], s2.at[k, i, j], r2.at[k, i, j], peer)
                    cp.start()
                    two[k, i, j] = cp
    for m in range(cols - 1):
        vec[1, m].wait_recv()
    value = v_b[0]
    for m in range(1, cols):
        value = value + v_b[m]
    v_a[a] = value
    for k in range(1, 4):
        vec[2, k] = remote(v_a.at[a], v_a.at[a], sv.at[nf + cols + k - 2], rv.at[nf + cols + k - 2], apeers[k - 1][1])
        vec[2, k].start()
    for k in order:
        for i in range(parts):
            value = own[k, i, f, b].astype(F32)
            if by_f[k]:
                for m in range(cols - 1):
                    two[k, i, m].wait_recv()
                    value = value + b_in2[k, i, m].astype(F32)
            else:
                for j in range(nf - 1):
                    two[k, i, j].wait_recv()
                    value = value + f_in2[k, i, j].astype(F32)
            if k != 0:
                own[k, i, f, b] = value.astype(BF16)
                cp = remote(own.at[k, i, f, b], a_in.at[k - 1, i], s3.at[k - 1, i], r3.at[k - 1, i], apeers[k - 1][1])
                cp.start()
                three[k, i] = cp
            else:
                own[k, i, f, b] = value.astype(BF16)
    for k in range(1, 4):
        vec[2, k].wait_recv()
    small_out[...] = v_a[0] + v_a[1] + v_a[2] + v_a[3]
    four, five, six = {}, {}, {}

    def piece(aa, bb, cc, i):
        return out.at[cc, aa, bb, i]

    pending = []
    for i in range(parts):
        value = own[0, i, f, b].astype(F32)
        for k in range(1, 4):
            three[k, i].wait_recv()
            value = value + a_in[k - 1, i].astype(F32)
        out[c, a, b, i] = value.astype(BF16)
        mine = piece(a, b, c, i)
        for k in (2, 1, 3):
            cp = remote(mine, mine, s4.at[k - 1, i], r4.at[k - 1, i], apeers[k - 1][1])
            cp.start()
            four[k, i] = cp
        for m, (bb, peer) in enumerate(bpeers):
            cp = remote(mine, mine, s5.at[0, i, m], r5.at[0, i, m], peer)
            cp.start()
            five[0, i, m] = cp
        cp = remote(mine, mine, s6.at[0, i, 0], r6.at[0, i, 0], sibling)
        cp.start()
        six[0, i, 0] = cp
    for i in range(parts):
        for k in (1, 3, 2):
            four[k, i].wait_recv()
            got = piece(lax.rem(a + 4 - k, 4), b, c, i)
            for m, (bb, peer) in enumerate(bpeers):
                cp = remote(got, got, s5.at[k, i, m], r5.at[k, i, m], peer)
                cp.start()
                five[k, i, m] = cp
            cp = remote(got, got, s6.at[k, i, 0], r6.at[k, i, 0], sibling)
            cp.start()
            six[k, i, 0] = cp
    for i in range(parts):
        for k in (0, 1, 3, 2):
            for m in range(cols - 1):
                five[k, i, m].wait_recv()
                got = piece(lax.rem(a + 4 - k, 4), lax.rem(b + cols - (m + 1), cols), c, i)
                cp = remote(got, got, s6.at[k, i, m + 1], r6.at[k, i, m + 1], sibling)
                cp.start()
                six[k, i, m + 1] = cp
    for cp in six.values():
        cp.wait_recv()
    vector.wait_send()
    for group in (cores, one, two, three, four, five, six, vec):
        for cp in group.values():
            cp.wait_send()

def reduce_grads(grads, small, nf, cols, ident):
    _, _, parts, _, _, rows, width = grads.shape
    block = (rows, width)
    m = max(cols - 1, 1)
    n = max((cols - 1) * nf, nf - 1)
    return pl.pallas_call(
        functools.partial(reduce_kernel, nf, cols, parts),
        out_shape=[jax.ShapeDtypeStruct((2, 4, cols, parts) + block, BF16), jax.ShapeDtypeStruct(small.shape[1:], F32)],
        in_specs=[pl.BlockSpec(memory_space=pl.ANY), vmem()], out_specs=[vmem()] * 2,
        scratch_shapes=[pltpu.VMEM((4, parts, nf, cols) + block, BF16), pltpu.VMEM((4, parts, nf, cols) + block, BF16),
                        pltpu.VMEM((4, parts, nf - 1, cols) + block, BF16), pltpu.VMEM((4, parts, m, nf) + block, BF16),
                        pltpu.VMEM((4, parts, nf - 1) + block, BF16), pltpu.VMEM((4, parts, m) + block, BF16),
                        pltpu.VMEM((3, parts) + block, BF16),
                        pltpu.VMEM(small.shape, F32), pltpu.VMEM(small.shape, F32), pltpu.VMEM((nf - 1,) + small.shape[1:], F32),
                        pltpu.VMEM((cols,) + small.shape[1:], F32), pltpu.VMEM((4,) + small.shape[1:], F32),
                        DMA((4, parts)), DMA((4, parts)), DMA((4, parts)), DMA((4, parts, n)), DMA((4, parts, n)),
                        DMA((4, parts, max(m, nf - 1))), DMA((4, parts, max(m, nf - 1))),
                        DMA((3, parts)), DMA((3, parts)), DMA((3, parts)), DMA((3, parts)),
                        DMA((4, parts, m)), DMA((4, parts, m)), DMA((4, parts, cols)), DMA((4, parts, cols)),
                        DMA((nf + cols + 2,)), DMA((nf + cols + 2,))],
        compiler_params=pltpu.CompilerParams(collective_id=ident, has_side_effects=True, vmem_limit_bytes=56 << 20),
        name="reduce_grads",
    )(grads, small)
KB = 256
SPAN = 256
MASKED = -1e30

def dot(x, y, dims):
    return lax.dot_general(x, y, (dims, ((), ())), preferred_element_type=F32)

NT = ((1,), (1,))
NN = ((1,), (0,))
TN = ((0,), (0,))

def bounds(lens, stream):
    ends, total = [], 0
    for j in range(4):
        total = total + lens[stream, j]
        ends.append(total)
    return ends

def doc_range(pos, ends):
    start = jnp.where(pos >= ends[0], ends[0], 0)
    stop = jnp.where(pos < ends[0], ends[0], ends[3])
    for j in (1, 2):
        start = jnp.where(pos >= ends[j], ends[j], start)
    for j in (2, 1, 0):
        stop = jnp.where(pos < ends[j], ends[j], stop)
    return start, stop

def block_range(base, ends):
    low, _ = doc_range(base, ends)
    _, high = doc_range(base + (SPAN - 1), ends)
    return low // KB, (high + (KB - 1)) // KB

def lane_head(shape, shift):
    lane = lax.broadcasted_iota(jnp.int32, shape, 1)
    return (lane - shift) // 64

def forward_kernel(cols, lens, q_ref, kv_ref, o_ref, ot_ref, lse_ref, qm, vt, acc):
    index = lax.axis_index("ctx")
    b, c = lax.rem(index // 2, cols), lax.rem(index, 2)
    ends = bounds(lens, c)
    total = kv_ref.shape[0]

    @pl.loop(0, total // KB)
    def _(n):
        rows = pl.ds(pl.multiple_of(n * KB, KB), KB)
        vt[:, rows] = kv_ref[rows, 128:384].astype(F32).T.astype(BF16)

    @pl.loop(0, 4)
    def _(stripe):
        base = SPAN * (stripe * cols + b)
        rows = pl.ds(pl.multiple_of(stripe * SPAN, SPAN), SPAN)
        head = lane_head((SPAN, 256), 0)
        q = q_ref[rows].astype(F32) * 0.125
        for h in range(3):
            qm[h] = jnp.where(head == h, q, 0.0).astype(BF16)
        qpos = base + lax.broadcasted_iota(jnp.int32, (1, SPAN), 1)
        start, stop = doc_range(qpos, ends)
        low, high = block_range(base, ends)
        acc[...] = jnp.zeros_like(acc)

        def step(n, state):
            krows = pl.ds(pl.multiple_of(n * KB, KB), KB)
            keys = kv_ref[krows, 0:256]
            kpos = n * KB + lax.broadcasted_iota(jnp.int32, (KB, 1), 0)
            allowed = (kpos >= start) & (kpos < stop)
            out = []
            for h in range(3):
                top, tot = state[h]
                s = jnp.where(allowed, dot(keys, qm[h], NT), MASKED)
                new = jnp.maximum(top, jnp.max(s, axis=0, keepdims=True))
                p = jnp.exp(s - new)
                scale = jnp.exp(top - new)
                hrows = pl.ds(64 * (h + 1), 64)
                acc[hrows] = acc[hrows] * scale + dot(vt[hrows, krows], p.astype(BF16), NN)
                out.append((new, tot * scale + jnp.sum(p, axis=0, keepdims=True)))
            return tuple(out)

        first = tuple((jnp.full((1, SPAN), MASKED, F32), jnp.zeros((1, SPAN), F32)) for _ in range(3))
        final = lax.fori_loop(low, high, step, first)
        for h in range(3):
            top, tot = final[h]
            hrows = pl.ds(64 * (h + 1), 64)
            acc[hrows] = acc[hrows] * (1.0 / tot)
            lse_ref[stripe, pl.ds(h, 1)] = top + jnp.log(tot)
        ot_ref[stripe] = acc[...]
        o_ref[rows] = acc[...].T.astype(BF16)

def vmem():
    return pl.BlockSpec(memory_space=pltpu.VMEM)

def attend_forward(lens, q, kv, cols):
    total = kv.shape[0]
    return pl.pallas_call(
        functools.partial(forward_kernel, cols),
        out_shape=[jax.ShapeDtypeStruct(q.shape, BF16), jax.ShapeDtypeStruct((4, 256, SPAN), F32),
                   jax.ShapeDtypeStruct((4, 8, SPAN), F32)],
        in_specs=[pl.BlockSpec(memory_space=pltpu.SMEM), vmem(), vmem()],
        out_specs=[vmem()] * 3,
        scratch_shapes=[pltpu.VMEM((3, SPAN, 256), BF16), pltpu.VMEM((256, total), BF16), pltpu.VMEM((256, SPAN), F32)],
        compiler_params=pltpu.CompilerParams(vmem_limit_bytes=32 << 20),
        name="attend_forward",
    )(lens, q, kv)

def backward_kernel(cols, lens, q_ref, kv_ref, do_ref, ot_ref, lse_ref, dq_ref, dkv_ref, qm, dm, kt, dk, dv, acc):
    index = lax.axis_index("ctx")
    b, c = lax.rem(index // 2, cols), lax.rem(index, 2)
    ends = bounds(lens, c)
    total = kv_ref.shape[0]

    @pl.loop(0, total // KB)
    def _(n):
        rows = pl.ds(pl.multiple_of(n * KB, KB), KB)
        kt[:, rows] = kv_ref[rows, 0:256].astype(F32).T.astype(BF16)
        dk[rows] = jnp.zeros((KB, 256), F32)
        dv[rows] = jnp.zeros((KB, 256), F32)

    @pl.loop(0, 4)
    def _(stripe):
        base = SPAN * (stripe * cols + b)
        rows = pl.ds(pl.multiple_of(stripe * SPAN, SPAN), SPAN)
        head = lane_head((SPAN, 256), 0)
        headv = lane_head((SPAN, 256), 64)
        q = q_ref[rows].astype(F32) * 0.125
        grad = do_ref[rows].astype(F32)
        for h in range(3):
            qm[h] = jnp.where(head == h, q, 0.0).astype(BF16)
            dm[h] = jnp.where(headv == h, grad, 0.0).astype(BF16)
        prod = grad.T * ot_ref[stripe]
        deltas = [jnp.sum(prod[64 * (h + 1):64 * (h + 2)], axis=0, keepdims=True) for h in range(3)]
        lses = [lse_ref[stripe, pl.ds(h, 1)] for h in range(3)]
        qpos = base + lax.broadcasted_iota(jnp.int32, (1, SPAN), 1)
        start, stop = doc_range(qpos, ends)
        low, high = block_range(base, ends)
        acc[...] = jnp.zeros_like(acc)

        @pl.loop(low, high)
        def _(n):
            krows = pl.ds(pl.multiple_of(n * KB, KB), KB)
            keys = kv_ref[krows, 0:256]
            vals = kv_ref[krows, 128:384]
            kpos = n * KB + lax.broadcasted_iota(jnp.int32, (KB, 1), 0)
            allowed = (kpos >= start) & (kpos < stop)
            newk, newv = dk[krows], dv[krows]
            for h in range(3):
                s = jnp.where(allowed, dot(keys, qm[h], NT), MASKED)
                p = jnp.exp(s - lses[h])
                gp = dot(vals, dm[h], NT)
                ds = (p * (gp - deltas[h])).astype(BF16)
                newv = newv + dot(p.astype(BF16), dm[h], NN)
                newk = newk + dot(ds, qm[h], NN)
                hrows = pl.ds(64 * h, 64)
                acc[hrows] = acc[hrows] + dot(kt[hrows, krows], ds, NN)
            dk[krows] = newk
            dv[krows] = newv

        dq_ref[rows] = (acc[...] * 0.125).T.astype(BF16)

    @pl.loop(0, total // KB)
    def _(n):
        rows = pl.ds(pl.multiple_of(n * KB, KB), KB)
        dkv_ref[rows, 0:128] = dk[rows, 0:128].astype(BF16)
        dkv_ref[rows, 128:256] = (dk[rows, 128:256] + dv[rows, 0:128]).astype(BF16)
        dkv_ref[rows, 256:384] = dv[rows, 128:256].astype(BF16)

def attend_backward(lens, q, kv, do, ot, lse, cols):
    total = kv.shape[0]
    return pl.pallas_call(
        functools.partial(backward_kernel, cols),
        out_shape=[jax.ShapeDtypeStruct(q.shape, BF16), jax.ShapeDtypeStruct(kv.shape, BF16)],
        in_specs=[pl.BlockSpec(memory_space=pltpu.SMEM)] + [vmem()] * 5,
        out_specs=[vmem()] * 2,
        scratch_shapes=[pltpu.VMEM((3, SPAN, 256), BF16), pltpu.VMEM((3, SPAN, 256), BF16), pltpu.VMEM((256, total), BF16),
                        pltpu.VMEM((total, 256), F32), pltpu.VMEM((total, 256), F32), pltpu.VMEM((256, SPAN), F32)],
        compiler_params=pltpu.CompilerParams(vmem_limit_bytes=40 << 20),
        name="attend_backward",
    )(lens, q, kv, do, ot, lse)


class Wires:
    def __init__(self, send, recv):
        self.send, self.recv, self.made = send, recv, []

    def go(self, source, target, peer):
        n = len(self.made)
        cp = remote(source, target, self.send.at[n], self.recv.at[n], peer)
        cp.start()
        self.made.append(cp)
        return cp


def transpose_into(target, source, base):
    width = source.shape[1]

    @pl.loop(0, width // 128)
    def _(n):
        at = pl.multiple_of(n * 128, 128)
        target[pl.ds(base + at, 128)] = source[:, pl.ds(at, 128)].astype(F32).T.astype(BF16)


def pair_columns(even, odd, lane, second):
    if second:
        return jnp.where(lane < 192, pltpu.roll(even, 192, 1), odd)
    return jnp.where(lane < 192, even, pltpu.roll(odd, 192, 1))


BLK = 48
Z1, X1, Y1, Z2, Y2, X2 = (0, 1152), (1152, 1920), (1920, 3456), (3456, 3840), (3840, 4224), (4224, 4608)


def gradient_kernel(tok, att, low, act, gbr, ghid, gsec, gfirst, wqkv, small, dq, dkv,
                    out, igrad, small_out,
                    xt, joined, mine, sib, cin, dqo, dkvo, rbuf, total,
                    y8, y4, x8, x4, z4, z1r, zyb, zxb, v_own, v_core, v_f, v_b, v_a, send, recv, here):
    a, b, c, f = place(2)
    me, peers = octet(a, b, c, f, 2)
    xp, yp, sp = device(a, 1 - b, c, f, 2), device(a, b, c, 1 - f, 2), device(a, b, 1 - c, f, 2)
    up, down = lax.rem(a + 1, 4), lax.rem(a + 3, 4)
    upp, downp = device(up, b, c, f, 2), device(down, b, c, f, 2)
    meet([p for _, p in peers] + [xp, yp])
    wires = Wires(send, recv)
    go = wires.go

    order = [other for other, _ in peers] + [me]

    def slot(block, bb):
        return (block // 2 * 2 + bb) * 2 + lax.rem(block, 2)

    crossed = [go(dkv.at[slot(block, 1 - b)], rbuf.at[n], xp) for n, block in enumerate(order)]
    swapped = [go(dq.at[other], dqo.at[me], peer) for other, peer in peers]
    own_q = pltpu.make_async_copy(dq.at[me], dqo.at[me], here.at[0])
    own_q.start()

    transpose_into(xt, att, 0)
    transpose_into(xt, low, 768)
    transpose_into(xt, act, 1536)
    transpose_into(xt, tok, 4608)

    def produce(kind, first, count, part, finish):
        @pl.loop(0, 2 * count)
        def _(n):
            ff, j = lax.rem(n, 2), first + n // 2
            if kind == "out":
                left, right = xt[pl.ds(pl.multiple_of(ff * 384, 128), 384)], gbr[:, pl.ds(pl.multiple_of(part * 384, 128), 384)]
                col = 0
            elif kind == "in":
                left = xt[pl.ds(pl.multiple_of(768 + ff * 384, 128), 384)]
                right = ghid[:, pl.ds(pl.multiple_of(part * 1536 + j * 384, 128), 384)]
                col = pl.multiple_of(384 + j * 384, 128)
            elif kind == "back":
                left = xt[pl.ds(pl.multiple_of(1536 + ff * 1536 + j * 384, 128), 384)]
                right = gsec[:, pl.ds(pl.multiple_of(part * 384, 128), 384)]
                col = pl.multiple_of(1920 + j * 384, 128)
            else:
                left = xt[pl.ds(pl.multiple_of(4608 + ff * 384, 128), 384)]
                right = joined[:, pl.ds(pl.multiple_of(part * 1152 + j * 384, 128), 384)]
                col = pl.multiple_of(3456 + j * 384, 128)
            finish(pl.ds(ff * 2, 2), pl.ds(col, 384), dot(left, right, NN).reshape(2, 4, BLK, 384))

    def keep(rows, cols, value):
        sib[rows, :, :, cols] = value.astype(BF16)

    def join(rows, cols, value):
        mine[rows, :, :, cols] = (value + cin[rows, :, :, cols].astype(F32)).astype(BF16)

    core = {}

    def share(span):
        cols = slice(span[0], span[1])
        core[span] = go(sib.at[:, :, :, cols], cin.at[:, :, :, cols], sp)

    def inside(span, group):
        base = 0
        for member in group:
            if member == span:
                return slice(base, base + span[1] - span[0])
            base += member[1] - member[0]

    YS, XS, ZS, RS = (Y1, Y2), (X1, X2), (Z1, Z2), (Y1, X1, Y2, X2)

    def add(target, source):
        def step(n):
            t, s = target(n), source(n)
            t[...] = (t[...].astype(F32) + s[...].astype(F32)).astype(BF16)
        return step

    def accumulate(target, source, count):
        pl.loop(0, count)(add(target, source))

    def start_y(span):
        cols, own = slice(span[0], span[1]), inside(span, YS)
        return go(mine.at[pl.ds((1 - f) * 2, 2), :, :, cols], y8.at[:, :, :, own], yp)

    def start_x(span):
        cols, own = slice(span[0], span[1]), inside(span, XS)
        return [go(mine.at[ff * 2 + 1 - b, :, :, cols], x8.at[ff, :, :, own], xp) for ff in range(2)]

    def next_y(span, cp):
        cols, own = slice(span[0], span[1]), inside(span, YS)
        cp.wait_recv()
        accumulate(lambda n: mine.at[f * 2 + n // 4, lax.rem(n, 4), :, cols], lambda n: y8.at[n // 4, lax.rem(n, 4), :, own], 8)
        return go(mine.at[f * 2 + 1 - b, :, :, cols], x4.at[:, :, own], xp)

    def next_x(span, cps):
        cols, own = slice(span[0], span[1]), inside(span, XS)
        for cp in cps:
            cp.wait_recv()
        accumulate(lambda n: mine.at[n // 4 * 2 + b, lax.rem(n, 4), :, cols], lambda n: x8.at[n // 4, lax.rem(n, 4), :, own], 8)
        return go(mine.at[(1 - f) * 2 + b, :, :, cols], y4.at[:, :, own], yp)

    def last_y(span, cp):
        cols, own = slice(span[0], span[1]), inside(span, YS)
        cp.wait_recv()
        accumulate(lambda n: mine.at[f * 2 + b, n, :, cols], lambda n: x4.at[n, :, own], 4)

    def last_x(span, cp):
        cols, own = slice(span[0], span[1]), inside(span, XS)
        cp.wait_recv()
        accumulate(lambda n: mine.at[f * 2 + b, n, :, cols], lambda n: y4.at[n, :, own], 4)

    def halves(span):
        tiles = (span[1] - span[0]) // 128
        mid = span[0] + tiles // 2 * 128
        return (span[0], mid), (mid, span[1])

    def landing(span, step, part, small_ring):
        base = inside(span, RS if small_ring else ZS).start - span[0]
        cols = slice(base + part[0], base + part[1])
        return z1r.at[step, :, cols] if small_ring else z4.at[step, :, :, cols]

    def ring_source(aa, part, small_ring):
        cols = slice(part[0], part[1])
        return mine.at[f * 2 + b, aa, :, cols] if small_ring else mine.at[:, aa, :, cols]

    def ring_send(span, step, small_ring):
        lo, hi = halves(span)
        ud, dd = lax.rem(a + 3 - step, 4), lax.rem(a + 1 + step, 4)
        return (go(ring_source(ud, lo, small_ring), landing(span, step, lo, small_ring), upp),
                go(ring_source(dd, hi, small_ring), landing(span, step, hi, small_ring), downp))

    def ring_add(span, step, small_ring, cps):
        lo, hi = halves(span)
        ud, dd = lax.rem(a + 6 - step, 4), lax.rem(a + 2 + step, 4)
        for cp, part, aa in zip(cps, (lo, hi), (ud, dd)):
            cp.wait_recv()
            got = landing(span, step, part, small_ring)
            if small_ring:
                add(lambda n: ring_source(aa, part, True), lambda n: got)(0)
            else:
                cols = slice(part[0], part[1])
                accumulate(lambda n: mine.at[n, aa, :, cols], lambda n: got.at[n], 4)

    def tail_z_y(span):
        cols, own = slice(span[0], span[1]), inside(span, ZS)
        return go(mine.at[pl.ds((1 - f) * 2, 2), a, :, cols], zyb.at[:, :, own], yp)

    def tail_z_x(span, cp):
        cols, own = slice(span[0], span[1]), inside(span, ZS)
        cp.wait_recv()
        accumulate(lambda n: mine.at[f * 2 + n, a, :, cols], lambda n: zyb.at[n, :, own], 2)
        return go(mine.at[f * 2 + 1 - b, a, :, cols], zxb.at[:, own], xp)

    def tail_z_end(span, cp):
        cols, own = slice(span[0], span[1]), inside(span, ZS)
        cp.wait_recv()
        add(lambda n: mine.at[f * 2 + b, a, :, cols], lambda n: zxb.at[:, own])(0)

    produce("out", 0, 1, 1 - c, keep)
    produce("in", 0, 2, 1 - c, keep)
    share(Z1)
    produce("back", 0, 4, 1 - c, keep)
    share(Y1)
    produce("in", 2, 2, 1 - c, keep)
    share(X1)
    core[Z1].wait_recv()
    produce("out", 0, 1, c, join)
    produce("in", 0, 2, c, join)
    z1 = ring_send(Z1, 0, False)
    core[Y1].wait_recv()
    produce("back", 0, 4, c, join)
    y1 = start_y(Y1)
    core[X1].wait_recv()
    produce("in", 2, 2, c, join)

    for n, block in enumerate(order):
        crossed[n].wait_recv()
        value = (dkv[slot(block, b)].astype(F32) + rbuf[n].astype(F32)).astype(BF16)
        if n < 7:
            total[n] = value
            swapped.append(go(total.at[n], dkvo.at[me], peers[n][1]))
        else:
            dkvo[me] = value
    x1 = start_x(X1)

    ring_add(Z1, 0, False, z1)
    z1 = ring_send(Z1, 1, False)
    y1 = next_y(Y1, y1)
    ring_add(Z1, 1, False, z1)
    z1 = ring_send(Z1, 2, False)
    x1 = next_x(X1, x1)

    own_q.wait()
    for cp in swapped:
        cp.wait_recv()
    lane = lax.broadcasted_iota(jnp.int32, (128, 384), 1)
    for s in range(2):
        rows = slice(s * 128, s * 128 + 128)
        for p in range(2):
            even, odd = 4 * p + s, 4 * p + 2 + s
            blank = jnp.zeros((128, 128), F32)
            qe = jnp.concatenate([dqo[even].astype(F32), blank], axis=1)
            qo = jnp.concatenate([dqo[odd].astype(F32), blank], axis=1)
            joined[rows, 384 * p:384 * p + 384] = pair_columns(qe, qo, lane, False).astype(BF16)
            ke, ko = dkvo[even].astype(F32), dkvo[odd].astype(F32)
            joined[rows, 768 + 384 * p:1152 + 384 * p] = pair_columns(ke, ko, lane, False).astype(BF16)
            joined[rows, 1536 + 384 * p:1920 + 384 * p] = pair_columns(ke, ko, lane, True).astype(BF16)
    produce("qkv", 0, 3, 1 - c, keep)
    for span in (Z2, Y2, X2):
        share(span)
    v_own[...] = small[...]
    v_own[0:1] = jnp.sum(joined[:, 0:768].astype(F32), axis=0, keepdims=True)
    v_own[1:2] = jnp.sum(joined[:, 1536:2304].astype(F32), axis=0, keepdims=True)
    vec = go(v_own, v_core, sp)
    for span in (Z2, Y2, X2):
        core[span].wait_recv()
    produce("qkv", 0, 3, c, join)
    z2 = ring_send(Z2, 0, False)
    y2 = start_y(Y2)
    x2 = start_x(X2)

    ring_add(Z1, 2, False, z1)
    z1 = tail_z_y(Z1)
    last_y(Y1, y1)
    y1 = ring_send(Y1, 0, True)
    last_x(X1, x1)
    x1 = ring_send(X1, 0, True)

    @pl.loop(0, 3)
    def _(n):
        rows = pl.ds(pl.multiple_of(n * 256, 256), 256)
        igrad[:, rows] = gfirst[:, rows] + dot(joined[...], wqkv[rows], NT)

    vec.wait_recv()
    v_own2 = v_own[...] + v_core[...]
    v_core[...] = v_own2
    vec = go(v_core.at[:, pl.ds(pl.multiple_of((1 - f) * 384, 128), 384)], v_f, yp)

    z1 = tail_z_x(Z1, z1)
    ring_add(Y1, 0, True, y1)
    y1 = ring_send(Y1, 1, True)
    ring_add(X1, 0, True, x1)
    x1 = ring_send(X1, 1, True)
    ring_add(Z2, 0, False, z2)
    z2 = ring_send(Z2, 1, False)
    y2 = next_y(Y2, y2)
    x2 = next_x(X2, x2)
    vec.wait_recv()
    v_b[b] = v_core[:, pl.ds(pl.multiple_of(f * 384, 128), 384)] + v_f[...]
    vec = go(v_b.at[b], v_b.at[b], xp)
    ring_add(Y1, 1, True, y1)
    y1 = ring_send(Y1, 2, True)
    ring_add(X1, 1, True, x1)
    x1 = ring_send(X1, 2, True)
    ring_add(Z2, 1, False, z2)
    z2 = ring_send(Z2, 2, False)
    tail_z_end(Z1, z1)
    vec.wait_recv()
    v_a[a] = v_b[0] + v_b[1]
    vec = [go(v_a.at[a], v_a.at[a], device(lax.rem(a + k, 4), b, c, f, 2)) for k in range(1, 4)]

    pending = []

    def piece(cc, bb, aa, span):
        return out.at[cc, bb * 4 + aa, :, span[0]:span[1]]

    class Gather:
        def __init__(self, span, first):
            self.span, self.first = span, first
            out[c, b * 4 + a, :, span[0]:span[1]] = mine[f * 2 + b, a, :, span[0]:span[1]]
            self.spread(b, a, span)
            self.ring = self.around(b)
            self.cross = go(piece(c, b, a, span), piece(c, b, a, span), xp)

        def spread(self, bb, aa, span):
            pending.append(go(piece(c, bb, aa, span), piece(c, bb, aa, span), sp))

        def around(self, bb):
            p = piece(c, bb, a, self.span)
            return go(p, p, upp), go(p, p, downp)

        def passed(self, bb, ring):
            lo, hi = halves(self.span)
            ring[0].wait_recv()
            p = piece(c, bb, down, lo)
            first = go(p, p, upp)
            ring[1].wait_recv()
            p = piece(c, bb, up, hi)
            second = go(p, p, downp)
            for aa in (down, up):
                self.spread(bb, aa, self.span)
            return first, second

        def arrived(self, bb, ring):
            for cp in ring:
                cp.wait_recv()
            self.spread(bb, lax.rem(a + 2, 4), self.span)

        def second(self):
            self.ring2 = self.passed(b, self.ring)
            if self.first == "b":
                self.cross.wait_recv()
                self.spread(1 - b, a, self.span)
                self.other = self.around(1 - b)
            else:
                self.more = [go(piece(c, b, aa, self.span), piece(c, b, aa, self.span), xp) for aa in (down, up)]

        def third(self):
            self.arrived(b, self.ring2)
            if self.first == "b":
                self.other2 = self.passed(1 - b, self.other)
            else:
                p = piece(c, b, lax.rem(a + 2, 4), self.span)
                self.more.append(go(p, p, xp))
                self.cross.wait_recv()
                self.spread(1 - b, a, self.span)

        def fourth(self):
            if self.first == "b":
                self.arrived(1 - b, self.other2)
            else:
                for cp, aa in zip(self.more, (down, up, lax.rem(a + 2, 4))):
                    cp.wait_recv()
                    self.spread(1 - b, aa, self.span)

    g_z1 = Gather(Z1, "a")
    ring_add(Y1, 2, True, y1)
    g_y1 = Gather(Y1, "b")
    ring_add(X1, 2, True, x1)
    g_x1 = Gather(X1, "b")
    ring_add(Z2, 2, False, z2)
    z2 = tail_z_y(Z2)
    last_y(Y2, y2)
    y2 = ring_send(Y2, 0, True)
    last_x(X2, x2)
    x2 = ring_send(X2, 0, True)
    g_z1.second()
    z2 = tail_z_x(Z2, z2)
    ring_add(Y2, 0, True, y2)
    y2 = ring_send(Y2, 1, True)
    ring_add(X2, 0, True, x2)
    x2 = ring_send(X2, 1, True)
    g_y1.second()
    g_x1.second()
    tail_z_end(Z2, z2)
    g_z2 = Gather(Z2, "a")
    ring_add(Y2, 1, True, y2)
    y2 = ring_send(Y2, 2, True)
    ring_add(X2, 1, True, x2)
    x2 = ring_send(X2, 2, True)
    g_z1.third()
    ring_add(Y2, 2, True, y2)
    g_y2 = Gather(Y2, "b")
    ring_add(X2, 2, True, x2)
    g_x2 = Gather(X2, "b")
    g_y1.third()
    g_x1.third()
    g_z1.fourth()
    g_z2.second()
    g_y2.second()
    g_x2.second()
    g_y1.fourth()
    g_x1.fourth()
    g_z2.third()
    g_y2.third()
    g_x2.third()
    g_z2.fourth()
    g_y2.fourth()
    g_x2.fourth()
    for cp in vec + pending:
        cp.wait_recv()
    small_out[...] = v_a[0] + v_a[1] + v_a[2] + v_a[3]
    for cp in wires.made:
        cp.wait_send()


def reduce_all(tok, att, low, act, gbr, ghid, gsec, gfirst, wqkv, small, dq, dkv, ident):
    block = (BLK,)
    wires = 192
    return pl.pallas_call(
        gradient_kernel,
        out_shape=[jax.ShapeDtypeStruct((2, 8, BLK, 4608), BF16), jax.ShapeDtypeStruct(gfirst.shape, F32), jax.ShapeDtypeStruct((16, 384), F32)],
        in_specs=[vmem()] * 12, out_specs=[vmem()] * 3,
        scratch_shapes=[
            pltpu.VMEM((5376, 256), BF16), pltpu.VMEM((256, 2304), BF16),
            pltpu.VMEM((4, 4, BLK, 4608), BF16), pltpu.VMEM((4, 4, BLK, 4608), BF16), pltpu.VMEM((4, 4, BLK, 4608), BF16),
            pltpu.VMEM(dq.shape, BF16), pltpu.VMEM((8,) + dkv.shape[1:], BF16),
            pltpu.VMEM((8,) + dkv.shape[1:], BF16), pltpu.VMEM((7,) + dkv.shape[1:], BF16),
            pltpu.VMEM((2, 4, BLK, 1920), BF16), pltpu.VMEM((4, BLK, 1152), BF16),
            pltpu.VMEM((2, 4, BLK, 1152), BF16), pltpu.VMEM((4, BLK, 1920), BF16),
            pltpu.VMEM((3, 4, BLK, 1536), BF16), pltpu.VMEM((3, BLK, 3072), BF16),
            pltpu.VMEM((2, BLK, 1536), BF16), pltpu.VMEM((BLK, 1536), BF16),
            pltpu.VMEM((16, 768), F32), pltpu.VMEM((16, 768), F32), pltpu.VMEM((16, 384), F32),
            pltpu.VMEM((2, 16, 384), F32), pltpu.VMEM((4, 16, 384), F32),
            DMA((wires,)), DMA((wires,)), DMA((1,))],
        compiler_params=pltpu.CompilerParams(collective_id=ident, has_side_effects=True, vmem_limit_bytes=62 << 20),
        name="reduce_all",
    )(tok, att, low, act, gbr, ghid, gsec, gfirst, wqkv, small, dq, dkv)


def widen_kernel(grads, g_qkv, g_out, g_in, g_back):
    for core in range(2):
        part = grads.at[core]
        g_out[:, core * 384:core * 384 + 384] = part[:, 0:384].astype(F32)
        g_in[:, core * 1536:core * 1536 + 1536] = part[:, 384:1920].astype(F32)
        for j in range(4):
            g_back[j, :, core * 384:core * 384 + 384] = part[:, 1920 + 384 * j:2304 + 384 * j].astype(F32)
        g_qkv[:, core * 1152:core * 1152 + 1152] = part[:, 3456:4608].astype(F32)


def widen(grads):
    rows, step = 384, 48
    spec = lambda wide: pl.BlockSpec((step, wide), lambda n: (n, 0))
    return pl.pallas_call(
        widen_kernel,
        grid=(rows // step,),
        out_shape=[jax.ShapeDtypeStruct((rows, 2304), F32), jax.ShapeDtypeStruct((rows, 768), F32),
                   jax.ShapeDtypeStruct((rows, 3072), F32), jax.ShapeDtypeStruct((4, rows, 768), F32)],
        in_specs=[pl.BlockSpec((2, step, 4608), lambda n: (0, n, 0))],
        out_specs=[spec(2304), spec(768), spec(3072), pl.BlockSpec((4, step, 768), lambda n: (0, n, 0))],
        name="widen",
    )(grads)

STEPS = ((1, 0), (3, 0), (1, 1), (3, 1), (2, 0), (0, 1), (2, 1))


class Octet:
    def __init__(self, go):
        self.go = go
        self.a, self.b, self.c, self.f = a, b, c, f = place(2)
        self.me = a * 2 + c
        self.others = [lax.rem(a + da, 4) * 2 + lax.rem(c + dc, 2) for da, dc in STEPS]
        self.sources = [lax.rem(a + 4 - da, 4) * 2 + lax.rem(c + dc, 2) for da, dc in STEPS]
        self.devices = [device(lax.rem(a + da, 4), b, lax.rem(c + dc, 2), f, 2) for da, dc in STEPS]
        self.relay, self.beyond = self.devices[3], self.devices[1]
        self.origin = lax.rem(a + 1, 4) * 2 + 1 - c

    def send(self, n, source, target, spare):
        if n < 6:
            return self.go(source, target(self.me), self.devices[n])
        return self.go(source, spare, self.relay)

    def forward(self, copy, target, spare):
        copy.wait_recv()
        return self.go(spare, target(self.origin), self.beyond)


def project_kernel(tokens, *refs):
    shards, vectors = refs[:4], refs[4:13]
    q_held, kv_held, f_qkv, f_out, f_in, f_back, vec = refs[13:20]
    own = refs[20:24]
    whole, acc, q_sent, kv_sent, v_own, token, q_spare, kv_spare = refs[24:32]
    flat, (send, recv, here) = refs[32:41], refs[41:]
    fulls = (f_qkv, f_out, f_in, f_back)
    a, b, c, f = place(2)
    group = Octet(None)
    me = group.me
    odd_a = lax.rem(a, 2)
    xp, yp, sp = device(a, 1 - b, c, f, 2), device(a, b, c, 1 - f, 2), device(a, b, 1 - c, f, 2)
    pairs = [device(lax.rem(a + 5 - 2 * odd_a, 4), b, c, f, 2), device(lax.rem(a + 3 + 2 * odd_a, 4), b, c, f, 2)]
    loads = [pltpu.make_async_copy(shards[w], own[w], here.at[w]) for w in range(4)]
    flats = [pltpu.make_async_copy(ref, flat[n], here.at[12 + n]) for n, ref in enumerate(vectors)]
    flats.append(pltpu.make_async_copy(tokens, token, here.at[11]))
    for cp in flats + loads:
        cp.start()
    meet(group.devices + [xp, yp])
    wires = Wires(send, recv)
    go = group.go = wires.go

    def rows_of(w, which, chunk):
        size = shards[w].shape[0] // 4
        return pl.multiple_of(which * 2 * size + chunk * size, 16), size

    def cols_of(w, cc):
        half = shards[w].shape[1] // 2
        return pl.ds(pl.multiple_of(cc * half, 128), half)

    def region(target, w, owner, which, cc, chunk):
        start, size = rows_of(w, which, chunk)
        return target.at[pl.ds(owner * shards[w].shape[0] + start, size), cols_of(w, cc)]

    def source(w, which, chunk):
        start, size = rows_of(w, which, chunk)
        return shards[w].at[pl.ds(start, size), cols_of(w, c)]

    other_f = 1 - f

    class Fetch:
        def __init__(self, target, w, chunk, pair=None):
            self.target, self.w, self.chunk = target, w, chunk
            self.which = b if pair is None else odd_a
            self.peer = xp if pair is None else pairs[pair]
            self.first = go(source(w, self.which, chunk), region(target, w, f, self.which, c, chunk), yp)

        def second(self):
            self.first.wait_recv()
            got = region(self.target, self.w, other_f, self.which, c, self.chunk)
            self.cross = go(got, got, self.peer)
            self.side = go(got, got, sp)

        def third(self):
            self.cross.wait_recv()
            got = region(self.target, self.w, other_f, 1 - self.which, c, self.chunk)
            self.side2 = go(got, got, sp)

        def end(self):
            self.side.wait_recv()
            self.side2.wait_recv()

    class Straight:
        def __init__(self, target, w, chunk, which):
            self.place = (target, w, other_f, which, c, chunk)
            self.first = go(source(w, which, chunk), region(target, w, f, which, c, chunk), yp)

        def second(self):
            self.first.wait_recv()
            got = region(*self.place)
            self.side = go(got, got, sp)

        def third(self):
            pass

        def end(self):
            self.side.wait_recv()

    qkv = [Fetch(whole, 0, 0)]
    for cp in flats:
        cp.wait()
    for n in range(9):
        value = flat[n][...].astype(F32)
        if n == 3:
            for j in range(4):
                v_own[8 + j:9 + j] = value[384 * j:384 * j + 384].reshape(1, 384)
        else:
            row = n if n < 3 else n - 1
            v_own[row:row + 1] = value.reshape(1, 384)
    v_own[12:16] = jnp.zeros((4, 384), F32)
    vec[f] = v_own[...]
    small = go(v_own, vec.at[f], yp)
    loads[0].wait()
    mine = pl.ds(pl.multiple_of(f * 384, 128), 384)
    theirs = pl.ds(pl.multiple_of(other_f * 384, 128), 384)

    @pl.loop(0, 6)
    def _(n):
        cols = pl.ds(pl.multiple_of(n * 384, 128), 384)
        acc[:, cols] = dot(token[:, mine], own[0][:, cols], NN)

    qkv[0].second()
    qkv.append(Fetch(whole, 0, 1))
    qkv[1].second()
    outer = [Fetch(f_back, 3, chunk, chunk) for chunk in range(2)]
    rest = [Fetch(f_out, 1, chunk) for chunk in range(2)]
    inner = [Straight(f_in, 2, chunk, which) for chunk in range(2) for which in range(2)]
    qkv[0].third()
    qkv[1].third()
    stores = []
    for w in range(4):
        if w > 0:
            loads[w].wait()
        rows = shards[w].shape[0]
        cp = pltpu.make_async_copy(own[w], fulls[w].at[pl.ds(pl.multiple_of(f * rows, 16), rows)], here.at[4 + w])
        cp.start()
        stores.append(cp)
    small.wait_recv()
    qkv[0].end()
    qkv[1].end()
    cp = pltpu.make_async_copy(whole.at[pl.ds(pl.multiple_of(other_f * 384, 16), 384)],
                               f_qkv.at[pl.ds(pl.multiple_of(other_f * 384, 16), 384)], here.at[8])
    cp.start()
    stores.append(cp)

    def column(n):
        cols = slice(384 * n, 384 * n + 384)
        value = acc[:, cols] + dot(token[:, theirs], whole[pl.ds(pl.multiple_of(other_f * 384, 16), 384), cols], NN)
        if n < 2:
            value = value + vec[n, 0:1]
        if n >= 4:
            value = value + vec[n - 4, 1:2]
        return value

    lane = lax.broadcasted_iota(jnp.int32, (256, 384), 1)
    for p in range(2):
        k, v = column(2 + p), column(4 + p)
        turned_k, turned_v = pltpu.roll(k, 192, 1), pltpu.roll(v, 192, 1)
        even = jnp.where(lane < 192, k, turned_v).astype(BF16)
        odd = jnp.where(lane < 192, turned_k, v).astype(BF16)
        q = column(p)
        q_even = jnp.where(lane < 192, q, 0.0)[:, :256].astype(BF16)
        q_odd = jnp.where(lane < 192, pltpu.roll(q, 192, 1), 0.0)[:, :256].astype(BF16)
        for s in range(2):
            rows = slice(128 * s, 128 * s + 128)
            kv_sent[4 * p + s], kv_sent[4 * p + 2 + s] = even[rows], odd[rows]
            q_sent[4 * p + s], q_sent[4 * p + 2 + s] = q_even[rows], q_odd[rows]

    def slot(block, bb):
        return (block // 2 * 2 + bb) * 2 + lax.rem(block, 2)

    kv_slot = lambda block: kv_held.at[slot(block, b)]
    q_slot = lambda block: q_held.at[block]
    first = [group.send(n, kv_sent.at[group.others[n]], kv_slot, kv_spare) for n in (6, 0, 1, 2, 3, 4, 5)]
    first = first[1:] + first[:1]
    own_kv = pltpu.make_async_copy(kv_sent.at[me], kv_held.at[slot(me, b)], here.at[9])
    own_kv.start()
    own_q = pltpu.make_async_copy(q_sent.at[me], q_held.at[me], here.at[10])
    own_q.start()
    crossed = [go(kv_sent.at[me], kv_held.at[slot(me, b)], xp)]
    third = [group.send(n, q_sent.at[group.others[n]], q_slot, q_spare) for n in (6, 0, 1, 2, 3, 4, 5)]
    third = third[1:] + third[:1]

    def onward(n):
        first[n].wait_recv()
        piece = kv_slot(group.sources[n])
        crossed.append(go(piece, piece, xp))

    onward(5)
    onward(0)
    onward(1)
    first[6] = group.forward(first[6], kv_slot, kv_spare)
    for cp in outer:
        cp.second()
    for cp in rest:
        cp.second()
    onward(2)
    onward(3)
    third[6] = group.forward(third[6], q_slot, q_spare)
    onward(4)
    onward(6)
    for cp in inner:
        cp.second()
    for cp in outer:
        cp.third()
    for cp in rest:
        cp.third()
    for cp in crossed + third:
        cp.wait_recv()
    for cp in rest + inner + outer:
        cp.end()
    for cp in wires.made:
        cp.wait_send()
    for cp in stores + [own_kv, own_q]:
        cp.wait()


def project(tokens, shards, vectors, ident):
    rows, width = tokens.shape
    anywhere = pl.BlockSpec(memory_space=pl.ANY)
    wires = 64
    return pl.pallas_call(
        project_kernel,
        out_shape=[jax.ShapeDtypeStruct((8, 128, 256), BF16), jax.ShapeDtypeStruct((16, 128, 384), BF16)]
        + [jax.ShapeDtypeStruct((2 * s.shape[0], s.shape[1]), BF16) for s in shards]
        + [jax.ShapeDtypeStruct((2, 16, 384), F32)],
        in_specs=[pl.BlockSpec(memory_space=pltpu.HBM)] * 14,
        out_specs=[vmem()] * 2 + [anywhere] * 4 + [vmem()],
        scratch_shapes=[pltpu.VMEM(s.shape, BF16) for s in shards]
        + [pltpu.VMEM((768, 2304), BF16), pltpu.VMEM((256, 2304), F32), pltpu.VMEM((8, 128, 256), BF16),
           pltpu.VMEM((8, 128, 384), BF16), pltpu.VMEM((16, 384), F32), pltpu.VMEM(tokens.shape, BF16),
           pltpu.VMEM((128, 256), BF16), pltpu.VMEM((128, 384), BF16),
           *[pltpu.VMEM(v.shape, BF16) for v in vectors], DMA((wires,)), DMA((wires,)), DMA((21,))],
        compiler_params=pltpu.CompilerParams(collective_id=ident, has_side_effects=True, vmem_limit_bytes=62 << 20),
        name="project",
    )(tokens, *shards, *vectors)


def layer_norm(values, gain_row, shift_row):
    average = jnp.mean(values, axis=-1, keepdims=True)
    centered = values - average
    variance = jnp.mean(centered * centered, axis=-1, keepdims=True)
    return centered * lax.rsqrt(variance + EPSILON) * gain_row + shift_row


def exact_gelu(values):
    return jax.nn.gelu(values, approximate=False)


def by_group(rows, micro, front, back):
    parts = rows.reshape(micro, -1, 4, 192).transpose(2, 0, 1, 3)
    parts = jnp.pad(parts, ((0, 0), (0, 0), (0, 0), (front, back)))
    return parts.reshape((-1,) + parts.shape[2:])


def from_group(blocks, micro, front):
    rows = blocks.shape[1]
    parts = blocks.reshape(4, micro, rows, -1)[..., front:front + 192]
    return parts.transpose(1, 2, 0, 3).reshape(micro * rows, 768)


def shards(tokens, cotangent, doc_lengths, w_qkv, w_out, w_in, w_back, *vectors):
    micro, per, width = tokens.shape
    nf, cols = lax.axis_size("fsdp"), lax.axis_size("ctx") // 8
    share = width // nf
    inputs = tokens.reshape(micro * per, width)
    cube = nf == 2 and cols == 2
    if cube:
        q_held, kv_held, full_qkv, full_out, full_in, full_back, sides = project(inputs, (w_qkv, w_out, w_in, w_back), vectors, 1)
        q_held = q_held.reshape(8 * per, 256)
        kv_held = kv_held.reshape(-1, 384)
        b_out, b_back, gain_one, shift_one, gain_two, shift_two = [sides[:, n].reshape(-1) for n in range(2, 8)]
        b_in = sides[:, 8:12].reshape(-1)
    else:
        tiny = jnp.concatenate(vectors).reshape(8, -1)
        full_qkv, full_out, full_in, full_back, tinies = gather_weights((w_qkv, w_out, w_in, w_back), tiny, nf, cols)
        tinies = tinies.reshape(nf, -1).astype(F32)
        named, at = [], 0
        for vector in vectors:
            size = vector.shape[0]
            named.append(tinies[:, at:at + size].reshape(-1))
            at += size
        b_query, b_value, b_out, b_in, b_back, gain_one, shift_one, gain_two, shift_two = named
        joined = jnp.dot(inputs, full_qkv, preferred_element_type=F32)
        bias = jnp.concatenate([b_query, jnp.zeros_like(b_query), b_value])
        joined = (joined + bias).astype(BF16)
        q_sent = by_group(joined[:, :width], micro, 0, 64)
        kv_sent = jnp.concatenate([by_group(joined[:, width:2 * width], micro, 0, 0), by_group(joined[:, 2 * width:], micro, 0, 0)], axis=2)
        q_held, kv_held = spread(q_sent, kv_sent, cols, 2)
        q_held = q_held.reshape(8 * per, 256)
        kv_held = kv_held.reshape(-1, 384)
    mixed, mixed_t, log_total = attend_forward(doc_lengths, q_held, kv_held, cols)
    (back,) = swap([mixed.reshape(8, per, 256)], cols, 3)
    attended = from_group(back, micro, 64)
    first_sum = inputs.astype(F32) + (jnp.dot(attended, full_out, preferred_element_type=F32) + b_out)
    normed = layer_norm(first_sum, gain_one, shift_one)
    normed_low = normed.astype(BF16)
    hidden = jnp.dot(normed_low, full_in, preferred_element_type=F32) + b_in
    activated = exact_gelu(hidden).astype(BF16)
    final_sum = normed + (jnp.dot(activated, full_back, preferred_element_type=F32) + b_back)
    output = layer_norm(final_sum, gain_two, shift_two).astype(BF16)

    upstream = cotangent.reshape(micro * per, width).astype(F32)
    grad_final, g_gain_two, g_shift_two = jax.vjp(layer_norm, final_sum, gain_two, shift_two)[1](upstream)
    grad_second = grad_final.astype(BF16)
    g_back_bias = jnp.sum(grad_second.astype(F32), axis=0)
    grad_activated = jnp.einsum("rm,km->rk", grad_second, full_back, preferred_element_type=F32)
    grad_hidden = jax.vjp(exact_gelu, hidden)[1](grad_activated)[0].astype(BF16)
    g_in_bias = jnp.sum(grad_hidden.astype(F32), axis=0)
    grad_normed = grad_final + jnp.einsum("rf,mf->rm", grad_hidden, full_in, preferred_element_type=F32)
    grad_first, g_gain_one, g_shift_one = jax.vjp(layer_norm, first_sum, gain_one, shift_one)[1](grad_normed)
    grad_branch = grad_first.astype(BF16)
    g_out_bias = jnp.sum(grad_branch.astype(F32), axis=0)
    grad_attended = jnp.einsum("rm,km->rk", grad_branch, full_out, preferred_element_type=F32).astype(BF16)
    (do_held,) = swap([by_group(grad_attended, micro, 64, 0)], cols, 4)
    if cube:
        small = [jnp.zeros((2, width), F32)] + [x[None] for x in (g_out_bias, g_back_bias, g_gain_one, g_shift_one, g_gain_two, g_shift_two)]
        small += [g_in_bias.reshape(2, 4, share).transpose(1, 0, 2).reshape(4, width), jnp.zeros((4, width), F32)]
    dq, dkv = attend_backward(doc_lengths, q_held, kv_held, do_held.reshape(8 * per, 256), mixed_t, log_total, cols)
    if cube:
        grads, input_grad, sums = reduce_all(
            inputs, attended, normed_low, activated, grad_branch, grad_hidden, grad_second, grad_first, full_qkv,
            jnp.concatenate(small), dq.reshape(8, per, 256), dkv.reshape(8 * cols, per, 384), 5)
        g_qkv, g_out, g_in, g_back = widen(grads.reshape(2, share, 4608))
        rows = [sums[0], sums[1], sums[2], sums[8:12].reshape(-1), sums[3], sums[4], sums[5], sums[6], sums[7]]
        return (output.reshape(tokens.shape), input_grad.reshape(tokens.shape), g_qkv, g_out, g_in, g_back.reshape(4 * share, width)) + tuple(rows)
    dq_own, dkv_own = collect(dq.reshape(8, per, 256), dkv.reshape(8 * cols, per, 384), cols, 5)
    grad_joined = jnp.concatenate(
        [from_group(dq_own, micro, 0), from_group(dkv_own, micro, 0), from_group(dkv_own, micro, 192)], axis=1)
    g_query_bias = jnp.sum(grad_joined[:, :width].astype(F32), axis=0)
    g_value_bias = jnp.sum(grad_joined[:, 2 * width:].astype(F32), axis=0)
    input_grad = grad_first + jnp.einsum("rc,mc->rm", grad_joined, full_qkv, preferred_element_type=F32)

    def halves(left, right):
        blocks = right.shape[1] // 384
        return jnp.einsum("rm,rhc->hmc", left, right.reshape(-1, blocks, 384), preferred_element_type=F32).astype(BF16)

    back_grads = jnp.einsum("rk,rm->km", activated, grad_second, preferred_element_type=F32).astype(BF16)
    back_grads = back_grads.reshape(nf, 4, share, 2, 384).transpose(1, 3, 0, 2, 4).reshape(8, width, 384)
    grads = jnp.concatenate(
        [halves(inputs, grad_joined), halves(attended, grad_branch), halves(normed_low, grad_hidden), back_grads])
    grads = grads.reshape(2, 4, 3, nf, cols, share // cols, 384)
    small = (g_query_bias, g_value_bias, g_out_bias, g_in_bias, g_back_bias, g_gain_one, g_shift_one, g_gain_two, g_shift_two)
    small = jnp.concatenate([x.reshape(nf, -1) for x in small], axis=1).reshape(nf, 8, -1)
    owned, small_owned = reduce_grads(grads, small, nf, cols, 6)
    owned = owned.transpose(0, 1, 3, 2, 4, 5).reshape(24, share, 384)

    def columns(first, last):
        return owned[first:last].transpose(1, 0, 2).reshape(share, -1).astype(F32)

    g_back = owned[16:].reshape(4, 2, share, 384).transpose(0, 2, 1, 3).reshape(4 * share, width).astype(F32)
    small_owned = small_owned.reshape(-1)
    small_grads, at = [], 0
    for vector in vectors:
        small_grads.append(small_owned[at:at + vector.shape[0]])
        at += vector.shape[0]
    return (output.reshape(tokens.shape), input_grad.reshape(tokens.shape), columns(0, 6), columns(6, 8), columns(8, 16), g_back) + tuple(small_grads)


def solution(mesh):
    rows, flat = P("fsdp", "ctx", None), P("fsdp", None)
    return jax.shard_map(
        shards,
        mesh=mesh,
        in_specs=(rows, rows, flat) + (flat,) * 4 + (P("fsdp"),) * 9,
        out_specs=(rows, rows) + (flat,) * 4 + (P("fsdp"),) * 9,
        check_vma=False,
    )
```

```python
import functools

import jax
import jax.numpy as jnp
from jax import lax
from jax.experimental import pallas as pl
from jax.experimental.pallas import tpu as pltpu
from jax.sharding import PartitionSpec as P

MESH = pl.DeviceIdType.MESH
DMA = pltpu.SemaphoreType.DMA
F32, BF16 = jnp.float32, jnp.bfloat16
EPSILON = 1e-12

def place(cols):
    index = lax.axis_index("ctx")
    return index // (2 * cols), lax.rem(index // 2, cols), lax.rem(index, 2), lax.axis_index("fsdp")

def device(a, b, c, f, cols):
    return {"ctx": (a * cols + b) * 2 + c, "fsdp": f}

def meet(peers):
    barrier = pltpu.get_barrier_semaphore()
    for peer in peers:
        pl.semaphore_signal(barrier, inc=1, device_id=peer, device_id_type=MESH)
    pl.semaphore_wait(barrier, len(peers))

def remote(source, target, send, recv, peer):
    return pltpu.make_async_remote_copy(
        src_ref=source, dst_ref=target, send_sem=send, recv_sem=recv, device_id=peer, device_id_type=MESH)

def gather_kernel(nf, cols, count, *refs):
    shards, tiny, fulls, tiny_out = refs[:count], refs[count], refs[count+1:2*count+1], refs[2*count+1]
    local_sem, s1, r1, s2, r2, s3, r3, st, rt = refs[2*count+2:]
    a, b, c, f = place(cols)
    other = 1 - c
    fpeers = [device(a, b, c, lax.rem(f + j, nf), cols) for j in range(1, nf)]
    bpeers = [device(a, lax.rem(b + k, cols), c, f, cols) for k in range(1, cols)]
    sibling = device(a, b, other, f, cols)
    meet(fpeers + bpeers + [sibling])

    def view(w, owner, bb, cc, base=0):
        rows, wide = shards[w].shape
        part, half = rows // cols, wide // 2
        return fulls[w].at[pl.ds(pl.multiple_of(owner * rows + bb * part, 8), part), pl.ds(pl.multiple_of(cc * half, 128), half)]

    waits = []
    for j in range(1, nf):
        cp = remote(tiny, tiny_out.at[f], st.at[j - 1], rt.at[j - 1], fpeers[j - 1])
        cp.start()
        waits.append(cp)
    locals_ = [pltpu.make_async_copy(tiny, tiny_out.at[f], local_sem.at[count])]
    locals_[0].start()
    first = {}
    for w in range(count):
        rows, wide = shards[w].shape
        part, half = rows // cols, wide // 2
        mine = shards[w].at[pl.ds(pl.multiple_of(b * part, 8), part), pl.ds(pl.multiple_of(c * half, 128), half)]
        for j in range(1, nf):
            cp = remote(mine, view(w, f, b, c), s1.at[w, j - 1], r1.at[w, j - 1], fpeers[j - 1])
            cp.start()
            first[w, j] = cp
    for w in range(count):
        rows = shards[w].shape[0]
        cp = pltpu.make_async_copy(shards[w], fulls[w].at[pl.ds(pl.multiple_of(f * rows, 8), rows)], local_sem.at[w])
        cp.start()
        locals_.append(cp)
    second, third = {}, []
    for w in range(count):
        for j in range(1, nf):
            owner = lax.rem(f + nf - j, nf)
            first[w, j].wait_recv()
            piece = view(w, owner, b, c)
            for k in range(1, cols):
                slot = (j - 1) * (cols - 1) + k - 1
                cp = remote(piece, piece, s2.at[w, slot], r2.at[w, slot], bpeers[k - 1])
                cp.start()
                second[w, j, k] = cp
            cp = remote(piece, piece, s3.at[w, (j - 1) * cols], r3.at[w, (j - 1) * cols], sibling)
            cp.start()
            third.append(cp)
    for w in range(count):
        for j in range(1, nf):
            owner = lax.rem(f + nf - j, nf)
            for k in range(1, cols):
                second[w, j, k].wait_recv()
                piece = view(w, owner, lax.rem(b + cols - k, cols), c)
                cp = remote(piece, piece, s3.at[w, (j - 1) * cols + k], r3.at[w, (j - 1) * cols + k], sibling)
                cp.start()
                third.append(cp)
    for cp in third:
        cp.wait_recv()
    for cp in waits:
        cp.wait()
    for cp in list(first.values()) + list(second.values()) + third:
        cp.wait_send()
    for cp in locals_:
        cp.wait()

def gather_weights(shards, tiny, nf, cols):
    count = len(shards)
    any_spec = pl.BlockSpec(memory_space=pl.ANY)
    dma = pltpu.SemaphoreType.DMA
    return pl.pallas_call(
        functools.partial(gather_kernel, nf, cols, count),
        out_shape=[jax.ShapeDtypeStruct((s.shape[0] * nf, s.shape[1]), s.dtype) for s in shards]
        + [jax.ShapeDtypeStruct((nf,) + tiny.shape, tiny.dtype)],
        in_specs=[pl.BlockSpec(memory_space=pltpu.VMEM)] * (count + 1),
        out_specs=[any_spec] * (count + 1),
        scratch_shapes=[dma((count + 1,)), dma((count, nf - 1)), dma((count, nf - 1)),
                        dma((count, (nf - 1) * (cols - 1))), dma((count, (nf - 1) * (cols - 1))),
                        dma((count, (nf - 1) * cols)), dma((count, (nf - 1) * cols)),
                        dma((nf - 1,)), dma((nf - 1,))],
        compiler_params=pltpu.CompilerParams(collective_id=1, has_side_effects=True, vmem_limit_bytes=32 << 20),
        name="gather_weights",
    )(*shards, tiny)

def octet(a, b, c, f, cols):
    me = a * 2 + c
    out = []
    for k in range(1, 8):
        other = lax.rem(me + k, 8)
        out.append((other, device(other // 2, b, lax.rem(other, 2), f, cols)))
    return me, out

def swap_kernel(cols, count, *refs):
    sources, targets = refs[:count], refs[count:2 * count]
    send, recv, here = refs[2 * count:]
    a, b, c, f = place(cols)
    me, peers = octet(a, b, c, f, cols)
    meet([p for _, p in peers])
    copies = []
    for k, (other, peer) in enumerate(peers):
        for i in range(count):
            cp = remote(sources[i].at[other], targets[i].at[me], send.at[i, k], recv.at[i, k], peer)
            cp.start()
            copies.append(cp)
    for i in range(count):
        cp = pltpu.make_async_copy(sources[i].at[me], targets[i].at[me], here.at[i])
        cp.start()
        copies.append(cp)
    for cp in copies:
        cp.wait()

def swap(arrays, cols, ident):
    count = len(arrays)
    return pl.pallas_call(
        functools.partial(swap_kernel, cols, count),
        out_shape=[jax.ShapeDtypeStruct(x.shape, x.dtype) for x in arrays],
        in_specs=[vmem()] * count, out_specs=[vmem()] * count,
        scratch_shapes=[DMA((count, 7)), DMA((count, 7)), DMA((count,))],
        compiler_params=pltpu.CompilerParams(collective_id=ident, has_side_effects=True, vmem_limit_bytes=16 << 20),
        name="swap",
    )(*arrays)

def spread_kernel(cols, q, kv, qg, full, sq, rq, sk, rk, s2, r2, here):
    a, b, c, f = place(cols)
    me, peers = octet(a, b, c, f, cols)
    bpeers = [device(a, lax.rem(b + k, cols), c, f, cols) for k in range(1, cols)]
    meet([p for _, p in peers] + bpeers)

    def slot(block, bb):
        return (block // 2 * cols + bb) * 2 + lax.rem(block, 2)

    first = []
    for k, (other, peer) in enumerate(peers):
        cp = remote(kv.at[other], full.at[slot(me, b)], sk.at[k], rk.at[k], peer)
        cp.start()
        first.append(cp)
    own = pltpu.make_async_copy(kv.at[me], full.at[slot(me, b)], here.at[0])
    own.start()
    ownq = pltpu.make_async_copy(q.at[me], qg.at[me], here.at[1])
    ownq.start()
    second = []
    for k, peer in enumerate(bpeers):
        cp = remote(kv.at[me], full.at[slot(me, b)], s2.at[7, k], r2.at[7, k], peer)
        cp.start()
        second.append(cp)
    third = []
    for k, (other, peer) in enumerate(peers):
        cp = remote(q.at[other], qg.at[me], sq.at[k], rq.at[k], peer)
        cp.start()
        third.append(cp)
    for k in range(7):
        first[k].wait_recv()
        source = lax.rem(me + 8 - (k + 1), 8)
        piece = full.at[slot(source, b)]
        for m, peer in enumerate(bpeers):
            cp = remote(piece, piece, s2.at[k, m], r2.at[k, m], peer)
            cp.start()
            second.append(cp)
    for cp in first:
        cp.wait_send()
    for cp in second + third:
        cp.wait()
    own.wait()
    ownq.wait()

def spread(q, kv, cols, ident):
    return pl.pallas_call(
        functools.partial(spread_kernel, cols),
        out_shape=[jax.ShapeDtypeStruct(q.shape, q.dtype), jax.ShapeDtypeStruct((8 * cols,) + kv.shape[1:], kv.dtype)],
        in_specs=[vmem()] * 2, out_specs=[vmem()] * 2,
        scratch_shapes=[DMA((7,))] * 4 + [DMA((8, max(cols - 1, 1)))] * 2 + [DMA((2,))],
        compiler_params=pltpu.CompilerParams(collective_id=ident, has_side_effects=True, vmem_limit_bytes=16 << 20),
        name="spread",
    )(q, kv)

def collect_kernel(cols, dq, dkv, dqo, dkvo, rbuf, total, sq, rq, sk, rk, s2, r2, here):
    a, b, c, f = place(cols)
    me, peers = octet(a, b, c, f, cols)
    bpeers = [(lax.rem(b + k, cols), device(a, lax.rem(b + k, cols), c, f, cols)) for k in range(1, cols)]
    meet([p for _, p in peers] + [p for _, p in bpeers])

    def slot(block, bb):
        return (block // 2 * cols + bb) * 2 + lax.rem(block, 2)

    order = [other for other, _ in peers] + [me]
    first = {}
    for n, block in enumerate(order):
        for k, (bb, peer) in enumerate(bpeers):
            cp = remote(dkv.at[slot(block, bb)], rbuf.at[k, n], s2.at[k, n], r2.at[k, n], peer)
            cp.start()
            first[k, n] = cp
    rest = []
    for k, (other, peer) in enumerate(peers):
        cp = remote(dq.at[other], dqo.at[me], sq.at[k], rq.at[k], peer)
        cp.start()
        rest.append(cp)
    own = pltpu.make_async_copy(dq.at[me], dqo.at[me], here.at[0])
    own.start()
    for n, block in enumerate(order):
        value = dkv[slot(block, b)].astype(F32)
        for k in range(cols - 1):
            first[k, n].wait_recv()
            value = value + rbuf[k, n].astype(F32)
        if n < 7:
            total[n] = value.astype(BF16)
            cp = remote(total.at[n], dkvo.at[me], sk.at[n], rk.at[n], peers[n][1])
            cp.start()
            rest.append(cp)
        else:
            dkvo[me] = value.astype(BF16)
    for cp in first.values():
        cp.wait_send()
    for cp in rest:
        cp.wait()
    own.wait()

def collect(dq, dkv, cols, ident):
    block = dkv.shape[1:]
    return pl.pallas_call(
        functools.partial(collect_kernel, cols),
        out_shape=[jax.ShapeDtypeStruct(dq.shape, dq.dtype), jax.ShapeDtypeStruct((8,) + block, dkv.dtype)],
        in_specs=[vmem()] * 2, out_specs=[vmem()] * 2,
        scratch_shapes=[pltpu.VMEM((max(cols - 1, 1), 8) + block, BF16), pltpu.VMEM((7,) + block, BF16)]
        + [DMA((7,))] * 4 + [DMA((max(cols - 1, 1), 8))] * 2 + [DMA((1,))],
        compiler_params=pltpu.CompilerParams(collective_id=ident, has_side_effects=True, vmem_limit_bytes=24 << 20),
        name="collect",
    )(dq, dkv)

def reduce_kernel(nf, cols, parts, grads, small, out, small_out, *refs):
    own, core_in, f_in, b_in, f_in2, b_in2, a_in, v_core, v_sum, v_f, v_b, v_a = refs[:12]
    load, sc, rc, s1, r1, s2, r2, s3, r3, s4, r4, s5, r5, s6, r6, sv, rv = refs[12:]
    a, b, c, f = place(cols)
    rows = grads.shape[5]
    fpeers = [(lax.rem(f + j, nf), device(a, b, c, lax.rem(f + j, nf), cols)) for j in range(1, nf)]
    bpeers = [(lax.rem(b + k, cols), device(a, lax.rem(b + k, cols), c, f, cols)) for k in range(1, cols)]
    apeers = [(lax.rem(a + k, 4), device(lax.rem(a + k, 4), b, c, f, cols)) for k in range(1, 4)]
    sibling = device(a, b, 1 - c, f, cols)
    meet([p for _, p in fpeers + bpeers + apeers] + [sibling])
    vector = remote(small, v_core, sv.at[0], rv.at[0], sibling)
    vector.start()
    order = [2, 1, 3, 0]
    dest = {k: lax.rem(a + k, 4) for k in range(4)}
    by_f = {k: k in (1, 2) for k in range(4)}
    loads, cores = {}, {}
    for k in order:
        for i in range(parts):
            cp = pltpu.make_async_copy(grads.at[c, dest[k], i], own.at[k, i], load.at[k, i])
            cp.start()
            loads[k, i] = cp
            cp = remote(grads.at[1 - c, dest[k], i], core_in.at[k, i], sc.at[k, i], rc.at[k, i], sibling)
            cp.start()
            cores[k, i] = cp
    one, two, three = {}, {}, {}
    vec = {}
    vector.wait_recv()
    v_sum[...] = small[...] + v_core[...]
    for j, (ff, peer) in enumerate(fpeers):
        vec[0, j] = remote(v_sum.at[ff], v_f.at[j], sv.at[1 + j], rv.at[1 + j], peer)
        vec[0, j].start()
    for k in order:
        for i in range(parts):
            loads[k, i].wait()
            cores[k, i].wait_recv()

            @pl.loop(0, nf * cols)
            def _(n):
                ff, bb = n // cols, lax.rem(n, cols)
                own[k, i, ff, bb] = (own[k, i, ff, bb].astype(F32) + core_in[k, i, ff, bb].astype(F32)).astype(BF16)

            if by_f[k]:
                for j, (ff, peer) in enumerate(fpeers):
                    cp = remote(own.at[k, i, ff], f_in.at[k, i, j], s1.at[k, i, j], r1.at[k, i, j], peer)
                    cp.start()
                    one[k, i, j] = cp
            else:
                for m, (bb, peer) in enumerate(bpeers):
                    for ff in range(nf):
                        cp = remote(own.at[k, i, ff, bb], b_in.at[k, i, m, ff], s1.at[k, i, m * nf + ff], r1.at[k, i, m * nf + ff], peer)
                        cp.start()
                        one[k, i, m * nf + ff] = cp
    value = v_sum[f]
    for j in range(nf - 1):
        vec[0, j].wait_recv()
        value = value + v_f[j]
    v_b[b] = value
    for m, (bb, peer) in enumerate(bpeers):
        vec[1, m] = remote(v_b.at[b], v_b.at[b], sv.at[nf + m], rv.at[nf + m], peer)
        vec[1, m].start()
    for k in order:
        for i in range(parts):
            if by_f[k]:
                for j in range(nf - 1):
                    one[k, i, j].wait_recv()

                @pl.loop(0, cols)
                def _(bb):
                    value = own[k, i, f, bb].astype(F32)
                    for j in range(nf - 1):
                        value = value + f_in[k, i, j, bb].astype(F32)
                    own[k, i, f, bb] = value.astype(BF16)

                for m, (bb, peer) in enumerate(bpeers):
                    cp = remote(own.at[k, i, f, bb], b_in2.at[k, i, m], s2.at[k, i, m], r2.at[k, i, m], peer)
                    cp.start()
                    two[k, i, m] = cp
            else:
                for m in range(cols - 1):
                    for ff in range(nf):
                        one[k, i, m * nf + ff].wait_recv()

                @pl.loop(0, nf)
                def _(ff):
                    value = own[k, i, ff, b].astype(F32)
                    for m in range(cols - 1):
                        value = value + b_in[k, i, m, ff].astype(F32)
                    own[k, i, ff, b] = value.astype(BF16)

                for j, (ff, peer) in enumerate(fpeers):
                    cp = remote(own.at[k, i, ff, b], f_in2.at[k, i, j], s2.at[k, i, j], r2.at[k, i, j], peer)
                    cp.start()
                    two[k, i, j] = cp
    for m in range(cols - 1):
        vec[1, m].wait_recv()
    value = v_b[0]
    for m in range(1, cols):
        value = value + v_b[m]
    v_a[a] = value
    for k in range(1, 4):
        vec[2, k] = remote(v_a.at[a], v_a.at[a], sv.at[nf + cols + k - 2], rv.at[nf + cols + k - 2], apeers[k - 1][1])
        vec[2, k].start()
    for k in order:
        for i in range(parts):
            value = own[k, i, f, b].astype(F32)
            if by_f[k]:
                for m in range(cols - 1):
                    two[k, i, m].wait_recv()
                    value = value + b_in2[k, i, m].astype(F32)
            else:
                for j in range(nf - 1):
                    two[k, i, j].wait_recv()
                    value = value + f_in2[k, i, j].astype(F32)
            if k != 0:
                own[k, i, f, b] = value.astype(BF16)
                cp = remote(own.at[k, i, f, b], a_in.at[k - 1, i], s3.at[k - 1, i], r3.at[k - 1, i], apeers[k - 1][1])
                cp.start()
                three[k, i] = cp
            else:
                own[k, i, f, b] = value.astype(BF16)
    for k in range(1, 4):
        vec[2, k].wait_recv()
    small_out[...] = v_a[0] + v_a[1] + v_a[2] + v_a[3]
    four, five, six = {}, {}, {}

    def piece(aa, bb, cc, i):
        return out.at[cc, aa, bb, i]

    pending = []
    for i in range(parts):
        value = own[0, i, f, b].astype(F32)
        for k in range(1, 4):
            three[k, i].wait_recv()
            value = value + a_in[k - 1, i].astype(F32)
        out[c, a, b, i] = value.astype(BF16)
        mine = piece(a, b, c, i)
        for k in (2, 1, 3):
            cp = remote(mine, mine, s4.at[k - 1, i], r4.at[k - 1, i], apeers[k - 1][1])
            cp.start()
            four[k, i] = cp
        for m, (bb, peer) in enumerate(bpeers):
            cp = remote(mine, mine, s5.at[0, i, m], r5.at[0, i, m], peer)
            cp.start()
            five[0, i, m] = cp
        cp = remote(mine, mine, s6.at[0, i, 0], r6.at[0, i, 0], sibling)
        cp.start()
        six[0, i, 0] = cp
    for i in range(parts):
        for k in (1, 3, 2):
            four[k, i].wait_recv()
            got = piece(lax.rem(a + 4 - k, 4), b, c, i)
            for m, (bb, peer) in enumerate(bpeers):
                cp = remote(got, got, s5.at[k, i, m], r5.at[k, i, m], peer)
                cp.start()
                five[k, i, m] = cp
            cp = remote(got, got, s6.at[k, i, 0], r6.at[k, i, 0], sibling)
            cp.start()
            six[k, i, 0] = cp
    for i in range(parts):
        for k in (0, 1, 3, 2):
            for m in range(cols - 1):
                five[k, i, m].wait_recv()
                got = piece(lax.rem(a + 4 - k, 4), lax.rem(b + cols - (m + 1), cols), c, i)
                cp = remote(got, got, s6.at[k, i, m + 1], r6.at[k, i, m + 1], sibling)
                cp.start()
                six[k, i, m + 1] = cp
    for cp in six.values():
        cp.wait_recv()
    vector.wait_send()
    for group in (cores, one, two, three, four, five, six, vec):
        for cp in group.values():
            cp.wait_send()

def reduce_grads(grads, small, nf, cols, ident):
    _, _, parts, _, _, rows, width = grads.shape
    block = (rows, width)
    m = max(cols - 1, 1)
    n = max((cols - 1) * nf, nf - 1)
    return pl.pallas_call(
        functools.partial(reduce_kernel, nf, cols, parts),
        out_shape=[jax.ShapeDtypeStruct((2, 4, cols, parts) + block, BF16), jax.ShapeDtypeStruct(small.shape[1:], F32)],
        in_specs=[pl.BlockSpec(memory_space=pl.ANY), vmem()], out_specs=[vmem()] * 2,
        scratch_shapes=[pltpu.VMEM((4, parts, nf, cols) + block, BF16), pltpu.VMEM((4, parts, nf, cols) + block, BF16),
                        pltpu.VMEM((4, parts, nf - 1, cols) + block, BF16), pltpu.VMEM((4, parts, m, nf) + block, BF16),
                        pltpu.VMEM((4, parts, nf - 1) + block, BF16), pltpu.VMEM((4, parts, m) + block, BF16),
                        pltpu.VMEM((3, parts) + block, BF16),
                        pltpu.VMEM(small.shape, F32), pltpu.VMEM(small.shape, F32), pltpu.VMEM((nf - 1,) + small.shape[1:], F32),
                        pltpu.VMEM((cols,) + small.shape[1:], F32), pltpu.VMEM((4,) + small.shape[1:], F32),
                        DMA((4, parts)), DMA((4, parts)), DMA((4, parts)), DMA((4, parts, n)), DMA((4, parts, n)),
                        DMA((4, parts, max(m, nf - 1))), DMA((4, parts, max(m, nf - 1))),
                        DMA((3, parts)), DMA((3, parts)), DMA((3, parts)), DMA((3, parts)),
                        DMA((4, parts, m)), DMA((4, parts, m)), DMA((4, parts, cols)), DMA((4, parts, cols)),
                        DMA((nf + cols + 2,)), DMA((nf + cols + 2,))],
        compiler_params=pltpu.CompilerParams(collective_id=ident, has_side_effects=True, vmem_limit_bytes=56 << 20),
        name="reduce_grads",
    )(grads, small)
KB = 256
SPAN = 256
MASKED = -1e30

def dot(x, y, dims):
    return lax.dot_general(x, y, (dims, ((), ())), preferred_element_type=F32)

NT = ((1,), (1,))
NN = ((1,), (0,))
TN = ((0,), (0,))

def bounds(lens, stream):
    ends, total = [], 0
    for j in range(4):
        total = total + lens[stream, j]
        ends.append(total)
    return ends

def doc_range(pos, ends):
    start = jnp.where(pos >= ends[0], ends[0], 0)
    stop = jnp.where(pos < ends[0], ends[0], ends[3])
    for j in (1, 2):
        start = jnp.where(pos >= ends[j], ends[j], start)
    for j in (2, 1, 0):
        stop = jnp.where(pos < ends[j], ends[j], stop)
    return start, stop

def block_range(base, ends):
    low, _ = doc_range(base, ends)
    _, high = doc_range(base + (SPAN - 1), ends)
    return low // KB, (high + (KB - 1)) // KB

def lane_head(shape, shift):
    lane = lax.broadcasted_iota(jnp.int32, shape, 1)
    return (lane - shift) // 64

def forward_kernel(cols, lens, q_ref, kv_ref, o_ref, ot_ref, lse_ref, qm, vt, acc):
    index = lax.axis_index("ctx")
    b, c = lax.rem(index // 2, cols), lax.rem(index, 2)
    ends = bounds(lens, c)
    total = kv_ref.shape[0]

    @pl.loop(0, total // KB)
    def _(n):
        rows = pl.ds(pl.multiple_of(n * KB, KB), KB)
        vt[:, rows] = kv_ref[rows, 128:384].astype(F32).T.astype(BF16)

    @pl.loop(0, 4)
    def _(stripe):
        base = SPAN * (stripe * cols + b)
        rows = pl.ds(pl.multiple_of(stripe * SPAN, SPAN), SPAN)
        head = lane_head((SPAN, 256), 0)
        q = q_ref[rows].astype(F32) * 0.125
        for h in range(3):
            qm[h] = jnp.where(head == h, q, 0.0).astype(BF16)
        qpos = base + lax.broadcasted_iota(jnp.int32, (1, SPAN), 1)
        start, stop = doc_range(qpos, ends)
        low, high = block_range(base, ends)
        acc[...] = jnp.zeros_like(acc)

        def step(n, state):
            krows = pl.ds(pl.multiple_of(n * KB, KB), KB)
            keys = kv_ref[krows, 0:256]
            kpos = n * KB + lax.broadcasted_iota(jnp.int32, (KB, 1), 0)
            allowed = (kpos >= start) & (kpos < stop)
            out = []
            for h in range(3):
                top, tot = state[h]
                s = jnp.where(allowed, dot(keys, qm[h], NT), MASKED)
                new = jnp.maximum(top, jnp.max(s, axis=0, keepdims=True))
                p = jnp.exp(s - new)
                scale = jnp.exp(top - new)
                hrows = pl.ds(64 * (h + 1), 64)
                acc[hrows] = acc[hrows] * scale + dot(vt[hrows, krows], p.astype(BF16), NN)
                out.append((new, tot * scale + jnp.sum(p, axis=0, keepdims=True)))
            return tuple(out)

        first = tuple((jnp.full((1, SPAN), MASKED, F32), jnp.zeros((1, SPAN), F32)) for _ in range(3))
        final = lax.fori_loop(low, high, step, first)
        for h in range(3):
            top, tot = final[h]
            hrows = pl.ds(64 * (h + 1), 64)
            acc[hrows] = acc[hrows] * (1.0 / tot)
            lse_ref[stripe, pl.ds(h, 1)] = top + jnp.log(tot)
        ot_ref[stripe] = acc[...]
        o_ref[rows] = acc[...].T.astype(BF16)

def vmem():
    return pl.BlockSpec(memory_space=pltpu.VMEM)

def attend_forward(lens, q, kv, cols):
    total = kv.shape[0]
    return pl.pallas_call(
        functools.partial(forward_kernel, cols),
        out_shape=[jax.ShapeDtypeStruct(q.shape, BF16), jax.ShapeDtypeStruct((4, 256, SPAN), F32),
                   jax.ShapeDtypeStruct((4, 8, SPAN), F32)],
        in_specs=[pl.BlockSpec(memory_space=pltpu.SMEM), vmem(), vmem()],
        out_specs=[vmem()] * 3,
        scratch_shapes=[pltpu.VMEM((3, SPAN, 256), BF16), pltpu.VMEM((256, total), BF16), pltpu.VMEM((256, SPAN), F32)],
        compiler_params=pltpu.CompilerParams(vmem_limit_bytes=32 << 20),
        name="attend_forward",
    )(lens, q, kv)

def backward_kernel(cols, lens, q_ref, kv_ref, do_ref, ot_ref, lse_ref, dq_ref, dkv_ref, qm, dm, kt, dk, dv, acc):
    index = lax.axis_index("ctx")
    b, c = lax.rem(index // 2, cols), lax.rem(index, 2)
    ends = bounds(lens, c)
    total = kv_ref.shape[0]

    @pl.loop(0, total // KB)
    def _(n):
        rows = pl.ds(pl.multiple_of(n * KB, KB), KB)
        kt[:, rows] = kv_ref[rows, 0:256].astype(F32).T.astype(BF16)
        dk[rows] = jnp.zeros((KB, 256), F32)
        dv[rows] = jnp.zeros((KB, 256), F32)

    @pl.loop(0, 4)
    def _(stripe):
        base = SPAN * (stripe * cols + b)
        rows = pl.ds(pl.multiple_of(stripe * SPAN, SPAN), SPAN)
        head = lane_head((SPAN, 256), 0)
        headv = lane_head((SPAN, 256), 64)
        q = q_ref[rows].astype(F32) * 0.125
        grad = do_ref[rows].astype(F32)
        for h in range(3):
            qm[h] = jnp.where(head == h, q, 0.0).astype(BF16)
            dm[h] = jnp.where(headv == h, grad, 0.0).astype(BF16)
        prod = grad.T * ot_ref[stripe]
        deltas = [jnp.sum(prod[64 * (h + 1):64 * (h + 2)], axis=0, keepdims=True) for h in range(3)]
        lses = [lse_ref[stripe, pl.ds(h, 1)] for h in range(3)]
        qpos = base + lax.broadcasted_iota(jnp.int32, (1, SPAN), 1)
        start, stop = doc_range(qpos, ends)
        low, high = block_range(base, ends)
        acc[...] = jnp.zeros_like(acc)

        @pl.loop(low, high)
        def _(n):
            krows = pl.ds(pl.multiple_of(n * KB, KB), KB)
            keys = kv_ref[krows, 0:256]
            vals = kv_ref[krows, 128:384]
            kpos = n * KB + lax.broadcasted_iota(jnp.int32, (KB, 1), 0)
            allowed = (kpos >= start) & (kpos < stop)
            newk, newv = dk[krows], dv[krows]
            for h in range(3):
                s = jnp.where(allowed, dot(keys, qm[h], NT), MASKED)
                p = jnp.exp(s - lses[h])
                gp = dot(vals, dm[h], NT)
                ds = (p * (gp - deltas[h])).astype(BF16)
                newv = newv + dot(p.astype(BF16), dm[h], NN)
                newk = newk + dot(ds, qm[h], NN)
                hrows = pl.ds(64 * h, 64)
                acc[hrows] = acc[hrows] + dot(kt[hrows, krows], ds, NN)
            dk[krows] = newk
            dv[krows] = newv

        dq_ref[rows] = (acc[...] * 0.125).T.astype(BF16)

    @pl.loop(0, total // KB)
    def _(n):
        rows = pl.ds(pl.multiple_of(n * KB, KB), KB)
        dkv_ref[rows, 0:128] = dk[rows, 0:128].astype(BF16)
        dkv_ref[rows, 128:256] = (dk[rows, 128:256] + dv[rows, 0:128]).astype(BF16)
        dkv_ref[rows, 256:384] = dv[rows, 128:256].astype(BF16)

def attend_backward(lens, q, kv, do, ot, lse, cols):
    total = kv.shape[0]
    return pl.pallas_call(
        functools.partial(backward_kernel, cols),
        out_shape=[jax.ShapeDtypeStruct(q.shape, BF16), jax.ShapeDtypeStruct(kv.shape, BF16)],
        in_specs=[pl.BlockSpec(memory_space=pltpu.SMEM)] + [vmem()] * 5,
        out_specs=[vmem()] * 2,
        scratch_shapes=[pltpu.VMEM((3, SPAN, 256), BF16), pltpu.VMEM((3, SPAN, 256), BF16), pltpu.VMEM((256, total), BF16),
                        pltpu.VMEM((total, 256), F32), pltpu.VMEM((total, 256), F32), pltpu.VMEM((256, SPAN), F32)],
        compiler_params=pltpu.CompilerParams(vmem_limit_bytes=40 << 20),
        name="attend_backward",
    )(lens, q, kv, do, ot, lse)


STEPS = ((1, 0), (3, 0), (1, 1), (3, 1), (2, 0), (0, 1), (2, 1))


class Octet:
    def __init__(self, go):
        self.go = go
        self.a, self.b, self.c, self.f = a, b, c, f = place(2)
        self.me = a * 2 + c
        self.others = [lax.rem(a + da, 4) * 2 + lax.rem(c + dc, 2) for da, dc in STEPS]
        self.sources = [lax.rem(a + 4 - da, 4) * 2 + lax.rem(c + dc, 2) for da, dc in STEPS]
        self.devices = [device(lax.rem(a + da, 4), b, lax.rem(c + dc, 2), f, 2) for da, dc in STEPS]
        self.relay, self.beyond = self.devices[3], self.devices[1]
        self.origin = lax.rem(a + 1, 4) * 2 + 1 - c

    def send(self, n, source, target, spare):
        if n < 6:
            return self.go(source, target(self.me), self.devices[n])
        return self.go(source, spare, self.relay)

    def forward(self, copy, target, spare):
        copy.wait_recv()
        return self.go(spare, target(self.origin), self.beyond)


def project_kernel(tokens, *refs):
    shards, vectors = refs[:4], refs[4:13]
    q_held, kv_held, f_qkv, f_out, f_in, f_back, vec, turned = refs[13:21]
    own = refs[21:25]
    whole, acc, q_sent, kv_sent, v_own, token, q_spare, kv_spare, held, held_spare = refs[25:35]
    flat, (send, recv, here) = refs[35:44], refs[44:]
    fulls = (f_qkv, f_out, f_in, f_back)
    a, b, c, f = place(2)
    group = Octet(None)
    me = group.me
    odd_a = lax.rem(a, 2)
    xp, yp, sp = device(a, 1 - b, c, f, 2), device(a, b, c, 1 - f, 2), device(a, b, 1 - c, f, 2)
    pairs = [device(lax.rem(a + 5 - 2 * odd_a, 4), b, c, f, 2), device(lax.rem(a + 3 + 2 * odd_a, 4), b, c, f, 2)]
    loads = [pltpu.make_async_copy(shards[w], own[w], here.at[w]) for w in range(4)]
    flats = [pltpu.make_async_copy(ref, flat[n], here.at[12 + n]) for n, ref in enumerate(vectors)]
    flats.append(pltpu.make_async_copy(tokens, token, here.at[11]))
    for cp in flats + loads:
        cp.start()
    meet(group.devices + [xp, yp])
    wires = Wires(send, recv)
    go = group.go = wires.go

    def rows_of(w, which, chunk):
        size = shards[w].shape[0] // 4
        return pl.multiple_of(which * 2 * size + chunk * size, 16), size

    def cols_of(w, cc):
        half = shards[w].shape[1] // 2
        return pl.ds(pl.multiple_of(cc * half, 128), half)

    def region(target, w, owner, which, cc, chunk):
        start, size = rows_of(w, which, chunk)
        return target.at[pl.ds(owner * shards[w].shape[0] + start, size), cols_of(w, cc)]

    def source(w, which, chunk):
        start, size = rows_of(w, which, chunk)
        return shards[w].at[pl.ds(start, size), cols_of(w, c)]

    other_f = 1 - f

    class Fetch:
        def __init__(self, target, w, chunk, pair=None):
            self.target, self.w, self.chunk = target, w, chunk
            self.which = b if pair is None else odd_a
            self.peer = xp if pair is None else pairs[pair]
            self.first = go(source(w, self.which, chunk), region(target, w, f, self.which, c, chunk), yp)

        def second(self):
            self.first.wait_recv()
            got = region(self.target, self.w, other_f, self.which, c, self.chunk)
            self.cross = go(got, got, self.peer)
            self.side = go(got, got, sp)

        def third(self):
            self.cross.wait_recv()
            got = region(self.target, self.w, other_f, 1 - self.which, c, self.chunk)
            self.side2 = go(got, got, sp)

        def end(self):
            self.side.wait_recv()
            self.side2.wait_recv()

    class Straight:
        def __init__(self, target, w, chunk, which):
            self.place = (target, w, other_f, which, c, chunk)
            self.first = go(source(w, which, chunk), region(target, w, f, which, c, chunk), yp)

        def second(self):
            self.first.wait_recv()
            got = region(*self.place)
            self.side = go(got, got, sp)

        def third(self):
            pass

        def end(self):
            self.side.wait_recv()

    qkv = [Fetch(whole, 0, 0)]
    for cp in flats:
        cp.wait()
    held_slot = lambda block: held.at[block]

    def token_block(dc):
        return token.at[pl.ds(pl.multiple_of(lax.rem(c + dc, 2) * 128, 128), 128)]

    toks = {n: group.send(n, token_block(STEPS[n][1]), held_slot, held_spare) for n in (6, 0, 1, 2, 3, 4, 5)}
    held[me] = token[pl.ds(pl.multiple_of(c * 128, 128), 128)]
    for n in range(9):
        value = flat[n][...].astype(F32)
        if n == 3:
            for j in range(4):
                v_own[8 + j:9 + j] = value[384 * j:384 * j + 384].reshape(1, 384)
        else:
            row = n if n < 3 else n - 1
            v_own[row:row + 1] = value.reshape(1, 384)
    v_own[12:16] = jnp.zeros((4, 384), F32)
    vec[f] = v_own[...]
    small = go(v_own, vec.at[f], yp)
    loads[0].wait()
    mine = pl.ds(pl.multiple_of(f * 384, 128), 384)
    theirs = pl.ds(pl.multiple_of(other_f * 384, 128), 384)

    @pl.loop(0, 6)
    def _(n):
        cols = pl.ds(pl.multiple_of(n * 384, 128), 384)
        acc[:, cols] = dot(token[:, mine], own[0][:, cols], NN)

    qkv[0].second()
    qkv.append(Fetch(whole, 0, 1))
    qkv[1].second()
    outer = [Fetch(f_back, 3, chunk, chunk) for chunk in range(2)]
    rest = [Fetch(f_out, 1, chunk) for chunk in range(2)]
    inner = [Straight(f_in, 2, chunk, which) for chunk in range(2) for which in range(2)]
    toks[6] = group.forward(toks[6], held_slot, held_spare)
    qkv[0].third()
    qkv[1].third()
    stores = []
    for w in range(4):
        if w > 0:
            loads[w].wait()
        rows = shards[w].shape[0]
        cp = pltpu.make_async_copy(own[w], fulls[w].at[pl.ds(pl.multiple_of(f * rows, 16), rows)], here.at[4 + w])
        cp.start()
        stores.append(cp)
    small.wait_recv()
    qkv[0].end()
    qkv[1].end()
    cp = pltpu.make_async_copy(whole.at[pl.ds(pl.multiple_of(other_f * 384, 16), 384)],
                               f_qkv.at[pl.ds(pl.multiple_of(other_f * 384, 16), 384)], here.at[8])
    cp.start()
    stores.append(cp)

    def column(n):
        cols = slice(384 * n, 384 * n + 384)
        value = acc[:, cols] + dot(token[:, theirs], whole[pl.ds(pl.multiple_of(other_f * 384, 16), 384), cols], NN)
        if n < 2:
            value = value + vec[n, 0:1]
        if n >= 4:
            value = value + vec[n - 4, 1:2]
        return value

    lane = lax.broadcasted_iota(jnp.int32, (256, 384), 1)
    for p in range(2):
        k, v = column(2 + p), column(4 + p)
        turned_k, turned_v = pltpu.roll(k, 192, 1), pltpu.roll(v, 192, 1)
        even = jnp.where(lane < 192, k, turned_v).astype(BF16)
        odd = jnp.where(lane < 192, turned_k, v).astype(BF16)
        q = column(p)
        q_even = jnp.where(lane < 192, q, 0.0)[:, :256].astype(BF16)
        q_odd = jnp.where(lane < 192, pltpu.roll(q, 192, 1), 0.0)[:, :256].astype(BF16)
        for s in range(2):
            rows = slice(128 * s, 128 * s + 128)
            kv_sent[4 * p + s], kv_sent[4 * p + 2 + s] = even[rows], odd[rows]
            q_sent[4 * p + s], q_sent[4 * p + 2 + s] = q_even[rows], q_odd[rows]

    def slot(block, bb):
        return (block // 2 * 2 + bb) * 2 + lax.rem(block, 2)

    kv_slot = lambda block: kv_held.at[slot(block, b)]
    q_slot = lambda block: q_held.at[block]
    first = [group.send(n, kv_sent.at[group.others[n]], kv_slot, kv_spare) for n in (6, 0, 1, 2, 3, 4, 5)]
    first = first[1:] + first[:1]
    own_kv = pltpu.make_async_copy(kv_sent.at[me], kv_held.at[slot(me, b)], here.at[9])
    own_kv.start()
    own_q = pltpu.make_async_copy(q_sent.at[me], q_held.at[me], here.at[10])
    own_q.start()
    crossed = [go(kv_sent.at[me], kv_held.at[slot(me, b)], xp)]
    third = [group.send(n, q_sent.at[group.others[n]], q_slot, q_spare) for n in (6, 0, 1, 2, 3, 4, 5)]
    third = third[1:] + third[:1]

    def onward(n):
        first[n].wait_recv()
        piece = kv_slot(group.sources[n])
        crossed.append(go(piece, piece, xp))

    onward(5)
    onward(0)
    onward(1)
    first[6] = group.forward(first[6], kv_slot, kv_spare)
    for cp in outer:
        cp.second()
    for cp in rest:
        cp.second()
    onward(2)
    onward(3)
    third[6] = group.forward(third[6], q_slot, q_spare)
    onward(4)
    onward(6)
    for cp in toks.values():
        cp.wait_recv()

    @pl.loop(0, 8)
    def _(n):
        @pl.loop(0, 6)
        def _(m):
            lanes = pl.ds(pl.multiple_of(m * 128, 128), 128)
            turned[n, lanes] = held[n, :, lanes].astype(F32).T.astype(BF16)

    for cp in inner:
        cp.second()
    for cp in outer:
        cp.third()
    for cp in rest:
        cp.third()
    for cp in crossed + third:
        cp.wait_recv()
    for cp in rest + inner + outer:
        cp.end()
    for cp in wires.made:
        cp.wait_send()
    for cp in stores + [own_kv, own_q]:
        cp.wait()


def project(tokens, shards, vectors, ident):
    rows, width = tokens.shape
    anywhere = pl.BlockSpec(memory_space=pl.ANY)
    wires = 80
    return pl.pallas_call(
        project_kernel,
        out_shape=[jax.ShapeDtypeStruct((8, 128, 256), BF16), jax.ShapeDtypeStruct((16, 128, 384), BF16)]
        + [jax.ShapeDtypeStruct((2 * s.shape[0], s.shape[1]), BF16) for s in shards]
        + [jax.ShapeDtypeStruct((2, 16, 384), F32), jax.ShapeDtypeStruct((8, 768, 128), BF16)],
        in_specs=[pl.BlockSpec(memory_space=pltpu.HBM)] * 14,
        out_specs=[vmem()] * 2 + [anywhere] * 4 + [vmem()] * 2,
        scratch_shapes=[pltpu.VMEM(s.shape, BF16) for s in shards]
        + [pltpu.VMEM((768, 2304), BF16), pltpu.VMEM((256, 2304), F32), pltpu.VMEM((8, 128, 256), BF16),
           pltpu.VMEM((8, 128, 384), BF16), pltpu.VMEM((16, 384), F32), pltpu.VMEM(tokens.shape, BF16),
           pltpu.VMEM((128, 256), BF16), pltpu.VMEM((128, 384), BF16),
           pltpu.VMEM((8, 128, 768), BF16), pltpu.VMEM((128, 768), BF16),
           *[pltpu.VMEM(v.shape, BF16) for v in vectors], DMA((wires,)), DMA((wires,)), DMA((21,))],
        compiler_params=pltpu.CompilerParams(collective_id=ident, has_side_effects=True, vmem_limit_bytes=62 << 20),
        name="project",
    )(tokens, *shards, *vectors)


BLK = 48
Z1, X1, Y1 = (0, 1152), (1152, 1920), (1920, 3456)
L0, L1 = (0, 256), (256, 640)


class Wires:
    def __init__(self, send, recv):
        self.send, self.recv, self.made = send, recv, []

    def go(self, source, target, peer):
        n = len(self.made)
        cp = remote(source, target, self.send.at[n], self.recv.at[n], peer)
        cp.start()
        self.made.append(cp)
        return cp


def transpose_into(target, source, base):
    width = source.shape[1]

    @pl.loop(0, width // 128)
    def _(n):
        at = pl.multiple_of(n * 128, 128)
        target[pl.ds(base + at, 128)] = source[:, pl.ds(at, 128)].astype(F32).T.astype(BF16)


def pair_columns(even, odd, lane, second):
    if second:
        return jnp.where(lane < 192, pltpu.roll(even, 192, 1), odd)
    return jnp.where(lane < 192, even, pltpu.roll(odd, 192, 1))


def halves(span):
    tiles = (span[1] - span[0]) // 128
    mid = span[0] + tiles // 2 * 128
    return (span[0], mid), (mid, span[1])


def within(span, group):
    base = 0
    for member in group:
        if member == span:
            return slice(base, base + span[1] - span[0])
        base += member[1] - member[0]


def gradient_kernel(lens, tt, att, low, act, gbr, ghid, gsec, small, do_sent, q_ref, kv_ref, ot_ref, lse_ref,
                    out, late_out, joined, small_out,
                    xt, mine, sib, cin, y8, y4, x8, x4, z4, z1r, zyb, zxb,
                    do_held, qm, dm, kt, dk, dv, acc, rowsc, delta, dq_all, dkv_all, dqo, dkvo, xsend, rbuf,
                    l_sib, l_in, l_acc, l_mine, ly, lx,
                    do_spare, dq_spare, dkv_spare, v_own, v_core, v_f, v_b, v_a, send, recv, here):
    group = Octet(None)
    a, b, c, f, me = group.a, group.b, group.c, group.f, group.me
    xp, yp, sp = device(a, 1 - b, c, f, 2), device(a, b, c, 1 - f, 2), device(a, b, 1 - c, f, 2)
    up, down = lax.rem(a + 1, 4), lax.rem(a + 3, 4)
    upp, downp = device(up, b, c, f, 2), device(down, b, c, f, 2)
    ends = bounds(lens, c)
    total = kv_ref.shape[0]
    meet(group.devices + [xp, yp])
    wires = Wires(send, recv)
    go = group.go = wires.go
    pending = []

    do_slot = lambda block: do_held.at[block]
    swaps = {n: group.send(n, do_sent.at[group.others[n]], do_slot, do_spare) for n in (6, 0, 1, 2, 3, 4, 5)}
    do_held[me] = do_sent[me]

    transpose_into(xt, act, 1536)

    def produce(kind, first, count, part, finish):
        @pl.loop(0, 2 * count)
        def _(n):
            ff, j = lax.rem(n, 2), first + n // 2
            if kind == "out":
                left, right = xt[pl.ds(pl.multiple_of(ff * 384, 128), 384)], gbr[:, pl.ds(pl.multiple_of(part * 384, 128), 384)]
                col = 0
            elif kind == "in":
                left = xt[pl.ds(pl.multiple_of(768 + ff * 384, 128), 384)]
                right = ghid[:, pl.ds(pl.multiple_of(part * 1536 + j * 384, 128), 384)]
                col = pl.multiple_of(384 + j * 384, 128)
            else:
                left = xt[pl.ds(pl.multiple_of(1536 + ff * 1536 + j * 384, 128), 384)]
                right = gsec[:, pl.ds(pl.multiple_of(part * 384, 128), 384)]
                col = pl.multiple_of(1920 + j * 384, 128)
            finish(pl.ds(ff * 2, 2), pl.ds(col, 384), dot(left, right, NN).reshape(2, 4, BLK, 384))

    def keep(rows, cols, value):
        sib[rows, :, :, cols] = value.astype(BF16)

    def join(rows, cols, value):
        mine[rows, :, :, cols] = (value + cin[rows, :, :, cols].astype(F32)).astype(BF16)

    core = {}

    def share(span):
        cols = slice(span[0], span[1])
        core[span] = go(sib.at[:, :, :, cols], cin.at[:, :, :, cols], sp)

    RS = (Y1, X1)

    def add(target, source):
        def step(n):
            t, s = target(n), source(n)
            t[...] = (t[...].astype(F32) + s[...].astype(F32)).astype(BF16)
        return step

    def accumulate(target, source, count):
        pl.loop(0, count)(add(target, source))

    ycols, xcols, zcols = slice(*Y1), slice(*X1), slice(*Z1)

    def start_y():
        return go(mine.at[pl.ds((1 - f) * 2, 2), :, :, ycols], y8, yp)

    def start_x():
        return [go(mine.at[ff * 2 + 1 - b, :, :, xcols], x8.at[ff], xp) for ff in range(2)]

    def next_y(cp):
        cp.wait_recv()
        accumulate(lambda n: mine.at[f * 2 + n // 4, lax.rem(n, 4), :, ycols], lambda n: y8.at[n // 4, lax.rem(n, 4)], 8)
        return go(mine.at[f * 2 + 1 - b, :, :, ycols], x4, xp)

    def next_x(cps):
        for cp in cps:
            cp.wait_recv()
        accumulate(lambda n: mine.at[n // 4 * 2 + b, lax.rem(n, 4), :, xcols], lambda n: x8.at[n // 4, lax.rem(n, 4)], 8)
        return go(mine.at[(1 - f) * 2 + b, :, :, xcols], y4, yp)

    def last_y(cp):
        cp.wait_recv()
        accumulate(lambda n: mine.at[f * 2 + b, n, :, ycols], lambda n: x4.at[n], 4)

    def last_x(cp):
        cp.wait_recv()
        accumulate(lambda n: mine.at[f * 2 + b, n, :, xcols], lambda n: y4.at[n], 4)

    def landing(span, step, part, single):
        if single:
            base = within(span, RS).start - span[0]
            return z1r.at[step, :, base + part[0]:base + part[1]]
        return z4.at[step, :, :, part[0]:part[1]]

    def ring_source(aa, part, single):
        cols = slice(part[0], part[1])
        return mine.at[f * 2 + b, aa, :, cols] if single else mine.at[:, aa, :, cols]

    def ring_send(span, step, single):
        lo, hi = halves(span)
        ud, dd = lax.rem(a + 3 - step, 4), lax.rem(a + 1 + step, 4)
        return (go(ring_source(ud, lo, single), landing(span, step, lo, single), upp),
                go(ring_source(dd, hi, single), landing(span, step, hi, single), downp))

    def ring_add(span, step, single, cps):
        lo, hi = halves(span)
        ud, dd = lax.rem(a + 6 - step, 4), lax.rem(a + 2 + step, 4)
        for cp, part, aa in zip(cps, (lo, hi), (ud, dd)):
            cp.wait_recv()
            got = landing(span, step, part, single)
            if single:
                add(lambda n: ring_source(aa, part, True), lambda n: got)(0)
            else:
                cols = slice(part[0], part[1])
                accumulate(lambda n: mine.at[n, aa, :, cols], lambda n: got.at[n], 4)

    def tail_z_y():
        return go(mine.at[pl.ds((1 - f) * 2, 2), a, :, zcols], zyb, yp)

    def tail_z_x(cp):
        cp.wait_recv()
        accumulate(lambda n: mine.at[f * 2 + n, a, :, zcols], lambda n: zyb.at[n], 2)
        return go(mine.at[f * 2 + 1 - b, a, :, zcols], zxb, xp)

    def tail_z_end(cp):
        cp.wait_recv()
        add(lambda n: mine.at[f * 2 + b, a, :, zcols], lambda n: zxb)(0)

    class Gather:
        def __init__(self, own, spot, span, first):
            self.span, self.first, self.spot = span, first, spot
            self.own = own
            self.copy = pltpu.make_async_copy(own, spot(b, a, span), here.at[len(locals_)])
            self.copy.start()
            locals_.append(self.copy)
            pending.append(go(own, spot(b, a, span), sp))
            self.ring = go(own, spot(b, a, span), upp), go(own, spot(b, a, span), downp)
            self.cross = go(own, spot(b, a, span), xp)

        def spread(self, bb, aa):
            p = self.spot(bb, aa, self.span)
            pending.append(go(p, p, sp))

        def passed(self, bb, ring):
            lo, hi = halves(self.span)
            ring[0].wait_recv()
            p = self.spot(bb, down, lo)
            first = go(p, p, upp)
            ring[1].wait_recv()
            p = self.spot(bb, up, hi)
            second = go(p, p, downp)
            for aa in (down, up):
                self.spread(bb, aa)
            return first, second

        def arrived(self, bb, ring):
            for cp in ring:
                cp.wait_recv()
            self.spread(bb, lax.rem(a + 2, 4))

        def second(self):
            self.ring2 = self.passed(b, self.ring)
            if self.first == "b":
                self.cross.wait_recv()
                self.spread(1 - b, a)
                p = self.spot(1 - b, a, self.span)
                self.other = go(p, p, upp), go(p, p, downp)
            else:
                spots = [self.spot(b, aa, self.span) for aa in (down, up)]
                self.more = [go(p, p, xp) for p in spots]

        def third(self):
            self.arrived(b, self.ring2)
            if self.first == "b":
                self.other2 = self.passed(1 - b, self.other)
            else:
                p = self.spot(b, lax.rem(a + 2, 4), self.span)
                self.more.append(go(p, p, xp))
                self.cross.wait_recv()
                self.spread(1 - b, a)

        def fourth(self):
            if self.first == "b":
                self.arrived(1 - b, self.other2)
            else:
                for cp, aa in zip(self.more, (down, up, lax.rem(a + 2, 4))):
                    cp.wait_recv()
                    self.spread(1 - b, aa)

    locals_ = []

    def early_spot(bb, aa, span):
        return out.at[c, bb * 4 + aa, :, span[0]:span[1]]

    def late_spot(bb, aa, span):
        return late_out.at[aa, bb * 2 + c, :, span[0]:span[1]]

    def early_gather(span, first):
        return Gather(mine.at[f * 2 + b, a, :, span[0]:span[1]], early_spot, span, first)

    def prepare():
        @pl.loop(0, total // KB)
        def _(n):
            rows = pl.ds(pl.multiple_of(n * KB, KB), KB)
            kt[:, rows] = kv_ref[rows, 0:256].astype(F32).T.astype(BF16)

        @pl.loop(0, 4)
        def _(stripe):
            head = lane_head((SPAN, 256), 0)
            headv = lane_head((SPAN, 256), 64)
            q = q_ref[pl.ds(stripe * 2, 2)].reshape(SPAN, 256).astype(F32) * 0.125
            grad = do_held[pl.ds(stripe * 2, 2)].reshape(SPAN, 256).astype(F32)
            for h in range(3):
                qm[stripe, h] = jnp.where(head == h, q, 0.0).astype(BF16)
                dm[stripe, h] = jnp.where(headv == h, grad, 0.0).astype(BF16)
            prod = grad.T * ot_ref[stripe]
            for h in range(3):
                delta[stripe, h:h + 1] = jnp.sum(prod[64 * (h + 1):64 * (h + 2)], axis=0, keepdims=True)
            qpos = SPAN * (stripe * 2 + b) + lax.broadcasted_iota(jnp.int32, (1, SPAN), 1)
            start, stop = doc_range(qpos, ends)
            rowsc[stripe, 0:1] = start
            rowsc[stripe, 1:2] = stop
            acc[stripe] = jnp.zeros((256, SPAN), F32)

    reach = total * 5 // 8 // KB

    def attend(da, parity):
        block = lax.rem(a + da, 4) * 2 + parity
        krows = pl.ds(pl.multiple_of(block * KB, KB), KB)
        dk[...] = jnp.zeros((KB, 256), F32)
        dv[...] = jnp.zeros((KB, 256), F32)
        @pl.loop(0, 4)
        def _(stripe):
            away = stripe * 2 + b - block

            @pl.when((away <= reach) & (away >= -reach))
            def _():
                keys = kv_ref[krows, 0:256]
                vals = kv_ref[krows, 128:384]
                kpos = block * KB + lax.broadcasted_iota(jnp.int32, (KB, 1), 0)
                allowed = (kpos >= rowsc[stripe, 0:1]) & (kpos < rowsc[stripe, 1:2])
                newk, newv = dk[...], dv[...]
                for h in range(3):
                    s = jnp.where(allowed, dot(keys, qm[stripe, h], NT), MASKED)
                    p = jnp.exp(s - lse_ref[stripe, h:h + 1])
                    gp = dot(vals, dm[stripe, h], NT)
                    ds = (p * (gp - delta[stripe, h:h + 1])).astype(BF16)
                    newv = newv + dot(p.astype(BF16), dm[stripe, h], NN)
                    newk = newk + dot(ds, qm[stripe, h], NN)
                    hrows = pl.ds(64 * h, 64)
                    acc[stripe, hrows] = acc[stripe, hrows] + dot(kt[hrows, krows], ds, NN)
                dk[...] = newk
                dv[...] = newv

    def slot(block, bb):
        return (block // 2 * 2 + bb) * 2 + lax.rem(block, 2)

    def grads_of(dc):
        rows = pl.ds(pl.multiple_of(lax.rem(c + dc, 2) * 128, 128), 128)
        k, v = dk[rows], dv[rows]
        return jnp.concatenate([k[:, :128], k[:, 128:] + v[:, :128], v[:, 128:]], axis=1)

    FAR, NEXT = ((6, 1), (4, 0)), ((0, 0), (2, 1))
    BACK, HERE = ((1, 0), (3, 1)), ((5, 1), (7, 0))
    crossed = {}

    def cross(members):
        for n, dc in members:
            xsend[n] = grads_of(dc).astype(BF16)
            crossed[n] = go(xsend.at[n], rbuf.at[n], xp)

    dkv_slot = lambda block: dkvo.at[block]
    dkvs = {}

    def settle(members):
        for n, dc in members:
            crossed[n].wait_recv()
            value = (grads_of(dc) + rbuf[n].astype(F32)).astype(BF16)
            if n == 7:
                dkv_all[me] = value
                dkvo[me] = value
            else:
                dkv_all[group.others[n]] = value
                dkvs[n] = group.send(n, dkv_all.at[group.others[n]], dkv_slot, dkv_spare)

    dq_slot = lambda block: dqo.at[block]
    dqs = {}

    produce("back", 0, 4, 1 - c, keep)
    share(Y1)
    swaps[6] = group.forward(swaps[6], do_slot, do_spare)
    transpose_into(xt, att, 0)
    transpose_into(xt, low, 768)
    produce("out", 0, 1, 1 - c, keep)
    produce("in", 0, 2, 1 - c, keep)
    share(Z1)
    core[Y1].wait_recv()
    produce("back", 0, 4, c, join)
    y1 = start_y()
    core[Z1].wait_recv()
    produce("out", 0, 1, c, join)
    produce("in", 0, 2, c, join)
    z1 = ring_send(Z1, 0, False)
    produce("in", 2, 2, 1 - c, keep)
    share(X1)
    for cp in swaps.values():
        cp.wait_recv()
    prepare()
    core[X1].wait_recv()
    produce("in", 2, 2, c, join)
    x1 = start_x()
    attend(2, 1 - b)
    cross(FAR)
    ring_add(Z1, 0, False, z1)
    z1 = ring_send(Z1, 1, False)
    attend(1, 1 - b)
    cross(NEXT)
    ring_add(Z1, 1, False, z1)
    z1 = ring_send(Z1, 2, False)
    attend(3, 1 - b)
    cross(BACK)
    x1 = next_x(x1)
    attend(0, 1 - b)
    cross(HERE)
    ring_add(Z1, 2, False, z1)
    z1 = tail_z_y()
    attend(2, b)
    settle(FAR)
    y1 = next_y(y1)
    attend(1, b)
    settle(NEXT)
    last_x(x1)
    x1 = ring_send(X1, 0, True)
    z1 = tail_z_x(z1)
    attend(3, b)
    settle(BACK)
    ring_add(X1, 0, True, x1)
    x1 = ring_send(X1, 1, True)
    tail_z_end(z1)
    g_z1 = early_gather(Z1, "a")
    attend(0, b)

    @pl.loop(0, 4)
    def _(stripe):
        dq_all[pl.ds(stripe * 2, 2)] = (acc[stripe] * 0.125).T.astype(BF16).reshape(2, 128, 256)

    for n in (6, 0, 1, 2, 3, 4, 5):
        dqs[n] = group.send(n, dq_all.at[group.others[n]], dq_slot, dq_spare)
    dqo[me] = dq_all[me]
    settle(HERE)
    dkvs[6] = group.forward(dkvs[6], dkv_slot, dkv_spare)

    def project_back(n, right):
        rows = pl.ds(pl.multiple_of(n * 96, 32), 96)
        value = dot(tt[0, rows], right[0], NN)
        for m in range(1, 8):
            value = value + dot(tt[m, rows], right[m], NN)
        return value

    @pl.loop(0, 4)
    def _(n):
        theirs, ours = n * 2 + 1 - c, n * 2 + c
        l_sib[n, :, 0:256] = project_back(theirs, dq_all).astype(BF16)
        l_sib[n, :, 256:640] = project_back(theirs, dkv_all).astype(BF16)
        l_acc[n, :, 0:256] = project_back(ours, dq_all)
        l_acc[n, :, 256:640] = project_back(ours, dkv_all)

    late = go(l_sib, l_in, sp)
    last_y(y1)
    y1 = ring_send(Y1, 0, True)
    dqs[6] = group.forward(dqs[6], dq_slot, dq_spare)
    late.wait_recv()

    @pl.loop(0, 4)
    def _(n):
        l_mine[n] = (l_acc[n] + l_in[n].astype(F32)).astype(BF16)

    late = go(l_mine.at[pl.ds((1 - f) * 2, 2)], ly, yp)
    ring_add(X1, 1, True, x1)
    x1 = ring_send(X1, 2, True)
    g_z1.second()
    ring_add(Y1, 0, True, y1)
    y1 = ring_send(Y1, 1, True)
    late.wait_recv()
    accumulate(lambda n: l_mine.at[f * 2 + n], lambda n: ly.at[n], 2)
    late = go(l_mine.at[f * 2 + 1 - b], lx, xp)
    ring_add(X1, 2, True, x1)
    g_x1 = early_gather(X1, "b")
    ring_add(Y1, 1, True, y1)
    y1 = ring_send(Y1, 2, True)

    for cp in list(dqs.values()) + list(dkvs.values()):
        cp.wait_recv()
    lane = lax.broadcasted_iota(jnp.int32, (128, 384), 1)
    for s in range(2):
        rows = slice(s * 128, s * 128 + 128)
        for p in range(2):
            even, odd = 4 * p + s, 4 * p + 2 + s
            blank = jnp.zeros((128, 128), F32)
            qe = jnp.concatenate([dqo[even].astype(F32), blank], axis=1)
            qo = jnp.concatenate([dqo[odd].astype(F32), blank], axis=1)
            joined[rows, 384 * p:384 * p + 384] = pair_columns(qe, qo, lane, False).astype(BF16)
            ke, ko = dkvo[even].astype(F32), dkvo[odd].astype(F32)
            joined[rows, 768 + 384 * p:1152 + 384 * p] = pair_columns(ke, ko, lane, False).astype(BF16)
            joined[rows, 1536 + 384 * p:1920 + 384 * p] = pair_columns(ke, ko, lane, True).astype(BF16)
    v_own[...] = small[...]
    v_own[0:1] = jnp.sum(joined[:, 0:768].astype(F32), axis=0, keepdims=True)
    v_own[1:2] = jnp.sum(joined[:, 1536:2304].astype(F32), axis=0, keepdims=True)
    vec = go(v_own, v_core, sp)

    late.wait_recv()
    add(lambda n: l_mine.at[f * 2 + b], lambda n: lx)(0)
    g_l0 = Gather(l_mine.at[f * 2 + b, :, L0[0]:L0[1]], late_spot, L0, "a")
    g_l1 = Gather(l_mine.at[f * 2 + b, :, L1[0]:L1[1]], late_spot, L1, "b")
    ring_add(Y1, 2, True, y1)
    g_y1 = early_gather(Y1, "b")
    vec.wait_recv()
    v_core[...] = v_own[...] + v_core[...]
    vec = go(v_core.at[:, pl.ds(pl.multiple_of((1 - f) * 384, 128), 384)], v_f, yp)
    g_z1.third()
    g_x1.second()
    g_l0.second()
    g_l1.second()
    vec.wait_recv()
    v_b[b] = v_core[:, pl.ds(pl.multiple_of(f * 384, 128), 384)] + v_f[...]
    vec = go(v_b.at[b], v_b.at[b], xp)
    g_y1.second()
    g_z1.fourth()
    g_x1.third()
    g_l0.third()
    g_l1.third()
    vec.wait_recv()
    v_a[a] = v_b[0] + v_b[1]
    vec = [go(v_a.at[a], v_a.at[a], device(lax.rem(a + k, 4), b, c, f, 2)) for k in range(1, 4)]
    g_y1.third()
    g_x1.fourth()
    g_l0.fourth()
    g_l1.fourth()
    g_y1.fourth()
    for cp in vec + pending:
        cp.wait_recv()
    small_out[...] = v_a[0] + v_a[1] + v_a[2] + v_a[3]
    for cp in locals_:
        cp.wait()
    for cp in wires.made:
        cp.wait_send()


def reduce_all(lens, tt, att, low, act, gbr, ghid, gsec, small, do_sent, q, kv, ot, lse, ident):
    wires = 192
    total = kv.shape[0]
    bf = lambda *shape: pltpu.VMEM(shape, BF16)
    fl = lambda *shape: pltpu.VMEM(shape, F32)
    anywhere = pl.BlockSpec(memory_space=pl.ANY)
    return pl.pallas_call(
        gradient_kernel,
        out_shape=[jax.ShapeDtypeStruct((2, 8, BLK, 3456), BF16), jax.ShapeDtypeStruct((4, 4, 96, 640), BF16),
                   jax.ShapeDtypeStruct((256, 2304), BF16), jax.ShapeDtypeStruct((16, 384), F32)],
        in_specs=[pl.BlockSpec(memory_space=pltpu.SMEM)] + [vmem()] * 13, out_specs=[anywhere] * 2 + [vmem()] * 2,
        scratch_shapes=[
            bf(4608, 256), bf(4, 4, BLK, 3456), bf(4, 4, BLK, 3456), bf(4, 4, BLK, 3456),
            bf(2, 4, BLK, 1536), bf(4, BLK, 768), bf(2, 4, BLK, 768), bf(4, BLK, 1536),
            bf(3, 4, BLK, 1152), bf(3, BLK, 2304), bf(2, BLK, 1152), bf(BLK, 1152),
            bf(8, 128, 256), bf(4, 3, SPAN, 256), bf(4, 3, SPAN, 256), bf(256, total), fl(KB, 256), fl(KB, 256), fl(4, 256, SPAN),
            pltpu.VMEM((4, 8, SPAN), jnp.int32), fl(4, 8, SPAN),
            bf(8, 128, 256), bf(8, 128, 384), bf(8, 128, 256), bf(8, 128, 384), bf(8, 128, 384), bf(8, 128, 384),
            bf(4, 96, 640), bf(4, 96, 640), fl(4, 96, 640), bf(4, 96, 640), bf(2, 96, 640), bf(96, 640),
            bf(128, 256), bf(128, 256), bf(128, 384),
            fl(16, 768), fl(16, 768), fl(16, 384), fl(2, 16, 384), fl(4, 16, 384),
            DMA((wires,)), DMA((wires,)), DMA((5,))],
        compiler_params=pltpu.CompilerParams(collective_id=ident, has_side_effects=True, vmem_limit_bytes=62 << 20),
        name="reduce_all",
    )(lens, tt, att, low, act, gbr, ghid, gsec, small, do_sent, q, kv, ot, lse)


def widen_kernel(grads, late, g_qkv, g_out, g_in, g_back):
    for core in range(2):
        part = grads.at[core]
        g_out[:, core * 384:core * 384 + 384] = part[:, 0:384].astype(F32)
        g_in[:, core * 1536:core * 1536 + 1536] = part[:, 384:1920].astype(F32)
        for j in range(4):
            g_back[j, :, core * 384:core * 384 + 384] = part[:, 1920 + 384 * j:2304 + 384 * j].astype(F32)
    lane = lax.broadcasted_iota(jnp.int32, (96, 384), 1)
    for p in range(2):
        even, odd = late[2 * p, 0].astype(F32), late[2 * p + 1, 0].astype(F32)
        g_qkv[:, 384 * p:384 * p + 384] = pair_columns(even[:, :384], odd[:, :384], lane, False)
        ke, ko = even[:, 256:], odd[:, 256:]
        g_qkv[:, 768 + 384 * p:1152 + 384 * p] = pair_columns(ke, ko, lane, False)
        g_qkv[:, 1536 + 384 * p:1920 + 384 * p] = pair_columns(ke, ko, lane, True)


def widen(grads, late):
    rows, step = 384, 96
    spec = lambda wide: pl.BlockSpec((step, wide), lambda n: (n, 0))
    return pl.pallas_call(
        widen_kernel,
        grid=(rows // step,),
        out_shape=[jax.ShapeDtypeStruct((rows, 2304), F32), jax.ShapeDtypeStruct((rows, 768), F32),
                   jax.ShapeDtypeStruct((rows, 3072), F32), jax.ShapeDtypeStruct((4, rows, 768), F32)],
        in_specs=[pl.BlockSpec((2, step, 3456), lambda n: (0, n, 0)), pl.BlockSpec((4, 1, step, 640), lambda n: (0, n, 0, 0))],
        out_specs=[spec(2304), spec(768), spec(3072), pl.BlockSpec((4, step, 768), lambda n: (0, n, 0))],
        compiler_params=pltpu.CompilerParams(vmem_limit_bytes=40 << 20),
        name="widen",
    )(grads, late)


def layer_norm(values, gain_row, shift_row):
    average = jnp.mean(values, axis=-1, keepdims=True)
    centered = values - average
    variance = jnp.mean(centered * centered, axis=-1, keepdims=True)
    return centered * lax.rsqrt(variance + EPSILON) * gain_row + shift_row


def exact_gelu(values):
    return jax.nn.gelu(values, approximate=False)


def by_group(rows, micro, front, back):
    parts = rows.reshape(micro, -1, 4, 192).transpose(2, 0, 1, 3)
    parts = jnp.pad(parts, ((0, 0), (0, 0), (0, 0), (front, back)))
    return parts.reshape((-1,) + parts.shape[2:])


def from_group(blocks, micro, front):
    rows = blocks.shape[1]
    parts = blocks.reshape(4, micro, rows, -1)[..., front:front + 192]
    return parts.transpose(1, 2, 0, 3).reshape(micro * rows, 768)


def shards(tokens, cotangent, doc_lengths, w_qkv, w_out, w_in, w_back, *vectors):
    micro, per, width = tokens.shape
    nf, cols = lax.axis_size("fsdp"), lax.axis_size("ctx") // 8
    share = width // nf
    inputs = tokens.reshape(micro * per, width)
    cube = nf == 2 and cols == 2
    if cube:
        q_held, kv_held, full_qkv, full_out, full_in, full_back, sides, turned = project(inputs, (w_qkv, w_out, w_in, w_back), vectors, 1)
        q_held = q_held.reshape(8 * per, 256)
        kv_held = kv_held.reshape(-1, 384)
        b_out, b_back, gain_one, shift_one, gain_two, shift_two = [sides[:, n].reshape(-1) for n in range(2, 8)]
        b_in = sides[:, 8:12].reshape(-1)
    else:
        tiny = jnp.concatenate(vectors).reshape(8, -1)
        full_qkv, full_out, full_in, full_back, tinies = gather_weights((w_qkv, w_out, w_in, w_back), tiny, nf, cols)
        tinies = tinies.reshape(nf, -1).astype(F32)
        named, at = [], 0
        for vector in vectors:
            size = vector.shape[0]
            named.append(tinies[:, at:at + size].reshape(-1))
            at += size
        b_query, b_value, b_out, b_in, b_back, gain_one, shift_one, gain_two, shift_two = named
        joined = jnp.dot(inputs, full_qkv, preferred_element_type=F32)
        bias = jnp.concatenate([b_query, jnp.zeros_like(b_query), b_value])
        joined = (joined + bias).astype(BF16)
        q_sent = by_group(joined[:, :width], micro, 0, 64)
        kv_sent = jnp.concatenate([by_group(joined[:, width:2 * width], micro, 0, 0), by_group(joined[:, 2 * width:], micro, 0, 0)], axis=2)
        q_held, kv_held = spread(q_sent, kv_sent, cols, 2)
        q_held = q_held.reshape(8 * per, 256)
        kv_held = kv_held.reshape(-1, 384)
    mixed, mixed_t, log_total = attend_forward(doc_lengths, q_held, kv_held, cols)
    (back,) = swap([mixed.reshape(8, per, 256)], cols, 3)
    attended = from_group(back, micro, 64)
    first_sum = inputs.astype(F32) + (jnp.dot(attended, full_out, preferred_element_type=F32) + b_out)
    normed = layer_norm(first_sum, gain_one, shift_one)
    normed_low = normed.astype(BF16)
    hidden = jnp.dot(normed_low, full_in, preferred_element_type=F32) + b_in
    activated = exact_gelu(hidden).astype(BF16)
    final_sum = normed + (jnp.dot(activated, full_back, preferred_element_type=F32) + b_back)
    output = layer_norm(final_sum, gain_two, shift_two).astype(BF16)

    upstream = cotangent.reshape(micro * per, width).astype(F32)
    grad_final, g_gain_two, g_shift_two = jax.vjp(layer_norm, final_sum, gain_two, shift_two)[1](upstream)
    grad_second = grad_final.astype(BF16)
    g_back_bias = jnp.sum(grad_second.astype(F32), axis=0)
    grad_activated = jnp.einsum("rm,km->rk", grad_second, full_back, preferred_element_type=F32)
    grad_hidden = jax.vjp(exact_gelu, hidden)[1](grad_activated)[0].astype(BF16)
    g_in_bias = jnp.sum(grad_hidden.astype(F32), axis=0)
    grad_normed = grad_final + jnp.einsum("rf,mf->rm", grad_hidden, full_in, preferred_element_type=F32)
    grad_first, g_gain_one, g_shift_one = jax.vjp(layer_norm, first_sum, gain_one, shift_one)[1](grad_normed)
    grad_branch = grad_first.astype(BF16)
    g_out_bias = jnp.sum(grad_branch.astype(F32), axis=0)
    grad_attended = jnp.einsum("rm,km->rk", grad_branch, full_out, preferred_element_type=F32).astype(BF16)
    do_sent = by_group(grad_attended, micro, 64, 0)
    if cube:
        small = [jnp.zeros((2, width), F32)] + [x[None] for x in (g_out_bias, g_back_bias, g_gain_one, g_shift_one, g_gain_two, g_shift_two)]
        small += [g_in_bias.reshape(2, 4, share).transpose(1, 0, 2).reshape(4, width), jnp.zeros((4, width), F32)]
        grads, late, grad_joined, sums = reduce_all(
            doc_lengths, turned, attended, normed_low, activated, grad_branch, grad_hidden, grad_second, jnp.concatenate(small),
            do_sent, q_held.reshape(8, per, 256), kv_held, mixed_t, log_total, 5)
        g_qkv, g_out, g_in, g_back = widen(grads.reshape(2, share, 3456), late)
        input_grad = grad_first + jnp.einsum("rc,mc->rm", grad_joined, full_qkv, preferred_element_type=F32)
        rows = [sums[0], sums[1], sums[2], sums[8:12].reshape(-1), sums[3], sums[4], sums[5], sums[6], sums[7]]
        return (output.reshape(tokens.shape), input_grad.reshape(tokens.shape), g_qkv, g_out, g_in, g_back.reshape(4 * share, width)) + tuple(rows)
    (do_held,) = swap([do_sent], cols, 4)
    dq, dkv = attend_backward(doc_lengths, q_held, kv_held, do_held.reshape(8 * per, 256), mixed_t, log_total, cols)
    dq_own, dkv_own = collect(dq.reshape(8, per, 256), dkv.reshape(8 * cols, per, 384), cols, 5)
    grad_joined = jnp.concatenate(
        [from_group(dq_own, micro, 0), from_group(dkv_own, micro, 0), from_group(dkv_own, micro, 192)], axis=1)
    g_query_bias = jnp.sum(grad_joined[:, :width].astype(F32), axis=0)
    g_value_bias = jnp.sum(grad_joined[:, 2 * width:].astype(F32), axis=0)
    input_grad = grad_first + jnp.einsum("rc,mc->rm", grad_joined, full_qkv, preferred_element_type=F32)

    def halves(left, right):
        blocks = right.shape[1] // 384
        return jnp.einsum("rm,rhc->hmc", left, right.reshape(-1, blocks, 384), preferred_element_type=F32).astype(BF16)

    back_grads = jnp.einsum("rk,rm->km", activated, grad_second, preferred_element_type=F32).astype(BF16)
    back_grads = back_grads.reshape(nf, 4, share, 2, 384).transpose(1, 3, 0, 2, 4).reshape(8, width, 384)
    grads = jnp.concatenate(
        [halves(inputs, grad_joined), halves(attended, grad_branch), halves(normed_low, grad_hidden), back_grads])
    grads = grads.reshape(2, 4, 3, nf, cols, share // cols, 384)
    small = (g_query_bias, g_value_bias, g_out_bias, g_in_bias, g_back_bias, g_gain_one, g_shift_one, g_gain_two, g_shift_two)
    small = jnp.concatenate([x.reshape(nf, -1) for x in small], axis=1).reshape(nf, 8, -1)
    owned, small_owned = reduce_grads(grads, small, nf, cols, 6)
    owned = owned.transpose(0, 1, 3, 2, 4, 5).reshape(24, share, 384)

    def columns(first, last):
        return owned[first:last].transpose(1, 0, 2).reshape(share, -1).astype(F32)

    g_back = owned[16:].reshape(4, 2, share, 384).transpose(0, 2, 1, 3).reshape(4 * share, width).astype(F32)
    small_owned = small_owned.reshape(-1)
    small_grads, at = [], 0
    for vector in vectors:
        small_grads.append(small_owned[at:at + vector.shape[0]])
        at += vector.shape[0]
    return (output.reshape(tokens.shape), input_grad.reshape(tokens.shape), columns(0, 6), columns(6, 8), columns(8, 16), g_back) + tuple(small_grads)


def solution(mesh):
    rows, flat = P("fsdp", "ctx", None), P("fsdp", None)
    return jax.shard_map(
        shards,
        mesh=mesh,
        in_specs=(rows, rows, flat) + (flat,) * 4 + (P("fsdp"),) * 9,
        out_specs=(rows, rows) + (flat,) * 4 + (P("fsdp"),) * 9,
        check_vma=False,
    )
```

```python
import functools

import jax
import jax.numpy as jnp
from jax import lax
from jax.experimental import pallas as pl
from jax.experimental.pallas import tpu as pltpu
from jax.sharding import PartitionSpec as P

MESH = pl.DeviceIdType.MESH
DMA = pltpu.SemaphoreType.DMA
F32, BF16 = jnp.float32, jnp.bfloat16
EPSILON = 1e-12

def place(cols):
    index = lax.axis_index("ctx")
    return index // (2 * cols), lax.rem(index // 2, cols), lax.rem(index, 2), lax.axis_index("fsdp")

def device(a, b, c, f, cols):
    return {"ctx": (a * cols + b) * 2 + c, "fsdp": f}

def meet(peers):
    barrier = pltpu.get_barrier_semaphore()
    for peer in peers:
        pl.semaphore_signal(barrier, inc=1, device_id=peer, device_id_type=MESH)
    pl.semaphore_wait(barrier, len(peers))

def remote(source, target, send, recv, peer):
    return pltpu.make_async_remote_copy(
        src_ref=source, dst_ref=target, send_sem=send, recv_sem=recv, device_id=peer, device_id_type=MESH)

def gather_kernel(nf, cols, count, *refs):
    shards, tiny, fulls, tiny_out = refs[:count], refs[count], refs[count+1:2*count+1], refs[2*count+1]
    local_sem, s1, r1, s2, r2, s3, r3, st, rt = refs[2*count+2:]
    a, b, c, f = place(cols)
    other = 1 - c
    fpeers = [device(a, b, c, lax.rem(f + j, nf), cols) for j in range(1, nf)]
    bpeers = [device(a, lax.rem(b + k, cols), c, f, cols) for k in range(1, cols)]
    sibling = device(a, b, other, f, cols)
    meet(fpeers + bpeers + [sibling])

    def view(w, owner, bb, cc, base=0):
        rows, wide = shards[w].shape
        part, half = rows // cols, wide // 2
        return fulls[w].at[pl.ds(pl.multiple_of(owner * rows + bb * part, 8), part), pl.ds(pl.multiple_of(cc * half, 128), half)]

    waits = []
    for j in range(1, nf):
        cp = remote(tiny, tiny_out.at[f], st.at[j - 1], rt.at[j - 1], fpeers[j - 1])
        cp.start()
        waits.append(cp)
    locals_ = [pltpu.make_async_copy(tiny, tiny_out.at[f], local_sem.at[count])]
    locals_[0].start()
    first = {}
    for w in range(count):
        rows, wide = shards[w].shape
        part, half = rows // cols, wide // 2
        mine = shards[w].at[pl.ds(pl.multiple_of(b * part, 8), part), pl.ds(pl.multiple_of(c * half, 128), half)]
        for j in range(1, nf):
            cp = remote(mine, view(w, f, b, c), s1.at[w, j - 1], r1.at[w, j - 1], fpeers[j - 1])
            cp.start()
            first[w, j] = cp
    for w in range(count):
        rows = shards[w].shape[0]
        cp = pltpu.make_async_copy(shards[w], fulls[w].at[pl.ds(pl.multiple_of(f * rows, 8), rows)], local_sem.at[w])
        cp.start()
        locals_.append(cp)
    second, third = {}, []
    for w in range(count):
        for j in range(1, nf):
            owner = lax.rem(f + nf - j, nf)
            first[w, j].wait_recv()
            piece = view(w, owner, b, c)
            for k in range(1, cols):
                slot = (j - 1) * (cols - 1) + k - 1
                cp = remote(piece, piece, s2.at[w, slot], r2.at[w, slot], bpeers[k - 1])
                cp.start()
                second[w, j, k] = cp
            cp = remote(piece, piece, s3.at[w, (j - 1) * cols], r3.at[w, (j - 1) * cols], sibling)
            cp.start()
            third.append(cp)
    for w in range(count):
        for j in range(1, nf):
            owner = lax.rem(f + nf - j, nf)
            for k in range(1, cols):
                second[w, j, k].wait_recv()
                piece = view(w, owner, lax.rem(b + cols - k, cols), c)
                cp = remote(piece, piece, s3.at[w, (j - 1) * cols + k], r3.at[w, (j - 1) * cols + k], sibling)
                cp.start()
                third.append(cp)
    for cp in third:
        cp.wait_recv()
    for cp in waits:
        cp.wait()
    for cp in list(first.values()) + list(second.values()) + third:
        cp.wait_send()
    for cp in locals_:
        cp.wait()

def gather_weights(shards, tiny, nf, cols):
    count = len(shards)
    any_spec = pl.BlockSpec(memory_space=pl.ANY)
    dma = pltpu.SemaphoreType.DMA
    return pl.pallas_call(
        functools.partial(gather_kernel, nf, cols, count),
        out_shape=[jax.ShapeDtypeStruct((s.shape[0] * nf, s.shape[1]), s.dtype) for s in shards]
        + [jax.ShapeDtypeStruct((nf,) + tiny.shape, tiny.dtype)],
        in_specs=[pl.BlockSpec(memory_space=pltpu.VMEM)] * (count + 1),
        out_specs=[any_spec] * (count + 1),
        scratch_shapes=[dma((count + 1,)), dma((count, nf - 1)), dma((count, nf - 1)),
                        dma((count, (nf - 1) * (cols - 1))), dma((count, (nf - 1) * (cols - 1))),
                        dma((count, (nf - 1) * cols)), dma((count, (nf - 1) * cols)),
                        dma((nf - 1,)), dma((nf - 1,))],
        compiler_params=pltpu.CompilerParams(collective_id=1, has_side_effects=True, vmem_limit_bytes=32 << 20),
        name="gather_weights",
    )(*shards, tiny)

def octet(a, b, c, f, cols):
    me = a * 2 + c
    out = []
    for k in range(1, 8):
        other = lax.rem(me + k, 8)
        out.append((other, device(other // 2, b, lax.rem(other, 2), f, cols)))
    return me, out

def swap_kernel(cols, count, *refs):
    sources, targets = refs[:count], refs[count:2 * count]
    send, recv, here = refs[2 * count:]
    a, b, c, f = place(cols)
    me, peers = octet(a, b, c, f, cols)
    meet([p for _, p in peers])
    copies = []
    for k, (other, peer) in enumerate(peers):
        for i in range(count):
            cp = remote(sources[i].at[other], targets[i].at[me], send.at[i, k], recv.at[i, k], peer)
            cp.start()
            copies.append(cp)
    for i in range(count):
        cp = pltpu.make_async_copy(sources[i].at[me], targets[i].at[me], here.at[i])
        cp.start()
        copies.append(cp)
    for cp in copies:
        cp.wait()

def swap(arrays, cols, ident):
    count = len(arrays)
    return pl.pallas_call(
        functools.partial(swap_kernel, cols, count),
        out_shape=[jax.ShapeDtypeStruct(x.shape, x.dtype) for x in arrays],
        in_specs=[vmem()] * count, out_specs=[vmem()] * count,
        scratch_shapes=[DMA((count, 7)), DMA((count, 7)), DMA((count,))],
        compiler_params=pltpu.CompilerParams(collective_id=ident, has_side_effects=True, vmem_limit_bytes=16 << 20),
        name="swap",
    )(*arrays)

def spread_kernel(cols, q, kv, qg, full, sq, rq, sk, rk, s2, r2, here):
    a, b, c, f = place(cols)
    me, peers = octet(a, b, c, f, cols)
    bpeers = [device(a, lax.rem(b + k, cols), c, f, cols) for k in range(1, cols)]
    meet([p for _, p in peers] + bpeers)

    def slot(block, bb):
        return (block // 2 * cols + bb) * 2 + lax.rem(block, 2)

    first = []
    for k, (other, peer) in enumerate(peers):
        cp = remote(kv.at[other], full.at[slot(me, b)], sk.at[k], rk.at[k], peer)
        cp.start()
        first.append(cp)
    own = pltpu.make_async_copy(kv.at[me], full.at[slot(me, b)], here.at[0])
    own.start()
    ownq = pltpu.make_async_copy(q.at[me], qg.at[me], here.at[1])
    ownq.start()
    second = []
    for k, peer in enumerate(bpeers):
        cp = remote(kv.at[me], full.at[slot(me, b)], s2.at[7, k], r2.at[7, k], peer)
        cp.start()
        second.append(cp)
    third = []
    for k, (other, peer) in enumerate(peers):
        cp = remote(q.at[other], qg.at[me], sq.at[k], rq.at[k], peer)
        cp.start()
        third.append(cp)
    for k in range(7):
        first[k].wait_recv()
        source = lax.rem(me + 8 - (k + 1), 8)
        piece = full.at[slot(source, b)]
        for m, peer in enumerate(bpeers):
            cp = remote(piece, piece, s2.at[k, m], r2.at[k, m], peer)
            cp.start()
            second.append(cp)
    for cp in first:
        cp.wait_send()
    for cp in second + third:
        cp.wait()
    own.wait()
    ownq.wait()

def spread(q, kv, cols, ident):
    return pl.pallas_call(
        functools.partial(spread_kernel, cols),
        out_shape=[jax.ShapeDtypeStruct(q.shape, q.dtype), jax.ShapeDtypeStruct((8 * cols,) + kv.shape[1:], kv.dtype)],
        in_specs=[vmem()] * 2, out_specs=[vmem()] * 2,
        scratch_shapes=[DMA((7,))] * 4 + [DMA((8, max(cols - 1, 1)))] * 2 + [DMA((2,))],
        compiler_params=pltpu.CompilerParams(collective_id=ident, has_side_effects=True, vmem_limit_bytes=16 << 20),
        name="spread",
    )(q, kv)

def collect_kernel(cols, dq, dkv, dqo, dkvo, rbuf, total, sq, rq, sk, rk, s2, r2, here):
    a, b, c, f = place(cols)
    me, peers = octet(a, b, c, f, cols)
    bpeers = [(lax.rem(b + k, cols), device(a, lax.rem(b + k, cols), c, f, cols)) for k in range(1, cols)]
    meet([p for _, p in peers] + [p for _, p in bpeers])

    def slot(block, bb):
        return (block // 2 * cols + bb) * 2 + lax.rem(block, 2)

    order = [other for other, _ in peers] + [me]
    first = {}
    for n, block in enumerate(order):
        for k, (bb, peer) in enumerate(bpeers):
            cp = remote(dkv.at[slot(block, bb)], rbuf.at[k, n], s2.at[k, n], r2.at[k, n], peer)
            cp.start()
            first[k, n] = cp
    rest = []
    for k, (other, peer) in enumerate(peers):
        cp = remote(dq.at[other], dqo.at[me], sq.at[k], rq.at[k], peer)
        cp.start()
        rest.append(cp)
    own = pltpu.make_async_copy(dq.at[me], dqo.at[me], here.at[0])
    own.start()
    for n, block in enumerate(order):
        value = dkv[slot(block, b)].astype(F32)
        for k in range(cols - 1):
            first[k, n].wait_recv()
            value = value + rbuf[k, n].astype(F32)
        if n < 7:
            total[n] = value.astype(BF16)
            cp = remote(total.at[n], dkvo.at[me], sk.at[n], rk.at[n], peers[n][1])
            cp.start()
            rest.append(cp)
        else:
            dkvo[me] = value.astype(BF16)
    for cp in first.values():
        cp.wait_send()
    for cp in rest:
        cp.wait()
    own.wait()

def collect(dq, dkv, cols, ident):
    block = dkv.shape[1:]
    return pl.pallas_call(
        functools.partial(collect_kernel, cols),
        out_shape=[jax.ShapeDtypeStruct(dq.shape, dq.dtype), jax.ShapeDtypeStruct((8,) + block, dkv.dtype)],
        in_specs=[vmem()] * 2, out_specs=[vmem()] * 2,
        scratch_shapes=[pltpu.VMEM((max(cols - 1, 1), 8) + block, BF16), pltpu.VMEM((7,) + block, BF16)]
        + [DMA((7,))] * 4 + [DMA((max(cols - 1, 1), 8))] * 2 + [DMA((1,))],
        compiler_params=pltpu.CompilerParams(collective_id=ident, has_side_effects=True, vmem_limit_bytes=24 << 20),
        name="collect",
    )(dq, dkv)

def reduce_kernel(nf, cols, parts, grads, small, out, small_out, *refs):
    own, core_in, f_in, b_in, f_in2, b_in2, a_in, v_core, v_sum, v_f, v_b, v_a = refs[:12]
    load, sc, rc, s1, r1, s2, r2, s3, r3, s4, r4, s5, r5, s6, r6, sv, rv = refs[12:]
    a, b, c, f = place(cols)
    rows = grads.shape[5]
    fpeers = [(lax.rem(f + j, nf), device(a, b, c, lax.rem(f + j, nf), cols)) for j in range(1, nf)]
    bpeers = [(lax.rem(b + k, cols), device(a, lax.rem(b + k, cols), c, f, cols)) for k in range(1, cols)]
    apeers = [(lax.rem(a + k, 4), device(lax.rem(a + k, 4), b, c, f, cols)) for k in range(1, 4)]
    sibling = device(a, b, 1 - c, f, cols)
    meet([p for _, p in fpeers + bpeers + apeers] + [sibling])
    vector = remote(small, v_core, sv.at[0], rv.at[0], sibling)
    vector.start()
    order = [2, 1, 3, 0]
    dest = {k: lax.rem(a + k, 4) for k in range(4)}
    by_f = {k: k in (1, 2) for k in range(4)}
    loads, cores = {}, {}
    for k in order:
        for i in range(parts):
            cp = pltpu.make_async_copy(grads.at[c, dest[k], i], own.at[k, i], load.at[k, i])
            cp.start()
            loads[k, i] = cp
            cp = remote(grads.at[1 - c, dest[k], i], core_in.at[k, i], sc.at[k, i], rc.at[k, i], sibling)
            cp.start()
            cores[k, i] = cp
    one, two, three = {}, {}, {}
    vec = {}
    vector.wait_recv()
    v_sum[...] = small[...] + v_core[...]
    for j, (ff, peer) in enumerate(fpeers):
        vec[0, j] = remote(v_sum.at[ff], v_f.at[j], sv.at[1 + j], rv.at[1 + j], peer)
        vec[0, j].start()
    for k in order:
        for i in range(parts):
            loads[k, i].wait()
            cores[k, i].wait_recv()

            @pl.loop(0, nf * cols)
            def _(n):
                ff, bb = n // cols, lax.rem(n, cols)
                own[k, i, ff, bb] = (own[k, i, ff, bb].astype(F32) + core_in[k, i, ff, bb].astype(F32)).astype(BF16)

            if by_f[k]:
                for j, (ff, peer) in enumerate(fpeers):
                    cp = remote(own.at[k, i, ff], f_in.at[k, i, j], s1.at[k, i, j], r1.at[k, i, j], peer)
                    cp.start()
                    one[k, i, j] = cp
            else:
                for m, (bb, peer) in enumerate(bpeers):
                    for ff in range(nf):
                        cp = remote(own.at[k, i, ff, bb], b_in.at[k, i, m, ff], s1.at[k, i, m * nf + ff], r1.at[k, i, m * nf + ff], peer)
                        cp.start()
                        one[k, i, m * nf + ff] = cp
    value = v_sum[f]
    for j in range(nf - 1):
        vec[0, j].wait_recv()
        value = value + v_f[j]
    v_b[b] = value
    for m, (bb, peer) in enumerate(bpeers):
        vec[1, m] = remote(v_b.at[b], v_b.at[b], sv.at[nf + m], rv.at[nf + m], peer)
        vec[1, m].start()
    for k in order:
        for i in range(parts):
            if by_f[k]:
                for j in range(nf - 1):
                    one[k, i, j].wait_recv()

                @pl.loop(0, cols)
                def _(bb):
                    value = own[k, i, f, bb].astype(F32)
                    for j in range(nf - 1):
                        value = value + f_in[k, i, j, bb].astype(F32)
                    own[k, i, f, bb] = value.astype(BF16)

                for m, (bb, peer) in enumerate(bpeers):
                    cp = remote(own.at[k, i, f, bb], b_in2.at[k, i, m], s2.at[k, i, m], r2.at[k, i, m], peer)
                    cp.start()
                    two[k, i, m] = cp
            else:
                for m in range(cols - 1):
                    for ff in range(nf):
                        one[k, i, m * nf + ff].wait_recv()

                @pl.loop(0, nf)
                def _(ff):
                    value = own[k, i, ff, b].astype(F32)
                    for m in range(cols - 1):
                        value = value + b_in[k, i, m, ff].astype(F32)
                    own[k, i, ff, b] = value.astype(BF16)

                for j, (ff, peer) in enumerate(fpeers):
                    cp = remote(own.at[k, i, ff, b], f_in2.at[k, i, j], s2.at[k, i, j], r2.at[k, i, j], peer)
                    cp.start()
                    two[k, i, j] = cp
    for m in range(cols - 1):
        vec[1, m].wait_recv()
    value = v_b[0]
    for m in range(1, cols):
        value = value + v_b[m]
    v_a[a] = value
    for k in range(1, 4):
        vec[2, k] = remote(v_a.at[a], v_a.at[a], sv.at[nf + cols + k - 2], rv.at[nf + cols + k - 2], apeers[k - 1][1])
        vec[2, k].start()
    for k in order:
        for i in range(parts):
            value = own[k, i, f, b].astype(F32)
            if by_f[k]:
                for m in range(cols - 1):
                    two[k, i, m].wait_recv()
                    value = value + b_in2[k, i, m].astype(F32)
            else:
                for j in range(nf - 1):
                    two[k, i, j].wait_recv()
                    value = value + f_in2[k, i, j].astype(F32)
            if k != 0:
                own[k, i, f, b] = value.astype(BF16)
                cp = remote(own.at[k, i, f, b], a_in.at[k - 1, i], s3.at[k - 1, i], r3.at[k - 1, i], apeers[k - 1][1])
                cp.start()
                three[k, i] = cp
            else:
                own[k, i, f, b] = value.astype(BF16)
    for k in range(1, 4):
        vec[2, k].wait_recv()
    small_out[...] = v_a[0] + v_a[1] + v_a[2] + v_a[3]
    four, five, six = {}, {}, {}

    def piece(aa, bb, cc, i):
        return out.at[cc, aa, bb, i]

    pending = []
    for i in range(parts):
        value = own[0, i, f, b].astype(F32)
        for k in range(1, 4):
            three[k, i].wait_recv()
            value = value + a_in[k - 1, i].astype(F32)
        out[c, a, b, i] = value.astype(BF16)
        mine = piece(a, b, c, i)
        for k in (2, 1, 3):
            cp = remote(mine, mine, s4.at[k - 1, i], r4.at[k - 1, i], apeers[k - 1][1])
            cp.start()
            four[k, i] = cp
        for m, (bb, peer) in enumerate(bpeers):
            cp = remote(mine, mine, s5.at[0, i, m], r5.at[0, i, m], peer)
            cp.start()
            five[0, i, m] = cp
        cp = remote(mine, mine, s6.at[0, i, 0], r6.at[0, i, 0], sibling)
        cp.start()
        six[0, i, 0] = cp
    for i in range(parts):
        for k in (1, 3, 2):
            four[k, i].wait_recv()
            got = piece(lax.rem(a + 4 - k, 4), b, c, i)
            for m, (bb, peer) in enumerate(bpeers):
                cp = remote(got, got, s5.at[k, i, m], r5.at[k, i, m], peer)
                cp.start()
                five[k, i, m] = cp
            cp = remote(got, got, s6.at[k, i, 0], r6.at[k, i, 0], sibling)
            cp.start()
            six[k, i, 0] = cp
    for i in range(parts):
        for k in (0, 1, 3, 2):
            for m in range(cols - 1):
                five[k, i, m].wait_recv()
                got = piece(lax.rem(a + 4 - k, 4), lax.rem(b + cols - (m + 1), cols), c, i)
                cp = remote(got, got, s6.at[k, i, m + 1], r6.at[k, i, m + 1], sibling)
                cp.start()
                six[k, i, m + 1] = cp
    for cp in six.values():
        cp.wait_recv()
    vector.wait_send()
    for group in (cores, one, two, three, four, five, six, vec):
        for cp in group.values():
            cp.wait_send()

def reduce_grads(grads, small, nf, cols, ident):
    _, _, parts, _, _, rows, width = grads.shape
    block = (rows, width)
    m = max(cols - 1, 1)
    n = max((cols - 1) * nf, nf - 1)
    return pl.pallas_call(
        functools.partial(reduce_kernel, nf, cols, parts),
        out_shape=[jax.ShapeDtypeStruct((2, 4, cols, parts) + block, BF16), jax.ShapeDtypeStruct(small.shape[1:], F32)],
        in_specs=[pl.BlockSpec(memory_space=pl.ANY), vmem()], out_specs=[vmem()] * 2,
        scratch_shapes=[pltpu.VMEM((4, parts, nf, cols) + block, BF16), pltpu.VMEM((4, parts, nf, cols) + block, BF16),
                        pltpu.VMEM((4, parts, nf - 1, cols) + block, BF16), pltpu.VMEM((4, parts, m, nf) + block, BF16),
                        pltpu.VMEM((4, parts, nf - 1) + block, BF16), pltpu.VMEM((4, parts, m) + block, BF16),
                        pltpu.VMEM((3, parts) + block, BF16),
                        pltpu.VMEM(small.shape, F32), pltpu.VMEM(small.shape, F32), pltpu.VMEM((nf - 1,) + small.shape[1:], F32),
                        pltpu.VMEM((cols,) + small.shape[1:], F32), pltpu.VMEM((4,) + small.shape[1:], F32),
                        DMA((4, parts)), DMA((4, parts)), DMA((4, parts)), DMA((4, parts, n)), DMA((4, parts, n)),
                        DMA((4, parts, max(m, nf - 1))), DMA((4, parts, max(m, nf - 1))),
                        DMA((3, parts)), DMA((3, parts)), DMA((3, parts)), DMA((3, parts)),
                        DMA((4, parts, m)), DMA((4, parts, m)), DMA((4, parts, cols)), DMA((4, parts, cols)),
                        DMA((nf + cols + 2,)), DMA((nf + cols + 2,))],
        compiler_params=pltpu.CompilerParams(collective_id=ident, has_side_effects=True, vmem_limit_bytes=56 << 20),
        name="reduce_grads",
    )(grads, small)
KB = 256
SPAN = 256
MASKED = -1e30

def dot(x, y, dims):
    return lax.dot_general(x, y, (dims, ((), ())), preferred_element_type=F32)

NT = ((1,), (1,))
NN = ((1,), (0,))
TN = ((0,), (0,))

def bounds(lens, stream):
    ends, total = [], 0
    for j in range(4):
        total = total + lens[stream, j]
        ends.append(total)
    return ends

def doc_range(pos, ends):
    start = jnp.where(pos >= ends[0], ends[0], 0)
    stop = jnp.where(pos < ends[0], ends[0], ends[3])
    for j in (1, 2):
        start = jnp.where(pos >= ends[j], ends[j], start)
    for j in (2, 1, 0):
        stop = jnp.where(pos < ends[j], ends[j], stop)
    return start, stop

def block_range(base, ends):
    low, _ = doc_range(base, ends)
    _, high = doc_range(base + (SPAN - 1), ends)
    return low // KB, (high + (KB - 1)) // KB

def lane_head(shape, shift):
    lane = lax.broadcasted_iota(jnp.int32, shape, 1)
    return (lane - shift) // 64

def forward_kernel(cols, lens, q_ref, kv_ref, o_ref, ot_ref, lse_ref, qm, vt, acc):
    index = lax.axis_index("ctx")
    b, c = lax.rem(index // 2, cols), lax.rem(index, 2)
    ends = bounds(lens, c)
    total = kv_ref.shape[0]

    @pl.loop(0, total // KB)
    def _(n):
        rows = pl.ds(pl.multiple_of(n * KB, KB), KB)
        vt[:, rows] = kv_ref[rows, 128:384].astype(F32).T.astype(BF16)

    @pl.loop(0, 4)
    def _(stripe):
        base = SPAN * (stripe * cols + b)
        rows = pl.ds(pl.multiple_of(stripe * SPAN, SPAN), SPAN)
        head = lane_head((SPAN, 256), 0)
        q = q_ref[rows].astype(F32) * 0.125
        for h in range(3):
            qm[h] = jnp.where(head == h, q, 0.0).astype(BF16)
        qpos = base + lax.broadcasted_iota(jnp.int32, (1, SPAN), 1)
        start, stop = doc_range(qpos, ends)
        low, high = block_range(base, ends)
        acc[...] = jnp.zeros_like(acc)

        def step(n, state):
            krows = pl.ds(pl.multiple_of(n * KB, KB), KB)
            keys = kv_ref[krows, 0:256]
            kpos = n * KB + lax.broadcasted_iota(jnp.int32, (KB, 1), 0)
            allowed = (kpos >= start) & (kpos < stop)
            out = []
            for h in range(3):
                top, tot = state[h]
                s = jnp.where(allowed, dot(keys, qm[h], NT), MASKED)
                new = jnp.maximum(top, jnp.max(s, axis=0, keepdims=True))
                p = jnp.exp(s - new)
                scale = jnp.exp(top - new)
                hrows = pl.ds(64 * (h + 1), 64)
                acc[hrows] = acc[hrows] * scale + dot(vt[hrows, krows], p.astype(BF16), NN)
                out.append((new, tot * scale + jnp.sum(p, axis=0, keepdims=True)))
            return tuple(out)

        first = tuple((jnp.full((1, SPAN), MASKED, F32), jnp.zeros((1, SPAN), F32)) for _ in range(3))
        final = lax.fori_loop(low, high, step, first)
        for h in range(3):
            top, tot = final[h]
            hrows = pl.ds(64 * (h + 1), 64)
            acc[hrows] = acc[hrows] * (1.0 / tot)
            lse_ref[stripe, pl.ds(h, 1)] = top + jnp.log(tot)
        ot_ref[stripe] = acc[...]
        o_ref[rows] = acc[...].T.astype(BF16)

def vmem():
    return pl.BlockSpec(memory_space=pltpu.VMEM)

def attend_forward(lens, q, kv, cols):
    total = kv.shape[0]
    return pl.pallas_call(
        functools.partial(forward_kernel, cols),
        out_shape=[jax.ShapeDtypeStruct(q.shape, BF16), jax.ShapeDtypeStruct((4, 256, SPAN), F32),
                   jax.ShapeDtypeStruct((4, 8, SPAN), F32)],
        in_specs=[pl.BlockSpec(memory_space=pltpu.SMEM), vmem(), vmem()],
        out_specs=[vmem()] * 3,
        scratch_shapes=[pltpu.VMEM((3, SPAN, 256), BF16), pltpu.VMEM((256, total), BF16), pltpu.VMEM((256, SPAN), F32)],
        compiler_params=pltpu.CompilerParams(vmem_limit_bytes=32 << 20),
        name="attend_forward",
    )(lens, q, kv)

def backward_kernel(cols, lens, q_ref, kv_ref, do_ref, ot_ref, lse_ref, dq_ref, dkv_ref, qm, dm, kt, dk, dv, acc):
    index = lax.axis_index("ctx")
    b, c = lax.rem(index // 2, cols), lax.rem(index, 2)
    ends = bounds(lens, c)
    total = kv_ref.shape[0]

    @pl.loop(0, total // KB)
    def _(n):
        rows = pl.ds(pl.multiple_of(n * KB, KB), KB)
        kt[:, rows] = kv_ref[rows, 0:256].astype(F32).T.astype(BF16)
        dk[rows] = jnp.zeros((KB, 256), F32)
        dv[rows] = jnp.zeros((KB, 256), F32)

    @pl.loop(0, 4)
    def _(stripe):
        base = SPAN * (stripe * cols + b)
        rows = pl.ds(pl.multiple_of(stripe * SPAN, SPAN), SPAN)
        head = lane_head((SPAN, 256), 0)
        headv = lane_head((SPAN, 256), 64)
        q = q_ref[rows].astype(F32) * 0.125
        grad = do_ref[rows].astype(F32)
        for h in range(3):
            qm[h] = jnp.where(head == h, q, 0.0).astype(BF16)
            dm[h] = jnp.where(headv == h, grad, 0.0).astype(BF16)
        prod = grad.T * ot_ref[stripe]
        deltas = [jnp.sum(prod[64 * (h + 1):64 * (h + 2)], axis=0, keepdims=True) for h in range(3)]
        lses = [lse_ref[stripe, pl.ds(h, 1)] for h in range(3)]
        qpos = base + lax.broadcasted_iota(jnp.int32, (1, SPAN), 1)
        start, stop = doc_range(qpos, ends)
        low, high = block_range(base, ends)
        acc[...] = jnp.zeros_like(acc)

        @pl.loop(low, high)
        def _(n):
            krows = pl.ds(pl.multiple_of(n * KB, KB), KB)
            keys = kv_ref[krows, 0:256]
            vals = kv_ref[krows, 128:384]
            kpos = n * KB + lax.broadcasted_iota(jnp.int32, (KB, 1), 0)
            allowed = (kpos >= start) & (kpos < stop)
            newk, newv = dk[krows], dv[krows]
            for h in range(3):
                s = jnp.where(allowed, dot(keys, qm[h], NT), MASKED)
                p = jnp.exp(s - lses[h])
                gp = dot(vals, dm[h], NT)
                ds = (p * (gp - deltas[h])).astype(BF16)
                newv = newv + dot(p.astype(BF16), dm[h], NN)
                newk = newk + dot(ds, qm[h], NN)
                hrows = pl.ds(64 * h, 64)
                acc[hrows] = acc[hrows] + dot(kt[hrows, krows], ds, NN)
            dk[krows] = newk
            dv[krows] = newv

        dq_ref[rows] = (acc[...] * 0.125).T.astype(BF16)

    @pl.loop(0, total // KB)
    def _(n):
        rows = pl.ds(pl.multiple_of(n * KB, KB), KB)
        dkv_ref[rows, 0:128] = dk[rows, 0:128].astype(BF16)
        dkv_ref[rows, 128:256] = (dk[rows, 128:256] + dv[rows, 0:128]).astype(BF16)
        dkv_ref[rows, 256:384] = dv[rows, 128:256].astype(BF16)

def attend_backward(lens, q, kv, do, ot, lse, cols):
    total = kv.shape[0]
    return pl.pallas_call(
        functools.partial(backward_kernel, cols),
        out_shape=[jax.ShapeDtypeStruct(q.shape, BF16), jax.ShapeDtypeStruct(kv.shape, BF16)],
        in_specs=[pl.BlockSpec(memory_space=pltpu.SMEM)] + [vmem()] * 5,
        out_specs=[vmem()] * 2,
        scratch_shapes=[pltpu.VMEM((3, SPAN, 256), BF16), pltpu.VMEM((3, SPAN, 256), BF16), pltpu.VMEM((256, total), BF16),
                        pltpu.VMEM((total, 256), F32), pltpu.VMEM((total, 256), F32), pltpu.VMEM((256, SPAN), F32)],
        compiler_params=pltpu.CompilerParams(vmem_limit_bytes=40 << 20),
        name="attend_backward",
    )(lens, q, kv, do, ot, lse)


STEPS = ((1, 0), (3, 0), (1, 1), (3, 1), (2, 0), (0, 1), (2, 1))


class Octet:
    def __init__(self, go):
        self.go = go
        self.a, self.b, self.c, self.f = a, b, c, f = place(2)
        self.me = a * 2 + c
        self.others = [lax.rem(a + da, 4) * 2 + lax.rem(c + dc, 2) for da, dc in STEPS]
        self.sources = [lax.rem(a + 4 - da, 4) * 2 + lax.rem(c + dc, 2) for da, dc in STEPS]
        self.devices = [device(lax.rem(a + da, 4), b, lax.rem(c + dc, 2), f, 2) for da, dc in STEPS]
        self.relay, self.beyond = self.devices[3], self.devices[1]
        self.origin = lax.rem(a + 1, 4) * 2 + 1 - c

    def send(self, n, source, target, spare):
        if n < 6:
            return self.go(source, target(self.me), self.devices[n])
        return self.go(source, spare, self.relay)

    def forward(self, copy, target, spare):
        copy.wait_recv()
        return self.go(spare, target(self.origin), self.beyond)


def project_kernel(tokens, *refs):
    shards, vectors = refs[:4], refs[4:13]
    q_held, kv_held, f_qkv, f_out, f_in, f_back, vec, turned = refs[13:21]
    own = refs[21:25]
    whole, acc, q_sent, kv_sent, v_own, token, q_spare, kv_spare, held = refs[25:34]
    flat, (send, recv, here) = refs[34:43], refs[43:]
    fulls = (f_qkv, f_out, f_in, f_back)
    a, b, c, f = place(2)
    group = Octet(None)
    me = group.me
    odd_a = lax.rem(a, 2)
    xp, yp, sp = device(a, 1 - b, c, f, 2), device(a, b, c, 1 - f, 2), device(a, b, 1 - c, f, 2)
    pairs = [device(lax.rem(a + 5 - 2 * odd_a, 4), b, c, f, 2), device(lax.rem(a + 3 + 2 * odd_a, 4), b, c, f, 2)]
    loads = [pltpu.make_async_copy(shards[w], own[w], here.at[w]) for w in range(4)]
    flats = [pltpu.make_async_copy(ref, flat[n], here.at[12 + n]) for n, ref in enumerate(vectors)]
    flats.append(pltpu.make_async_copy(tokens, token, here.at[11]))
    for cp in flats + loads:
        cp.start()
    meet(group.devices + [xp, yp])
    wires = Wires(send, recv)
    go = group.go = wires.go

    def rows_of(w, which, chunk):
        size = shards[w].shape[0] // 4
        return pl.multiple_of(which * 2 * size + chunk * size, 16), size

    def cols_of(w, cc):
        half = shards[w].shape[1] // 2
        return pl.ds(pl.multiple_of(cc * half, 128), half)

    def region(target, w, owner, which, cc, chunk):
        start, size = rows_of(w, which, chunk)
        return target.at[pl.ds(owner * shards[w].shape[0] + start, size), cols_of(w, cc)]

    def source(w, which, chunk):
        start, size = rows_of(w, which, chunk)
        return shards[w].at[pl.ds(start, size), cols_of(w, c)]

    other_f = 1 - f

    class Fetch:
        def __init__(self, target, w, chunk, pair=None):
            self.target, self.w, self.chunk = target, w, chunk
            self.which = b if pair is None else odd_a
            self.peer = xp if pair is None else pairs[pair]
            self.first = go(source(w, self.which, chunk), region(target, w, f, self.which, c, chunk), yp)

        def second(self):
            self.first.wait_recv()
            got = region(self.target, self.w, other_f, self.which, c, self.chunk)
            self.cross = go(got, got, self.peer)
            self.side = go(got, got, sp)

        def third(self):
            self.cross.wait_recv()
            got = region(self.target, self.w, other_f, 1 - self.which, c, self.chunk)
            self.side2 = go(got, got, sp)

        def end(self):
            self.side.wait_recv()
            self.side2.wait_recv()

    class Straight:
        def __init__(self, target, w, chunk, which):
            self.place = (target, w, other_f, which, c, chunk)
            self.first = go(source(w, which, chunk), region(target, w, f, which, c, chunk), yp)

        def second(self):
            self.first.wait_recv()
            got = region(*self.place)
            self.side = go(got, got, sp)

        def third(self):
            pass

        def end(self):
            self.side.wait_recv()

    qkv = [Fetch(whole, 0, 0)]
    for cp in flats:
        cp.wait()

    def token_block(dc):
        return token.at[pl.ds(pl.multiple_of(lax.rem(c + dc, 2) * 128, 128), 128)]

    toks = [go(token_block(STEPS[n][1]), held.at[m], group.devices[n]) for m, n in enumerate((0, 1, 2, 3, 5))]
    held[5] = token[pl.ds(pl.multiple_of(c * 128, 128), 128)]
    for n in range(9):
        value = flat[n][...].astype(F32)
        if n == 3:
            for j in range(4):
                v_own[8 + j:9 + j] = value[384 * j:384 * j + 384].reshape(1, 384)
        else:
            row = n if n < 3 else n - 1
            v_own[row:row + 1] = value.reshape(1, 384)
    v_own[12:16] = jnp.zeros((4, 384), F32)
    vec[f] = v_own[...]
    small = go(v_own, vec.at[f], yp)
    loads[0].wait()
    mine = pl.ds(pl.multiple_of(f * 384, 128), 384)
    theirs = pl.ds(pl.multiple_of(other_f * 384, 128), 384)

    @pl.loop(0, 6)
    def _(n):
        cols = pl.ds(pl.multiple_of(n * 384, 128), 384)
        acc[:, cols] = dot(token[:, mine], own[0][:, cols], NN)

    qkv[0].second()
    qkv.append(Fetch(whole, 0, 1))
    qkv[1].second()
    outer = [Fetch(f_back, 3, chunk, chunk) for chunk in range(2)]
    rest = [Fetch(f_out, 1, chunk) for chunk in range(2)]
    inner = [Straight(f_in, 2, chunk, which) for chunk in range(2) for which in range(2)]
    qkv[0].third()
    qkv[1].third()
    stores = []
    for w in range(4):
        if w > 0:
            loads[w].wait()
        rows = shards[w].shape[0]
        cp = pltpu.make_async_copy(own[w], fulls[w].at[pl.ds(pl.multiple_of(f * rows, 16), rows)], here.at[4 + w])
        cp.start()
        stores.append(cp)
    small.wait_recv()
    qkv[0].end()
    qkv[1].end()
    cp = pltpu.make_async_copy(whole.at[pl.ds(pl.multiple_of(other_f * 384, 16), 384)],
                               f_qkv.at[pl.ds(pl.multiple_of(other_f * 384, 16), 384)], here.at[8])
    cp.start()
    stores.append(cp)

    def column(n):
        cols = slice(384 * n, 384 * n + 384)
        value = acc[:, cols] + dot(token[:, theirs], whole[pl.ds(pl.multiple_of(other_f * 384, 16), 384), cols], NN)
        if n < 2:
            value = value + vec[n, 0:1]
        if n >= 4:
            value = value + vec[n - 4, 1:2]
        return value

    lane = lax.broadcasted_iota(jnp.int32, (256, 384), 1)
    for p in range(2):
        k, v = column(2 + p), column(4 + p)
        turned_k, turned_v = pltpu.roll(k, 192, 1), pltpu.roll(v, 192, 1)
        even = jnp.where(lane < 192, k, turned_v).astype(BF16)
        odd = jnp.where(lane < 192, turned_k, v).astype(BF16)
        q = column(p)
        q_even = jnp.where(lane < 192, q, 0.0)[:, :256].astype(BF16)
        q_odd = jnp.where(lane < 192, pltpu.roll(q, 192, 1), 0.0)[:, :256].astype(BF16)
        for s in range(2):
            rows = slice(128 * s, 128 * s + 128)
            kv_sent[4 * p + s], kv_sent[4 * p + 2 + s] = even[rows], odd[rows]
            q_sent[4 * p + s], q_sent[4 * p + 2 + s] = q_even[rows], q_odd[rows]

    def slot(block, bb):
        return (block // 2 * 2 + bb) * 2 + lax.rem(block, 2)

    kv_slot = lambda block: kv_held.at[slot(block, b)]
    q_slot = lambda block: q_held.at[block]
    first = [group.send(n, kv_sent.at[group.others[n]], kv_slot, kv_spare) for n in (6, 0, 1, 2, 3, 4, 5)]
    first = first[1:] + first[:1]
    own_kv = pltpu.make_async_copy(kv_sent.at[me], kv_held.at[slot(me, b)], here.at[9])
    own_kv.start()
    own_q = pltpu.make_async_copy(q_sent.at[me], q_held.at[me], here.at[10])
    own_q.start()
    crossed = [go(kv_sent.at[me], kv_held.at[slot(me, b)], xp)]
    third = [group.send(n, q_sent.at[group.others[n]], q_slot, q_spare) for n in (6, 0, 1, 2, 3, 4, 5)]
    third = third[1:] + third[:1]

    def onward(n):
        first[n].wait_recv()
        piece = kv_slot(group.sources[n])
        crossed.append(go(piece, piece, xp))

    onward(5)
    onward(0)
    onward(1)
    first[6] = group.forward(first[6], kv_slot, kv_spare)
    for cp in outer:
        cp.second()
    for cp in rest:
        cp.second()
    onward(2)
    onward(3)
    third[6] = group.forward(third[6], q_slot, q_spare)
    onward(4)
    onward(6)
    for cp in toks:
        cp.wait_recv()

    @pl.loop(0, 6)
    def _(n):
        @pl.loop(0, 6)
        def _(m):
            lanes = pl.ds(pl.multiple_of(m * 128, 128), 128)
            turned[n, lanes] = held[n, :, lanes].astype(F32).T.astype(BF16)

    for cp in inner:
        cp.second()
    for cp in outer:
        cp.third()
    for cp in rest:
        cp.third()
    for cp in crossed + third:
        cp.wait_recv()
    for cp in rest + inner + outer:
        cp.end()
    for cp in wires.made:
        cp.wait_send()
    for cp in stores + [own_kv, own_q]:
        cp.wait()


def project(tokens, shards, vectors, ident):
    rows, width = tokens.shape
    anywhere = pl.BlockSpec(memory_space=pl.ANY)
    wires = 80
    return pl.pallas_call(
        project_kernel,
        out_shape=[jax.ShapeDtypeStruct((8, 128, 256), BF16), jax.ShapeDtypeStruct((16, 128, 384), BF16)]
        + [jax.ShapeDtypeStruct((2 * s.shape[0], s.shape[1]), BF16) for s in shards]
        + [jax.ShapeDtypeStruct((2, 16, 384), F32), jax.ShapeDtypeStruct((6, 768, 128), BF16)],
        in_specs=[pl.BlockSpec(memory_space=pltpu.HBM)] * 14,
        out_specs=[vmem()] * 2 + [anywhere] * 4 + [vmem()] * 2,
        scratch_shapes=[pltpu.VMEM(s.shape, BF16) for s in shards]
        + [pltpu.VMEM((768, 2304), BF16), pltpu.VMEM((256, 2304), F32), pltpu.VMEM((8, 128, 256), BF16),
           pltpu.VMEM((8, 128, 384), BF16), pltpu.VMEM((16, 384), F32), pltpu.VMEM(tokens.shape, BF16),
           pltpu.VMEM((128, 256), BF16), pltpu.VMEM((128, 384), BF16),
           pltpu.VMEM((6, 128, 768), BF16),
           *[pltpu.VMEM(v.shape, BF16) for v in vectors], DMA((wires,)), DMA((wires,)), DMA((21,))],
        compiler_params=pltpu.CompilerParams(collective_id=ident, has_side_effects=True, vmem_limit_bytes=62 << 20),
        name="project",
    )(tokens, *shards, *vectors)


BLK = 48
Z1, X1, Y1 = (0, 768), (768, 1920), (1920, 3456)
LATE = (0, 640)


class Wires:
    def __init__(self, send, recv):
        self.send, self.recv, self.made = send, recv, []

    def go(self, source, target, peer):
        n = len(self.made)
        cp = remote(source, target, self.send.at[n], self.recv.at[n], peer)
        cp.start()
        self.made.append(cp)
        return cp


def transpose_into(target, source, base):
    width = source.shape[1]

    @pl.loop(0, width // 128)
    def _(n):
        at = pl.multiple_of(n * 128, 128)
        target[pl.ds(base + at, 128)] = source[:, pl.ds(at, 128)].astype(F32).T.astype(BF16)


def pair_columns(even, odd, lane, second):
    if second:
        return jnp.where(lane < 192, pltpu.roll(even, 192, 1), odd)
    return jnp.where(lane < 192, even, pltpu.roll(odd, 192, 1))


def halves(span):
    tiles = (span[1] - span[0]) // 128
    mid = span[0] + tiles // 2 * 128
    return (span[0], mid), (mid, span[1])


def within(span, group):
    base = 0
    for member in group:
        if member == span:
            return slice(base, base + span[1] - span[0])
        base += member[1] - member[0]


def gradient_kernel(lens, wqkv, gfirst, near, far, xt, gbr, ghid, gsec, small, do_sent, q_ref, kv_ref, ot_ref, lse_ref,
                    out, late_out, igrad, small_out,
                    joined, wqkv_held, mine, sib, cin, y8, y4, x8, x4, z4, z1r, zyb, zxb,
                    do_held, qm, dm, kt, dk, dv, acc, rowsc, delta, dq_all, dkv_all, dqo, dkvo, xsend, rbuf,
                    l_sib, l_in, l_acc, l_mine, ly, lx,
                    do_spare, dq_spare, dkv_spare, v_own, v_core, v_f, v_b, v_a, send, recv, here):
    weights = pltpu.make_async_copy(wqkv, wqkv_held, here.at[5])
    weights.start()
    group = Octet(None)
    a, b, c, f, me = group.a, group.b, group.c, group.f, group.me
    xp, yp, sp = device(a, 1 - b, c, f, 2), device(a, b, c, 1 - f, 2), device(a, b, 1 - c, f, 2)
    up, down = lax.rem(a + 1, 4), lax.rem(a + 3, 4)
    upp, downp = device(up, b, c, f, 2), device(down, b, c, f, 2)
    ends = bounds(lens, c)
    total = kv_ref.shape[0]
    meet(group.devices + [xp, yp])
    wires = Wires(send, recv)
    go = group.go = wires.go
    pending = []

    do_slot = lambda block: do_held.at[block]
    swaps = {n: group.send(n, do_sent.at[group.others[n]], do_slot, do_spare) for n in (6, 0, 1, 2, 3, 4, 5)}
    do_held[me] = do_sent[me]


    def produce(kind, first, count, part, finish):
        @pl.loop(0, 2 * count)
        def _(n):
            ff, j = lax.rem(n, 2), first + n // 2
            if kind == "out":
                left, right = xt[pl.ds(pl.multiple_of(ff * 384, 128), 384)], gbr[:, pl.ds(pl.multiple_of(part * 384, 128), 384)]
                col = 768
            elif kind == "in":
                left = xt[pl.ds(pl.multiple_of(768 + ff * 384, 128), 384)]
                right = ghid[:, pl.ds(pl.multiple_of(part * 1536 + j * 384, 128), 384)]
                col = pl.multiple_of(j * 384 + (384 if first else 0), 128)
            else:
                left = xt[pl.ds(pl.multiple_of(1536 + ff * 1536 + j * 384, 128), 384)]
                right = gsec[:, pl.ds(pl.multiple_of(part * 384, 128), 384)]
                col = pl.multiple_of(1920 + j * 384, 128)
            finish(pl.ds(ff * 2, 2), pl.ds(col, 384), dot(left, right, NN).reshape(2, 4, BLK, 384))

    def keep(rows, cols, value):
        sib[rows, :, :, cols] = value.astype(BF16)

    def join(rows, cols, value):
        mine[rows, :, :, cols] = (value + cin[rows, :, :, cols].astype(F32)).astype(BF16)

    core = {}

    def share(span):
        cols = slice(span[0], span[1])
        core[span] = go(sib.at[:, :, :, cols], cin.at[:, :, :, cols], sp)

    RS = (Y1, X1)

    def add(target, source):
        def step(n):
            t, s = target(n), source(n)
            t[...] = (t[...].astype(F32) + s[...].astype(F32)).astype(BF16)
        return step

    def accumulate(target, source, count):
        pl.loop(0, count)(add(target, source))

    ycols, xcols, zcols = slice(*Y1), slice(*X1), slice(*Z1)

    def start_y():
        return go(mine.at[pl.ds((1 - f) * 2, 2), :, :, ycols], y8, yp)

    def start_x():
        return [go(mine.at[ff * 2 + 1 - b, :, :, xcols], x8.at[ff], xp) for ff in range(2)]

    def next_y(cp):
        cp.wait_recv()
        accumulate(lambda n: mine.at[f * 2 + n // 4, lax.rem(n, 4), :, ycols], lambda n: y8.at[n // 4, lax.rem(n, 4)], 8)
        return go(mine.at[f * 2 + 1 - b, :, :, ycols], x4, xp)

    def next_x(cps):
        for cp in cps:
            cp.wait_recv()
        accumulate(lambda n: mine.at[n // 4 * 2 + b, lax.rem(n, 4), :, xcols], lambda n: x8.at[n // 4, lax.rem(n, 4)], 8)
        return go(mine.at[(1 - f) * 2 + b, :, :, xcols], y4, yp)

    def last_y(cp):
        cp.wait_recv()
        accumulate(lambda n: mine.at[f * 2 + b, n, :, ycols], lambda n: x4.at[n], 4)

    def last_x(cp):
        cp.wait_recv()
        accumulate(lambda n: mine.at[f * 2 + b, n, :, xcols], lambda n: y4.at[n], 4)

    def landing(span, step, part, single):
        if single:
            base = within(span, RS).start - span[0]
            return z1r.at[step, :, base + part[0]:base + part[1]]
        return z4.at[step, :, :, part[0]:part[1]]

    def ring_source(aa, part, single):
        cols = slice(part[0], part[1])
        return mine.at[f * 2 + b, aa, :, cols] if single else mine.at[:, aa, :, cols]

    def ring_send(span, step, single):
        lo, hi = halves(span)
        ud, dd = lax.rem(a + 3 - step, 4), lax.rem(a + 1 + step, 4)
        return (go(ring_source(ud, lo, single), landing(span, step, lo, single), upp),
                go(ring_source(dd, hi, single), landing(span, step, hi, single), downp))

    def ring_add(span, step, single, cps):
        lo, hi = halves(span)
        ud, dd = lax.rem(a + 6 - step, 4), lax.rem(a + 2 + step, 4)
        for cp, part, aa in zip(cps, (lo, hi), (ud, dd)):
            cp.wait_recv()
            got = landing(span, step, part, single)
            if single:
                add(lambda n: ring_source(aa, part, True), lambda n: got)(0)
            else:
                cols = slice(part[0], part[1])
                accumulate(lambda n: mine.at[n, aa, :, cols], lambda n: got.at[n], 4)

    def tail_z_y():
        return go(mine.at[pl.ds((1 - f) * 2, 2), a, :, zcols], zyb, yp)

    def tail_z_x(cp):
        cp.wait_recv()
        accumulate(lambda n: mine.at[f * 2 + n, a, :, zcols], lambda n: zyb.at[n], 2)
        return go(mine.at[f * 2 + 1 - b, a, :, zcols], zxb, xp)

    def tail_z_end(cp):
        cp.wait_recv()
        add(lambda n: mine.at[f * 2 + b, a, :, zcols], lambda n: zxb)(0)

    class Gather:
        def __init__(self, own, spot, span, first):
            self.span, self.first, self.spot = span, first, spot
            self.own = own
            self.copy = pltpu.make_async_copy(own, spot(b, a, span), here.at[len(locals_)])
            self.copy.start()
            locals_.append(self.copy)
            pending.append(go(own, spot(b, a, span), sp))
            self.ring = go(own, spot(b, a, span), upp), go(own, spot(b, a, span), downp)
            self.cross = go(own, spot(b, a, span), xp)

        def spread(self, bb, aa):
            p = self.spot(bb, aa, self.span)
            pending.append(go(p, p, sp))

        def passed(self, bb, ring):
            lo, hi = halves(self.span)
            ring[0].wait_recv()
            p = self.spot(bb, down, lo)
            first = go(p, p, upp)
            ring[1].wait_recv()
            p = self.spot(bb, up, hi)
            second = go(p, p, downp)
            for aa in (down, up):
                self.spread(bb, aa)
            return first, second

        def arrived(self, bb, ring):
            for cp in ring:
                cp.wait_recv()
            self.spread(bb, lax.rem(a + 2, 4))

        def second(self):
            self.ring2 = self.passed(b, self.ring)
            if self.first == "b":
                self.cross.wait_recv()
                self.spread(1 - b, a)
                p = self.spot(1 - b, a, self.span)
                self.other = go(p, p, upp), go(p, p, downp)
            else:
                spots = [self.spot(b, aa, self.span) for aa in (down, up)]
                self.more = [go(p, p, xp) for p in spots]

        def third(self):
            self.arrived(b, self.ring2)
            if self.first == "b":
                self.other2 = self.passed(1 - b, self.other)
            else:
                p = self.spot(b, lax.rem(a + 2, 4), self.span)
                self.more.append(go(p, p, xp))
                self.cross.wait_recv()
                self.spread(1 - b, a)

        def fourth(self):
            if self.first == "b":
                self.arrived(1 - b, self.other2)
            else:
                for cp, aa in zip(self.more, (down, up, lax.rem(a + 2, 4))):
                    cp.wait_recv()
                    self.spread(1 - b, aa)

    locals_ = []

    def early_spot(bb, aa, span):
        return out.at[c, bb * 4 + aa, :, span[0]:span[1]]

    def late_spot(bb, aa, span):
        return late_out.at[aa, bb * 2 + c, :, span[0]:span[1]]

    def early_gather(span, first):
        return Gather(mine.at[f * 2 + b, a, :, span[0]:span[1]], early_spot, span, first)

    def prepare():
        @pl.loop(0, total // KB)
        def _(n):
            rows = pl.ds(pl.multiple_of(n * KB, KB), KB)
            kt[:, rows] = kv_ref[rows, 0:256].astype(F32).T.astype(BF16)

        @pl.loop(0, 4)
        def _(stripe):
            head = lane_head((SPAN, 256), 0)
            headv = lane_head((SPAN, 256), 64)
            q = q_ref[pl.ds(stripe * 2, 2)].reshape(SPAN, 256).astype(F32) * 0.125
            grad = do_held[pl.ds(stripe * 2, 2)].reshape(SPAN, 256).astype(F32)
            for h in range(3):
                qm[stripe, h] = jnp.where(head == h, q, 0.0).astype(BF16)
                dm[stripe, h] = jnp.where(headv == h, grad, 0.0).astype(BF16)
            prod = grad.T * ot_ref[stripe]
            for h in range(3):
                delta[stripe, h:h + 1] = jnp.sum(prod[64 * (h + 1):64 * (h + 2)], axis=0, keepdims=True)
            qpos = SPAN * (stripe * 2 + b) + lax.broadcasted_iota(jnp.int32, (1, SPAN), 1)
            start, stop = doc_range(qpos, ends)
            rowsc[stripe, 0:1] = start
            rowsc[stripe, 1:2] = stop
            acc[stripe] = jnp.zeros((256, SPAN), F32)

    reach = total * 5 // 8 // KB

    def attend(da, parity):
        block = lax.rem(a + da, 4) * 2 + parity
        krows = pl.ds(pl.multiple_of(block * KB, KB), KB)
        dk[...] = jnp.zeros((KB, 256), F32)
        dv[...] = jnp.zeros((KB, 256), F32)
        @pl.loop(0, 4)
        def _(stripe):
            away = stripe * 2 + b - block

            @pl.when((away <= reach) & (away >= -reach))
            def _():
                keys = kv_ref[krows, 0:256]
                vals = kv_ref[krows, 128:384]
                kpos = block * KB + lax.broadcasted_iota(jnp.int32, (KB, 1), 0)
                allowed = (kpos >= rowsc[stripe, 0:1]) & (kpos < rowsc[stripe, 1:2])
                newk, newv = dk[...], dv[...]
                for h in range(3):
                    s = jnp.where(allowed, dot(keys, qm[stripe, h], NT), MASKED)
                    p = jnp.exp(s - lse_ref[stripe, h:h + 1])
                    gp = dot(vals, dm[stripe, h], NT)
                    ds = (p * (gp - delta[stripe, h:h + 1])).astype(BF16)
                    newv = newv + dot(p.astype(BF16), dm[stripe, h], NN)
                    newk = newk + dot(ds, qm[stripe, h], NN)
                    hrows = pl.ds(64 * h, 64)
                    acc[stripe, hrows] = acc[stripe, hrows] + dot(kt[hrows, krows], ds, NN)
                dk[...] = newk
                dv[...] = newv

    def slot(block, bb):
        return (block // 2 * 2 + bb) * 2 + lax.rem(block, 2)

    def grads_of(dc):
        rows = pl.ds(pl.multiple_of(lax.rem(c + dc, 2) * 128, 128), 128)
        k, v = dk[rows], dv[rows]
        return jnp.concatenate([k[:, :128], k[:, 128:] + v[:, :128], v[:, 128:]], axis=1)

    FAR, NEXT = ((6, 1), (4, 0)), ((0, 0), (2, 1))
    BACK, HERE = ((1, 0), (3, 1)), ((5, 1), (7, 0))
    crossed = {}

    def cross(members):
        for n, dc in members:
            xsend[n] = grads_of(dc).astype(BF16)
            crossed[n] = go(xsend.at[n], rbuf.at[n], xp)

    dkv_slot = lambda block: dkvo.at[block]
    dkvs = {}

    def settle(members):
        for n, dc in members:
            crossed[n].wait_recv()
            value = (grads_of(dc) + rbuf[n].astype(F32)).astype(BF16)
            if n == 7:
                dkv_all[me] = value
                dkvo[me] = value
            else:
                dkv_all[group.others[n]] = value
                dkvs[n] = group.send(n, dkv_all.at[group.others[n]], dkv_slot, dkv_spare)

    dq_slot = lambda block: dqo.at[block]
    dqs = {}

    produce("out", 0, 1, 1 - c, keep)
    produce("in", 2, 2, 1 - c, keep)
    share(X1)
    produce("back", 0, 4, 1 - c, keep)
    share(Y1)
    core[X1].wait_recv()
    produce("out", 0, 1, c, join)
    produce("in", 2, 2, c, join)
    x1 = start_x()
    swaps[6] = group.forward(swaps[6], do_slot, do_spare)
    core[Y1].wait_recv()
    produce("back", 0, 4, c, join)
    y1 = start_y()
    produce("in", 0, 2, 1 - c, keep)
    share(Z1)
    for cp in swaps.values():
        cp.wait_recv()
    prepare()
    core[Z1].wait_recv()
    produce("in", 0, 2, c, join)
    z1 = ring_send(Z1, 0, False)
    attend(2, 1 - b)
    cross(FAR)
    attend(1, 1 - b)
    cross(NEXT)
    ring_add(Z1, 0, False, z1)
    z1 = ring_send(Z1, 1, False)
    attend(3, 1 - b)
    cross(BACK)
    attend(0, 1 - b)
    cross(HERE)
    x1 = next_x(x1)
    ring_add(Z1, 1, False, z1)
    z1 = ring_send(Z1, 2, False)
    attend(2, b)
    settle(FAR)
    attend(1, b)
    settle(NEXT)
    ring_add(Z1, 2, False, z1)
    z1 = tail_z_y()
    attend(3, b)
    settle(BACK)
    y1 = next_y(y1)
    attend(0, b)

    @pl.loop(0, 4)
    def _(stripe):
        dq_all[pl.ds(stripe * 2, 2)] = (acc[stripe] * 0.125).T.astype(BF16).reshape(2, 128, 256)

    for n in (6, 0, 1, 2, 3, 4, 5):
        dqs[n] = group.send(n, dq_all.at[group.others[n]], dq_slot, dq_spare)
    dqo[me] = dq_all[me]
    settle(HERE)
    dkvs[6] = group.forward(dkvs[6], dkv_slot, dkv_spare)

    def project_back(n, right):
        rows = pl.ds(pl.multiple_of(n * 96, 32), 96)
        value = dot(near[5, rows], right[me], NN)
        for m, k in enumerate((0, 1, 2, 3, 5)):
            value = value + dot(near[m, rows], right[group.sources[k]], NN)
        for m, k in ((0, 4), (1, 6)):
            value = value + dot(far[m, rows], right[group.sources[k]], NN)
        return value

    @pl.loop(0, 4)
    def _(n):
        theirs, ours = n * 2 + 1 - c, n * 2 + c
        l_sib[n, :, 0:256] = project_back(theirs, dq_all).astype(BF16)
        l_sib[n, :, 256:640] = project_back(theirs, dkv_all).astype(BF16)
        l_acc[n, :, 0:256] = project_back(ours, dq_all)
        l_acc[n, :, 256:640] = project_back(ours, dkv_all)

    late = go(l_sib, l_in, sp)
    last_x(x1)
    x1 = ring_send(X1, 0, True)
    z1 = tail_z_x(z1)
    dqs[6] = group.forward(dqs[6], dq_slot, dq_spare)
    late.wait_recv()

    @pl.loop(0, 4)
    def _(n):
        l_mine[n] = (l_acc[n] + l_in[n].astype(F32)).astype(BF16)

    late = go(l_mine.at[pl.ds((1 - f) * 2, 2)], ly, yp)
    ring_add(X1, 0, True, x1)
    x1 = ring_send(X1, 1, True)
    tail_z_end(z1)
    late.wait_recv()
    accumulate(lambda n: l_mine.at[f * 2 + n], lambda n: ly.at[n], 2)
    late = go(l_mine.at[f * 2 + 1 - b], lx, xp)
    last_y(y1)
    y1 = ring_send(Y1, 0, True)
    ring_add(X1, 1, True, x1)
    x1 = ring_send(X1, 2, True)
    g_z1 = early_gather(Z1, "a")
    late.wait_recv()
    add(lambda n: l_mine.at[f * 2 + b], lambda n: lx)(0)
    g_l = Gather(l_mine.at[f * 2 + b], late_spot, LATE, "a")
    ring_add(Y1, 0, True, y1)
    y1 = ring_send(Y1, 1, True)
    ring_add(X1, 2, True, x1)
    g_x1 = early_gather(X1, "a")
    ring_add(Y1, 1, True, y1)
    y1 = ring_send(Y1, 2, True)
    g_z1.second()

    for cp in list(dqs.values()) + list(dkvs.values()):
        cp.wait_recv()
    lane = lax.broadcasted_iota(jnp.int32, (128, 384), 1)
    for s in range(2):
        rows = slice(s * 128, s * 128 + 128)
        for p in range(2):
            even, odd = 4 * p + s, 4 * p + 2 + s
            blank = jnp.zeros((128, 128), F32)
            qe = jnp.concatenate([dqo[even].astype(F32), blank], axis=1)
            qo = jnp.concatenate([dqo[odd].astype(F32), blank], axis=1)
            joined[rows, 384 * p:384 * p + 384] = pair_columns(qe, qo, lane, False).astype(BF16)
            ke, ko = dkvo[even].astype(F32), dkvo[odd].astype(F32)
            joined[rows, 768 + 384 * p:1152 + 384 * p] = pair_columns(ke, ko, lane, False).astype(BF16)
            joined[rows, 1536 + 384 * p:1920 + 384 * p] = pair_columns(ke, ko, lane, True).astype(BF16)
    v_own[...] = small[...]
    v_own[0:1] = jnp.sum(joined[:, 0:768].astype(F32), axis=0, keepdims=True)
    v_own[1:2] = jnp.sum(joined[:, 1536:2304].astype(F32), axis=0, keepdims=True)
    vec = go(v_own, v_core, sp)

    ring_add(Y1, 2, True, y1)
    g_y1 = early_gather(Y1, "a")
    vec.wait_recv()
    v_core[...] = v_own[...] + v_core[...]
    vec = go(v_core.at[:, pl.ds(pl.multiple_of((1 - f) * 384, 128), 384)], v_f, yp)
    g_l.second()
    g_x1.second()
    g_z1.third()
    vec.wait_recv()
    v_b[b] = v_core[:, pl.ds(pl.multiple_of(f * 384, 128), 384)] + v_f[...]
    vec = go(v_b.at[b], v_b.at[b], xp)
    weights.wait()

    @pl.loop(0, 3)
    def _(n):
        rows = pl.ds(pl.multiple_of(n * 256, 256), 256)
        igrad[:, rows] = gfirst[:, rows] + dot(joined[...], wqkv_held[rows], NT)

    g_y1.second()
    g_l.third()
    g_x1.third()
    g_z1.fourth()
    vec.wait_recv()
    v_a[a] = v_b[0] + v_b[1]
    vec = [go(v_a.at[a], v_a.at[a], device(lax.rem(a + k, 4), b, c, f, 2)) for k in range(1, 4)]
    g_y1.third()
    g_l.fourth()
    g_x1.fourth()
    g_y1.fourth()
    for cp in vec + pending:
        cp.wait_recv()
    small_out[...] = v_a[0] + v_a[1] + v_a[2] + v_a[3]
    for cp in locals_:
        cp.wait()
    for cp in wires.made:
        cp.wait_send()


def reduce_all(lens, wqkv, gfirst, near, far, xt, gbr, ghid, gsec, small, do_sent, q, kv, ot, lse, ident):
    wires = 192
    total = kv.shape[0]
    bf = lambda *shape: pltpu.VMEM(shape, BF16)
    fl = lambda *shape: pltpu.VMEM(shape, F32)
    anywhere = pl.BlockSpec(memory_space=pl.ANY)
    return pl.pallas_call(
        gradient_kernel,
        out_shape=[jax.ShapeDtypeStruct((2, 8, BLK, 3456), BF16), jax.ShapeDtypeStruct((4, 4, 96, 640), BF16),
                   jax.ShapeDtypeStruct((256, 768), F32), jax.ShapeDtypeStruct((16, 384), F32)],
        in_specs=[pl.BlockSpec(memory_space=pltpu.SMEM), anywhere] + [vmem()] * 13, out_specs=[anywhere] * 2 + [vmem()] * 2,
        scratch_shapes=[
            bf(256, 2304), bf(768, 2304), bf(4, 4, BLK, 3456), bf(4, 4, BLK, 3456), bf(4, 4, BLK, 3456),
            bf(2, 4, BLK, 1536), bf(4, BLK, 1152), bf(2, 4, BLK, 1152), bf(4, BLK, 1536),
            bf(3, 4, BLK, 768), bf(3, BLK, 2688), bf(2, BLK, 768), bf(BLK, 768),
            bf(8, 128, 256), bf(4, 3, SPAN, 256), bf(4, 3, SPAN, 256), bf(256, total), fl(KB, 256), fl(KB, 256), fl(4, 256, SPAN),
            pltpu.VMEM((4, 8, SPAN), jnp.int32), fl(4, 8, SPAN),
            bf(8, 128, 256), bf(8, 128, 384), bf(8, 128, 256), bf(8, 128, 384), bf(8, 128, 384), bf(8, 128, 384),
            bf(4, 96, 640), bf(4, 96, 640), fl(4, 96, 640), bf(4, 96, 640), bf(2, 96, 640), bf(96, 640),
            bf(128, 256), bf(128, 256), bf(128, 384),
            fl(16, 768), fl(16, 768), fl(16, 384), fl(2, 16, 384), fl(4, 16, 384),
            DMA((wires,)), DMA((wires,)), DMA((6,))],
        compiler_params=pltpu.CompilerParams(collective_id=ident, has_side_effects=True, vmem_limit_bytes=62 << 20),
        name="reduce_all",
    )(lens, wqkv, gfirst, near, far, xt, gbr, ghid, gsec, small, do_sent, q, kv, ot, lse)


def widen_kernel(grads, late, g_qkv, g_out, g_in, g_back):
    for core in range(2):
        part = grads.at[core]
        g_out[:, core * 384:core * 384 + 384] = part[:, 768:1152].astype(F32)
        g_in[:, core * 1536:core * 1536 + 768] = part[:, 0:768].astype(F32)
        g_in[:, core * 1536 + 768:core * 1536 + 1536] = part[:, 1152:1920].astype(F32)
        for j in range(4):
            g_back[j, :, core * 384:core * 384 + 384] = part[:, 1920 + 384 * j:2304 + 384 * j].astype(F32)
    lane = lax.broadcasted_iota(jnp.int32, (96, 384), 1)
    for p in range(2):
        even, odd = late[2 * p, 0].astype(F32), late[2 * p + 1, 0].astype(F32)
        g_qkv[:, 384 * p:384 * p + 384] = pair_columns(even[:, :384], odd[:, :384], lane, False)
        ke, ko = even[:, 256:], odd[:, 256:]
        g_qkv[:, 768 + 384 * p:1152 + 384 * p] = pair_columns(ke, ko, lane, False)
        g_qkv[:, 1536 + 384 * p:1920 + 384 * p] = pair_columns(ke, ko, lane, True)


def widen(grads, late):
    rows, step = 384, 96
    spec = lambda wide: pl.BlockSpec((step, wide), lambda n: (n, 0))
    return pl.pallas_call(
        widen_kernel,
        grid=(rows // step,),
        out_shape=[jax.ShapeDtypeStruct((rows, 2304), F32), jax.ShapeDtypeStruct((rows, 768), F32),
                   jax.ShapeDtypeStruct((rows, 3072), F32), jax.ShapeDtypeStruct((4, rows, 768), F32)],
        in_specs=[pl.BlockSpec((2, step, 3456), lambda n: (0, n, 0)), pl.BlockSpec((4, 1, step, 640), lambda n: (0, n, 0, 0))],
        out_specs=[spec(2304), spec(768), spec(3072), pl.BlockSpec((4, step, 768), lambda n: (0, n, 0))],
        compiler_params=pltpu.CompilerParams(vmem_limit_bytes=40 << 20),
        name="widen",
    )(grads, late)


def middle_kernel(o_sent, tokens, cotangent, w_out, w_in, w_back, vec,
                  output, gfirst, xt, gbr, ghid, gsec, do_sent, small, far,
                  o_held, o_spare, f_held, f_spare, v_out, v_in, v_back, normed, xhat1, final, slope, act, send, recv, here):
    group = Octet(None)
    a, b, c, f, me = group.a, group.b, group.c, group.f, group.me
    loads = [pltpu.make_async_copy(s, t, here.at[n]) for n, (s, t) in enumerate(((w_out, v_out), (w_in, v_in), (w_back, v_back)))]
    for cp in loads:
        cp.start()
    meet(group.devices)
    wires = Wires(send, recv)
    go = group.go = wires.go
    o_slot = lambda block: o_held.at[block]
    swaps = {n: group.send(n, o_sent.at[group.others[n]], o_slot, o_spare) for n in (6, 0, 1, 2, 3, 4, 5)}
    o_held[me] = o_sent[me]
    swaps[6] = group.forward(swaps[6], o_slot, o_spare)

    def token_block(dc):
        return tokens.at[pl.ds(pl.multiple_of(lax.rem(c + dc, 2) * 128, 128), 128)]

    beyond = [go(token_block(dc), f_held.at[dc], group.devices[n]) for dc, n in ((0, 4),)]
    relayed = go(token_block(1), f_spare, group.relay)

    def row(n):
        return jnp.concatenate([vec[0, n:n + 1], vec[1, n:n + 1]], axis=1)

    def sums(n, value):
        small[n:n + 1] = jnp.sum(value, axis=0, keepdims=True)

    for cp in swaps.values():
        cp.wait_recv()
    lane = lax.broadcasted_iota(jnp.int32, (128, 384), 1)
    blank = jnp.zeros((128, 128), F32)
    att = act
    for s in range(2):
        rows = slice(s * 128, s * 128 + 128)
        for p in range(2):
            sides = [jnp.concatenate([pltpu.roll(o_held[4 * p + 2 * k + s].astype(F32), 192, 1), blank], axis=1) for k in range(2)]
            att[rows, 384 * p:384 * p + 384] = pair_columns(sides[0], sides[1], lane, False).astype(BF16)
    transpose_into(xt, att.at[:, 0:768], 0)

    def norm(value):
        mean = jnp.sum(value, axis=1, keepdims=True) * (1.0 / 768)
        centered = value - mean
        variance = jnp.sum(centered * centered, axis=1, keepdims=True) * (1.0 / 768)
        inverse = lax.rsqrt(variance + EPSILON)
        return centered * inverse, inverse

    def norm_back(upstream, gain, hat, inverse):
        scaled = upstream * gain
        first = jnp.sum(scaled, axis=1, keepdims=True) * (1.0 / 768)
        second = jnp.sum(scaled * hat, axis=1, keepdims=True) * (1.0 / 768)
        return inverse * (scaled - first - hat * second)

    loads[0].wait()
    hat, inverse1 = norm(tokens[...].astype(F32) + (dot(att[:, 0:768], v_out[...], NN) + row(2)))
    xhat1[...] = hat
    value = hat * row(4) + row(5)
    normed[...] = value
    output[...] = value.astype(BF16)
    transpose_into(xt, output, 768)
    loads[1].wait()

    @pl.loop(0, 4)
    def _(n):
        cols = pl.ds(pl.multiple_of(n * 768, 128), 768)
        ff, j = n // 2, lax.rem(n, 2) * 2
        bias = jnp.concatenate([vec[ff, pl.ds(8 + j, 1)], vec[ff, pl.ds(9 + j, 1)]], axis=1)
        hidden = dot(output[...], v_in[:, cols], NN) + bias
        half = 0.5 * (1.0 + lax.erf(hidden * 0.7071067811865476))
        slope[:, cols] = half + hidden * (jnp.exp(-0.5 * hidden * hidden) * 0.3989422804014327)
        act[:, cols] = (hidden * half).astype(BF16)

    relayed.wait_recv()
    beyond.append(go(f_spare, f_held.at[1], group.beyond))
    transpose_into(xt, act, 1536)
    loads[2].wait()
    final[...] = normed[...] + (dot(act[...], v_back[...], NN) + row(3))
    hat2, inverse2 = norm(final[...])
    output[...] = (hat2 * row(6) + row(7)).astype(BF16)
    upstream = cotangent[...].astype(F32)
    sums(6, upstream * hat2)
    sums(7, upstream)
    gfinal = norm_back(upstream, row(6), hat2, inverse2)
    final[...] = gfinal
    gsec[...] = gfinal.astype(BF16)
    sums(3, gsec[...].astype(F32))

    @pl.loop(0, 4)
    def _(n):
        cols = pl.ds(pl.multiple_of(n * 768, 128), 768)
        ff, j = n // 2, lax.rem(n, 2) * 2
        value = (dot(gsec[...], v_back[cols], NT) * slope[:, cols]).astype(BF16)
        ghid[:, cols] = value
        total = jnp.sum(value.astype(F32), axis=0, keepdims=True)
        lanes = pl.ds(pl.multiple_of(ff * 384, 128), 384)
        small[pl.ds(8 + j, 1), lanes] = total[:, :384]
        small[pl.ds(9 + j, 1), lanes] = total[:, 384:]

    small[0:2] = jnp.zeros((2, 768), F32)
    small[12:16] = jnp.zeros((4, 768), F32)

    @pl.loop(0, 3)
    def _(n):
        cols = pl.ds(pl.multiple_of(n * 256, 128), 256)
        final[:, cols] = final[:, cols] + dot(ghid[...], v_in[cols], NT)

    hat = xhat1[...]
    upstream = final[...]
    sums(4, upstream * hat)
    sums(5, upstream)
    value = norm_back(upstream, row(4), hat, inverse1)
    gfirst[...] = value
    gbr[...] = value.astype(BF16)
    sums(2, gbr[...].astype(F32))
    normed[...] = dot(gbr[...], v_out[...], NT)
    wide = lax.broadcasted_iota(jnp.int32, (256, 256), 1)
    for p in range(2):
        part = normed[:, 384 * p:384 * p + 384]
        for k in range(2):
            turned = part if k == 0 else pltpu.roll(part, 192, 1)
            block = pltpu.roll(jnp.where(wide < 192, turned[:, :256], 0.0), 64, 1).astype(BF16)
            for s in range(2):
                do_sent[4 * p + 2 * k + s] = block[128 * s:128 * s + 128]
    for cp in beyond:
        cp.wait_recv()
    for n in range(2):
        @pl.loop(0, 6)
        def _(m):
            lanes = pl.ds(pl.multiple_of(m * 128, 128), 128)
            far[n, lanes] = f_held[n, :, lanes].astype(F32).T.astype(BF16)
    for cp in wires.made:
        cp.wait_send()


def middle(o_sent, tokens, cotangent, w_out, w_in, w_back, vec, ident):
    bf = lambda *shape: pltpu.VMEM(shape, BF16)
    fl = lambda *shape: pltpu.VMEM(shape, F32)
    out = lambda d, *shape: jax.ShapeDtypeStruct(shape, d)
    anywhere = pl.BlockSpec(memory_space=pl.ANY)
    wires = 16
    return pl.pallas_call(
        middle_kernel,
        out_shape=[out(BF16, 256, 768), out(F32, 256, 768), out(BF16, 4608, 256), out(BF16, 256, 768), out(BF16, 256, 3072),
                   out(BF16, 256, 768), out(BF16, 8, 128, 256), out(F32, 16, 768), out(BF16, 2, 768, 128)],
        in_specs=[vmem()] * 3 + [anywhere] * 3 + [vmem()], out_specs=[vmem()] * 9,
        scratch_shapes=[bf(8, 128, 256), bf(128, 256), bf(2, 128, 768), bf(128, 768), bf(768, 768), bf(768, 3072), bf(3072, 768),
                        fl(256, 768), fl(256, 768), fl(256, 768), fl(256, 3072), bf(256, 3072),
                        DMA((wires,)), DMA((wires,)), DMA((3,))],
        compiler_params=pltpu.CompilerParams(collective_id=ident, has_side_effects=True, vmem_limit_bytes=60 << 20),
        name="middle",
    )(o_sent, tokens, cotangent, w_out, w_in, w_back, vec)


def layer_norm(values, gain_row, shift_row):
    average = jnp.mean(values, axis=-1, keepdims=True)
    centered = values - average
    variance = jnp.mean(centered * centered, axis=-1, keepdims=True)
    return centered * lax.rsqrt(variance + EPSILON) * gain_row + shift_row


def exact_gelu(values):
    return jax.nn.gelu(values, approximate=False)


def by_group(rows, micro, front, back):
    parts = rows.reshape(micro, -1, 4, 192).transpose(2, 0, 1, 3)
    parts = jnp.pad(parts, ((0, 0), (0, 0), (0, 0), (front, back)))
    return parts.reshape((-1,) + parts.shape[2:])


def from_group(blocks, micro, front):
    rows = blocks.shape[1]
    parts = blocks.reshape(4, micro, rows, -1)[..., front:front + 192]
    return parts.transpose(1, 2, 0, 3).reshape(micro * rows, 768)


def shards(tokens, cotangent, doc_lengths, w_qkv, w_out, w_in, w_back, *vectors):
    micro, per, width = tokens.shape
    nf, cols = lax.axis_size("fsdp"), lax.axis_size("ctx") // 8
    share = width // nf
    inputs = tokens.reshape(micro * per, width)
    cube = nf == 2 and cols == 2
    if cube:
        q_held, kv_held, full_qkv, full_out, full_in, full_back, sides, near = project(inputs, (w_qkv, w_out, w_in, w_back), vectors, 1)
        kv_held = kv_held.reshape(-1, 384)
        mixed, mixed_t, log_total = attend_forward(doc_lengths, q_held.reshape(8 * per, 256), kv_held, cols)
        output, grad_first, xt, grad_branch, grad_hidden, grad_second, do_sent, small, far = middle(
            mixed.reshape(8, per, 256), inputs, cotangent.reshape(inputs.shape), full_out, full_in, full_back, sides, 3)
        grads, late, input_grad, sums = reduce_all(
            doc_lengths, full_qkv, grad_first, near, far, xt, grad_branch, grad_hidden, grad_second, small, do_sent, q_held, kv_held,
            mixed_t, log_total, 5)
        g_qkv, g_out, g_in, g_back = widen(grads.reshape(2, share, 3456), late)
        rows = [sums[0], sums[1], sums[2], sums[8:12].reshape(-1), sums[3], sums[4], sums[5], sums[6], sums[7]]
        return (output.reshape(tokens.shape), input_grad.reshape(tokens.shape), g_qkv, g_out, g_in, g_back.reshape(4 * share, width)) + tuple(rows)
    tiny = jnp.concatenate(vectors).reshape(8, -1)
    full_qkv, full_out, full_in, full_back, tinies = gather_weights((w_qkv, w_out, w_in, w_back), tiny, nf, cols)
    tinies = tinies.reshape(nf, -1).astype(F32)
    named, at = [], 0
    for vector in vectors:
        size = vector.shape[0]
        named.append(tinies[:, at:at + size].reshape(-1))
        at += size
    b_query, b_value, b_out, b_in, b_back, gain_one, shift_one, gain_two, shift_two = named
    joined = jnp.dot(inputs, full_qkv, preferred_element_type=F32)
    bias = jnp.concatenate([b_query, jnp.zeros_like(b_query), b_value])
    joined = (joined + bias).astype(BF16)
    q_sent = by_group(joined[:, :width], micro, 0, 64)
    kv_sent = jnp.concatenate([by_group(joined[:, width:2 * width], micro, 0, 0), by_group(joined[:, 2 * width:], micro, 0, 0)], axis=2)
    q_held, kv_held = spread(q_sent, kv_sent, cols, 2)
    q_held = q_held.reshape(8 * per, 256)
    kv_held = kv_held.reshape(-1, 384)
    mixed, mixed_t, log_total = attend_forward(doc_lengths, q_held, kv_held, cols)
    (back,) = swap([mixed.reshape(8, per, 256)], cols, 3)
    attended = from_group(back, micro, 64)
    first_sum = inputs.astype(F32) + (jnp.dot(attended, full_out, preferred_element_type=F32) + b_out)
    normed = layer_norm(first_sum, gain_one, shift_one)
    normed_low = normed.astype(BF16)
    hidden = jnp.dot(normed_low, full_in, preferred_element_type=F32) + b_in
    activated = exact_gelu(hidden).astype(BF16)
    final_sum = normed + (jnp.dot(activated, full_back, preferred_element_type=F32) + b_back)
    output = layer_norm(final_sum, gain_two, shift_two).astype(BF16)

    upstream = cotangent.reshape(micro * per, width).astype(F32)
    grad_final, g_gain_two, g_shift_two = jax.vjp(layer_norm, final_sum, gain_two, shift_two)[1](upstream)
    grad_second = grad_final.astype(BF16)
    g_back_bias = jnp.sum(grad_second.astype(F32), axis=0)
    grad_activated = jnp.einsum("rm,km->rk", grad_second, full_back, preferred_element_type=F32)
    grad_hidden = jax.vjp(exact_gelu, hidden)[1](grad_activated)[0].astype(BF16)
    g_in_bias = jnp.sum(grad_hidden.astype(F32), axis=0)
    grad_normed = grad_final + jnp.einsum("rf,mf->rm", grad_hidden, full_in, preferred_element_type=F32)
    grad_first, g_gain_one, g_shift_one = jax.vjp(layer_norm, first_sum, gain_one, shift_one)[1](grad_normed)
    grad_branch = grad_first.astype(BF16)
    g_out_bias = jnp.sum(grad_branch.astype(F32), axis=0)
    grad_attended = jnp.einsum("rm,km->rk", grad_branch, full_out, preferred_element_type=F32).astype(BF16)
    (do_held,) = swap([by_group(grad_attended, micro, 64, 0)], cols, 4)
    dq, dkv = attend_backward(doc_lengths, q_held, kv_held, do_held.reshape(8 * per, 256), mixed_t, log_total, cols)
    dq_own, dkv_own = collect(dq.reshape(8, per, 256), dkv.reshape(8 * cols, per, 384), cols, 5)
    grad_joined = jnp.concatenate(
        [from_group(dq_own, micro, 0), from_group(dkv_own, micro, 0), from_group(dkv_own, micro, 192)], axis=1)
    g_query_bias = jnp.sum(grad_joined[:, :width].astype(F32), axis=0)
    g_value_bias = jnp.sum(grad_joined[:, 2 * width:].astype(F32), axis=0)
    input_grad = grad_first + jnp.einsum("rc,mc->rm", grad_joined, full_qkv, preferred_element_type=F32)

    def halves(left, right):
        blocks = right.shape[1] // 384
        return jnp.einsum("rm,rhc->hmc", left, right.reshape(-1, blocks, 384), preferred_element_type=F32).astype(BF16)

    back_grads = jnp.einsum("rk,rm->km", activated, grad_second, preferred_element_type=F32).astype(BF16)
    back_grads = back_grads.reshape(nf, 4, share, 2, 384).transpose(1, 3, 0, 2, 4).reshape(8, width, 384)
    grads = jnp.concatenate(
        [halves(inputs, grad_joined), halves(attended, grad_branch), halves(normed_low, grad_hidden), back_grads])
    grads = grads.reshape(2, 4, 3, nf, cols, share // cols, 384)
    small = (g_query_bias, g_value_bias, g_out_bias, g_in_bias, g_back_bias, g_gain_one, g_shift_one, g_gain_two, g_shift_two)
    small = jnp.concatenate([x.reshape(nf, -1) for x in small], axis=1).reshape(nf, 8, -1)
    owned, small_owned = reduce_grads(grads, small, nf, cols, 6)
    owned = owned.transpose(0, 1, 3, 2, 4, 5).reshape(24, share, 384)

    def columns(first, last):
        return owned[first:last].transpose(1, 0, 2).reshape(share, -1).astype(F32)

    g_back = owned[16:].reshape(4, 2, share, 384).transpose(0, 2, 1, 3).reshape(4 * share, width).astype(F32)
    small_owned = small_owned.reshape(-1)
    small_grads, at = [], 0
    for vector in vectors:
        small_grads.append(small_owned[at:at + vector.shape[0]])
        at += vector.shape[0]
    return (output.reshape(tokens.shape), input_grad.reshape(tokens.shape), columns(0, 6), columns(6, 8), columns(8, 16), g_back) + tuple(small_grads)


def solution(mesh):
    rows, flat = P("fsdp", "ctx", None), P("fsdp", None)
    return jax.shard_map(
        shards,
        mesh=mesh,
        in_specs=(rows, rows, flat) + (flat,) * 4 + (P("fsdp"),) * 9,
        out_specs=(rows, rows) + (flat,) * 4 + (P("fsdp"),) * 9,
        check_vma=False,
    )
```

```python
import functools

import jax
import jax.numpy as jnp
from jax import lax
from jax.experimental import pallas as pl
from jax.experimental.pallas import tpu as pltpu
from jax.sharding import PartitionSpec as P

MESH = pl.DeviceIdType.MESH
DMA = pltpu.SemaphoreType.DMA
F32, BF16 = jnp.float32, jnp.bfloat16
EPSILON = 1e-12

def place(cols):
    index = lax.axis_index("ctx")
    return index // (2 * cols), lax.rem(index // 2, cols), lax.rem(index, 2), lax.axis_index("fsdp")

def device(a, b, c, f, cols):
    return {"ctx": (a * cols + b) * 2 + c, "fsdp": f}

def meet(peers):
    barrier = pltpu.get_barrier_semaphore()
    for peer in peers:
        pl.semaphore_signal(barrier, inc=1, device_id=peer, device_id_type=MESH)
    pl.semaphore_wait(barrier, len(peers))

def remote(source, target, send, recv, peer):
    return pltpu.make_async_remote_copy(
        src_ref=source, dst_ref=target, send_sem=send, recv_sem=recv, device_id=peer, device_id_type=MESH)

def gather_kernel(nf, cols, count, *refs):
    shards, tiny, fulls, tiny_out = refs[:count], refs[count], refs[count+1:2*count+1], refs[2*count+1]
    local_sem, s1, r1, s2, r2, s3, r3, st, rt = refs[2*count+2:]
    a, b, c, f = place(cols)
    other = 1 - c
    fpeers = [device(a, b, c, lax.rem(f + j, nf), cols) for j in range(1, nf)]
    bpeers = [device(a, lax.rem(b + k, cols), c, f, cols) for k in range(1, cols)]
    sibling = device(a, b, other, f, cols)
    meet(fpeers + bpeers + [sibling])

    def view(w, owner, bb, cc, base=0):
        rows, wide = shards[w].shape
        part, half = rows // cols, wide // 2
        return fulls[w].at[pl.ds(pl.multiple_of(owner * rows + bb * part, 8), part), pl.ds(pl.multiple_of(cc * half, 128), half)]

    waits = []
    for j in range(1, nf):
        cp = remote(tiny, tiny_out.at[f], st.at[j - 1], rt.at[j - 1], fpeers[j - 1])
        cp.start()
        waits.append(cp)
    locals_ = [pltpu.make_async_copy(tiny, tiny_out.at[f], local_sem.at[count])]
    locals_[0].start()
    first = {}
    for w in range(count):
        rows, wide = shards[w].shape
        part, half = rows // cols, wide // 2
        mine = shards[w].at[pl.ds(pl.multiple_of(b * part, 8), part), pl.ds(pl.multiple_of(c * half, 128), half)]
        for j in range(1, nf):
            cp = remote(mine, view(w, f, b, c), s1.at[w, j - 1], r1.at[w, j - 1], fpeers[j - 1])
            cp.start()
            first[w, j] = cp
    for w in range(count):
        rows = shards[w].shape[0]
        cp = pltpu.make_async_copy(shards[w], fulls[w].at[pl.ds(pl.multiple_of(f * rows, 8), rows)], local_sem.at[w])
        cp.start()
        locals_.append(cp)
    second, third = {}, []
    for w in range(count):
        for j in range(1, nf):
            owner = lax.rem(f + nf - j, nf)
            first[w, j].wait_recv()
            piece = view(w, owner, b, c)
            for k in range(1, cols):
                slot = (j - 1) * (cols - 1) + k - 1
                cp = remote(piece, piece, s2.at[w, slot], r2.at[w, slot], bpeers[k - 1])
                cp.start()
                second[w, j, k] = cp
            cp = remote(piece, piece, s3.at[w, (j - 1) * cols], r3.at[w, (j - 1) * cols], sibling)
            cp.start()
            third.append(cp)
    for w in range(count):
        for j in range(1, nf):
            owner = lax.rem(f + nf - j, nf)
            for k in range(1, cols):
                second[w, j, k].wait_recv()
                piece = view(w, owner, lax.rem(b + cols - k, cols), c)
                cp = remote(piece, piece, s3.at[w, (j - 1) * cols + k], r3.at[w, (j - 1) * cols + k], sibling)
                cp.start()
                third.append(cp)
    for cp in third:
        cp.wait_recv()
    for cp in waits:
        cp.wait()
    for cp in list(first.values()) + list(second.values()) + third:
        cp.wait_send()
    for cp in locals_:
        cp.wait()

def gather_weights(shards, tiny, nf, cols):
    count = len(shards)
    any_spec = pl.BlockSpec(memory_space=pl.ANY)
    dma = pltpu.SemaphoreType.DMA
    return pl.pallas_call(
        functools.partial(gather_kernel, nf, cols, count),
        out_shape=[jax.ShapeDtypeStruct((s.shape[0] * nf, s.shape[1]), s.dtype) for s in shards]
        + [jax.ShapeDtypeStruct((nf,) + tiny.shape, tiny.dtype)],
        in_specs=[pl.BlockSpec(memory_space=pltpu.VMEM)] * (count + 1),
        out_specs=[any_spec] * (count + 1),
        scratch_shapes=[dma((count + 1,)), dma((count, nf - 1)), dma((count, nf - 1)),
                        dma((count, (nf - 1) * (cols - 1))), dma((count, (nf - 1) * (cols - 1))),
                        dma((count, (nf - 1) * cols)), dma((count, (nf - 1) * cols)),
                        dma((nf - 1,)), dma((nf - 1,))],
        compiler_params=pltpu.CompilerParams(collective_id=1, has_side_effects=True, vmem_limit_bytes=32 << 20),
        name="gather_weights",
    )(*shards, tiny)

def octet(a, b, c, f, cols):
    me = a * 2 + c
    out = []
    for k in range(1, 8):
        other = lax.rem(me + k, 8)
        out.append((other, device(other // 2, b, lax.rem(other, 2), f, cols)))
    return me, out

def swap_kernel(cols, count, *refs):
    sources, targets = refs[:count], refs[count:2 * count]
    send, recv, here = refs[2 * count:]
    a, b, c, f = place(cols)
    me, peers = octet(a, b, c, f, cols)
    meet([p for _, p in peers])
    copies = []
    for k, (other, peer) in enumerate(peers):
        for i in range(count):
            cp = remote(sources[i].at[other], targets[i].at[me], send.at[i, k], recv.at[i, k], peer)
            cp.start()
            copies.append(cp)
    for i in range(count):
        cp = pltpu.make_async_copy(sources[i].at[me], targets[i].at[me], here.at[i])
        cp.start()
        copies.append(cp)
    for cp in copies:
        cp.wait()

def swap(arrays, cols, ident):
    count = len(arrays)
    return pl.pallas_call(
        functools.partial(swap_kernel, cols, count),
        out_shape=[jax.ShapeDtypeStruct(x.shape, x.dtype) for x in arrays],
        in_specs=[vmem()] * count, out_specs=[vmem()] * count,
        scratch_shapes=[DMA((count, 7)), DMA((count, 7)), DMA((count,))],
        compiler_params=pltpu.CompilerParams(collective_id=ident, has_side_effects=True, vmem_limit_bytes=16 << 20),
        name="swap",
    )(*arrays)

def spread_kernel(cols, q, kv, qg, full, sq, rq, sk, rk, s2, r2, here):
    a, b, c, f = place(cols)
    me, peers = octet(a, b, c, f, cols)
    bpeers = [device(a, lax.rem(b + k, cols), c, f, cols) for k in range(1, cols)]
    meet([p for _, p in peers] + bpeers)

    def slot(block, bb):
        return (block // 2 * cols + bb) * 2 + lax.rem(block, 2)

    first = []
    for k, (other, peer) in enumerate(peers):
        cp = remote(kv.at[other], full.at[slot(me, b)], sk.at[k], rk.at[k], peer)
        cp.start()
        first.append(cp)
    own = pltpu.make_async_copy(kv.at[me], full.at[slot(me, b)], here.at[0])
    own.start()
    ownq = pltpu.make_async_copy(q.at[me], qg.at[me], here.at[1])
    ownq.start()
    second = []
    for k, peer in enumerate(bpeers):
        cp = remote(kv.at[me], full.at[slot(me, b)], s2.at[7, k], r2.at[7, k], peer)
        cp.start()
        second.append(cp)
    third = []
    for k, (other, peer) in enumerate(peers):
        cp = remote(q.at[other], qg.at[me], sq.at[k], rq.at[k], peer)
        cp.start()
        third.append(cp)
    for k in range(7):
        first[k].wait_recv()
        source = lax.rem(me + 8 - (k + 1), 8)
        piece = full.at[slot(source, b)]
        for m, peer in enumerate(bpeers):
            cp = remote(piece, piece, s2.at[k, m], r2.at[k, m], peer)
            cp.start()
            second.append(cp)
    for cp in first:
        cp.wait_send()
    for cp in second + third:
        cp.wait()
    own.wait()
    ownq.wait()

def spread(q, kv, cols, ident):
    return pl.pallas_call(
        functools.partial(spread_kernel, cols),
        out_shape=[jax.ShapeDtypeStruct(q.shape, q.dtype), jax.ShapeDtypeStruct((8 * cols,) + kv.shape[1:], kv.dtype)],
        in_specs=[vmem()] * 2, out_specs=[vmem()] * 2,
        scratch_shapes=[DMA((7,))] * 4 + [DMA((8, max(cols - 1, 1)))] * 2 + [DMA((2,))],
        compiler_params=pltpu.CompilerParams(collective_id=ident, has_side_effects=True, vmem_limit_bytes=16 << 20),
        name="spread",
    )(q, kv)

def collect_kernel(cols, dq, dkv, dqo, dkvo, rbuf, total, sq, rq, sk, rk, s2, r2, here):
    a, b, c, f = place(cols)
    me, peers = octet(a, b, c, f, cols)
    bpeers = [(lax.rem(b + k, cols), device(a, lax.rem(b + k, cols), c, f, cols)) for k in range(1, cols)]
    meet([p for _, p in peers] + [p for _, p in bpeers])

    def slot(block, bb):
        return (block // 2 * cols + bb) * 2 + lax.rem(block, 2)

    order = [other for other, _ in peers] + [me]
    first = {}
    for n, block in enumerate(order):
        for k, (bb, peer) in enumerate(bpeers):
            cp = remote(dkv.at[slot(block, bb)], rbuf.at[k, n], s2.at[k, n], r2.at[k, n], peer)
            cp.start()
            first[k, n] = cp
    rest = []
    for k, (other, peer) in enumerate(peers):
        cp = remote(dq.at[other], dqo.at[me], sq.at[k], rq.at[k], peer)
        cp.start()
        rest.append(cp)
    own = pltpu.make_async_copy(dq.at[me], dqo.at[me], here.at[0])
    own.start()
    for n, block in enumerate(order):
        value = dkv[slot(block, b)].astype(F32)
        for k in range(cols - 1):
            first[k, n].wait_recv()
            value = value + rbuf[k, n].astype(F32)
        if n < 7:
            total[n] = value.astype(BF16)
            cp = remote(total.at[n], dkvo.at[me], sk.at[n], rk.at[n], peers[n][1])
            cp.start()
            rest.append(cp)
        else:
            dkvo[me] = value.astype(BF16)
    for cp in first.values():
        cp.wait_send()
    for cp in rest:
        cp.wait()
    own.wait()

def collect(dq, dkv, cols, ident):
    block = dkv.shape[1:]
    return pl.pallas_call(
        functools.partial(collect_kernel, cols),
        out_shape=[jax.ShapeDtypeStruct(dq.shape, dq.dtype), jax.ShapeDtypeStruct((8,) + block, dkv.dtype)],
        in_specs=[vmem()] * 2, out_specs=[vmem()] * 2,
        scratch_shapes=[pltpu.VMEM((max(cols - 1, 1), 8) + block, BF16), pltpu.VMEM((7,) + block, BF16)]
        + [DMA((7,))] * 4 + [DMA((max(cols - 1, 1), 8))] * 2 + [DMA((1,))],
        compiler_params=pltpu.CompilerParams(collective_id=ident, has_side_effects=True, vmem_limit_bytes=24 << 20),
        name="collect",
    )(dq, dkv)

def reduce_kernel(nf, cols, parts, grads, small, out, small_out, *refs):
    own, core_in, f_in, b_in, f_in2, b_in2, a_in, v_core, v_sum, v_f, v_b, v_a = refs[:12]
    load, sc, rc, s1, r1, s2, r2, s3, r3, s4, r4, s5, r5, s6, r6, sv, rv = refs[12:]
    a, b, c, f = place(cols)
    rows = grads.shape[5]
    fpeers = [(lax.rem(f + j, nf), device(a, b, c, lax.rem(f + j, nf), cols)) for j in range(1, nf)]
    bpeers = [(lax.rem(b + k, cols), device(a, lax.rem(b + k, cols), c, f, cols)) for k in range(1, cols)]
    apeers = [(lax.rem(a + k, 4), device(lax.rem(a + k, 4), b, c, f, cols)) for k in range(1, 4)]
    sibling = device(a, b, 1 - c, f, cols)
    meet([p for _, p in fpeers + bpeers + apeers] + [sibling])
    vector = remote(small, v_core, sv.at[0], rv.at[0], sibling)
    vector.start()
    order = [2, 1, 3, 0]
    dest = {k: lax.rem(a + k, 4) for k in range(4)}
    by_f = {k: k in (1, 2) for k in range(4)}
    loads, cores = {}, {}
    for k in order:
        for i in range(parts):
            cp = pltpu.make_async_copy(grads.at[c, dest[k], i], own.at[k, i], load.at[k, i])
            cp.start()
            loads[k, i] = cp
            cp = remote(grads.at[1 - c, dest[k], i], core_in.at[k, i], sc.at[k, i], rc.at[k, i], sibling)
            cp.start()
            cores[k, i] = cp
    one, two, three = {}, {}, {}
    vec = {}
    vector.wait_recv()
    v_sum[...] = small[...] + v_core[...]
    for j, (ff, peer) in enumerate(fpeers):
        vec[0, j] = remote(v_sum.at[ff], v_f.at[j], sv.at[1 + j], rv.at[1 + j], peer)
        vec[0, j].start()
    for k in order:
        for i in range(parts):
            loads[k, i].wait()
            cores[k, i].wait_recv()

            @pl.loop(0, nf * cols)
            def _(n):
                ff, bb = n // cols, lax.rem(n, cols)
                own[k, i, ff, bb] = (own[k, i, ff, bb].astype(F32) + core_in[k, i, ff, bb].astype(F32)).astype(BF16)

            if by_f[k]:
                for j, (ff, peer) in enumerate(fpeers):
                    cp = remote(own.at[k, i, ff], f_in.at[k, i, j], s1.at[k, i, j], r1.at[k, i, j], peer)
                    cp.start()
                    one[k, i, j] = cp
            else:
                for m, (bb, peer) in enumerate(bpeers):
                    for ff in range(nf):
                        cp = remote(own.at[k, i, ff, bb], b_in.at[k, i, m, ff], s1.at[k, i, m * nf + ff], r1.at[k, i, m * nf + ff], peer)
                        cp.start()
                        one[k, i, m * nf + ff] = cp
    value = v_sum[f]
    for j in range(nf - 1):
        vec[0, j].wait_recv()
        value = value + v_f[j]
    v_b[b] = value
    for m, (bb, peer) in enumerate(bpeers):
        vec[1, m] = remote(v_b.at[b], v_b.at[b], sv.at[nf + m], rv.at[nf + m], peer)
        vec[1, m].start()
    for k in order:
        for i in range(parts):
            if by_f[k]:
                for j in range(nf - 1):
                    one[k, i, j].wait_recv()

                @pl.loop(0, cols)
                def _(bb):
                    value = own[k, i, f, bb].astype(F32)
                    for j in range(nf - 1):
                        value = value + f_in[k, i, j, bb].astype(F32)
                    own[k, i, f, bb] = value.astype(BF16)

                for m, (bb, peer) in enumerate(bpeers):
                    cp = remote(own.at[k, i, f, bb], b_in2.at[k, i, m], s2.at[k, i, m], r2.at[k, i, m], peer)
                    cp.start()
                    two[k, i, m] = cp
            else:
                for m in range(cols - 1):
                    for ff in range(nf):
                        one[k, i, m * nf + ff].wait_recv()

                @pl.loop(0, nf)
                def _(ff):
                    value = own[k, i, ff, b].astype(F32)
                    for m in range(cols - 1):
                        value = value + b_in[k, i, m, ff].astype(F32)
                    own[k, i, ff, b] = value.astype(BF16)

                for j, (ff, peer) in enumerate(fpeers):
                    cp = remote(own.at[k, i, ff, b], f_in2.at[k, i, j], s2.at[k, i, j], r2.at[k, i, j], peer)
                    cp.start()
                    two[k, i, j] = cp
    for m in range(cols - 1):
        vec[1, m].wait_recv()
    value = v_b[0]
    for m in range(1, cols):
        value = value + v_b[m]
    v_a[a] = value
    for k in range(1, 4):
        vec[2, k] = remote(v_a.at[a], v_a.at[a], sv.at[nf + cols + k - 2], rv.at[nf + cols + k - 2], apeers[k - 1][1])
        vec[2, k].start()
    for k in order:
        for i in range(parts):
            value = own[k, i, f, b].astype(F32)
            if by_f[k]:
                for m in range(cols - 1):
                    two[k, i, m].wait_recv()
                    value = value + b_in2[k, i, m].astype(F32)
            else:
                for j in range(nf - 1):
                    two[k, i, j].wait_recv()
                    value = value + f_in2[k, i, j].astype(F32)
            if k != 0:
                own[k, i, f, b] = value.astype(BF16)
                cp = remote(own.at[k, i, f, b], a_in.at[k - 1, i], s3.at[k - 1, i], r3.at[k - 1, i], apeers[k - 1][1])
                cp.start()
                three[k, i] = cp
            else:
                own[k, i, f, b] = value.astype(BF16)
    for k in range(1, 4):
        vec[2, k].wait_recv()
    small_out[...] = v_a[0] + v_a[1] + v_a[2] + v_a[3]
    four, five, six = {}, {}, {}

    def piece(aa, bb, cc, i):
        return out.at[cc, aa, bb, i]

    pending = []
    for i in range(parts):
        value = own[0, i, f, b].astype(F32)
        for k in range(1, 4):
            three[k, i].wait_recv()
            value = value + a_in[k - 1, i].astype(F32)
        out[c, a, b, i] = value.astype(BF16)
        mine = piece(a, b, c, i)
        for k in (2, 1, 3):
            cp = remote(mine, mine, s4.at[k - 1, i], r4.at[k - 1, i], apeers[k - 1][1])
            cp.start()
            four[k, i] = cp
        for m, (bb, peer) in enumerate(bpeers):
            cp = remote(mine, mine, s5.at[0, i, m], r5.at[0, i, m], peer)
            cp.start()
            five[0, i, m] = cp
        cp = remote(mine, mine, s6.at[0, i, 0], r6.at[0, i, 0], sibling)
        cp.start()
        six[0, i, 0] = cp
    for i in range(parts):
        for k in (1, 3, 2):
            four[k, i].wait_recv()
            got = piece(lax.rem(a + 4 - k, 4), b, c, i)
            for m, (bb, peer) in enumerate(bpeers):
                cp = remote(got, got, s5.at[k, i, m], r5.at[k, i, m], peer)
                cp.start()
                five[k, i, m] = cp
            cp = remote(got, got, s6.at[k, i, 0], r6.at[k, i, 0], sibling)
            cp.start()
            six[k, i, 0] = cp
    for i in range(parts):
        for k in (0, 1, 3, 2):
            for m in range(cols - 1):
                five[k, i, m].wait_recv()
                got = piece(lax.rem(a + 4 - k, 4), lax.rem(b + cols - (m + 1), cols), c, i)
                cp = remote(got, got, s6.at[k, i, m + 1], r6.at[k, i, m + 1], sibling)
                cp.start()
                six[k, i, m + 1] = cp
    for cp in six.values():
        cp.wait_recv()
    vector.wait_send()
    for group in (cores, one, two, three, four, five, six, vec):
        for cp in group.values():
            cp.wait_send()

def reduce_grads(grads, small, nf, cols, ident):
    _, _, parts, _, _, rows, width = grads.shape
    block = (rows, width)
    m = max(cols - 1, 1)
    n = max((cols - 1) * nf, nf - 1)
    return pl.pallas_call(
        functools.partial(reduce_kernel, nf, cols, parts),
        out_shape=[jax.ShapeDtypeStruct((2, 4, cols, parts) + block, BF16), jax.ShapeDtypeStruct(small.shape[1:], F32)],
        in_specs=[pl.BlockSpec(memory_space=pl.ANY), vmem()], out_specs=[vmem()] * 2,
        scratch_shapes=[pltpu.VMEM((4, parts, nf, cols) + block, BF16), pltpu.VMEM((4, parts, nf, cols) + block, BF16),
                        pltpu.VMEM((4, parts, nf - 1, cols) + block, BF16), pltpu.VMEM((4, parts, m, nf) + block, BF16),
                        pltpu.VMEM((4, parts, nf - 1) + block, BF16), pltpu.VMEM((4, parts, m) + block, BF16),
                        pltpu.VMEM((3, parts) + block, BF16),
                        pltpu.VMEM(small.shape, F32), pltpu.VMEM(small.shape, F32), pltpu.VMEM((nf - 1,) + small.shape[1:], F32),
                        pltpu.VMEM((cols,) + small.shape[1:], F32), pltpu.VMEM((4,) + small.shape[1:], F32),
                        DMA((4, parts)), DMA((4, parts)), DMA((4, parts)), DMA((4, parts, n)), DMA((4, parts, n)),
                        DMA((4, parts, max(m, nf - 1))), DMA((4, parts, max(m, nf - 1))),
                        DMA((3, parts)), DMA((3, parts)), DMA((3, parts)), DMA((3, parts)),
                        DMA((4, parts, m)), DMA((4, parts, m)), DMA((4, parts, cols)), DMA((4, parts, cols)),
                        DMA((nf + cols + 2,)), DMA((nf + cols + 2,))],
        compiler_params=pltpu.CompilerParams(collective_id=ident, has_side_effects=True, vmem_limit_bytes=56 << 20),
        name="reduce_grads",
    )(grads, small)
KB = 256
SPAN = 256
MASKED = -1e30

def dot(x, y, dims):
    return lax.dot_general(x, y, (dims, ((), ())), preferred_element_type=F32)

NT = ((1,), (1,))
NN = ((1,), (0,))
TN = ((0,), (0,))

def bounds(lens, stream):
    ends, total = [], 0
    for j in range(4):
        total = total + lens[stream, j]
        ends.append(total)
    return ends

def doc_range(pos, ends):
    start = jnp.where(pos >= ends[0], ends[0], 0)
    stop = jnp.where(pos < ends[0], ends[0], ends[3])
    for j in (1, 2):
        start = jnp.where(pos >= ends[j], ends[j], start)
    for j in (2, 1, 0):
        stop = jnp.where(pos < ends[j], ends[j], stop)
    return start, stop

def block_range(base, ends):
    low, _ = doc_range(base, ends)
    _, high = doc_range(base + (SPAN - 1), ends)
    return low // KB, (high + (KB - 1)) // KB

def lane_head(shape, shift):
    lane = lax.broadcasted_iota(jnp.int32, shape, 1)
    return (lane - shift) // 64

def forward_kernel(cols, lens, q_ref, kv_ref, o_ref, ot_ref, lse_ref, qm, vt, acc):
    index = lax.axis_index("ctx")
    b, c = lax.rem(index // 2, cols), lax.rem(index, 2)
    ends = bounds(lens, c)
    total = kv_ref.shape[0]

    @pl.loop(0, total // KB)
    def _(n):
        rows = pl.ds(pl.multiple_of(n * KB, KB), KB)
        vt[:, rows] = kv_ref[rows, 128:384].astype(F32).T.astype(BF16)

    @pl.loop(0, 4)
    def _(stripe):
        base = SPAN * (stripe * cols + b)
        rows = pl.ds(pl.multiple_of(stripe * SPAN, SPAN), SPAN)
        head = lane_head((SPAN, 256), 0)
        q = q_ref[rows].astype(F32) * 0.125
        for h in range(3):
            qm[h] = jnp.where(head == h, q, 0.0).astype(BF16)
        qpos = base + lax.broadcasted_iota(jnp.int32, (1, SPAN), 1)
        start, stop = doc_range(qpos, ends)
        low, high = block_range(base, ends)
        acc[...] = jnp.zeros_like(acc)

        def step(n, state):
            krows = pl.ds(pl.multiple_of(n * KB, KB), KB)
            keys = kv_ref[krows, 0:256]
            kpos = n * KB + lax.broadcasted_iota(jnp.int32, (KB, 1), 0)
            allowed = (kpos >= start) & (kpos < stop)
            out = []
            for h in range(3):
                top, tot = state[h]
                s = jnp.where(allowed, dot(keys, qm[h], NT), MASKED)
                new = jnp.maximum(top, jnp.max(s, axis=0, keepdims=True))
                p = jnp.exp(s - new)
                scale = jnp.exp(top - new)
                hrows = pl.ds(64 * (h + 1), 64)
                acc[hrows] = acc[hrows] * scale + dot(vt[hrows, krows], p.astype(BF16), NN)
                out.append((new, tot * scale + jnp.sum(p, axis=0, keepdims=True)))
            return tuple(out)

        first = tuple((jnp.full((1, SPAN), MASKED, F32), jnp.zeros((1, SPAN), F32)) for _ in range(3))
        final = lax.fori_loop(low, high, step, first)
        for h in range(3):
            top, tot = final[h]
            hrows = pl.ds(64 * (h + 1), 64)
            acc[hrows] = acc[hrows] * (1.0 / tot)
            lse_ref[stripe, pl.ds(h, 1)] = top + jnp.log(tot)
        ot_ref[stripe] = acc[...]
        o_ref[rows] = acc[...].T.astype(BF16)

def vmem():
    return pl.BlockSpec(memory_space=pltpu.VMEM)

def attend_forward(lens, q, kv, cols):
    total = kv.shape[0]
    return pl.pallas_call(
        functools.partial(forward_kernel, cols),
        out_shape=[jax.ShapeDtypeStruct(q.shape, BF16), jax.ShapeDtypeStruct((4, 256, SPAN), F32),
                   jax.ShapeDtypeStruct((4, 8, SPAN), F32)],
        in_specs=[pl.BlockSpec(memory_space=pltpu.SMEM), vmem(), vmem()],
        out_specs=[vmem()] * 3,
        scratch_shapes=[pltpu.VMEM((3, SPAN, 256), BF16), pltpu.VMEM((256, total), BF16), pltpu.VMEM((256, SPAN), F32)],
        compiler_params=pltpu.CompilerParams(vmem_limit_bytes=62 << 20),
        name="attend_forward",
    )(lens, q, kv)

def backward_kernel(cols, lens, q_ref, kv_ref, do_ref, ot_ref, lse_ref, dq_ref, dkv_ref, qm, dm, kt, dk, dv, acc):
    index = lax.axis_index("ctx")
    b, c = lax.rem(index // 2, cols), lax.rem(index, 2)
    ends = bounds(lens, c)
    total = kv_ref.shape[0]

    @pl.loop(0, total // KB)
    def _(n):
        rows = pl.ds(pl.multiple_of(n * KB, KB), KB)
        kt[:, rows] = kv_ref[rows, 0:256].astype(F32).T.astype(BF16)
        dk[rows] = jnp.zeros((KB, 256), F32)
        dv[rows] = jnp.zeros((KB, 256), F32)

    @pl.loop(0, 4)
    def _(stripe):
        base = SPAN * (stripe * cols + b)
        rows = pl.ds(pl.multiple_of(stripe * SPAN, SPAN), SPAN)
        head = lane_head((SPAN, 256), 0)
        headv = lane_head((SPAN, 256), 64)
        q = q_ref[rows].astype(F32) * 0.125
        grad = do_ref[rows].astype(F32)
        for h in range(3):
            qm[h] = jnp.where(head == h, q, 0.0).astype(BF16)
            dm[h] = jnp.where(headv == h, grad, 0.0).astype(BF16)
        prod = grad.T * ot_ref[stripe]
        deltas = [jnp.sum(prod[64 * (h + 1):64 * (h + 2)], axis=0, keepdims=True) for h in range(3)]
        lses = [lse_ref[stripe, pl.ds(h, 1)] for h in range(3)]
        qpos = base + lax.broadcasted_iota(jnp.int32, (1, SPAN), 1)
        start, stop = doc_range(qpos, ends)
        low, high = block_range(base, ends)
        acc[...] = jnp.zeros_like(acc)

        @pl.loop(low, high)
        def _(n):
            krows = pl.ds(pl.multiple_of(n * KB, KB), KB)
            keys = kv_ref[krows, 0:256]
            vals = kv_ref[krows, 128:384]
            kpos = n * KB + lax.broadcasted_iota(jnp.int32, (KB, 1), 0)
            allowed = (kpos >= start) & (kpos < stop)
            newk, newv = dk[krows], dv[krows]
            for h in range(3):
                s = jnp.where(allowed, dot(keys, qm[h], NT), MASKED)
                p = jnp.exp(s - lses[h])
                gp = dot(vals, dm[h], NT)
                ds = (p * (gp - deltas[h])).astype(BF16)
                newv = newv + dot(p.astype(BF16), dm[h], NN)
                newk = newk + dot(ds, qm[h], NN)
                hrows = pl.ds(64 * h, 64)
                acc[hrows] = acc[hrows] + dot(kt[hrows, krows], ds, NN)
            dk[krows] = newk
            dv[krows] = newv

        dq_ref[rows] = (acc[...] * 0.125).T.astype(BF16)

    @pl.loop(0, total // KB)
    def _(n):
        rows = pl.ds(pl.multiple_of(n * KB, KB), KB)
        dkv_ref[rows, 0:128] = dk[rows, 0:128].astype(BF16)
        dkv_ref[rows, 128:256] = (dk[rows, 128:256] + dv[rows, 0:128]).astype(BF16)
        dkv_ref[rows, 256:384] = dv[rows, 128:256].astype(BF16)

def attend_backward(lens, q, kv, do, ot, lse, cols):
    total = kv.shape[0]
    return pl.pallas_call(
        functools.partial(backward_kernel, cols),
        out_shape=[jax.ShapeDtypeStruct(q.shape, BF16), jax.ShapeDtypeStruct(kv.shape, BF16)],
        in_specs=[pl.BlockSpec(memory_space=pltpu.SMEM)] + [vmem()] * 5,
        out_specs=[vmem()] * 2,
        scratch_shapes=[pltpu.VMEM((3, SPAN, 256), BF16), pltpu.VMEM((3, SPAN, 256), BF16), pltpu.VMEM((256, total), BF16),
                        pltpu.VMEM((total, 256), F32), pltpu.VMEM((total, 256), F32), pltpu.VMEM((256, SPAN), F32)],
        compiler_params=pltpu.CompilerParams(vmem_limit_bytes=40 << 20),
        name="attend_backward",
    )(lens, q, kv, do, ot, lse)


STEPS = ((1, 0), (3, 0), (1, 1), (3, 1), (2, 0), (0, 1), (2, 1))


class Octet:
    def __init__(self, go):
        self.go = go
        self.a, self.b, self.c, self.f = a, b, c, f = place(2)
        self.me = a * 2 + c
        self.others = [lax.rem(a + da, 4) * 2 + lax.rem(c + dc, 2) for da, dc in STEPS]
        self.sources = [lax.rem(a + 4 - da, 4) * 2 + lax.rem(c + dc, 2) for da, dc in STEPS]
        self.devices = [device(lax.rem(a + da, 4), b, lax.rem(c + dc, 2), f, 2) for da, dc in STEPS]

    def send(self, n, source, target):
        return self.go(source, target(self.me), self.devices[n])


def project_kernel(tokens, *refs):
    shards, vectors = refs[:4], refs[4:13]
    q_held, kv_held, f_qkv, f_out, f_in, f_back, vec, turned = refs[13:21]
    own = refs[21:25]
    whole, acc, q_sent, kv_sent, v_own, token, held = refs[25:32]
    flat, (send, recv, here) = refs[32:41], refs[41:]
    fulls = (f_qkv, f_out, f_in, f_back)
    a, b, c, f = place(2)
    group = Octet(None)
    me = group.me
    odd_a = lax.rem(a, 2)
    xp, yp, sp = device(a, 1 - b, c, f, 2), device(a, b, c, 1 - f, 2), device(a, b, 1 - c, f, 2)
    pairs = [device(lax.rem(a + 5 - 2 * odd_a, 4), b, c, f, 2), device(lax.rem(a + 3 + 2 * odd_a, 4), b, c, f, 2)]
    loads = [pltpu.make_async_copy(shards[w], own[w], here.at[w]) for w in range(4)]
    flats = [pltpu.make_async_copy(ref, flat[n], here.at[12 + n]) for n, ref in enumerate(vectors)]
    flats.append(pltpu.make_async_copy(tokens, token, here.at[11]))
    for cp in flats + loads:
        cp.start()
    meet(group.devices + [xp, yp])
    wires = Wires(send, recv)
    go = group.go = wires.go

    def rows_of(w, which, chunk):
        size = shards[w].shape[0] // 4
        return pl.multiple_of(which * 2 * size + chunk * size, 16), size

    def cols_of(w, cc):
        half = shards[w].shape[1] // 2
        return pl.ds(pl.multiple_of(cc * half, 128), half)

    def region(target, w, owner, which, cc, chunk):
        start, size = rows_of(w, which, chunk)
        return target.at[pl.ds(owner * shards[w].shape[0] + start, size), cols_of(w, cc)]

    def source(w, which, chunk):
        start, size = rows_of(w, which, chunk)
        return shards[w].at[pl.ds(start, size), cols_of(w, c)]

    other_f = 1 - f

    class Fetch:
        def __init__(self, target, w, chunk, pair=None):
            self.target, self.w, self.chunk = target, w, chunk
            self.which = b if pair is None else odd_a
            self.peer = xp if pair is None else pairs[pair]
            self.first = go(source(w, self.which, chunk), region(target, w, f, self.which, c, chunk), yp)

        def second(self):
            self.first.wait_recv()
            got = region(self.target, self.w, other_f, self.which, c, self.chunk)
            self.cross = go(got, got, self.peer)
            self.side = go(got, got, sp)

        def third(self):
            self.cross.wait_recv()
            got = region(self.target, self.w, other_f, 1 - self.which, c, self.chunk)
            self.side2 = go(got, got, sp)

        def end(self):
            self.side.wait_recv()
            self.side2.wait_recv()

    class Straight:
        def __init__(self, target, w, chunk, which):
            self.place = (target, w, other_f, which, c, chunk)
            self.first = go(source(w, which, chunk), region(target, w, f, which, c, chunk), yp)

        def second(self):
            self.first.wait_recv()
            got = region(*self.place)
            self.side = go(got, got, sp)

        def third(self):
            pass

        def end(self):
            self.side.wait_recv()

    qkv = [Fetch(whole, 0, 0)]
    for cp in flats:
        cp.wait()

    def token_block(dc):
        return token.at[pl.ds(pl.multiple_of(lax.rem(c + dc, 2) * 128, 128), 128)]

    toks = [go(token_block(STEPS[n][1]), held.at[m], group.devices[n]) for m, n in enumerate((0, 1, 2, 3, 5))]
    held[5] = token[pl.ds(pl.multiple_of(c * 128, 128), 128)]
    for n in range(9):
        value = flat[n][...].astype(F32)
        if n == 3:
            for j in range(4):
                v_own[8 + j:9 + j] = value[384 * j:384 * j + 384].reshape(1, 384)
        else:
            row = n if n < 3 else n - 1
            v_own[row:row + 1] = value.reshape(1, 384)
    v_own[12:16] = jnp.zeros((4, 384), F32)
    vec[f] = v_own[...]
    small = go(v_own, vec.at[f], yp)
    loads[0].wait()
    mine = pl.ds(pl.multiple_of(f * 384, 128), 384)
    theirs = pl.ds(pl.multiple_of(other_f * 384, 128), 384)

    @pl.loop(0, 6)
    def _(n):
        cols = pl.ds(pl.multiple_of(n * 384, 128), 384)
        acc[:, cols] = dot(token[:, mine], own[0][:, cols], NN)

    qkv[0].second()
    qkv.append(Fetch(whole, 0, 1))
    qkv[1].second()
    outer = [Fetch(f_back, 3, chunk) for chunk in range(2)]
    rest = [Fetch(f_out, 1, chunk) for chunk in range(2)]
    inner = [Straight(f_in, 2, chunk, which) for chunk in range(2) for which in range(2)]
    qkv[0].third()
    qkv[1].third()
    stores = []
    for w in range(4):
        if w > 0:
            loads[w].wait()
        rows = shards[w].shape[0]
        cp = pltpu.make_async_copy(own[w], fulls[w].at[pl.ds(pl.multiple_of(f * rows, 16), rows)], here.at[4 + w])
        cp.start()
        stores.append(cp)
    small.wait_recv()
    qkv[0].end()
    qkv[1].end()
    cp = pltpu.make_async_copy(whole.at[pl.ds(pl.multiple_of(other_f * 384, 16), 384)],
                               f_qkv.at[pl.ds(pl.multiple_of(other_f * 384, 16), 384)], here.at[8])
    cp.start()
    stores.append(cp)

    def column(n):
        cols = slice(384 * n, 384 * n + 384)
        value = acc[:, cols] + dot(token[:, theirs], whole[pl.ds(pl.multiple_of(other_f * 384, 16), 384), cols], NN)
        if n < 2:
            value = value + vec[n, 0:1]
        if n >= 4:
            value = value + vec[n - 4, 1:2]
        return value

    lane = lax.broadcasted_iota(jnp.int32, (256, 384), 1)
    for p in range(2):
        k, v = column(2 + p), column(4 + p)
        turned_k, turned_v = pltpu.roll(k, 192, 1), pltpu.roll(v, 192, 1)
        even = jnp.where(lane < 192, k, turned_v).astype(BF16)
        odd = jnp.where(lane < 192, turned_k, v).astype(BF16)
        q = column(p)
        q_even = jnp.where(lane < 192, q, 0.0)[:, :256].astype(BF16)
        q_odd = jnp.where(lane < 192, pltpu.roll(q, 192, 1), 0.0)[:, :256].astype(BF16)
        for s in range(2):
            rows = slice(128 * s, 128 * s + 128)
            kv_sent[4 * p + s], kv_sent[4 * p + 2 + s] = even[rows], odd[rows]
            q_sent[4 * p + s], q_sent[4 * p + 2 + s] = q_even[rows], q_odd[rows]

    def slot(block, bb):
        return (block // 2 * 2 + bb) * 2 + lax.rem(block, 2)

    kv_slot = lambda block: kv_held.at[slot(block, b)]
    q_slot = lambda block: q_held.at[block]
    first = [group.send(n, kv_sent.at[group.others[n]], kv_slot) for n in (6, 0, 1, 2, 3, 4, 5)]
    first = first[1:] + first[:1]
    own_kv = pltpu.make_async_copy(kv_sent.at[me], kv_held.at[slot(me, b)], here.at[9])
    own_kv.start()
    own_q = pltpu.make_async_copy(q_sent.at[me], q_held.at[me], here.at[10])
    own_q.start()
    crossed = [go(kv_sent.at[me], kv_held.at[slot(me, b)], xp)]
    third = [group.send(n, q_sent.at[group.others[n]], q_slot) for n in (6, 0, 1, 2, 3, 4, 5)]
    third = third[1:] + third[:1]

    def onward(n):
        first[n].wait_recv()
        piece = kv_slot(group.sources[n])
        crossed.append(go(piece, piece, xp))

    onward(5)
    onward(0)
    onward(1)
    for cp in outer:
        cp.second()
    for cp in rest:
        cp.second()
    onward(2)
    onward(3)
    onward(4)
    onward(6)
    for cp in toks:
        cp.wait_recv()

    @pl.loop(0, 6)
    def _(n):
        @pl.loop(0, 6)
        def _(m):
            lanes = pl.ds(pl.multiple_of(m * 128, 128), 128)
            turned[n, lanes] = held[n, :, lanes].astype(F32).T.astype(BF16)

    for cp in inner:
        cp.second()
    for cp in outer:
        cp.third()
    for cp in rest:
        cp.third()
    for cp in crossed + third:
        cp.wait_recv()
    for cp in rest + inner + outer:
        cp.end()
    for cp in wires.made:
        cp.wait_send()
    for cp in stores + [own_kv, own_q]:
        cp.wait()


def project(tokens, shards, vectors, ident):
    rows, width = tokens.shape
    anywhere = pl.BlockSpec(memory_space=pl.ANY)
    wires = 80
    return pl.pallas_call(
        project_kernel,
        out_shape=[jax.ShapeDtypeStruct((8, 128, 256), BF16), jax.ShapeDtypeStruct((16, 128, 384), BF16)]
        + [jax.ShapeDtypeStruct((2 * s.shape[0], s.shape[1]), BF16) for s in shards]
        + [jax.ShapeDtypeStruct((2, 16, 384), F32), jax.ShapeDtypeStruct((6, 768, 128), BF16)],
        in_specs=[pl.BlockSpec(memory_space=pltpu.HBM)] * 14,
        out_specs=[vmem()] * 2 + [anywhere] * 4 + [vmem()] * 2,
        scratch_shapes=[pltpu.VMEM(s.shape, BF16) for s in shards]
        + [pltpu.VMEM((768, 2304), BF16), pltpu.VMEM((256, 2304), F32), pltpu.VMEM((8, 128, 256), BF16),
           pltpu.VMEM((8, 128, 384), BF16), pltpu.VMEM((16, 384), F32), pltpu.VMEM(tokens.shape, BF16),
           pltpu.VMEM((6, 128, 768), BF16),
           *[pltpu.VMEM(v.shape, BF16) for v in vectors], DMA((wires,)), DMA((wires,)), DMA((21,))],
        compiler_params=pltpu.CompilerParams(collective_id=ident, has_side_effects=True, vmem_limit_bytes=62 << 20),
        name="project",
    )(tokens, *shards, *vectors)


BLK = 48
Z1, X1, Y1 = (0, 768), (768, 1920), (1920, 3456)
LATE = (0, 640)


class Wires:
    def __init__(self, send, recv):
        self.send, self.recv, self.made = send, recv, []

    def go(self, source, target, peer):
        n = len(self.made)
        cp = remote(source, target, self.send.at[n], self.recv.at[n], peer)
        cp.start()
        self.made.append(cp)
        return cp


def transpose_into(target, source, base):
    width = source.shape[1]

    @pl.loop(0, width // 128)
    def _(n):
        at = pl.multiple_of(n * 128, 128)
        target[pl.ds(base + at, 128)] = source[:, pl.ds(at, 128)].astype(F32).T.astype(BF16)


def pair_columns(even, odd, lane, second):
    if second:
        return jnp.where(lane < 192, pltpu.roll(even, 192, 1), odd)
    return jnp.where(lane < 192, even, pltpu.roll(odd, 192, 1))


def halves(span):
    tiles = (span[1] - span[0]) // 128
    mid = span[0] + tiles // 2 * 128
    return (span[0], mid), (mid, span[1])


def within(span, group):
    base = 0
    for member in group:
        if member == span:
            return slice(base, base + span[1] - span[0])
        base += member[1] - member[0]


def gradient_kernel(lens, wqkv, gfirst, near, far, xt, gbr, ghid, gsec, small, do_sent, q_ref, kv_ref, ot_ref, lse_ref,
                    out, late_out, igrad, small_out,
                    joined, wqkv_held, mine, sib, cin, y8, y4, x8, x4, z4, z1r, zyb, zxb,
                    do_held, qm, dm, kt, dk, dv, acc, rowsc, delta, dq_all, dkv_all, dqo, dkvo, xsend, rbuf,
                    l_sib, l_in, l_acc, l_mine, ly, lx,
                    v_own, v_core, v_f, v_b, v_a, send, recv, here):
    weights = pltpu.make_async_copy(wqkv, wqkv_held, here.at[5])
    weights.start()
    group = Octet(None)
    a, b, c, f, me = group.a, group.b, group.c, group.f, group.me
    xp, yp, sp = device(a, 1 - b, c, f, 2), device(a, b, c, 1 - f, 2), device(a, b, 1 - c, f, 2)
    up, down = lax.rem(a + 1, 4), lax.rem(a + 3, 4)
    upp, downp = device(up, b, c, f, 2), device(down, b, c, f, 2)
    ends = bounds(lens, c)
    total = kv_ref.shape[0]
    meet(group.devices + [xp, yp])
    wires = Wires(send, recv)
    go = group.go = wires.go
    pending = []

    do_slot = lambda block: do_held.at[block]
    swaps = {n: group.send(n, do_sent.at[group.others[n]], do_slot) for n in (6, 0, 1, 2, 3, 4, 5)}
    do_held[me] = do_sent[me]


    def produce(kind, first, count, part, finish):
        @pl.loop(0, 2 * count)
        def _(n):
            ff, j = lax.rem(n, 2), first + n // 2
            if kind == "out":
                left, right = xt[pl.ds(pl.multiple_of(ff * 384, 128), 384)], gbr[:, pl.ds(pl.multiple_of(part * 384, 128), 384)]
                col = 768
            elif kind == "in":
                left = xt[pl.ds(pl.multiple_of(768 + ff * 384, 128), 384)]
                right = ghid[:, pl.ds(pl.multiple_of(part * 1536 + j * 384, 128), 384)]
                col = pl.multiple_of(j * 384 + (384 if first else 0), 128)
            else:
                left = xt[pl.ds(pl.multiple_of(1536 + ff * 1536 + j * 384, 128), 384)]
                right = gsec[:, pl.ds(pl.multiple_of(part * 384, 128), 384)]
                col = pl.multiple_of(1920 + j * 384, 128)
            finish(pl.ds(ff * 2, 2), pl.ds(col, 384), dot(left, right, NN).reshape(2, 4, BLK, 384))

    def keep(rows, cols, value):
        sib[rows, :, :, cols] = value.astype(BF16)

    def join(rows, cols, value):
        mine[rows, :, :, cols] = (value + cin[rows, :, :, cols].astype(F32)).astype(BF16)

    core = {}

    def share(span):
        cols = slice(span[0], span[1])
        core[span] = go(sib.at[:, :, :, cols], cin.at[:, :, :, cols], sp)

    RS = (Y1, X1)

    def add(target, source):
        def step(n):
            t, s = target(n), source(n)
            t[...] = (t[...].astype(F32) + s[...].astype(F32)).astype(BF16)
        return step

    def accumulate(target, source, count):
        pl.loop(0, count)(add(target, source))

    ycols, xcols, zcols = slice(*Y1), slice(*X1), slice(*Z1)

    def start_y():
        return go(mine.at[pl.ds((1 - f) * 2, 2), :, :, ycols], y8, yp)

    def start_x():
        return [go(mine.at[ff * 2 + 1 - b, :, :, xcols], x8.at[ff], xp) for ff in range(2)]

    def next_y(cp):
        cp.wait_recv()
        accumulate(lambda n: mine.at[f * 2 + n // 4, lax.rem(n, 4), :, ycols], lambda n: y8.at[n // 4, lax.rem(n, 4)], 8)
        return go(mine.at[f * 2 + 1 - b, :, :, ycols], x4, xp)

    def next_x(cps):
        for cp in cps:
            cp.wait_recv()
        accumulate(lambda n: mine.at[n // 4 * 2 + b, lax.rem(n, 4), :, xcols], lambda n: x8.at[n // 4, lax.rem(n, 4)], 8)
        return go(mine.at[(1 - f) * 2 + b, :, :, xcols], y4, yp)

    def last_y(cp):
        cp.wait_recv()
        accumulate(lambda n: mine.at[f * 2 + b, n, :, ycols], lambda n: x4.at[n], 4)

    def last_x(cp):
        cp.wait_recv()
        accumulate(lambda n: mine.at[f * 2 + b, n, :, xcols], lambda n: y4.at[n], 4)

    def landing(span, step, part, single):
        if single:
            base = within(span, RS).start - span[0]
            return z1r.at[step, :, base + part[0]:base + part[1]]
        return z4.at[step, :, :, part[0]:part[1]]

    def ring_source(aa, part, single):
        cols = slice(part[0], part[1])
        return mine.at[f * 2 + b, aa, :, cols] if single else mine.at[:, aa, :, cols]

    def ring_send(span, step, single):
        lo, hi = halves(span)
        ud, dd = lax.rem(a + 3 - step, 4), lax.rem(a + 1 + step, 4)
        return (go(ring_source(ud, lo, single), landing(span, step, lo, single), upp),
                go(ring_source(dd, hi, single), landing(span, step, hi, single), downp))

    def ring_add(span, step, single, cps):
        lo, hi = halves(span)
        ud, dd = lax.rem(a + 6 - step, 4), lax.rem(a + 2 + step, 4)
        for cp, part, aa in zip(cps, (lo, hi), (ud, dd)):
            cp.wait_recv()
            got = landing(span, step, part, single)
            if single:
                add(lambda n: ring_source(aa, part, True), lambda n: got)(0)
            else:
                cols = slice(part[0], part[1])
                accumulate(lambda n: mine.at[n, aa, :, cols], lambda n: got.at[n], 4)

    def tail_z_y():
        return go(mine.at[pl.ds((1 - f) * 2, 2), a, :, zcols], zyb, yp)

    def tail_z_x(cp):
        cp.wait_recv()
        accumulate(lambda n: mine.at[f * 2 + n, a, :, zcols], lambda n: zyb.at[n], 2)
        return go(mine.at[f * 2 + 1 - b, a, :, zcols], zxb, xp)

    def tail_z_end(cp):
        cp.wait_recv()
        add(lambda n: mine.at[f * 2 + b, a, :, zcols], lambda n: zxb)(0)

    class Gather:
        def __init__(self, own, spot, span, first):
            self.span, self.first, self.spot = span, first, spot
            self.own = own
            self.copy = pltpu.make_async_copy(own, spot(b, a, span), here.at[len(locals_)])
            self.copy.start()
            locals_.append(self.copy)
            pending.append(go(own, spot(b, a, span), sp))
            self.ring = go(own, spot(b, a, span), upp), go(own, spot(b, a, span), downp)
            self.cross = go(own, spot(b, a, span), xp)

        def spread(self, bb, aa):
            p = self.spot(bb, aa, self.span)
            pending.append(go(p, p, sp))

        def passed(self, bb, ring):
            lo, hi = halves(self.span)
            ring[0].wait_recv()
            p = self.spot(bb, down, lo)
            first = go(p, p, upp)
            ring[1].wait_recv()
            p = self.spot(bb, up, hi)
            second = go(p, p, downp)
            for aa in (down, up):
                self.spread(bb, aa)
            return first, second

        def arrived(self, bb, ring):
            for cp in ring:
                cp.wait_recv()
            self.spread(bb, lax.rem(a + 2, 4))

        def second(self):
            self.ring2 = self.passed(b, self.ring)
            if self.first == "b":
                self.cross.wait_recv()
                self.spread(1 - b, a)
                p = self.spot(1 - b, a, self.span)
                self.other = go(p, p, upp), go(p, p, downp)
            else:
                spots = [self.spot(b, aa, self.span) for aa in (down, up)]
                self.more = [go(p, p, xp) for p in spots]

        def third(self):
            self.arrived(b, self.ring2)
            if self.first == "b":
                self.other2 = self.passed(1 - b, self.other)
            else:
                p = self.spot(b, lax.rem(a + 2, 4), self.span)
                self.more.append(go(p, p, xp))
                self.cross.wait_recv()
                self.spread(1 - b, a)

        def fourth(self):
            if self.first == "b":
                self.arrived(1 - b, self.other2)
            else:
                for cp, aa in zip(self.more, (down, up, lax.rem(a + 2, 4))):
                    cp.wait_recv()
                    self.spread(1 - b, aa)

    locals_ = []

    def early_spot(bb, aa, span):
        return out.at[c, bb * 4 + aa, :, span[0]:span[1]]

    def late_spot(bb, aa, span):
        return late_out.at[aa, bb * 2 + c, :, span[0]:span[1]]

    def early_gather(span, first):
        return Gather(mine.at[f * 2 + b, a, :, span[0]:span[1]], early_spot, span, first)

    def prepare():
        @pl.loop(0, total // KB)
        def _(n):
            rows = pl.ds(pl.multiple_of(n * KB, KB), KB)
            kt[:, rows] = kv_ref[rows, 0:256].astype(F32).T.astype(BF16)

        @pl.loop(0, 4)
        def _(stripe):
            head = lane_head((SPAN, 256), 0)
            headv = lane_head((SPAN, 256), 64)
            q = q_ref[pl.ds(stripe * 2, 2)].reshape(SPAN, 256).astype(F32) * 0.125
            grad = do_held[pl.ds(stripe * 2, 2)].reshape(SPAN, 256).astype(F32)
            for h in range(3):
                qm[stripe, h] = jnp.where(head == h, q, 0.0).astype(BF16)
                dm[stripe, h] = jnp.where(headv == h, grad, 0.0).astype(BF16)
            prod = grad.T * ot_ref[stripe]
            for h in range(3):
                delta[stripe, h:h + 1] = jnp.sum(prod[64 * (h + 1):64 * (h + 2)], axis=0, keepdims=True)
            qpos = SPAN * (stripe * 2 + b) + lax.broadcasted_iota(jnp.int32, (1, SPAN), 1)
            start, stop = doc_range(qpos, ends)
            rowsc[stripe, 0:1] = start
            rowsc[stripe, 1:2] = stop
            acc[stripe] = jnp.zeros((256, SPAN), F32)

    reach = total * 5 // 8 // KB

    def attend(da, parity):
        block = lax.rem(a + da, 4) * 2 + parity
        krows = pl.ds(pl.multiple_of(block * KB, KB), KB)
        dk[...] = jnp.zeros((KB, 256), F32)
        dv[...] = jnp.zeros((KB, 256), F32)
        @pl.loop(0, 4)
        def _(stripe):
            away = stripe * 2 + b - block

            @pl.when((away <= reach) & (away >= -reach))
            def _():
                keys = kv_ref[krows, 0:256]
                vals = kv_ref[krows, 128:384]
                kpos = block * KB + lax.broadcasted_iota(jnp.int32, (KB, 1), 0)
                allowed = (kpos >= rowsc[stripe, 0:1]) & (kpos < rowsc[stripe, 1:2])
                newk, newv = dk[...], dv[...]
                for h in range(3):
                    s = jnp.where(allowed, dot(keys, qm[stripe, h], NT), MASKED)
                    p = jnp.exp(s - lse_ref[stripe, h:h + 1])
                    gp = dot(vals, dm[stripe, h], NT)
                    ds = (p * (gp - delta[stripe, h:h + 1])).astype(BF16)
                    newv = newv + dot(p.astype(BF16), dm[stripe, h], NN)
                    newk = newk + dot(ds, qm[stripe, h], NN)
                    hrows = pl.ds(64 * h, 64)
                    acc[stripe, hrows] = acc[stripe, hrows] + dot(kt[hrows, krows], ds, NN)
                dk[...] = newk
                dv[...] = newv

    def slot(block, bb):
        return (block // 2 * 2 + bb) * 2 + lax.rem(block, 2)

    def grads_of(dc):
        rows = pl.ds(pl.multiple_of(lax.rem(c + dc, 2) * 128, 128), 128)
        k, v = dk[rows], dv[rows]
        return jnp.concatenate([k[:, :128], k[:, 128:] + v[:, :128], v[:, 128:]], axis=1)

    FAR, NEXT = ((6, 1), (4, 0)), ((0, 0), (2, 1))
    BACK, HERE = ((1, 0), (3, 1)), ((5, 1), (7, 0))
    crossed = {}

    def cross(members):
        for n, dc in members:
            xsend[n] = grads_of(dc).astype(BF16)
            crossed[n] = go(xsend.at[n], rbuf.at[n], xp)

    dkv_slot = lambda block: dkvo.at[block]
    dkvs = {}

    def settle(members):
        for n, dc in members:
            crossed[n].wait_recv()
            value = (grads_of(dc) + rbuf[n].astype(F32)).astype(BF16)
            if n == 7:
                dkv_all[me] = value
                dkvo[me] = value
            else:
                dkv_all[group.others[n]] = value
                dkvs[n] = group.send(n, dkv_all.at[group.others[n]], dkv_slot)

    dq_slot = lambda block: dqo.at[block]
    dqs = {}

    produce("out", 0, 1, 1 - c, keep)
    produce("in", 2, 2, 1 - c, keep)
    share(X1)
    produce("back", 0, 4, 1 - c, keep)
    share(Y1)
    core[X1].wait_recv()
    produce("out", 0, 1, c, join)
    produce("in", 2, 2, c, join)
    x1 = start_x()
    core[Y1].wait_recv()
    produce("back", 0, 4, c, join)
    y1 = start_y()
    produce("in", 0, 2, 1 - c, keep)
    share(Z1)
    for cp in swaps.values():
        cp.wait_recv()
    prepare()
    core[Z1].wait_recv()
    produce("in", 0, 2, c, join)
    z1 = ring_send(Z1, 0, False)
    attend(2, 1 - b)
    cross(FAR)
    attend(1, 1 - b)
    cross(NEXT)
    ring_add(Z1, 0, False, z1)
    z1 = ring_send(Z1, 1, False)
    attend(3, 1 - b)
    cross(BACK)
    attend(0, 1 - b)
    cross(HERE)
    x1 = next_x(x1)
    ring_add(Z1, 1, False, z1)
    z1 = ring_send(Z1, 2, False)
    attend(2, b)
    settle(FAR)
    y1 = next_y(y1)
    attend(1, b)
    settle(NEXT)
    ring_add(Z1, 2, False, z1)
    z1 = tail_z_y()
    attend(3, b)
    settle(BACK)
    last_x(x1)
    x1 = ring_send(X1, 0, True)
    attend(0, b)

    @pl.loop(0, 4)
    def _(stripe):
        dq_all[pl.ds(stripe * 2, 2)] = (acc[stripe] * 0.125).T.astype(BF16).reshape(2, 128, 256)

    def send_dq(*which):
        for n in which:
            dqs[n] = group.send(n, dq_all.at[group.others[n]], dq_slot)

    dqo[me] = dq_all[me]
    settle(HERE)
    z1 = tail_z_x(z1)
    ring_add(X1, 0, True, x1)
    x1 = ring_send(X1, 1, True)

    def project_back(n, right):
        rows = pl.ds(pl.multiple_of(n * 96, 32), 96)
        value = dot(near[5, rows], right[me], NN)
        for m, k in enumerate((0, 1, 2, 3, 5)):
            value = value + dot(near[m, rows], right[group.sources[k]], NN)
        for m, k in ((0, 4), (1, 6)):
            value = value + dot(far[m, rows], right[group.sources[k]], NN)
        return value

    @pl.loop(0, 4)
    def _(n):
        theirs, ours = n * 2 + 1 - c, n * 2 + c
        l_sib[n, :, 0:256] = project_back(theirs, dq_all).astype(BF16)
        l_sib[n, :, 256:640] = project_back(theirs, dkv_all).astype(BF16)
        l_acc[n, :, 0:256] = project_back(ours, dq_all)
        l_acc[n, :, 256:640] = project_back(ours, dkv_all)

    late = go(l_sib, l_in, sp)
    send_dq(6, 4)
    last_y(y1)
    y1 = ring_send(Y1, 0, True)
    ring_add(X1, 1, True, x1)
    x1 = ring_send(X1, 2, True)
    send_dq(0, 2)
    late.wait_recv()

    @pl.loop(0, 4)
    def _(n):
        l_mine[n] = (l_acc[n] + l_in[n].astype(F32)).astype(BF16)

    late = go(l_mine.at[pl.ds((1 - f) * 2, 2)], ly, yp)
    tail_z_end(z1)
    g_z1 = early_gather(Z1, "a")
    ring_add(Y1, 0, True, y1)
    y1 = ring_send(Y1, 1, True)
    send_dq(1, 3)
    late.wait_recv()
    accumulate(lambda n: l_mine.at[f * 2 + n], lambda n: ly.at[n], 2)
    late = go(l_mine.at[f * 2 + 1 - b], lx, xp)
    ring_add(X1, 2, True, x1)
    g_x1 = early_gather(X1, "a")
    send_dq(5)
    ring_add(Y1, 1, True, y1)
    y1 = ring_send(Y1, 2, True)
    late.wait_recv()
    add(lambda n: l_mine.at[f * 2 + b], lambda n: lx)(0)
    g_l = Gather(l_mine.at[f * 2 + b], late_spot, LATE, "a")
    g_z1.second()
    g_x1.second()
    ring_add(Y1, 2, True, y1)
    g_y1 = early_gather(Y1, "a")

    for cp in list(dqs.values()) + list(dkvs.values()):
        cp.wait_recv()
    lane = lax.broadcasted_iota(jnp.int32, (128, 384), 1)
    for s in range(2):
        rows = slice(s * 128, s * 128 + 128)
        for p in range(2):
            even, odd = 4 * p + s, 4 * p + 2 + s
            blank = jnp.zeros((128, 128), F32)
            qe = jnp.concatenate([dqo[even].astype(F32), blank], axis=1)
            qo = jnp.concatenate([dqo[odd].astype(F32), blank], axis=1)
            joined[rows, 384 * p:384 * p + 384] = pair_columns(qe, qo, lane, False).astype(BF16)
            ke, ko = dkvo[even].astype(F32), dkvo[odd].astype(F32)
            joined[rows, 768 + 384 * p:1152 + 384 * p] = pair_columns(ke, ko, lane, False).astype(BF16)
            joined[rows, 1536 + 384 * p:1920 + 384 * p] = pair_columns(ke, ko, lane, True).astype(BF16)
    v_own[...] = small[...]
    v_own[0:1] = jnp.sum(joined[:, 0:768].astype(F32), axis=0, keepdims=True)
    v_own[1:2] = jnp.sum(joined[:, 1536:2304].astype(F32), axis=0, keepdims=True)
    vec = go(v_own, v_core, sp)

    g_l.second()
    vec.wait_recv()
    v_core[...] = v_own[...] + v_core[...]
    vec = go(v_core.at[:, pl.ds(pl.multiple_of((1 - f) * 384, 128), 384)], v_f, yp)
    g_z1.third()
    g_x1.third()
    vec.wait_recv()
    v_b[b] = v_core[:, pl.ds(pl.multiple_of(f * 384, 128), 384)] + v_f[...]
    vec = go(v_b.at[b], v_b.at[b], xp)
    weights.wait()

    @pl.loop(0, 3)
    def _(n):
        rows = pl.ds(pl.multiple_of(n * 256, 256), 256)
        igrad[:, rows] = gfirst[:, rows] + dot(joined[...], wqkv_held[rows], NT)

    g_y1.second()
    g_l.third()
    g_z1.fourth()
    g_x1.fourth()
    vec.wait_recv()
    v_a[a] = v_b[0] + v_b[1]
    vec = [go(v_a.at[a], v_a.at[a], device(lax.rem(a + k, 4), b, c, f, 2)) for k in range(1, 4)]
    g_y1.third()
    g_l.fourth()
    g_y1.fourth()
    for cp in vec + pending:
        cp.wait_recv()
    small_out[...] = v_a[0] + v_a[1] + v_a[2] + v_a[3]
    for cp in locals_:
        cp.wait()
    for cp in wires.made:
        cp.wait_send()


def reduce_all(lens, wqkv, gfirst, near, far, xt, gbr, ghid, gsec, small, do_sent, q, kv, ot, lse, ident):
    wires = 192
    total = kv.shape[0]
    bf = lambda *shape: pltpu.VMEM(shape, BF16)
    fl = lambda *shape: pltpu.VMEM(shape, F32)
    anywhere = pl.BlockSpec(memory_space=pl.ANY)
    return pl.pallas_call(
        gradient_kernel,
        out_shape=[jax.ShapeDtypeStruct((2, 8, BLK, 3456), BF16), jax.ShapeDtypeStruct((4, 4, 96, 640), BF16),
                   jax.ShapeDtypeStruct((256, 768), F32), jax.ShapeDtypeStruct((16, 384), F32)],
        in_specs=[pl.BlockSpec(memory_space=pltpu.SMEM), anywhere] + [vmem()] * 13, out_specs=[anywhere] * 2 + [vmem()] * 2,
        scratch_shapes=[
            bf(256, 2304), bf(768, 2304), bf(4, 4, BLK, 3456), bf(4, 4, BLK, 3456), bf(4, 4, BLK, 3456),
            bf(2, 4, BLK, 1536), bf(4, BLK, 1152), bf(2, 4, BLK, 1152), bf(4, BLK, 1536),
            bf(3, 4, BLK, 768), bf(3, BLK, 2688), bf(2, BLK, 768), bf(BLK, 768),
            bf(8, 128, 256), bf(4, 3, SPAN, 256), bf(4, 3, SPAN, 256), bf(256, total), fl(KB, 256), fl(KB, 256), fl(4, 256, SPAN),
            pltpu.VMEM((4, 8, SPAN), jnp.int32), fl(4, 8, SPAN),
            bf(8, 128, 256), bf(8, 128, 384), bf(8, 128, 256), bf(8, 128, 384), bf(8, 128, 384), bf(8, 128, 384),
            bf(4, 96, 640), bf(4, 96, 640), fl(4, 96, 640), bf(4, 96, 640), bf(2, 96, 640), bf(96, 640),
            fl(16, 768), fl(16, 768), fl(16, 384), fl(2, 16, 384), fl(4, 16, 384),
            DMA((wires,)), DMA((wires,)), DMA((6,))],
        compiler_params=pltpu.CompilerParams(collective_id=ident, has_side_effects=True, vmem_limit_bytes=62 << 20),
        name="reduce_all",
    )(lens, wqkv, gfirst, near, far, xt, gbr, ghid, gsec, small, do_sent, q, kv, ot, lse)


def widen_kernel(grads, late, low, igrad, sums, g_qkv, g_out, g_in, g_back, low_out, igrad_out, *vectors):
    for core in range(2):
        part = grads.at[core]
        g_out[:, core * 384:core * 384 + 384] = part[:, 768:1152].astype(F32)
        g_in[:, core * 1536:core * 1536 + 768] = part[:, 0:768].astype(F32)
        g_in[:, core * 1536 + 768:core * 1536 + 1536] = part[:, 1152:1920].astype(F32)
        for j in range(4):
            g_back[j, :, core * 384:core * 384 + 384] = part[:, 1920 + 384 * j:2304 + 384 * j].astype(F32)
    lane = lax.broadcasted_iota(jnp.int32, (96, 384), 1)
    for p in range(2):
        even, odd = late[2 * p, 0].astype(F32), late[2 * p + 1, 0].astype(F32)
        g_qkv[:, 384 * p:384 * p + 384] = pair_columns(even[:, :384], odd[:, :384], lane, False)
        ke, ko = even[:, 256:], odd[:, 256:]
        g_qkv[:, 768 + 384 * p:1152 + 384 * p] = pair_columns(ke, ko, lane, False)
        g_qkv[:, 1536 + 384 * p:1920 + 384 * p] = pair_columns(ke, ko, lane, True)
    low_out[...] = low[...]
    igrad_out[...] = igrad[...]

    @pl.when(pl.program_id(0) == 0)
    def _():
        for n, ref in enumerate(vectors):
            if n == 3:
                for j in range(4):
                    ref[384 * j:384 * j + 384] = sums[8 + j:9 + j].reshape(384)
            else:
                row = n if n < 3 else n - 1
                ref[...] = sums[row:row + 1].reshape(384)


def widen(grads, late, low, igrad, sums):
    rows, step = 384, 96
    spec = lambda tall, wide: pl.BlockSpec((tall, wide), lambda n: (n, 0))
    flat = lambda size: pl.BlockSpec((size,), lambda n: (0,))
    sizes = [384] * 3 + [1536] + [384] * 5
    return pl.pallas_call(
        widen_kernel,
        grid=(rows // step,),
        out_shape=[jax.ShapeDtypeStruct((rows, 2304), F32), jax.ShapeDtypeStruct((rows, 768), F32),
                   jax.ShapeDtypeStruct((rows, 3072), F32), jax.ShapeDtypeStruct((4, rows, 768), F32),
                   jax.ShapeDtypeStruct(low.shape, BF16), jax.ShapeDtypeStruct(igrad.shape, F32)]
        + [jax.ShapeDtypeStruct((size,), F32) for size in sizes],
        in_specs=[pl.BlockSpec((2, step, 3456), lambda n: (0, n, 0)), pl.BlockSpec((4, 1, step, 640), lambda n: (0, n, 0, 0)),
                  spec(64, 768), spec(64, 768), pl.BlockSpec((16, 384), lambda n: (0, 0))],
        out_specs=[spec(step, 2304), spec(step, 768), spec(step, 3072), pl.BlockSpec((4, step, 768), lambda n: (0, n, 0)),
                   spec(64, 768), spec(64, 768)] + [flat(size) for size in sizes],
        compiler_params=pltpu.CompilerParams(vmem_limit_bytes=62 << 20),
        name="widen",
    )(grads, late, low, igrad, sums)


def middle_kernel(o_sent, tokens, cotangent, w_out, w_in, w_back, vec,
                  output, gfirst, xt, gbr, ghid, gsec, do_sent, small, far,
                  o_held, f_held, v_out, v_in, v_back, normed, xhat1, final, slope, act, send, recv, here):
    group = Octet(None)
    a, b, c, f, me = group.a, group.b, group.c, group.f, group.me
    loads = [pltpu.make_async_copy(s, t, here.at[n]) for n, (s, t) in enumerate(((w_out, v_out), (w_in, v_in), (w_back, v_back)))]
    for cp in loads:
        cp.start()
    meet(group.devices)
    wires = Wires(send, recv)
    go = group.go = wires.go
    o_slot = lambda block: o_held.at[block]
    swaps = {n: group.send(n, o_sent.at[group.others[n]], o_slot) for n in (6, 0, 1, 2, 3, 4, 5)}
    o_held[me] = o_sent[me]

    def token_block(dc):
        return tokens.at[pl.ds(pl.multiple_of(lax.rem(c + dc, 2) * 128, 128), 128)]

    beyond = [go(token_block(dc), f_held.at[dc], group.devices[n]) for dc, n in ((0, 4), (1, 6))]

    def row(n):
        return jnp.concatenate([vec[0, n:n + 1], vec[1, n:n + 1]], axis=1)

    def sums(n, value):
        small[n:n + 1] = jnp.sum(value, axis=0, keepdims=True)

    for cp in swaps.values():
        cp.wait_recv()
    lane = lax.broadcasted_iota(jnp.int32, (128, 384), 1)
    blank = jnp.zeros((128, 128), F32)
    att = act
    for s in range(2):
        rows = slice(s * 128, s * 128 + 128)
        for p in range(2):
            sides = [jnp.concatenate([pltpu.roll(o_held[4 * p + 2 * k + s].astype(F32), 192, 1), blank], axis=1) for k in range(2)]
            att[rows, 384 * p:384 * p + 384] = pair_columns(sides[0], sides[1], lane, False).astype(BF16)
    transpose_into(xt, att.at[:, 0:768], 0)

    def norm(value):
        mean = jnp.sum(value, axis=1, keepdims=True) * (1.0 / 768)
        centered = value - mean
        variance = jnp.sum(centered * centered, axis=1, keepdims=True) * (1.0 / 768)
        inverse = lax.rsqrt(variance + EPSILON)
        return centered * inverse, inverse

    def norm_back(upstream, gain, hat, inverse):
        scaled = upstream * gain
        first = jnp.sum(scaled, axis=1, keepdims=True) * (1.0 / 768)
        second = jnp.sum(scaled * hat, axis=1, keepdims=True) * (1.0 / 768)
        return inverse * (scaled - first - hat * second)

    loads[0].wait()
    hat, inverse1 = norm(tokens[...].astype(F32) + (dot(att[:, 0:768], v_out[...], NN) + row(2)))
    xhat1[...] = hat
    value = hat * row(4) + row(5)
    normed[...] = value
    output[...] = value.astype(BF16)
    transpose_into(xt, output, 768)
    loads[1].wait()

    @pl.loop(0, 4)
    def _(n):
        cols = pl.ds(pl.multiple_of(n * 768, 128), 768)
        ff, j = n // 2, lax.rem(n, 2) * 2
        bias = jnp.concatenate([vec[ff, pl.ds(8 + j, 1)], vec[ff, pl.ds(9 + j, 1)]], axis=1)
        hidden = dot(output[...], v_in[:, cols], NN) + bias
        half = 0.5 * (1.0 + lax.erf(hidden * 0.7071067811865476))
        slope[:, cols] = half + hidden * (jnp.exp(-0.5 * hidden * hidden) * 0.3989422804014327)
        act[:, cols] = (hidden * half).astype(BF16)

    transpose_into(xt, act, 1536)
    loads[2].wait()
    final[...] = normed[...] + (dot(act[...], v_back[...], NN) + row(3))
    hat2, inverse2 = norm(final[...])
    output[...] = (hat2 * row(6) + row(7)).astype(BF16)
    upstream = cotangent[...].astype(F32)
    sums(6, upstream * hat2)
    sums(7, upstream)
    gfinal = norm_back(upstream, row(6), hat2, inverse2)
    final[...] = gfinal
    gsec[...] = gfinal.astype(BF16)
    sums(3, gsec[...].astype(F32))

    @pl.loop(0, 4)
    def _(n):
        cols = pl.ds(pl.multiple_of(n * 768, 128), 768)
        ff, j = n // 2, lax.rem(n, 2) * 2
        value = (dot(gsec[...], v_back[cols], NT) * slope[:, cols]).astype(BF16)
        ghid[:, cols] = value
        total = jnp.sum(value.astype(F32), axis=0, keepdims=True)
        lanes = pl.ds(pl.multiple_of(ff * 384, 128), 384)
        small[pl.ds(8 + j, 1), lanes] = total[:, :384]
        small[pl.ds(9 + j, 1), lanes] = total[:, 384:]

    small[0:2] = jnp.zeros((2, 768), F32)
    small[12:16] = jnp.zeros((4, 768), F32)

    @pl.loop(0, 3)
    def _(n):
        cols = pl.ds(pl.multiple_of(n * 256, 128), 256)
        final[:, cols] = final[:, cols] + dot(ghid[...], v_in[cols], NT)

    hat = xhat1[...]
    upstream = final[...]
    sums(4, upstream * hat)
    sums(5, upstream)
    value = norm_back(upstream, row(4), hat, inverse1)
    gfirst[...] = value
    gbr[...] = value.astype(BF16)
    sums(2, gbr[...].astype(F32))
    normed[...] = dot(gbr[...], v_out[...], NT)
    wide = lax.broadcasted_iota(jnp.int32, (256, 256), 1)
    for p in range(2):
        part = normed[:, 384 * p:384 * p + 384]
        for k in range(2):
            turned = part if k == 0 else pltpu.roll(part, 192, 1)
            block = pltpu.roll(jnp.where(wide < 192, turned[:, :256], 0.0), 64, 1).astype(BF16)
            for s in range(2):
                do_sent[4 * p + 2 * k + s] = block[128 * s:128 * s + 128]
    for cp in beyond:
        cp.wait_recv()
    for n in range(2):
        @pl.loop(0, 6)
        def _(m):
            lanes = pl.ds(pl.multiple_of(m * 128, 128), 128)
            far[n, lanes] = f_held[n, :, lanes].astype(F32).T.astype(BF16)
    for cp in wires.made:
        cp.wait_send()


def middle(o_sent, tokens, cotangent, w_out, w_in, w_back, vec, ident):
    bf = lambda *shape: pltpu.VMEM(shape, BF16)
    fl = lambda *shape: pltpu.VMEM(shape, F32)
    out = lambda d, *shape: jax.ShapeDtypeStruct(shape, d)
    anywhere = pl.BlockSpec(memory_space=pl.ANY)
    wires = 16
    return pl.pallas_call(
        middle_kernel,
        out_shape=[out(BF16, 256, 768), out(F32, 256, 768), out(BF16, 4608, 256), out(BF16, 256, 768), out(BF16, 256, 3072),
                   out(BF16, 256, 768), out(BF16, 8, 128, 256), out(F32, 16, 768), out(BF16, 2, 768, 128)],
        in_specs=[vmem()] * 3 + [anywhere] * 3 + [vmem()], out_specs=[vmem()] * 9,
        scratch_shapes=[bf(8, 128, 256), bf(2, 128, 768), bf(768, 768), bf(768, 3072), bf(3072, 768),
                        fl(256, 768), fl(256, 768), fl(256, 768), fl(256, 3072), bf(256, 3072),
                        DMA((wires,)), DMA((wires,)), DMA((3,))],
        compiler_params=pltpu.CompilerParams(collective_id=ident, has_side_effects=True, vmem_limit_bytes=60 << 20),
        name="middle",
    )(o_sent, tokens, cotangent, w_out, w_in, w_back, vec)


def layer_norm(values, gain_row, shift_row):
    average = jnp.mean(values, axis=-1, keepdims=True)
    centered = values - average
    variance = jnp.mean(centered * centered, axis=-1, keepdims=True)
    return centered * lax.rsqrt(variance + EPSILON) * gain_row + shift_row


def exact_gelu(values):
    return jax.nn.gelu(values, approximate=False)


def by_group(rows, micro, front, back):
    parts = rows.reshape(micro, -1, 4, 192).transpose(2, 0, 1, 3)
    parts = jnp.pad(parts, ((0, 0), (0, 0), (0, 0), (front, back)))
    return parts.reshape((-1,) + parts.shape[2:])


def from_group(blocks, micro, front):
    rows = blocks.shape[1]
    parts = blocks.reshape(4, micro, rows, -1)[..., front:front + 192]
    return parts.transpose(1, 2, 0, 3).reshape(micro * rows, 768)


def shards(tokens, cotangent, doc_lengths, w_qkv, w_out, w_in, w_back, *vectors):
    micro, per, width = tokens.shape
    nf, cols = lax.axis_size("fsdp"), lax.axis_size("ctx") // 8
    share = width // nf
    inputs = tokens.reshape(micro * per, width)
    cube = nf == 2 and cols == 2
    if cube:
        q_held, kv_held, full_qkv, full_out, full_in, full_back, sides, near = project(inputs, (w_qkv, w_out, w_in, w_back), vectors, 1)
        kv_held = kv_held.reshape(-1, 384)
        mixed, mixed_t, log_total = attend_forward(doc_lengths, q_held.reshape(8 * per, 256), kv_held, cols)
        output, grad_first, xt, grad_branch, grad_hidden, grad_second, do_sent, small, far = middle(
            mixed.reshape(8, per, 256), inputs, cotangent.reshape(inputs.shape), full_out, full_in, full_back, sides, 3)
        grads, late, input_grad, sums = reduce_all(
            doc_lengths, full_qkv, grad_first, near, far, xt, grad_branch, grad_hidden, grad_second, small, do_sent, q_held, kv_held,
            mixed_t, log_total, 5)
        g_qkv, g_out, g_in, g_back, output, input_grad, *rows = widen(grads.reshape(2, share, 3456), late, output, input_grad, sums)
        return (output.reshape(tokens.shape), input_grad.reshape(tokens.shape), g_qkv, g_out, g_in, g_back.reshape(4 * share, width)) + tuple(rows)
    tiny = jnp.concatenate(vectors).reshape(8, -1)
    full_qkv, full_out, full_in, full_back, tinies = gather_weights((w_qkv, w_out, w_in, w_back), tiny, nf, cols)
    tinies = tinies.reshape(nf, -1).astype(F32)
    named, at = [], 0
    for vector in vectors:
        size = vector.shape[0]
        named.append(tinies[:, at:at + size].reshape(-1))
        at += size
    b_query, b_value, b_out, b_in, b_back, gain_one, shift_one, gain_two, shift_two = named
    joined = jnp.dot(inputs, full_qkv, preferred_element_type=F32)
    bias = jnp.concatenate([b_query, jnp.zeros_like(b_query), b_value])
    joined = (joined + bias).astype(BF16)
    q_sent = by_group(joined[:, :width], micro, 0, 64)
    kv_sent = jnp.concatenate([by_group(joined[:, width:2 * width], micro, 0, 0), by_group(joined[:, 2 * width:], micro, 0, 0)], axis=2)
    q_held, kv_held = spread(q_sent, kv_sent, cols, 2)
    q_held = q_held.reshape(8 * per, 256)
    kv_held = kv_held.reshape(-1, 384)
    mixed, mixed_t, log_total = attend_forward(doc_lengths, q_held, kv_held, cols)
    (back,) = swap([mixed.reshape(8, per, 256)], cols, 3)
    attended = from_group(back, micro, 64)
    first_sum = inputs.astype(F32) + (jnp.dot(attended, full_out, preferred_element_type=F32) + b_out)
    normed = layer_norm(first_sum, gain_one, shift_one)
    normed_low = normed.astype(BF16)
    hidden = jnp.dot(normed_low, full_in, preferred_element_type=F32) + b_in
    activated = exact_gelu(hidden).astype(BF16)
    final_sum = normed + (jnp.dot(activated, full_back, preferred_element_type=F32) + b_back)
    output = layer_norm(final_sum, gain_two, shift_two).astype(BF16)

    upstream = cotangent.reshape(micro * per, width).astype(F32)
    grad_final, g_gain_two, g_shift_two = jax.vjp(layer_norm, final_sum, gain_two, shift_two)[1](upstream)
    grad_second = grad_final.astype(BF16)
    g_back_bias = jnp.sum(grad_second.astype(F32), axis=0)
    grad_activated = jnp.einsum("rm,km->rk", grad_second, full_back, preferred_element_type=F32)
    grad_hidden = jax.vjp(exact_gelu, hidden)[1](grad_activated)[0].astype(BF16)
    g_in_bias = jnp.sum(grad_hidden.astype(F32), axis=0)
    grad_normed = grad_final + jnp.einsum("rf,mf->rm", grad_hidden, full_in, preferred_element_type=F32)
    grad_first, g_gain_one, g_shift_one = jax.vjp(layer_norm, first_sum, gain_one, shift_one)[1](grad_normed)
    grad_branch = grad_first.astype(BF16)
    g_out_bias = jnp.sum(grad_branch.astype(F32), axis=0)
    grad_attended = jnp.einsum("rm,km->rk", grad_branch, full_out, preferred_element_type=F32).astype(BF16)
    (do_held,) = swap([by_group(grad_attended, micro, 64, 0)], cols, 4)
    dq, dkv = attend_backward(doc_lengths, q_held, kv_held, do_held.reshape(8 * per, 256), mixed_t, log_total, cols)
    dq_own, dkv_own = collect(dq.reshape(8, per, 256), dkv.reshape(8 * cols, per, 384), cols, 5)
    grad_joined = jnp.concatenate(
        [from_group(dq_own, micro, 0), from_group(dkv_own, micro, 0), from_group(dkv_own, micro, 192)], axis=1)
    g_query_bias = jnp.sum(grad_joined[:, :width].astype(F32), axis=0)
    g_value_bias = jnp.sum(grad_joined[:, 2 * width:].astype(F32), axis=0)
    input_grad = grad_first + jnp.einsum("rc,mc->rm", grad_joined, full_qkv, preferred_element_type=F32)

    def halves(left, right):
        blocks = right.shape[1] // 384
        return jnp.einsum("rm,rhc->hmc", left, right.reshape(-1, blocks, 384), preferred_element_type=F32).astype(BF16)

    back_grads = jnp.einsum("rk,rm->km", activated, grad_second, preferred_element_type=F32).astype(BF16)
    back_grads = back_grads.reshape(nf, 4, share, 2, 384).transpose(1, 3, 0, 2, 4).reshape(8, width, 384)
    grads = jnp.concatenate(
        [halves(inputs, grad_joined), halves(attended, grad_branch), halves(normed_low, grad_hidden), back_grads])
    grads = grads.reshape(2, 4, 3, nf, cols, share // cols, 384)
    small = (g_query_bias, g_value_bias, g_out_bias, g_in_bias, g_back_bias, g_gain_one, g_shift_one, g_gain_two, g_shift_two)
    small = jnp.concatenate([x.reshape(nf, -1) for x in small], axis=1).reshape(nf, 8, -1)
    owned, small_owned = reduce_grads(grads, small, nf, cols, 6)
    owned = owned.transpose(0, 1, 3, 2, 4, 5).reshape(24, share, 384)

    def columns(first, last):
        return owned[first:last].transpose(1, 0, 2).reshape(share, -1).astype(F32)

    g_back = owned[16:].reshape(4, 2, share, 384).transpose(0, 2, 1, 3).reshape(4 * share, width).astype(F32)
    small_owned = small_owned.reshape(-1)
    small_grads, at = [], 0
    for vector in vectors:
        small_grads.append(small_owned[at:at + vector.shape[0]])
        at += vector.shape[0]
    return (output.reshape(tokens.shape), input_grad.reshape(tokens.shape), columns(0, 6), columns(6, 8), columns(8, 16), g_back) + tuple(small_grads)


def solution(mesh):
    rows, flat = P("fsdp", "ctx", None), P("fsdp", None)
    return jax.shard_map(
        shards,
        mesh=mesh,
        in_specs=(rows, rows, flat) + (flat,) * 4 + (P("fsdp"),) * 9,
        out_specs=(rows, rows) + (flat,) * 4 + (P("fsdp"),) * 9,
        check_vma=False,
    )
```

```python
import functools

import jax
import jax.numpy as jnp
from jax import lax
from jax.experimental import pallas as pl
from jax.experimental.pallas import tpu as pltpu
from jax.sharding import PartitionSpec as P

MESH = pl.DeviceIdType.MESH
DMA = pltpu.SemaphoreType.DMA
F32, BF16 = jnp.float32, jnp.bfloat16
EPSILON = 1e-12

def place(cols):
    index = lax.axis_index("ctx")
    return index // (2 * cols), lax.rem(index // 2, cols), lax.rem(index, 2), lax.axis_index("fsdp")

def device(a, b, c, f, cols):
    return {"ctx": (a * cols + b) * 2 + c, "fsdp": f}

def meet(peers):
    barrier = pltpu.get_barrier_semaphore()
    for peer in peers:
        pl.semaphore_signal(barrier, inc=1, device_id=peer, device_id_type=MESH)
    pl.semaphore_wait(barrier, len(peers))

def remote(source, target, send, recv, peer):
    return pltpu.make_async_remote_copy(
        src_ref=source, dst_ref=target, send_sem=send, recv_sem=recv, device_id=peer, device_id_type=MESH)

def gather_kernel(nf, cols, count, *refs):
    shards, tiny, fulls, tiny_out = refs[:count], refs[count], refs[count+1:2*count+1], refs[2*count+1]
    local_sem, s1, r1, s2, r2, s3, r3, st, rt = refs[2*count+2:]
    a, b, c, f = place(cols)
    other = 1 - c
    fpeers = [device(a, b, c, lax.rem(f + j, nf), cols) for j in range(1, nf)]
    bpeers = [device(a, lax.rem(b + k, cols), c, f, cols) for k in range(1, cols)]
    sibling = device(a, b, other, f, cols)
    meet(fpeers + bpeers + [sibling])

    def view(w, owner, bb, cc, base=0):
        rows, wide = shards[w].shape
        part, half = rows // cols, wide // 2
        return fulls[w].at[pl.ds(pl.multiple_of(owner * rows + bb * part, 8), part), pl.ds(pl.multiple_of(cc * half, 128), half)]

    waits = []
    for j in range(1, nf):
        cp = remote(tiny, tiny_out.at[f], st.at[j - 1], rt.at[j - 1], fpeers[j - 1])
        cp.start()
        waits.append(cp)
    locals_ = [pltpu.make_async_copy(tiny, tiny_out.at[f], local_sem.at[count])]
    locals_[0].start()
    first = {}
    for w in range(count):
        rows, wide = shards[w].shape
        part, half = rows // cols, wide // 2
        mine = shards[w].at[pl.ds(pl.multiple_of(b * part, 8), part), pl.ds(pl.multiple_of(c * half, 128), half)]
        for j in range(1, nf):
            cp = remote(mine, view(w, f, b, c), s1.at[w, j - 1], r1.at[w, j - 1], fpeers[j - 1])
            cp.start()
            first[w, j] = cp
    for w in range(count):
        rows = shards[w].shape[0]
        cp = pltpu.make_async_copy(shards[w], fulls[w].at[pl.ds(pl.multiple_of(f * rows, 8), rows)], local_sem.at[w])
        cp.start()
        locals_.append(cp)
    second, third = {}, []
    for w in range(count):
        for j in range(1, nf):
            owner = lax.rem(f + nf - j, nf)
            first[w, j].wait_recv()
            piece = view(w, owner, b, c)
            for k in range(1, cols):
                slot = (j - 1) * (cols - 1) + k - 1
                cp = remote(piece, piece, s2.at[w, slot], r2.at[w, slot], bpeers[k - 1])
                cp.start()
                second[w, j, k] = cp
            cp = remote(piece, piece, s3.at[w, (j - 1) * cols], r3.at[w, (j - 1) * cols], sibling)
            cp.start()
            third.append(cp)
    for w in range(count):
        for j in range(1, nf):
            owner = lax.rem(f + nf - j, nf)
            for k in range(1, cols):
                second[w, j, k].wait_recv()
                piece = view(w, owner, lax.rem(b + cols - k, cols), c)
                cp = remote(piece, piece, s3.at[w, (j - 1) * cols + k], r3.at[w, (j - 1) * cols + k], sibling)
                cp.start()
                third.append(cp)
    for cp in third:
        cp.wait_recv()
    for cp in waits:
        cp.wait()
    for cp in list(first.values()) + list(second.values()) + third:
        cp.wait_send()
    for cp in locals_:
        cp.wait()

def gather_weights(shards, tiny, nf, cols):
    count = len(shards)
    any_spec = pl.BlockSpec(memory_space=pl.ANY)
    dma = pltpu.SemaphoreType.DMA
    return pl.pallas_call(
        functools.partial(gather_kernel, nf, cols, count),
        out_shape=[jax.ShapeDtypeStruct((s.shape[0] * nf, s.shape[1]), s.dtype) for s in shards]
        + [jax.ShapeDtypeStruct((nf,) + tiny.shape, tiny.dtype)],
        in_specs=[pl.BlockSpec(memory_space=pltpu.VMEM)] * (count + 1),
        out_specs=[any_spec] * (count + 1),
        scratch_shapes=[dma((count + 1,)), dma((count, nf - 1)), dma((count, nf - 1)),
                        dma((count, (nf - 1) * (cols - 1))), dma((count, (nf - 1) * (cols - 1))),
                        dma((count, (nf - 1) * cols)), dma((count, (nf - 1) * cols)),
                        dma((nf - 1,)), dma((nf - 1,))],
        compiler_params=pltpu.CompilerParams(collective_id=1, has_side_effects=True, vmem_limit_bytes=32 << 20),
        name="gather_weights",
    )(*shards, tiny)

def octet(a, b, c, f, cols):
    me = a * 2 + c
    out = []
    for k in range(1, 8):
        other = lax.rem(me + k, 8)
        out.append((other, device(other // 2, b, lax.rem(other, 2), f, cols)))
    return me, out

def swap_kernel(cols, count, *refs):
    sources, targets = refs[:count], refs[count:2 * count]
    send, recv, here = refs[2 * count:]
    a, b, c, f = place(cols)
    me, peers = octet(a, b, c, f, cols)
    meet([p for _, p in peers])
    copies = []
    for k, (other, peer) in enumerate(peers):
        for i in range(count):
            cp = remote(sources[i].at[other], targets[i].at[me], send.at[i, k], recv.at[i, k], peer)
            cp.start()
            copies.append(cp)
    for i in range(count):
        cp = pltpu.make_async_copy(sources[i].at[me], targets[i].at[me], here.at[i])
        cp.start()
        copies.append(cp)
    for cp in copies:
        cp.wait()

def swap(arrays, cols, ident):
    count = len(arrays)
    return pl.pallas_call(
        functools.partial(swap_kernel, cols, count),
        out_shape=[jax.ShapeDtypeStruct(x.shape, x.dtype) for x in arrays],
        in_specs=[vmem()] * count, out_specs=[vmem()] * count,
        scratch_shapes=[DMA((count, 7)), DMA((count, 7)), DMA((count,))],
        compiler_params=pltpu.CompilerParams(collective_id=ident, has_side_effects=True, vmem_limit_bytes=16 << 20),
        name="swap",
    )(*arrays)

def spread_kernel(cols, q, kv, qg, full, sq, rq, sk, rk, s2, r2, here):
    a, b, c, f = place(cols)
    me, peers = octet(a, b, c, f, cols)
    bpeers = [device(a, lax.rem(b + k, cols), c, f, cols) for k in range(1, cols)]
    meet([p for _, p in peers] + bpeers)

    def slot(block, bb):
        return (block // 2 * cols + bb) * 2 + lax.rem(block, 2)

    first = []
    for k, (other, peer) in enumerate(peers):
        cp = remote(kv.at[other], full.at[slot(me, b)], sk.at[k], rk.at[k], peer)
        cp.start()
        first.append(cp)
    own = pltpu.make_async_copy(kv.at[me], full.at[slot(me, b)], here.at[0])
    own.start()
    ownq = pltpu.make_async_copy(q.at[me], qg.at[me], here.at[1])
    ownq.start()
    second = []
    for k, peer in enumerate(bpeers):
        cp = remote(kv.at[me], full.at[slot(me, b)], s2.at[7, k], r2.at[7, k], peer)
        cp.start()
        second.append(cp)
    third = []
    for k, (other, peer) in enumerate(peers):
        cp = remote(q.at[other], qg.at[me], sq.at[k], rq.at[k], peer)
        cp.start()
        third.append(cp)
    for k in range(7):
        first[k].wait_recv()
        source = lax.rem(me + 8 - (k + 1), 8)
        piece = full.at[slot(source, b)]
        for m, peer in enumerate(bpeers):
            cp = remote(piece, piece, s2.at[k, m], r2.at[k, m], peer)
            cp.start()
            second.append(cp)
    for cp in first:
        cp.wait_send()
    for cp in second + third:
        cp.wait()
    own.wait()
    ownq.wait()

def spread(q, kv, cols, ident):
    return pl.pallas_call(
        functools.partial(spread_kernel, cols),
        out_shape=[jax.ShapeDtypeStruct(q.shape, q.dtype), jax.ShapeDtypeStruct((8 * cols,) + kv.shape[1:], kv.dtype)],
        in_specs=[vmem()] * 2, out_specs=[vmem()] * 2,
        scratch_shapes=[DMA((7,))] * 4 + [DMA((8, max(cols - 1, 1)))] * 2 + [DMA((2,))],
        compiler_params=pltpu.CompilerParams(collective_id=ident, has_side_effects=True, vmem_limit_bytes=16 << 20),
        name="spread",
    )(q, kv)

def collect_kernel(cols, dq, dkv, dqo, dkvo, rbuf, total, sq, rq, sk, rk, s2, r2, here):
    a, b, c, f = place(cols)
    me, peers = octet(a, b, c, f, cols)
    bpeers = [(lax.rem(b + k, cols), device(a, lax.rem(b + k, cols), c, f, cols)) for k in range(1, cols)]
    meet([p for _, p in peers] + [p for _, p in bpeers])

    def slot(block, bb):
        return (block // 2 * cols + bb) * 2 + lax.rem(block, 2)

    order = [other for other, _ in peers] + [me]
    first = {}
    for n, block in enumerate(order):
        for k, (bb, peer) in enumerate(bpeers):
            cp = remote(dkv.at[slot(block, bb)], rbuf.at[k, n], s2.at[k, n], r2.at[k, n], peer)
            cp.start()
            first[k, n] = cp
    rest = []
    for k, (other, peer) in enumerate(peers):
        cp = remote(dq.at[other], dqo.at[me], sq.at[k], rq.at[k], peer)
        cp.start()
        rest.append(cp)
    own = pltpu.make_async_copy(dq.at[me], dqo.at[me], here.at[0])
    own.start()
    for n, block in enumerate(order):
        value = dkv[slot(block, b)].astype(F32)
        for k in range(cols - 1):
            first[k, n].wait_recv()
            value = value + rbuf[k, n].astype(F32)
        if n < 7:
            total[n] = value.astype(BF16)
            cp = remote(total.at[n], dkvo.at[me], sk.at[n], rk.at[n], peers[n][1])
            cp.start()
            rest.append(cp)
        else:
            dkvo[me] = value.astype(BF16)
    for cp in first.values():
        cp.wait_send()
    for cp in rest:
        cp.wait()
    own.wait()

def collect(dq, dkv, cols, ident):
    block = dkv.shape[1:]
    return pl.pallas_call(
        functools.partial(collect_kernel, cols),
        out_shape=[jax.ShapeDtypeStruct(dq.shape, dq.dtype), jax.ShapeDtypeStruct((8,) + block, dkv.dtype)],
        in_specs=[vmem()] * 2, out_specs=[vmem()] * 2,
        scratch_shapes=[pltpu.VMEM((max(cols - 1, 1), 8) + block, BF16), pltpu.VMEM((7,) + block, BF16)]
        + [DMA((7,))] * 4 + [DMA((max(cols - 1, 1), 8))] * 2 + [DMA((1,))],
        compiler_params=pltpu.CompilerParams(collective_id=ident, has_side_effects=True, vmem_limit_bytes=24 << 20),
        name="collect",
    )(dq, dkv)

def reduce_kernel(nf, cols, parts, grads, small, out, small_out, *refs):
    own, core_in, f_in, b_in, f_in2, b_in2, a_in, v_core, v_sum, v_f, v_b, v_a = refs[:12]
    load, sc, rc, s1, r1, s2, r2, s3, r3, s4, r4, s5, r5, s6, r6, sv, rv = refs[12:]
    a, b, c, f = place(cols)
    rows = grads.shape[5]
    fpeers = [(lax.rem(f + j, nf), device(a, b, c, lax.rem(f + j, nf), cols)) for j in range(1, nf)]
    bpeers = [(lax.rem(b + k, cols), device(a, lax.rem(b + k, cols), c, f, cols)) for k in range(1, cols)]
    apeers = [(lax.rem(a + k, 4), device(lax.rem(a + k, 4), b, c, f, cols)) for k in range(1, 4)]
    sibling = device(a, b, 1 - c, f, cols)
    meet([p for _, p in fpeers + bpeers + apeers] + [sibling])
    vector = remote(small, v_core, sv.at[0], rv.at[0], sibling)
    vector.start()
    order = [2, 1, 3, 0]
    dest = {k: lax.rem(a + k, 4) for k in range(4)}
    by_f = {k: k in (1, 2) for k in range(4)}
    loads, cores = {}, {}
    for k in order:
        for i in range(parts):
            cp = pltpu.make_async_copy(grads.at[c, dest[k], i], own.at[k, i], load.at[k, i])
            cp.start()
            loads[k, i] = cp
            cp = remote(grads.at[1 - c, dest[k], i], core_in.at[k, i], sc.at[k, i], rc.at[k, i], sibling)
            cp.start()
            cores[k, i] = cp
    one, two, three = {}, {}, {}
    vec = {}
    vector.wait_recv()
    v_sum[...] = small[...] + v_core[...]
    for j, (ff, peer) in enumerate(fpeers):
        vec[0, j] = remote(v_sum.at[ff], v_f.at[j], sv.at[1 + j], rv.at[1 + j], peer)
        vec[0, j].start()
    for k in order:
        for i in range(parts):
            loads[k, i].wait()
            cores[k, i].wait_recv()

            @pl.loop(0, nf * cols)
            def _(n):
                ff, bb = n // cols, lax.rem(n, cols)
                own[k, i, ff, bb] = (own[k, i, ff, bb].astype(F32) + core_in[k, i, ff, bb].astype(F32)).astype(BF16)

            if by_f[k]:
                for j, (ff, peer) in enumerate(fpeers):
                    cp = remote(own.at[k, i, ff], f_in.at[k, i, j], s1.at[k, i, j], r1.at[k, i, j], peer)
                    cp.start()
                    one[k, i, j] = cp
            else:
                for m, (bb, peer) in enumerate(bpeers):
                    for ff in range(nf):
                        cp = remote(own.at[k, i, ff, bb], b_in.at[k, i, m, ff], s1.at[k, i, m * nf + ff], r1.at[k, i, m * nf + ff], peer)
                        cp.start()
                        one[k, i, m * nf + ff] = cp
    value = v_sum[f]
    for j in range(nf - 1):
        vec[0, j].wait_recv()
        value = value + v_f[j]
    v_b[b] = value
    for m, (bb, peer) in enumerate(bpeers):
        vec[1, m] = remote(v_b.at[b], v_b.at[b], sv.at[nf + m], rv.at[nf + m], peer)
        vec[1, m].start()
    for k in order:
        for i in range(parts):
            if by_f[k]:
                for j in range(nf - 1):
                    one[k, i, j].wait_recv()

                @pl.loop(0, cols)
                def _(bb):
                    value = own[k, i, f, bb].astype(F32)
                    for j in range(nf - 1):
                        value = value + f_in[k, i, j, bb].astype(F32)
                    own[k, i, f, bb] = value.astype(BF16)

                for m, (bb, peer) in enumerate(bpeers):
                    cp = remote(own.at[k, i, f, bb], b_in2.at[k, i, m], s2.at[k, i, m], r2.at[k, i, m], peer)
                    cp.start()
                    two[k, i, m] = cp
            else:
                for m in range(cols - 1):
                    for ff in range(nf):
                        one[k, i, m * nf + ff].wait_recv()

                @pl.loop(0, nf)
                def _(ff):
                    value = own[k, i, ff, b].astype(F32)
                    for m in range(cols - 1):
                        value = value + b_in[k, i, m, ff].astype(F32)
                    own[k, i, ff, b] = value.astype(BF16)

                for j, (ff, peer) in enumerate(fpeers):
                    cp = remote(own.at[k, i, ff, b], f_in2.at[k, i, j], s2.at[k, i, j], r2.at[k, i, j], peer)
                    cp.start()
                    two[k, i, j] = cp
    for m in range(cols - 1):
        vec[1, m].wait_recv()
    value = v_b[0]
    for m in range(1, cols):
        value = value + v_b[m]
    v_a[a] = value
    for k in range(1, 4):
        vec[2, k] = remote(v_a.at[a], v_a.at[a], sv.at[nf + cols + k - 2], rv.at[nf + cols + k - 2], apeers[k - 1][1])
        vec[2, k].start()
    for k in order:
        for i in range(parts):
            value = own[k, i, f, b].astype(F32)
            if by_f[k]:
                for m in range(cols - 1):
                    two[k, i, m].wait_recv()
                    value = value + b_in2[k, i, m].astype(F32)
            else:
                for j in range(nf - 1):
                    two[k, i, j].wait_recv()
                    value = value + f_in2[k, i, j].astype(F32)
            if k != 0:
                own[k, i, f, b] = value.astype(BF16)
                cp = remote(own.at[k, i, f, b], a_in.at[k - 1, i], s3.at[k - 1, i], r3.at[k - 1, i], apeers[k - 1][1])
                cp.start()
                three[k, i] = cp
            else:
                own[k, i, f, b] = value.astype(BF16)
    for k in range(1, 4):
        vec[2, k].wait_recv()
    small_out[...] = v_a[0] + v_a[1] + v_a[2] + v_a[3]
    four, five, six = {}, {}, {}

    def piece(aa, bb, cc, i):
        return out.at[cc, aa, bb, i]

    pending = []
    for i in range(parts):
        value = own[0, i, f, b].astype(F32)
        for k in range(1, 4):
            three[k, i].wait_recv()
            value = value + a_in[k - 1, i].astype(F32)
        out[c, a, b, i] = value.astype(BF16)
        mine = piece(a, b, c, i)
        for k in (2, 1, 3):
            cp = remote(mine, mine, s4.at[k - 1, i], r4.at[k - 1, i], apeers[k - 1][1])
            cp.start()
            four[k, i] = cp
        for m, (bb, peer) in enumerate(bpeers):
            cp = remote(mine, mine, s5.at[0, i, m], r5.at[0, i, m], peer)
            cp.start()
            five[0, i, m] = cp
        cp = remote(mine, mine, s6.at[0, i, 0], r6.at[0, i, 0], sibling)
        cp.start()
        six[0, i, 0] = cp
    for i in range(parts):
        for k in (1, 3, 2):
            four[k, i].wait_recv()
            got = piece(lax.rem(a + 4 - k, 4), b, c, i)
            for m, (bb, peer) in enumerate(bpeers):
                cp = remote(got, got, s5.at[k, i, m], r5.at[k, i, m], peer)
                cp.start()
                five[k, i, m] = cp
            cp = remote(got, got, s6.at[k, i, 0], r6.at[k, i, 0], sibling)
            cp.start()
            six[k, i, 0] = cp
    for i in range(parts):
        for k in (0, 1, 3, 2):
            for m in range(cols - 1):
                five[k, i, m].wait_recv()
                got = piece(lax.rem(a + 4 - k, 4), lax.rem(b + cols - (m + 1), cols), c, i)
                cp = remote(got, got, s6.at[k, i, m + 1], r6.at[k, i, m + 1], sibling)
                cp.start()
                six[k, i, m + 1] = cp
    for cp in six.values():
        cp.wait_recv()
    vector.wait_send()
    for group in (cores, one, two, three, four, five, six, vec):
        for cp in group.values():
            cp.wait_send()

def reduce_grads(grads, small, nf, cols, ident):
    _, _, parts, _, _, rows, width = grads.shape
    block = (rows, width)
    m = max(cols - 1, 1)
    n = max((cols - 1) * nf, nf - 1)
    return pl.pallas_call(
        functools.partial(reduce_kernel, nf, cols, parts),
        out_shape=[jax.ShapeDtypeStruct((2, 4, cols, parts) + block, BF16), jax.ShapeDtypeStruct(small.shape[1:], F32)],
        in_specs=[pl.BlockSpec(memory_space=pl.ANY), vmem()], out_specs=[vmem()] * 2,
        scratch_shapes=[pltpu.VMEM((4, parts, nf, cols) + block, BF16), pltpu.VMEM((4, parts, nf, cols) + block, BF16),
                        pltpu.VMEM((4, parts, nf - 1, cols) + block, BF16), pltpu.VMEM((4, parts, m, nf) + block, BF16),
                        pltpu.VMEM((4, parts, nf - 1) + block, BF16), pltpu.VMEM((4, parts, m) + block, BF16),
                        pltpu.VMEM((3, parts) + block, BF16),
                        pltpu.VMEM(small.shape, F32), pltpu.VMEM(small.shape, F32), pltpu.VMEM((nf - 1,) + small.shape[1:], F32),
                        pltpu.VMEM((cols,) + small.shape[1:], F32), pltpu.VMEM((4,) + small.shape[1:], F32),
                        DMA((4, parts)), DMA((4, parts)), DMA((4, parts)), DMA((4, parts, n)), DMA((4, parts, n)),
                        DMA((4, parts, max(m, nf - 1))), DMA((4, parts, max(m, nf - 1))),
                        DMA((3, parts)), DMA((3, parts)), DMA((3, parts)), DMA((3, parts)),
                        DMA((4, parts, m)), DMA((4, parts, m)), DMA((4, parts, cols)), DMA((4, parts, cols)),
                        DMA((nf + cols + 2,)), DMA((nf + cols + 2,))],
        compiler_params=pltpu.CompilerParams(collective_id=ident, has_side_effects=True, vmem_limit_bytes=56 << 20),
        name="reduce_grads",
    )(grads, small)
KB = 256
SPAN = 256
MASKED = -1e30

def dot(x, y, dims):
    return lax.dot_general(x, y, (dims, ((), ())), preferred_element_type=F32)

NT = ((1,), (1,))
NN = ((1,), (0,))
TN = ((0,), (0,))

def bounds(lens, stream):
    ends, total = [], 0
    for j in range(4):
        total = total + lens[stream, j]
        ends.append(total)
    return ends

def doc_range(pos, ends):
    start = jnp.where(pos >= ends[0], ends[0], 0)
    stop = jnp.where(pos < ends[0], ends[0], ends[3])
    for j in (1, 2):
        start = jnp.where(pos >= ends[j], ends[j], start)
    for j in (2, 1, 0):
        stop = jnp.where(pos < ends[j], ends[j], stop)
    return start, stop

def block_range(base, ends):
    low, _ = doc_range(base, ends)
    _, high = doc_range(base + (SPAN - 1), ends)
    return low // KB, (high + (KB - 1)) // KB

def lane_head(shape, shift):
    lane = lax.broadcasted_iota(jnp.int32, shape, 1)
    return (lane - shift) // 64

def forward_kernel(cols, packed, lens, q_ref, kv_ref, o_ref, ot_ref, lse_ref, qm, vt, acc):
    index = lax.axis_index("ctx")
    b, c = lax.rem(index // 2, cols), lax.rem(index, 2)
    ends = bounds(lens, c)
    total = kv_ref.shape[0]

    @pl.loop(0, total // KB)
    def _(n):
        rows = pl.ds(pl.multiple_of(n * KB, KB), KB)
        vt[:, rows] = kv_ref[rows, 128:384].astype(F32).T.astype(BF16)

    @pl.loop(0, 4)
    def _(stripe):
        base = SPAN * (stripe * cols + b)
        rows = pl.ds(pl.multiple_of(stripe * SPAN, SPAN), SPAN)
        head = lane_head((SPAN, 256), 0)
        if packed:
            q = jnp.concatenate([unpack(q_ref[stripe * 2 + i].astype(F32), 0) for i in range(2)], axis=0) * 0.125
        else:
            q = q_ref[rows].astype(F32) * 0.125
        for h in range(3):
            qm[h] = jnp.where(head == h, q, 0.0).astype(BF16)
        qpos = base + lax.broadcasted_iota(jnp.int32, (1, SPAN), 1)
        start, stop = doc_range(qpos, ends)
        low, high = block_range(base, ends)
        acc[...] = jnp.zeros_like(acc)

        def step(n, state):
            krows = pl.ds(pl.multiple_of(n * KB, KB), KB)
            keys = kv_ref[krows, 0:256]
            kpos = n * KB + lax.broadcasted_iota(jnp.int32, (KB, 1), 0)
            allowed = (kpos >= start) & (kpos < stop)
            out = []
            for h in range(3):
                top, tot = state[h]
                s = jnp.where(allowed, dot(keys, qm[h], NT), MASKED)
                new = jnp.maximum(top, jnp.max(s, axis=0, keepdims=True))
                p = jnp.exp(s - new)
                scale = jnp.exp(top - new)
                hrows = pl.ds(64 * (h + 1), 64)
                acc[hrows] = acc[hrows] * scale + dot(vt[hrows, krows], p.astype(BF16), NN)
                out.append((new, tot * scale + jnp.sum(p, axis=0, keepdims=True)))
            return tuple(out)

        first = tuple((jnp.full((1, SPAN), MASKED, F32), jnp.zeros((1, SPAN), F32)) for _ in range(3))
        final = lax.fori_loop(low, high, step, first)
        for h in range(3):
            top, tot = final[h]
            hrows = pl.ds(64 * (h + 1), 64)
            acc[hrows] = acc[hrows] * (1.0 / tot)
            lse_ref[stripe, pl.ds(h, 1)] = top + jnp.log(tot)
        ot_ref[stripe] = acc[...]
        value = acc[...].T
        if packed:
            for i in range(2):
                o_ref[stripe * 2 + i] = pack(value[128 * i:128 * i + 128], 64).astype(BF16)
        else:
            o_ref[rows] = value.astype(BF16)

def vmem():
    return pl.BlockSpec(memory_space=pltpu.VMEM)

def attend_forward(lens, q, kv, cols, packed=False):
    total = kv.shape[0]
    return pl.pallas_call(
        functools.partial(forward_kernel, cols, packed),
        out_shape=[jax.ShapeDtypeStruct(q.shape, BF16), jax.ShapeDtypeStruct((4, 256, SPAN), F32),
                   jax.ShapeDtypeStruct((4, 8, SPAN), F32)],
        in_specs=[pl.BlockSpec(memory_space=pltpu.SMEM), vmem(), vmem()],
        out_specs=[vmem()] * 3,
        scratch_shapes=[pltpu.VMEM((3, SPAN, 256), BF16), pltpu.VMEM((256, total), BF16), pltpu.VMEM((256, SPAN), F32)],
        compiler_params=pltpu.CompilerParams(vmem_limit_bytes=62 << 20),
        name="attend_forward",
    )(lens, q, kv)

def backward_kernel(cols, lens, q_ref, kv_ref, do_ref, ot_ref, lse_ref, dq_ref, dkv_ref, qm, dm, kt, dk, dv, acc):
    index = lax.axis_index("ctx")
    b, c = lax.rem(index // 2, cols), lax.rem(index, 2)
    ends = bounds(lens, c)
    total = kv_ref.shape[0]

    @pl.loop(0, total // KB)
    def _(n):
        rows = pl.ds(pl.multiple_of(n * KB, KB), KB)
        kt[:, rows] = kv_ref[rows, 0:256].astype(F32).T.astype(BF16)
        dk[rows] = jnp.zeros((KB, 256), F32)
        dv[rows] = jnp.zeros((KB, 256), F32)

    @pl.loop(0, 4)
    def _(stripe):
        base = SPAN * (stripe * cols + b)
        rows = pl.ds(pl.multiple_of(stripe * SPAN, SPAN), SPAN)
        head = lane_head((SPAN, 256), 0)
        headv = lane_head((SPAN, 256), 64)
        q = q_ref[rows].astype(F32) * 0.125
        grad = do_ref[rows].astype(F32)
        for h in range(3):
            qm[h] = jnp.where(head == h, q, 0.0).astype(BF16)
            dm[h] = jnp.where(headv == h, grad, 0.0).astype(BF16)
        prod = grad.T * ot_ref[stripe]
        deltas = [jnp.sum(prod[64 * (h + 1):64 * (h + 2)], axis=0, keepdims=True) for h in range(3)]
        lses = [lse_ref[stripe, pl.ds(h, 1)] for h in range(3)]
        qpos = base + lax.broadcasted_iota(jnp.int32, (1, SPAN), 1)
        start, stop = doc_range(qpos, ends)
        low, high = block_range(base, ends)
        acc[...] = jnp.zeros_like(acc)

        @pl.loop(low, high)
        def _(n):
            krows = pl.ds(pl.multiple_of(n * KB, KB), KB)
            keys = kv_ref[krows, 0:256]
            vals = kv_ref[krows, 128:384]
            kpos = n * KB + lax.broadcasted_iota(jnp.int32, (KB, 1), 0)
            allowed = (kpos >= start) & (kpos < stop)
            newk, newv = dk[krows], dv[krows]
            for h in range(3):
                s = jnp.where(allowed, dot(keys, qm[h], NT), MASKED)
                p = jnp.exp(s - lses[h])
                gp = dot(vals, dm[h], NT)
                ds = (p * (gp - deltas[h])).astype(BF16)
                newv = newv + dot(p.astype(BF16), dm[h], NN)
                newk = newk + dot(ds, qm[h], NN)
                hrows = pl.ds(64 * h, 64)
                acc[hrows] = acc[hrows] + dot(kt[hrows, krows], ds, NN)
            dk[krows] = newk
            dv[krows] = newv

        dq_ref[rows] = (acc[...] * 0.125).T.astype(BF16)

    @pl.loop(0, total // KB)
    def _(n):
        rows = pl.ds(pl.multiple_of(n * KB, KB), KB)
        dkv_ref[rows, 0:128] = dk[rows, 0:128].astype(BF16)
        dkv_ref[rows, 128:256] = (dk[rows, 128:256] + dv[rows, 0:128]).astype(BF16)
        dkv_ref[rows, 256:384] = dv[rows, 128:256].astype(BF16)

def attend_backward(lens, q, kv, do, ot, lse, cols):
    total = kv.shape[0]
    return pl.pallas_call(
        functools.partial(backward_kernel, cols),
        out_shape=[jax.ShapeDtypeStruct(q.shape, BF16), jax.ShapeDtypeStruct(kv.shape, BF16)],
        in_specs=[pl.BlockSpec(memory_space=pltpu.SMEM)] + [vmem()] * 5,
        out_specs=[vmem()] * 2,
        scratch_shapes=[pltpu.VMEM((3, SPAN, 256), BF16), pltpu.VMEM((3, SPAN, 256), BF16), pltpu.VMEM((256, total), BF16),
                        pltpu.VMEM((total, 256), F32), pltpu.VMEM((total, 256), F32), pltpu.VMEM((256, SPAN), F32)],
        compiler_params=pltpu.CompilerParams(vmem_limit_bytes=40 << 20),
        name="attend_backward",
    )(lens, q, kv, do, ot, lse)


def pack(block, base):
    free = 0 if base else 192
    lane = lax.broadcasted_iota(jnp.int32, (32, 256), 1)
    tail = block[96:128]
    rows = []
    for k in range(3):
        moved = pltpu.roll(tail, (free - base - 64 * k) % 256, 1)
        rows.append(jnp.where((lane >= free) & (lane < free + 64), moved, block[32 * k:32 * k + 32]))
    return jnp.concatenate(rows, axis=0)


def unpack(packed, base):
    free = 0 if base else 192
    lane = lax.broadcasted_iota(jnp.int32, (32, 256), 1)
    tail = jnp.zeros((32, 256), F32)
    rows = []
    for k in range(3):
        part = packed[32 * k:32 * k + 32]
        rows.append(jnp.where((lane >= free) & (lane < free + 64), 0.0, part))
        spot = base + 64 * k
        tail = jnp.where((lane >= spot) & (lane < spot + 64), pltpu.roll(part, (spot - free) % 256, 1), tail)
    return jnp.concatenate(rows + [tail], axis=0)


STEPS = ((1, 0), (3, 0), (1, 1), (3, 1), (2, 0), (0, 1), (2, 1))


class Octet:
    def __init__(self, go):
        self.go = go
        self.a, self.b, self.c, self.f = a, b, c, f = place(2)
        self.me = a * 2 + c
        self.others = [lax.rem(a + da, 4) * 2 + lax.rem(c + dc, 2) for da, dc in STEPS]
        self.sources = [lax.rem(a + 4 - da, 4) * 2 + lax.rem(c + dc, 2) for da, dc in STEPS]
        self.devices = [device(lax.rem(a + da, 4), b, lax.rem(c + dc, 2), f, 2) for da, dc in STEPS]

    def send(self, n, source, target):
        return self.go(source, target(self.me), self.devices[n])


def project_kernel(tokens, *refs):
    shards, vectors = refs[:4], refs[4:13]
    q_held, kv_held, f_qkv, f_out, f_in, f_back, vec, turned = refs[13:21]
    own = refs[21:25]
    whole, acc, q_sent, kv_sent, v_own, token, held = refs[25:32]
    flat, (send, recv, here) = refs[32:41], refs[41:]
    fulls = (f_qkv, f_out, f_in, f_back)
    a, b, c, f = place(2)
    group = Octet(None)
    me = group.me
    odd_a = lax.rem(a, 2)
    xp, yp, sp = device(a, 1 - b, c, f, 2), device(a, b, c, 1 - f, 2), device(a, b, 1 - c, f, 2)
    pairs = [device(lax.rem(a + 5 - 2 * odd_a, 4), b, c, f, 2), device(lax.rem(a + 3 + 2 * odd_a, 4), b, c, f, 2)]
    loads = [pltpu.make_async_copy(shards[w], own[w], here.at[w]) for w in range(4)]
    flats = [pltpu.make_async_copy(ref, flat[n], here.at[12 + n]) for n, ref in enumerate(vectors)]
    flats.append(pltpu.make_async_copy(tokens, token, here.at[11]))
    for cp in flats + loads:
        cp.start()
    meet(group.devices + [xp, yp])
    wires = Wires(send, recv)
    go = group.go = wires.go

    def rows_of(w, which, chunk):
        size = shards[w].shape[0] // 4
        return pl.multiple_of(which * 2 * size + chunk * size, 16), size

    def cols_of(w, cc):
        half = shards[w].shape[1] // 2
        return pl.ds(pl.multiple_of(cc * half, 128), half)

    def region(target, w, owner, which, cc, chunk):
        start, size = rows_of(w, which, chunk)
        return target.at[pl.ds(owner * shards[w].shape[0] + start, size), cols_of(w, cc)]

    def source(w, which, chunk):
        start, size = rows_of(w, which, chunk)
        return shards[w].at[pl.ds(start, size), cols_of(w, c)]

    other_f = 1 - f

    class Fetch:
        def __init__(self, target, w, chunk, pair=None):
            self.target, self.w, self.chunk = target, w, chunk
            self.which = b if pair is None else odd_a
            self.peer = xp if pair is None else pairs[pair]
            self.first = go(source(w, self.which, chunk), region(target, w, f, self.which, c, chunk), yp)

        def second(self):
            self.first.wait_recv()
            got = region(self.target, self.w, other_f, self.which, c, self.chunk)
            self.cross = go(got, got, self.peer)
            self.side = go(got, got, sp)

        def third(self):
            self.cross.wait_recv()
            got = region(self.target, self.w, other_f, 1 - self.which, c, self.chunk)
            self.side2 = go(got, got, sp)

        def end(self):
            self.side.wait_recv()
            self.side2.wait_recv()

    class Straight:
        def __init__(self, target, w, chunk, which):
            self.place = (target, w, other_f, which, c, chunk)
            self.first = go(source(w, which, chunk), region(target, w, f, which, c, chunk), yp)

        def second(self):
            self.first.wait_recv()
            got = region(*self.place)
            self.side = go(got, got, sp)

        def third(self):
            pass

        def end(self):
            self.side.wait_recv()

    qkv = [Fetch(whole, 0, 0)]
    for cp in flats:
        cp.wait()

    def token_block(dc):
        return token.at[pl.ds(pl.multiple_of(lax.rem(c + dc, 2) * 128, 128), 128)]

    toks = [go(token_block(STEPS[n][1]), held.at[m], group.devices[n]) for m, n in enumerate((0, 1, 2, 3, 5))]
    held[5] = token[pl.ds(pl.multiple_of(c * 128, 128), 128)]
    for n in range(9):
        value = flat[n][...].astype(F32)
        if n == 3:
            for j in range(4):
                v_own[8 + j:9 + j] = value[384 * j:384 * j + 384].reshape(1, 384)
        else:
            row = n if n < 3 else n - 1
            v_own[row:row + 1] = value.reshape(1, 384)
    v_own[12:16] = jnp.zeros((4, 384), F32)
    vec[f] = v_own[...]
    small = go(v_own, vec.at[f], yp)
    loads[0].wait()
    mine = pl.ds(pl.multiple_of(f * 384, 128), 384)
    theirs = pl.ds(pl.multiple_of(other_f * 384, 128), 384)

    @pl.loop(0, 6)
    def _(n):
        cols = pl.ds(pl.multiple_of(n * 384, 128), 384)
        acc[:, cols] = dot(token[:, mine], own[0][:, cols], NN)

    qkv[0].second()
    qkv.append(Fetch(whole, 0, 1))
    qkv[1].second()
    outer = [Fetch(f_back, 3, chunk) for chunk in range(2)]
    rest = [Fetch(f_out, 1, chunk) for chunk in range(2)]
    inner = [Straight(f_in, 2, chunk, which) for chunk in range(2) for which in range(2)]
    qkv[0].third()
    qkv[1].third()
    stores = []
    for w in range(4):
        if w > 0:
            loads[w].wait()
        rows = shards[w].shape[0]
        cp = pltpu.make_async_copy(own[w], fulls[w].at[pl.ds(pl.multiple_of(f * rows, 16), rows)], here.at[4 + w])
        cp.start()
        stores.append(cp)
    small.wait_recv()
    qkv[0].end()
    qkv[1].end()
    cp = pltpu.make_async_copy(whole.at[pl.ds(pl.multiple_of(other_f * 384, 16), 384)],
                               f_qkv.at[pl.ds(pl.multiple_of(other_f * 384, 16), 384)], here.at[8])
    cp.start()
    stores.append(cp)

    def column(n):
        cols = slice(384 * n, 384 * n + 384)
        value = acc[:, cols] + dot(token[:, theirs], whole[pl.ds(pl.multiple_of(other_f * 384, 16), 384), cols], NN)
        if n < 2:
            value = value + vec[n, 0:1]
        if n >= 4:
            value = value + vec[n - 4, 1:2]
        return value

    lane = lax.broadcasted_iota(jnp.int32, (256, 384), 1)
    for p in range(2):
        k, v = column(2 + p), column(4 + p)
        turned_k, turned_v = pltpu.roll(k, 192, 1), pltpu.roll(v, 192, 1)
        even = jnp.where(lane < 192, k, turned_v).astype(BF16)
        odd = jnp.where(lane < 192, turned_k, v).astype(BF16)
        q = column(p)
        q_even, q_odd = q[:, :256], pltpu.roll(q, 192, 1)[:, :256]
        for s in range(2):
            rows = slice(128 * s, 128 * s + 128)
            kv_sent[4 * p + s], kv_sent[4 * p + 2 + s] = even[rows], odd[rows]
            q_sent[4 * p + s], q_sent[4 * p + 2 + s] = pack(q_even[rows], 0).astype(BF16), pack(q_odd[rows], 0).astype(BF16)

    def slot(block, bb):
        return (block // 2 * 2 + bb) * 2 + lax.rem(block, 2)

    kv_slot = lambda block: kv_held.at[slot(block, b)]
    q_slot = lambda block: q_held.at[block]
    first = [group.send(n, kv_sent.at[group.others[n]], kv_slot) for n in (6, 0, 1, 2, 3, 4, 5)]
    first = first[1:] + first[:1]
    own_kv = pltpu.make_async_copy(kv_sent.at[me], kv_held.at[slot(me, b)], here.at[9])
    own_kv.start()
    own_q = pltpu.make_async_copy(q_sent.at[me], q_held.at[me], here.at[10])
    own_q.start()
    crossed = [go(kv_sent.at[me], kv_held.at[slot(me, b)], xp)]
    third = [group.send(n, q_sent.at[group.others[n]], q_slot) for n in (6, 0, 1, 2, 3, 4, 5)]
    third = third[1:] + third[:1]

    def onward(n):
        first[n].wait_recv()
        piece = kv_slot(group.sources[n])
        crossed.append(go(piece, piece, xp))

    onward(5)
    onward(0)
    onward(1)
    for cp in outer:
        cp.second()
    for cp in rest:
        cp.second()
    onward(2)
    onward(3)
    onward(4)
    onward(6)
    for cp in toks:
        cp.wait_recv()

    @pl.loop(0, 6)
    def _(n):
        @pl.loop(0, 6)
        def _(m):
            lanes = pl.ds(pl.multiple_of(m * 128, 128), 128)
            turned[n, lanes] = held[n, :, lanes].astype(F32).T.astype(BF16)

    for cp in inner:
        cp.second()
    for cp in outer:
        cp.third()
    for cp in rest:
        cp.third()
    for cp in crossed + third:
        cp.wait_recv()
    for cp in rest + inner + outer:
        cp.end()
    for cp in wires.made:
        cp.wait_send()
    for cp in stores + [own_kv, own_q]:
        cp.wait()


def project(tokens, shards, vectors, ident):
    rows, width = tokens.shape
    anywhere = pl.BlockSpec(memory_space=pl.ANY)
    wires = 80
    return pl.pallas_call(
        project_kernel,
        out_shape=[jax.ShapeDtypeStruct((8, 96, 256), BF16), jax.ShapeDtypeStruct((16, 128, 384), BF16)]
        + [jax.ShapeDtypeStruct((2 * s.shape[0], s.shape[1]), BF16) for s in shards]
        + [jax.ShapeDtypeStruct((2, 16, 384), F32), jax.ShapeDtypeStruct((6, 768, 128), BF16)],
        in_specs=[pl.BlockSpec(memory_space=pltpu.HBM)] * 14,
        out_specs=[vmem()] * 2 + [anywhere] * 4 + [vmem()] * 2,
        scratch_shapes=[pltpu.VMEM(s.shape, BF16) for s in shards]
        + [pltpu.VMEM((768, 2304), BF16), pltpu.VMEM((256, 2304), F32), pltpu.VMEM((8, 96, 256), BF16),
           pltpu.VMEM((8, 128, 384), BF16), pltpu.VMEM((16, 384), F32), pltpu.VMEM(tokens.shape, BF16),
           pltpu.VMEM((6, 128, 768), BF16),
           *[pltpu.VMEM(v.shape, BF16) for v in vectors], DMA((wires,)), DMA((wires,)), DMA((21,))],
        compiler_params=pltpu.CompilerParams(collective_id=ident, has_side_effects=True, vmem_limit_bytes=62 << 20),
        name="project",
    )(tokens, *shards, *vectors)


BLK = 48
Z1, X1, Y1 = (0, 768), (768, 1920), (1920, 3456)
LATE = (0, 640)


class Wires:
    def __init__(self, send, recv):
        self.send, self.recv, self.made = send, recv, []

    def go(self, source, target, peer):
        n = len(self.made)
        cp = remote(source, target, self.send.at[n], self.recv.at[n], peer)
        cp.start()
        self.made.append(cp)
        return cp


def transpose_into(target, source, base):
    width = source.shape[1]

    @pl.loop(0, width // 128)
    def _(n):
        at = pl.multiple_of(n * 128, 128)
        target[pl.ds(base + at, 128)] = source[:, pl.ds(at, 128)].astype(F32).T.astype(BF16)


def pair_columns(even, odd, lane, second):
    if second:
        return jnp.where(lane < 192, pltpu.roll(even, 192, 1), odd)
    return jnp.where(lane < 192, even, pltpu.roll(odd, 192, 1))


def halves(span):
    tiles = (span[1] - span[0]) // 128
    mid = span[0] + tiles // 2 * 128
    return (span[0], mid), (mid, span[1])


def within(span, group):
    base = 0
    for member in group:
        if member == span:
            return slice(base, base + span[1] - span[0])
        base += member[1] - member[0]


def gradient_kernel(lens, wqkv, gfirst_hbm, near_hbm, far_hbm, q_hbm, kv_hbm, ot_hbm, xt, gbr, ghid, gsec, small, do_sent, lse_ref,
                    out, late_out, igrad, small_out,
                    joined, wqkv_held, gfirst, near, far, q_held, kv_ref, ot_ref, mine, sib, cin, y8, y4, x8, x4, z4, z1r, zyb, zxb,
                    do_held, qm, dm, kt, dk, dv, acc, rowsc, delta, dq_sent, dq_all, dkv_all, dqo, dkvo, xsend, rbuf,
                    l_sib, l_in, l_acc, l_mine, ly, lx,
                    v_own, v_core, v_f, v_b, v_a, send, recv, here):
    inputs = [pltpu.make_async_copy(s, t, here.at[5 + n]) for n, (s, t) in enumerate(
        ((kv_hbm, kv_ref), (q_hbm, q_held), (ot_hbm, ot_ref), (near_hbm, near), (far_hbm, far), (gfirst_hbm, gfirst), (wqkv, wqkv_held)))]
    for cp in inputs:
        cp.start()
    group = Octet(None)
    a, b, c, f, me = group.a, group.b, group.c, group.f, group.me
    xp, yp, sp = device(a, 1 - b, c, f, 2), device(a, b, c, 1 - f, 2), device(a, b, 1 - c, f, 2)
    up, down = lax.rem(a + 1, 4), lax.rem(a + 3, 4)
    upp, downp = device(up, b, c, f, 2), device(down, b, c, f, 2)
    ends = bounds(lens, c)
    total = kv_ref.shape[0]
    meet(group.devices + [xp, yp])
    wires = Wires(send, recv)
    go = group.go = wires.go
    pending = []

    do_slot = lambda block: do_held.at[block]
    swaps = {n: group.send(n, do_sent.at[group.others[n]], do_slot) for n in (6, 0, 1, 2, 3, 4, 5)}
    do_held[me] = do_sent[me]


    def produce(kind, first, count, part, finish):
        @pl.loop(0, 2 * count)
        def _(n):
            ff, j = lax.rem(n, 2), first + n // 2
            if kind == "out":
                left, right = xt[pl.ds(pl.multiple_of(ff * 384, 128), 384)], gbr[:, pl.ds(pl.multiple_of(part * 384, 128), 384)]
                col = 768
            elif kind == "in":
                left = xt[pl.ds(pl.multiple_of(768 + ff * 384, 128), 384)]
                right = ghid[:, pl.ds(pl.multiple_of(part * 1536 + j * 384, 128), 384)]
                col = pl.multiple_of(j * 384 + (384 if first else 0), 128)
            else:
                left = xt[pl.ds(pl.multiple_of(1536 + ff * 1536 + j * 384, 128), 384)]
                right = gsec[:, pl.ds(pl.multiple_of(part * 384, 128), 384)]
                col = pl.multiple_of(1920 + j * 384, 128)
            finish(pl.ds(ff * 2, 2), pl.ds(col, 384), dot(left, right, NN).reshape(2, 4, BLK, 384))

    def keep(rows, cols, value):
        sib[rows, :, :, cols] = value.astype(BF16)

    def join(rows, cols, value):
        mine[rows, :, :, cols] = (value + cin[rows, :, :, cols].astype(F32)).astype(BF16)

    core = {}

    def share(span):
        cols = slice(span[0], span[1])
        core[span] = go(sib.at[:, :, :, cols], cin.at[:, :, :, cols], sp)

    RS = (Y1, X1)

    def add(target, source):
        def step(n):
            t, s = target(n), source(n)
            t[...] = (t[...].astype(F32) + s[...].astype(F32)).astype(BF16)
        return step

    def accumulate(target, source, count):
        pl.loop(0, count)(add(target, source))

    ycols, xcols, zcols = slice(*Y1), slice(*X1), slice(*Z1)

    def start_y():
        return go(mine.at[pl.ds((1 - f) * 2, 2), :, :, ycols], y8, yp)

    def start_x():
        return [go(mine.at[ff * 2 + 1 - b, :, :, xcols], x8.at[ff], xp) for ff in range(2)]

    def next_y(cp):
        cp.wait_recv()
        accumulate(lambda n: mine.at[f * 2 + n // 4, lax.rem(n, 4), :, ycols], lambda n: y8.at[n // 4, lax.rem(n, 4)], 8)
        return go(mine.at[f * 2 + 1 - b, :, :, ycols], x4, xp)

    def next_x(cps):
        for cp in cps:
            cp.wait_recv()
        accumulate(lambda n: mine.at[n // 4 * 2 + b, lax.rem(n, 4), :, xcols], lambda n: x8.at[n // 4, lax.rem(n, 4)], 8)
        return go(mine.at[(1 - f) * 2 + b, :, :, xcols], y4, yp)

    def last_y(cp):
        cp.wait_recv()
        accumulate(lambda n: mine.at[f * 2 + b, n, :, ycols], lambda n: x4.at[n], 4)

    def last_x(cp):
        cp.wait_recv()
        accumulate(lambda n: mine.at[f * 2 + b, n, :, xcols], lambda n: y4.at[n], 4)

    def landing(span, step, part, single):
        if single:
            base = within(span, RS).start - span[0]
            return z1r.at[step, :, base + part[0]:base + part[1]]
        return z4.at[step, :, :, part[0]:part[1]]

    def ring_source(aa, part, single):
        cols = slice(part[0], part[1])
        return mine.at[f * 2 + b, aa, :, cols] if single else mine.at[:, aa, :, cols]

    def ring_send(span, step, single):
        lo, hi = halves(span)
        ud, dd = lax.rem(a + 3 - step, 4), lax.rem(a + 1 + step, 4)
        return (go(ring_source(ud, lo, single), landing(span, step, lo, single), upp),
                go(ring_source(dd, hi, single), landing(span, step, hi, single), downp))

    def ring_add(span, step, single, cps):
        lo, hi = halves(span)
        ud, dd = lax.rem(a + 6 - step, 4), lax.rem(a + 2 + step, 4)
        for cp, part, aa in zip(cps, (lo, hi), (ud, dd)):
            cp.wait_recv()
            got = landing(span, step, part, single)
            if single:
                add(lambda n: ring_source(aa, part, True), lambda n: got)(0)
            else:
                cols = slice(part[0], part[1])
                accumulate(lambda n: mine.at[n, aa, :, cols], lambda n: got.at[n], 4)

    def tail_z_y():
        return go(mine.at[pl.ds((1 - f) * 2, 2), a, :, zcols], zyb, yp)

    def tail_z_x(cp):
        cp.wait_recv()
        accumulate(lambda n: mine.at[f * 2 + n, a, :, zcols], lambda n: zyb.at[n], 2)
        return go(mine.at[f * 2 + 1 - b, a, :, zcols], zxb, xp)

    def tail_z_end(cp):
        cp.wait_recv()
        add(lambda n: mine.at[f * 2 + b, a, :, zcols], lambda n: zxb)(0)

    class Gather:
        def __init__(self, own, spot, span, first):
            self.span, self.first, self.spot = span, first, spot
            self.own = own
            self.copy = pltpu.make_async_copy(own, spot(b, a, span), here.at[len(locals_)])
            self.copy.start()
            locals_.append(self.copy)
            pending.append(go(own, spot(b, a, span), sp))
            self.ring = go(own, spot(b, a, span), upp), go(own, spot(b, a, span), downp)
            self.cross = go(own, spot(b, a, span), xp)

        def spread(self, bb, aa):
            p = self.spot(bb, aa, self.span)
            pending.append(go(p, p, sp))

        def passed(self, bb, ring):
            lo, hi = halves(self.span)
            ring[0].wait_recv()
            p = self.spot(bb, down, lo)
            first = go(p, p, upp)
            ring[1].wait_recv()
            p = self.spot(bb, up, hi)
            second = go(p, p, downp)
            for aa in (down, up):
                self.spread(bb, aa)
            return first, second

        def arrived(self, bb, ring):
            for cp in ring:
                cp.wait_recv()
            self.spread(bb, lax.rem(a + 2, 4))

        def second(self):
            self.ring2 = self.passed(b, self.ring)
            if self.first == "b":
                self.cross.wait_recv()
                self.spread(1 - b, a)
                p = self.spot(1 - b, a, self.span)
                self.other = go(p, p, upp), go(p, p, downp)
            else:
                spots = [self.spot(b, aa, self.span) for aa in (down, up)]
                self.more = [go(p, p, xp) for p in spots]

        def third(self):
            self.arrived(b, self.ring2)
            if self.first == "b":
                self.other2 = self.passed(1 - b, self.other)
            else:
                p = self.spot(b, lax.rem(a + 2, 4), self.span)
                self.more.append(go(p, p, xp))
                self.cross.wait_recv()
                self.spread(1 - b, a)

        def fourth(self):
            if self.first == "b":
                self.arrived(1 - b, self.other2)
            else:
                for cp, aa in zip(self.more, (down, up, lax.rem(a + 2, 4))):
                    cp.wait_recv()
                    self.spread(1 - b, aa)

    locals_ = []

    def early_spot(bb, aa, span):
        return out.at[c, bb * 4 + aa, :, span[0]:span[1]]

    def late_spot(bb, aa, span):
        return late_out.at[aa, bb * 2 + c, :, span[0]:span[1]]

    def early_gather(span, first):
        return Gather(mine.at[f * 2 + b, a, :, span[0]:span[1]], early_spot, span, first)

    def prepare():
        @pl.loop(0, total // KB)
        def _(n):
            rows = pl.ds(pl.multiple_of(n * KB, KB), KB)
            kt[:, rows] = kv_ref[rows, 0:256].astype(F32).T.astype(BF16)

        @pl.loop(0, 4)
        def _(stripe):
            head = lane_head((SPAN, 256), 0)
            headv = lane_head((SPAN, 256), 64)
            q = jnp.concatenate([unpack(q_held[stripe * 2 + i].astype(F32), 0) for i in range(2)], axis=0) * 0.125
            grad = jnp.concatenate([unpack(do_held[stripe * 2 + i].astype(F32), 64) for i in range(2)], axis=0)
            for h in range(3):
                qm[stripe, h] = jnp.where(head == h, q, 0.0).astype(BF16)
                dm[stripe, h] = jnp.where(headv == h, grad, 0.0).astype(BF16)
            prod = grad.T * ot_ref[stripe]
            for h in range(3):
                delta[stripe, h:h + 1] = jnp.sum(prod[64 * (h + 1):64 * (h + 2)], axis=0, keepdims=True)
            qpos = SPAN * (stripe * 2 + b) + lax.broadcasted_iota(jnp.int32, (1, SPAN), 1)
            start, stop = doc_range(qpos, ends)
            rowsc[stripe, 0:1] = start
            rowsc[stripe, 1:2] = stop
            acc[stripe] = jnp.zeros((256, SPAN), F32)

    reach = total * 5 // 8 // KB

    def attend(da, parity):
        block = lax.rem(a + da, 4) * 2 + parity
        krows = pl.ds(pl.multiple_of(block * KB, KB), KB)
        dk[...] = jnp.zeros((KB, 256), F32)
        dv[...] = jnp.zeros((KB, 256), F32)
        @pl.loop(0, 4)
        def _(stripe):
            away = stripe * 2 + b - block

            @pl.when((away <= reach) & (away >= -reach))
            def _():
                keys = kv_ref[krows, 0:256]
                vals = kv_ref[krows, 128:384]
                kpos = block * KB + lax.broadcasted_iota(jnp.int32, (KB, 1), 0)
                allowed = (kpos >= rowsc[stripe, 0:1]) & (kpos < rowsc[stripe, 1:2])
                newk, newv = dk[...], dv[...]
                for h in range(3):
                    s = jnp.where(allowed, dot(keys, qm[stripe, h], NT), MASKED)
                    p = jnp.exp(s - lse_ref[stripe, h:h + 1])
                    gp = dot(vals, dm[stripe, h], NT)
                    ds = (p * (gp - delta[stripe, h:h + 1])).astype(BF16)
                    newv = newv + dot(p.astype(BF16), dm[stripe, h], NN)
                    newk = newk + dot(ds, qm[stripe, h], NN)
                    hrows = pl.ds(64 * h, 64)
                    acc[stripe, hrows] = acc[stripe, hrows] + dot(kt[hrows, krows], ds, NN)
                dk[...] = newk
                dv[...] = newv

    def slot(block, bb):
        return (block // 2 * 2 + bb) * 2 + lax.rem(block, 2)

    def grads_of(dc):
        rows = pl.ds(pl.multiple_of(lax.rem(c + dc, 2) * 128, 128), 128)
        k, v = dk[rows], dv[rows]
        return jnp.concatenate([k[:, :128], k[:, 128:] + v[:, :128], v[:, 128:]], axis=1)

    FAR, NEXT = ((6, 1), (4, 0)), ((0, 0), (2, 1))
    BACK, HERE = ((1, 0), (3, 1)), ((5, 1), (7, 0))
    crossed = {}

    def cross(members):
        for n, dc in members:
            xsend[n] = grads_of(dc).astype(BF16)
            crossed[n] = go(xsend.at[n], rbuf.at[n], xp)

    dkv_slot = lambda block: dkvo.at[block]
    dkvs = {}

    def settle(members):
        for n, dc in members:
            crossed[n].wait_recv()
            value = (grads_of(dc) + rbuf[n].astype(F32)).astype(BF16)
            if n == 7:
                dkv_all[me] = value
                dkvo[me] = value
            else:
                dkv_all[group.others[n]] = value
                dkvs[n] = group.send(n, dkv_all.at[group.others[n]], dkv_slot)

    dq_slot = lambda block: dqo.at[block]
    dqs = {}

    produce("out", 0, 1, 1 - c, keep)
    produce("in", 2, 2, 1 - c, keep)
    share(X1)
    produce("back", 0, 4, 1 - c, keep)
    share(Y1)
    core[X1].wait_recv()
    produce("out", 0, 1, c, join)
    produce("in", 2, 2, c, join)
    x1 = start_x()
    core[Y1].wait_recv()
    produce("back", 0, 4, c, join)
    y1 = start_y()
    produce("in", 0, 2, 1 - c, keep)
    share(Z1)
    for cp in swaps.values():
        cp.wait_recv()
    for cp in inputs[:3]:
        cp.wait()
    prepare()
    core[Z1].wait_recv()
    produce("in", 0, 2, c, join)
    z1 = ring_send(Z1, 0, False)
    attend(2, 1 - b)
    cross(FAR)
    attend(1, 1 - b)
    cross(NEXT)
    ring_add(Z1, 0, False, z1)
    z1 = ring_send(Z1, 1, False)
    attend(3, 1 - b)
    cross(BACK)
    attend(0, 1 - b)
    cross(HERE)
    x1 = next_x(x1)
    ring_add(Z1, 1, False, z1)
    z1 = ring_send(Z1, 2, False)
    attend(2, b)
    settle(FAR)
    y1 = next_y(y1)
    attend(1, b)
    settle(NEXT)
    ring_add(Z1, 2, False, z1)
    z1 = tail_z_y()
    attend(3, b)
    settle(BACK)
    last_x(x1)
    x1 = ring_send(X1, 0, True)
    attend(0, b)

    @pl.loop(0, 4)
    def _(stripe):
        value = (acc[stripe] * 0.125).T
        dq_all[pl.ds(stripe * 2, 2)] = value.astype(BF16).reshape(2, 128, 256)
        for i in range(2):
            dq_sent[stripe * 2 + i] = pack(value[128 * i:128 * i + 128], 0).astype(BF16)

    def send_dq(*which):
        for n in which:
            dqs[n] = group.send(n, dq_sent.at[group.others[n]], dq_slot)

    dqo[me] = dq_sent[me]
    settle(HERE)
    z1 = tail_z_x(z1)
    ring_add(X1, 0, True, x1)
    x1 = ring_send(X1, 1, True)

    def project_back(n, right):
        rows = pl.ds(pl.multiple_of(n * 96, 32), 96)
        value = dot(near[5, rows], right[me], NN)
        for m, k in enumerate((0, 1, 2, 3, 5)):
            value = value + dot(near[m, rows], right[group.sources[k]], NN)
        for m, k in ((0, 4), (1, 6)):
            value = value + dot(far[m, rows], right[group.sources[k]], NN)
        return value

    for cp in inputs[3:]:
        cp.wait()

    @pl.loop(0, 4)
    def _(n):
        theirs, ours = n * 2 + 1 - c, n * 2 + c
        l_sib[n, :, 0:256] = project_back(theirs, dq_all).astype(BF16)
        l_sib[n, :, 256:640] = project_back(theirs, dkv_all).astype(BF16)
        l_acc[n, :, 0:256] = project_back(ours, dq_all)
        l_acc[n, :, 256:640] = project_back(ours, dkv_all)

    late = go(l_sib, l_in, sp)
    send_dq(6, 4)
    last_y(y1)
    y1 = ring_send(Y1, 0, True)
    ring_add(X1, 1, True, x1)
    x1 = ring_send(X1, 2, True)
    send_dq(0, 2)
    late.wait_recv()

    @pl.loop(0, 4)
    def _(n):
        l_mine[n] = (l_acc[n] + l_in[n].astype(F32)).astype(BF16)

    late = go(l_mine.at[pl.ds((1 - f) * 2, 2)], ly, yp)
    tail_z_end(z1)
    g_z1 = early_gather(Z1, "a")
    ring_add(Y1, 0, True, y1)
    y1 = ring_send(Y1, 1, True)
    send_dq(1, 3)
    late.wait_recv()
    accumulate(lambda n: l_mine.at[f * 2 + n], lambda n: ly.at[n], 2)
    late = go(l_mine.at[f * 2 + 1 - b], lx, xp)
    ring_add(X1, 2, True, x1)
    g_x1 = early_gather(X1, "a")
    send_dq(5)
    ring_add(Y1, 1, True, y1)
    y1 = ring_send(Y1, 2, True)
    late.wait_recv()
    add(lambda n: l_mine.at[f * 2 + b], lambda n: lx)(0)
    g_l = Gather(l_mine.at[f * 2 + b], late_spot, LATE, "a")
    g_z1.second()
    g_x1.second()
    ring_add(Y1, 2, True, y1)
    g_y1 = early_gather(Y1, "a")

    for cp in list(dqs.values()) + list(dkvs.values()):
        cp.wait_recv()
    lane = lax.broadcasted_iota(jnp.int32, (128, 384), 1)
    for s in range(2):
        rows = slice(s * 128, s * 128 + 128)
        for p in range(2):
            even, odd = 4 * p + s, 4 * p + 2 + s
            blank = jnp.zeros((128, 128), F32)
            qe = jnp.concatenate([unpack(dqo[even].astype(F32), 0), blank], axis=1)
            qo = jnp.concatenate([unpack(dqo[odd].astype(F32), 0), blank], axis=1)
            joined[rows, 384 * p:384 * p + 384] = pair_columns(qe, qo, lane, False).astype(BF16)
            ke, ko = dkvo[even].astype(F32), dkvo[odd].astype(F32)
            joined[rows, 768 + 384 * p:1152 + 384 * p] = pair_columns(ke, ko, lane, False).astype(BF16)
            joined[rows, 1536 + 384 * p:1920 + 384 * p] = pair_columns(ke, ko, lane, True).astype(BF16)
    v_own[...] = small[...]
    v_own[0:1] = jnp.sum(joined[:, 0:768].astype(F32), axis=0, keepdims=True)
    v_own[1:2] = jnp.sum(joined[:, 1536:2304].astype(F32), axis=0, keepdims=True)
    vec = go(v_own, v_core, sp)

    g_l.second()
    vec.wait_recv()
    v_core[...] = v_own[...] + v_core[...]
    vec = go(v_core.at[:, pl.ds(pl.multiple_of((1 - f) * 384, 128), 384)], v_f, yp)
    g_z1.third()
    g_x1.third()
    vec.wait_recv()
    v_b[b] = v_core[:, pl.ds(pl.multiple_of(f * 384, 128), 384)] + v_f[...]
    vec = go(v_b.at[b], v_b.at[b], xp)

    @pl.loop(0, 3)
    def _(n):
        rows = pl.ds(pl.multiple_of(n * 256, 256), 256)
        igrad[:, rows] = gfirst[:, rows] + dot(joined[...], wqkv_held[rows], NT)

    g_y1.second()
    g_l.third()
    g_z1.fourth()
    g_x1.fourth()
    vec.wait_recv()
    v_a[a] = v_b[0] + v_b[1]
    vec = [go(v_a.at[a], v_a.at[a], device(lax.rem(a + k, 4), b, c, f, 2)) for k in range(1, 4)]
    g_y1.third()
    g_l.fourth()
    g_y1.fourth()
    for cp in vec + pending:
        cp.wait_recv()
    small_out[...] = v_a[0] + v_a[1] + v_a[2] + v_a[3]
    for cp in locals_:
        cp.wait()
    for cp in wires.made:
        cp.wait_send()


def reduce_all(lens, wqkv, gfirst, near, far, xt, gbr, ghid, gsec, small, do_sent, q, kv, ot, lse, ident):
    wires = 192
    total = kv.shape[0]
    bf = lambda *shape: pltpu.VMEM(shape, BF16)
    fl = lambda *shape: pltpu.VMEM(shape, F32)
    anywhere = pl.BlockSpec(memory_space=pl.ANY)
    return pl.pallas_call(
        gradient_kernel,
        out_shape=[jax.ShapeDtypeStruct((2, 8, BLK, 3456), BF16), jax.ShapeDtypeStruct((4, 4, 96, 640), BF16),
                   jax.ShapeDtypeStruct((256, 768), F32), jax.ShapeDtypeStruct((16, 384), F32)],
        in_specs=[pl.BlockSpec(memory_space=pltpu.SMEM)] + [anywhere] * 7 + [vmem()] * 7, out_specs=[anywhere] * 2 + [vmem()] * 2,
        scratch_shapes=[
            bf(256, 2304), bf(768, 2304), fl(256, 768), bf(6, 768, 128), bf(2, 768, 128), bf(8, 96, 256), bf(total, 384), fl(4, 256, SPAN),
            bf(4, 4, BLK, 3456), bf(4, 4, BLK, 3456), bf(4, 4, BLK, 3456),
            bf(2, 4, BLK, 1536), bf(4, BLK, 1152), bf(2, 4, BLK, 1152), bf(4, BLK, 1536),
            bf(3, 4, BLK, 768), bf(3, BLK, 2688), bf(2, BLK, 768), bf(BLK, 768),
            bf(8, 96, 256), bf(4, 3, SPAN, 256), bf(4, 3, SPAN, 256), bf(256, total), fl(KB, 256), fl(KB, 256), fl(4, 256, SPAN),
            pltpu.VMEM((4, 8, SPAN), jnp.int32), fl(4, 8, SPAN),
            bf(8, 96, 256), bf(8, 128, 256), bf(8, 128, 384), bf(8, 96, 256), bf(8, 128, 384), bf(8, 128, 384), bf(8, 128, 384),
            bf(4, 96, 640), bf(4, 96, 640), fl(4, 96, 640), bf(4, 96, 640), bf(2, 96, 640), bf(96, 640),
            fl(16, 768), fl(16, 768), fl(16, 384), fl(2, 16, 384), fl(4, 16, 384),
            DMA((wires,)), DMA((wires,)), DMA((12,))],
        compiler_params=pltpu.CompilerParams(collective_id=ident, has_side_effects=True, vmem_limit_bytes=62 << 20),
        name="reduce_all",
    )(lens, wqkv, gfirst, near, far, q, kv, ot, xt, gbr, ghid, gsec, small, do_sent, lse)


def widen_kernel(grads, late, low, igrad, sums, g_qkv, g_out, g_in, g_back, low_out, igrad_out, *vectors):
    for core in range(2):
        part = grads.at[core]
        g_out[:, core * 384:core * 384 + 384] = part[:, 768:1152].astype(F32)
        g_in[:, core * 1536:core * 1536 + 768] = part[:, 0:768].astype(F32)
        g_in[:, core * 1536 + 768:core * 1536 + 1536] = part[:, 1152:1920].astype(F32)
        for j in range(4):
            g_back[j, :, core * 384:core * 384 + 384] = part[:, 1920 + 384 * j:2304 + 384 * j].astype(F32)
    lane = lax.broadcasted_iota(jnp.int32, (96, 384), 1)
    for p in range(2):
        even, odd = late[2 * p, 0].astype(F32), late[2 * p + 1, 0].astype(F32)
        g_qkv[:, 384 * p:384 * p + 384] = pair_columns(even[:, :384], odd[:, :384], lane, False)
        ke, ko = even[:, 256:], odd[:, 256:]
        g_qkv[:, 768 + 384 * p:1152 + 384 * p] = pair_columns(ke, ko, lane, False)
        g_qkv[:, 1536 + 384 * p:1920 + 384 * p] = pair_columns(ke, ko, lane, True)
    low_out[...] = low[...]
    igrad_out[...] = igrad[...]

    @pl.when(pl.program_id(0) == 0)
    def _():
        for n, ref in enumerate(vectors):
            if n == 3:
                for j in range(4):
                    ref[384 * j:384 * j + 384] = sums[8 + j:9 + j].reshape(384)
            else:
                row = n if n < 3 else n - 1
                ref[...] = sums[row:row + 1].reshape(384)


def widen(grads, late, low, igrad, sums):
    rows, step = 384, 96
    spec = lambda tall, wide: pl.BlockSpec((tall, wide), lambda n: (n, 0))
    flat = lambda size: pl.BlockSpec((size,), lambda n: (0,))
    sizes = [384] * 3 + [1536] + [384] * 5
    return pl.pallas_call(
        widen_kernel,
        grid=(rows // step,),
        out_shape=[jax.ShapeDtypeStruct((rows, 2304), F32), jax.ShapeDtypeStruct((rows, 768), F32),
                   jax.ShapeDtypeStruct((rows, 3072), F32), jax.ShapeDtypeStruct((4, rows, 768), F32),
                   jax.ShapeDtypeStruct(low.shape, BF16), jax.ShapeDtypeStruct(igrad.shape, F32)]
        + [jax.ShapeDtypeStruct((size,), F32) for size in sizes],
        in_specs=[pl.BlockSpec((2, step, 3456), lambda n: (0, n, 0)), pl.BlockSpec((4, 1, step, 640), lambda n: (0, n, 0, 0)),
                  spec(64, 768), spec(64, 768), pl.BlockSpec((16, 384), lambda n: (0, 0))],
        out_specs=[spec(step, 2304), spec(step, 768), spec(step, 3072), pl.BlockSpec((4, step, 768), lambda n: (0, n, 0)),
                   spec(64, 768), spec(64, 768)] + [flat(size) for size in sizes],
        compiler_params=pltpu.CompilerParams(vmem_limit_bytes=62 << 20),
        name="widen",
    )(grads, late, low, igrad, sums)


def middle_kernel(o_sent, tokens, cotangent, w_out, w_in, w_back, vec,
                  output, gfirst, xt, gbr, ghid, gsec, do_sent, small, far,
                  o_held, f_held, v_out, v_in, v_back, normed, xhat1, final, slope, act, send, recv, here):
    group = Octet(None)
    a, b, c, f, me = group.a, group.b, group.c, group.f, group.me
    loads = [pltpu.make_async_copy(s, t, here.at[n]) for n, (s, t) in enumerate(((w_out, v_out), (w_in, v_in), (w_back, v_back)))]
    for cp in loads:
        cp.start()
    meet(group.devices)
    wires = Wires(send, recv)
    go = group.go = wires.go
    o_slot = lambda block: o_held.at[block]
    swaps = {n: group.send(n, o_sent.at[group.others[n]], o_slot) for n in (6, 0, 1, 2, 3, 4, 5)}
    o_held[me] = o_sent[me]

    def token_block(dc):
        return tokens.at[pl.ds(pl.multiple_of(lax.rem(c + dc, 2) * 128, 128), 128)]


    def row(n):
        return jnp.concatenate([vec[0, n:n + 1], vec[1, n:n + 1]], axis=1)

    def sums(n, value):
        small[n:n + 1] = jnp.sum(value, axis=0, keepdims=True)

    for cp in swaps.values():
        cp.wait_recv()
    beyond = [go(token_block(dc), f_held.at[dc], group.devices[n]) for dc, n in ((0, 4), (1, 6))]
    lane = lax.broadcasted_iota(jnp.int32, (128, 384), 1)
    blank = jnp.zeros((128, 128), F32)
    att = act
    for s in range(2):
        rows = slice(s * 128, s * 128 + 128)
        for p in range(2):
            sides = [jnp.concatenate([pltpu.roll(unpack(o_held[4 * p + 2 * k + s].astype(F32), 64), 192, 1), blank], axis=1) for k in range(2)]
            att[rows, 384 * p:384 * p + 384] = pair_columns(sides[0], sides[1], lane, False).astype(BF16)
    transpose_into(xt, att.at[:, 0:768], 0)

    def norm(value):
        mean = jnp.sum(value, axis=1, keepdims=True) * (1.0 / 768)
        centered = value - mean
        variance = jnp.sum(centered * centered, axis=1, keepdims=True) * (1.0 / 768)
        inverse = lax.rsqrt(variance + EPSILON)
        return centered * inverse, inverse

    def norm_back(upstream, gain, hat, inverse):
        scaled = upstream * gain
        first = jnp.sum(scaled, axis=1, keepdims=True) * (1.0 / 768)
        second = jnp.sum(scaled * hat, axis=1, keepdims=True) * (1.0 / 768)
        return inverse * (scaled - first - hat * second)

    loads[0].wait()
    hat, inverse1 = norm(tokens[...].astype(F32) + (dot(att[:, 0:768], v_out[...], NN) + row(2)))
    xhat1[...] = hat
    value = hat * row(4) + row(5)
    normed[...] = value
    output[...] = value.astype(BF16)
    transpose_into(xt, output, 768)
    loads[1].wait()

    @pl.loop(0, 4)
    def _(n):
        cols = pl.ds(pl.multiple_of(n * 768, 128), 768)
        ff, j = n // 2, lax.rem(n, 2) * 2
        bias = jnp.concatenate([vec[ff, pl.ds(8 + j, 1)], vec[ff, pl.ds(9 + j, 1)]], axis=1)
        hidden = dot(output[...], v_in[:, cols], NN) + bias
        half = 0.5 * (1.0 + lax.erf(hidden * 0.7071067811865476))
        slope[:, cols] = half + hidden * (jnp.exp(-0.5 * hidden * hidden) * 0.3989422804014327)
        act[:, cols] = (hidden * half).astype(BF16)

    transpose_into(xt, act, 1536)
    loads[2].wait()
    final[...] = normed[...] + (dot(act[...], v_back[...], NN) + row(3))
    hat2, inverse2 = norm(final[...])
    output[...] = (hat2 * row(6) + row(7)).astype(BF16)
    upstream = cotangent[...].astype(F32)
    sums(6, upstream * hat2)
    sums(7, upstream)
    gfinal = norm_back(upstream, row(6), hat2, inverse2)
    final[...] = gfinal
    gsec[...] = gfinal.astype(BF16)
    sums(3, gsec[...].astype(F32))

    @pl.loop(0, 4)
    def _(n):
        cols = pl.ds(pl.multiple_of(n * 768, 128), 768)
        ff, j = n // 2, lax.rem(n, 2) * 2
        value = (dot(gsec[...], v_back[cols], NT) * slope[:, cols]).astype(BF16)
        ghid[:, cols] = value
        total = jnp.sum(value.astype(F32), axis=0, keepdims=True)
        lanes = pl.ds(pl.multiple_of(ff * 384, 128), 384)
        small[pl.ds(8 + j, 1), lanes] = total[:, :384]
        small[pl.ds(9 + j, 1), lanes] = total[:, 384:]

    small[0:2] = jnp.zeros((2, 768), F32)
    small[12:16] = jnp.zeros((4, 768), F32)

    @pl.loop(0, 3)
    def _(n):
        cols = pl.ds(pl.multiple_of(n * 256, 128), 256)
        final[:, cols] = final[:, cols] + dot(ghid[...], v_in[cols], NT)

    hat = xhat1[...]
    upstream = final[...]
    sums(4, upstream * hat)
    sums(5, upstream)
    value = norm_back(upstream, row(4), hat, inverse1)
    gfirst[...] = value
    gbr[...] = value.astype(BF16)
    sums(2, gbr[...].astype(F32))
    normed[...] = dot(gbr[...], v_out[...], NT)
    wide = lax.broadcasted_iota(jnp.int32, (256, 256), 1)
    for p in range(2):
        part = normed[:, 384 * p:384 * p + 384]
        for k in range(2):
            turned = part if k == 0 else pltpu.roll(part, 192, 1)
            block = pltpu.roll(jnp.where(wide < 192, turned[:, :256], 0.0), 64, 1)
            for s in range(2):
                do_sent[4 * p + 2 * k + s] = pack(block[128 * s:128 * s + 128], 64).astype(BF16)
    for cp in beyond:
        cp.wait_recv()
    for n in range(2):
        @pl.loop(0, 6)
        def _(m):
            lanes = pl.ds(pl.multiple_of(m * 128, 128), 128)
            far[n, lanes] = f_held[n, :, lanes].astype(F32).T.astype(BF16)
    for cp in wires.made:
        cp.wait_send()


def middle(o_sent, tokens, cotangent, w_out, w_in, w_back, vec, ident):
    bf = lambda *shape: pltpu.VMEM(shape, BF16)
    fl = lambda *shape: pltpu.VMEM(shape, F32)
    out = lambda d, *shape: jax.ShapeDtypeStruct(shape, d)
    anywhere = pl.BlockSpec(memory_space=pl.ANY)
    wires = 16
    return pl.pallas_call(
        middle_kernel,
        out_shape=[out(BF16, 256, 768), out(F32, 256, 768), out(BF16, 4608, 256), out(BF16, 256, 768), out(BF16, 256, 3072),
                   out(BF16, 256, 768), out(BF16, 8, 96, 256), out(F32, 16, 768), out(BF16, 2, 768, 128)],
        in_specs=[vmem()] * 3 + [anywhere] * 3 + [vmem()], out_specs=[vmem()] * 9,
        scratch_shapes=[bf(8, 96, 256), bf(2, 128, 768), bf(768, 768), bf(768, 3072), bf(3072, 768),
                        fl(256, 768), fl(256, 768), fl(256, 768), fl(256, 3072), bf(256, 3072),
                        DMA((wires,)), DMA((wires,)), DMA((3,))],
        compiler_params=pltpu.CompilerParams(collective_id=ident, has_side_effects=True, vmem_limit_bytes=60 << 20),
        name="middle",
    )(o_sent, tokens, cotangent, w_out, w_in, w_back, vec)


def layer_norm(values, gain_row, shift_row):
    average = jnp.mean(values, axis=-1, keepdims=True)
    centered = values - average
    variance = jnp.mean(centered * centered, axis=-1, keepdims=True)
    return centered * lax.rsqrt(variance + EPSILON) * gain_row + shift_row


def exact_gelu(values):
    return jax.nn.gelu(values, approximate=False)


def by_group(rows, micro, front, back):
    parts = rows.reshape(micro, -1, 4, 192).transpose(2, 0, 1, 3)
    parts = jnp.pad(parts, ((0, 0), (0, 0), (0, 0), (front, back)))
    return parts.reshape((-1,) + parts.shape[2:])


def from_group(blocks, micro, front):
    rows = blocks.shape[1]
    parts = blocks.reshape(4, micro, rows, -1)[..., front:front + 192]
    return parts.transpose(1, 2, 0, 3).reshape(micro * rows, 768)


def shards(tokens, cotangent, doc_lengths, w_qkv, w_out, w_in, w_back, *vectors):
    micro, per, width = tokens.shape
    nf, cols = lax.axis_size("fsdp"), lax.axis_size("ctx") // 8
    share = width // nf
    inputs = tokens.reshape(micro * per, width)
    cube = nf == 2 and cols == 2
    if cube:
        q_held, kv_held, full_qkv, full_out, full_in, full_back, sides, near = project(inputs, (w_qkv, w_out, w_in, w_back), vectors, 1)
        kv_held = kv_held.reshape(-1, 384)
        mixed, mixed_t, log_total = attend_forward(doc_lengths, q_held, kv_held, cols, True)
        output, grad_first, xt, grad_branch, grad_hidden, grad_second, do_sent, small, far = middle(
            mixed, inputs, cotangent.reshape(inputs.shape), full_out, full_in, full_back, sides, 3)
        grads, late, input_grad, sums = reduce_all(
            doc_lengths, full_qkv, grad_first, near, far, xt, grad_branch, grad_hidden, grad_second, small, do_sent, q_held, kv_held,
            mixed_t, log_total, 5)
        g_qkv, g_out, g_in, g_back, output, input_grad, *rows = widen(grads.reshape(2, share, 3456), late, output, input_grad, sums)
        return (output.reshape(tokens.shape), input_grad.reshape(tokens.shape), g_qkv, g_out, g_in, g_back.reshape(4 * share, width)) + tuple(rows)
    tiny = jnp.concatenate(vectors).reshape(8, -1)
    full_qkv, full_out, full_in, full_back, tinies = gather_weights((w_qkv, w_out, w_in, w_back), tiny, nf, cols)
    tinies = tinies.reshape(nf, -1).astype(F32)
    named, at = [], 0
    for vector in vectors:
        size = vector.shape[0]
        named.append(tinies[:, at:at + size].reshape(-1))
        at += size
    b_query, b_value, b_out, b_in, b_back, gain_one, shift_one, gain_two, shift_two = named
    joined = jnp.dot(inputs, full_qkv, preferred_element_type=F32)
    bias = jnp.concatenate([b_query, jnp.zeros_like(b_query), b_value])
    joined = (joined + bias).astype(BF16)
    q_sent = by_group(joined[:, :width], micro, 0, 64)
    kv_sent = jnp.concatenate([by_group(joined[:, width:2 * width], micro, 0, 0), by_group(joined[:, 2 * width:], micro, 0, 0)], axis=2)
    q_held, kv_held = spread(q_sent, kv_sent, cols, 2)
    q_held = q_held.reshape(8 * per, 256)
    kv_held = kv_held.reshape(-1, 384)
    mixed, mixed_t, log_total = attend_forward(doc_lengths, q_held, kv_held, cols)
    (back,) = swap([mixed.reshape(8, per, 256)], cols, 3)
    attended = from_group(back, micro, 64)
    first_sum = inputs.astype(F32) + (jnp.dot(attended, full_out, preferred_element_type=F32) + b_out)
    normed = layer_norm(first_sum, gain_one, shift_one)
    normed_low = normed.astype(BF16)
    hidden = jnp.dot(normed_low, full_in, preferred_element_type=F32) + b_in
    activated = exact_gelu(hidden).astype(BF16)
    final_sum = normed + (jnp.dot(activated, full_back, preferred_element_type=F32) + b_back)
    output = layer_norm(final_sum, gain_two, shift_two).astype(BF16)

    upstream = cotangent.reshape(micro * per, width).astype(F32)
    grad_final, g_gain_two, g_shift_two = jax.vjp(layer_norm, final_sum, gain_two, shift_two)[1](upstream)
    grad_second = grad_final.astype(BF16)
    g_back_bias = jnp.sum(grad_second.astype(F32), axis=0)
    grad_activated = jnp.einsum("rm,km->rk", grad_second, full_back, preferred_element_type=F32)
    grad_hidden = jax.vjp(exact_gelu, hidden)[1](grad_activated)[0].astype(BF16)
    g_in_bias = jnp.sum(grad_hidden.astype(F32), axis=0)
    grad_normed = grad_final + jnp.einsum("rf,mf->rm", grad_hidden, full_in, preferred_element_type=F32)
    grad_first, g_gain_one, g_shift_one = jax.vjp(layer_norm, first_sum, gain_one, shift_one)[1](grad_normed)
    grad_branch = grad_first.astype(BF16)
    g_out_bias = jnp.sum(grad_branch.astype(F32), axis=0)
    grad_attended = jnp.einsum("rm,km->rk", grad_branch, full_out, preferred_element_type=F32).astype(BF16)
    (do_held,) = swap([by_group(grad_attended, micro, 64, 0)], cols, 4)
    dq, dkv = attend_backward(doc_lengths, q_held, kv_held, do_held.reshape(8 * per, 256), mixed_t, log_total, cols)
    dq_own, dkv_own = collect(dq.reshape(8, per, 256), dkv.reshape(8 * cols, per, 384), cols, 5)
    grad_joined = jnp.concatenate(
        [from_group(dq_own, micro, 0), from_group(dkv_own, micro, 0), from_group(dkv_own, micro, 192)], axis=1)
    g_query_bias = jnp.sum(grad_joined[:, :width].astype(F32), axis=0)
    g_value_bias = jnp.sum(grad_joined[:, 2 * width:].astype(F32), axis=0)
    input_grad = grad_first + jnp.einsum("rc,mc->rm", grad_joined, full_qkv, preferred_element_type=F32)

    def halves(left, right):
        blocks = right.shape[1] // 384
        return jnp.einsum("rm,rhc->hmc", left, right.reshape(-1, blocks, 384), preferred_element_type=F32).astype(BF16)

    back_grads = jnp.einsum("rk,rm->km", activated, grad_second, preferred_element_type=F32).astype(BF16)
    back_grads = back_grads.reshape(nf, 4, share, 2, 384).transpose(1, 3, 0, 2, 4).reshape(8, width, 384)
    grads = jnp.concatenate(
        [halves(inputs, grad_joined), halves(attended, grad_branch), halves(normed_low, grad_hidden), back_grads])
    grads = grads.reshape(2, 4, 3, nf, cols, share // cols, 384)
    small = (g_query_bias, g_value_bias, g_out_bias, g_in_bias, g_back_bias, g_gain_one, g_shift_one, g_gain_two, g_shift_two)
    small = jnp.concatenate([x.reshape(nf, -1) for x in small], axis=1).reshape(nf, 8, -1)
    owned, small_owned = reduce_grads(grads, small, nf, cols, 6)
    owned = owned.transpose(0, 1, 3, 2, 4, 5).reshape(24, share, 384)

    def columns(first, last):
        return owned[first:last].transpose(1, 0, 2).reshape(share, -1).astype(F32)

    g_back = owned[16:].reshape(4, 2, share, 384).transpose(0, 2, 1, 3).reshape(4 * share, width).astype(F32)
    small_owned = small_owned.reshape(-1)
    small_grads, at = [], 0
    for vector in vectors:
        small_grads.append(small_owned[at:at + vector.shape[0]])
        at += vector.shape[0]
    return (output.reshape(tokens.shape), input_grad.reshape(tokens.shape), columns(0, 6), columns(6, 8), columns(8, 16), g_back) + tuple(small_grads)


def solution(mesh):
    rows, flat = P("fsdp", "ctx", None), P("fsdp", None)
    return jax.shard_map(
        shards,
        mesh=mesh,
        in_specs=(rows, rows, flat) + (flat,) * 4 + (P("fsdp"),) * 9,
        out_specs=(rows, rows) + (flat,) * 4 + (P("fsdp"),) * 9,
        check_vma=False,
    )
```

```python
import functools

import jax
import jax.numpy as jnp
from jax import lax
from jax.experimental import pallas as pl
from jax.experimental.pallas import tpu as pltpu
from jax.sharding import PartitionSpec as P

MESH = pl.DeviceIdType.MESH
DMA = pltpu.SemaphoreType.DMA
F32, BF16 = jnp.float32, jnp.bfloat16
EPSILON = 1e-12

def place(cols):
    index = lax.axis_index("ctx")
    return index // (2 * cols), lax.rem(index // 2, cols), lax.rem(index, 2), lax.axis_index("fsdp")

def device(a, b, c, f, cols):
    return {"ctx": (a * cols + b) * 2 + c, "fsdp": f}

def meet(peers):
    barrier = pltpu.get_barrier_semaphore()
    for peer in peers:
        pl.semaphore_signal(barrier, inc=1, device_id=peer, device_id_type=MESH)
    pl.semaphore_wait(barrier, len(peers))

def remote(source, target, send, recv, peer):
    return pltpu.make_async_remote_copy(
        src_ref=source, dst_ref=target, send_sem=send, recv_sem=recv, device_id=peer, device_id_type=MESH)

def gather_kernel(nf, cols, count, *refs):
    shards, tiny, fulls, tiny_out = refs[:count], refs[count], refs[count+1:2*count+1], refs[2*count+1]
    local_sem, s1, r1, s2, r2, s3, r3, st, rt = refs[2*count+2:]
    a, b, c, f = place(cols)
    other = 1 - c
    fpeers = [device(a, b, c, lax.rem(f + j, nf), cols) for j in range(1, nf)]
    bpeers = [device(a, lax.rem(b + k, cols), c, f, cols) for k in range(1, cols)]
    sibling = device(a, b, other, f, cols)
    meet(fpeers + bpeers + [sibling])

    def view(w, owner, bb, cc, base=0):
        rows, wide = shards[w].shape
        part, half = rows // cols, wide // 2
        return fulls[w].at[pl.ds(pl.multiple_of(owner * rows + bb * part, 8), part), pl.ds(pl.multiple_of(cc * half, 128), half)]

    waits = []
    for j in range(1, nf):
        cp = remote(tiny, tiny_out.at[f], st.at[j - 1], rt.at[j - 1], fpeers[j - 1])
        cp.start()
        waits.append(cp)
    locals_ = [pltpu.make_async_copy(tiny, tiny_out.at[f], local_sem.at[count])]
    locals_[0].start()
    first = {}
    for w in range(count):
        rows, wide = shards[w].shape
        part, half = rows // cols, wide // 2
        mine = shards[w].at[pl.ds(pl.multiple_of(b * part, 8), part), pl.ds(pl.multiple_of(c * half, 128), half)]
        for j in range(1, nf):
            cp = remote(mine, view(w, f, b, c), s1.at[w, j - 1], r1.at[w, j - 1], fpeers[j - 1])
            cp.start()
            first[w, j] = cp
    for w in range(count):
        rows = shards[w].shape[0]
        cp = pltpu.make_async_copy(shards[w], fulls[w].at[pl.ds(pl.multiple_of(f * rows, 8), rows)], local_sem.at[w])
        cp.start()
        locals_.append(cp)
    second, third = {}, []
    for w in range(count):
        for j in range(1, nf):
            owner = lax.rem(f + nf - j, nf)
            first[w, j].wait_recv()
            piece = view(w, owner, b, c)
            for k in range(1, cols):
                slot = (j - 1) * (cols - 1) + k - 1
                cp = remote(piece, piece, s2.at[w, slot], r2.at[w, slot], bpeers[k - 1])
                cp.start()
                second[w, j, k] = cp
            cp = remote(piece, piece, s3.at[w, (j - 1) * cols], r3.at[w, (j - 1) * cols], sibling)
            cp.start()
            third.append(cp)
    for w in range(count):
        for j in range(1, nf):
            owner = lax.rem(f + nf - j, nf)
            for k in range(1, cols):
                second[w, j, k].wait_recv()
                piece = view(w, owner, lax.rem(b + cols - k, cols), c)
                cp = remote(piece, piece, s3.at[w, (j - 1) * cols + k], r3.at[w, (j - 1) * cols + k], sibling)
                cp.start()
                third.append(cp)
    for cp in third:
        cp.wait_recv()
    for cp in waits:
        cp.wait()
    for cp in list(first.values()) + list(second.values()) + third:
        cp.wait_send()
    for cp in locals_:
        cp.wait()

def gather_weights(shards, tiny, nf, cols):
    count = len(shards)
    any_spec = pl.BlockSpec(memory_space=pl.ANY)
    dma = pltpu.SemaphoreType.DMA
    return pl.pallas_call(
        functools.partial(gather_kernel, nf, cols, count),
        out_shape=[jax.ShapeDtypeStruct((s.shape[0] * nf, s.shape[1]), s.dtype) for s in shards]
        + [jax.ShapeDtypeStruct((nf,) + tiny.shape, tiny.dtype)],
        in_specs=[pl.BlockSpec(memory_space=pltpu.VMEM)] * (count + 1),
        out_specs=[any_spec] * (count + 1),
        scratch_shapes=[dma((count + 1,)), dma((count, nf - 1)), dma((count, nf - 1)),
                        dma((count, (nf - 1) * (cols - 1))), dma((count, (nf - 1) * (cols - 1))),
                        dma((count, (nf - 1) * cols)), dma((count, (nf - 1) * cols)),
                        dma((nf - 1,)), dma((nf - 1,))],
        compiler_params=pltpu.CompilerParams(collective_id=1, has_side_effects=True, vmem_limit_bytes=32 << 20),
        name="gather_weights",
    )(*shards, tiny)

def octet(a, b, c, f, cols):
    me = a * 2 + c
    out = []
    for k in range(1, 8):
        other = lax.rem(me + k, 8)
        out.append((other, device(other // 2, b, lax.rem(other, 2), f, cols)))
    return me, out

def swap_kernel(cols, count, *refs):
    sources, targets = refs[:count], refs[count:2 * count]
    send, recv, here = refs[2 * count:]
    a, b, c, f = place(cols)
    me, peers = octet(a, b, c, f, cols)
    meet([p for _, p in peers])
    copies = []
    for k, (other, peer) in enumerate(peers):
        for i in range(count):
            cp = remote(sources[i].at[other], targets[i].at[me], send.at[i, k], recv.at[i, k], peer)
            cp.start()
            copies.append(cp)
    for i in range(count):
        cp = pltpu.make_async_copy(sources[i].at[me], targets[i].at[me], here.at[i])
        cp.start()
        copies.append(cp)
    for cp in copies:
        cp.wait()

def swap(arrays, cols, ident):
    count = len(arrays)
    return pl.pallas_call(
        functools.partial(swap_kernel, cols, count),
        out_shape=[jax.ShapeDtypeStruct(x.shape, x.dtype) for x in arrays],
        in_specs=[vmem()] * count, out_specs=[vmem()] * count,
        scratch_shapes=[DMA((count, 7)), DMA((count, 7)), DMA((count,))],
        compiler_params=pltpu.CompilerParams(collective_id=ident, has_side_effects=True, vmem_limit_bytes=16 << 20),
        name="swap",
    )(*arrays)

def spread_kernel(cols, q, kv, qg, full, sq, rq, sk, rk, s2, r2, here):
    a, b, c, f = place(cols)
    me, peers = octet(a, b, c, f, cols)
    bpeers = [device(a, lax.rem(b + k, cols), c, f, cols) for k in range(1, cols)]
    meet([p for _, p in peers] + bpeers)

    def slot(block, bb):
        return (block // 2 * cols + bb) * 2 + lax.rem(block, 2)

    first = []
    for k, (other, peer) in enumerate(peers):
        cp = remote(kv.at[other], full.at[slot(me, b)], sk.at[k], rk.at[k], peer)
        cp.start()
        first.append(cp)
    own = pltpu.make_async_copy(kv.at[me], full.at[slot(me, b)], here.at[0])
    own.start()
    ownq = pltpu.make_async_copy(q.at[me], qg.at[me], here.at[1])
    ownq.start()
    second = []
    for k, peer in enumerate(bpeers):
        cp = remote(kv.at[me], full.at[slot(me, b)], s2.at[7, k], r2.at[7, k], peer)
        cp.start()
        second.append(cp)
    third = []
    for k, (other, peer) in enumerate(peers):
        cp = remote(q.at[other], qg.at[me], sq.at[k], rq.at[k], peer)
        cp.start()
        third.append(cp)
    for k in range(7):
        first[k].wait_recv()
        source = lax.rem(me + 8 - (k + 1), 8)
        piece = full.at[slot(source, b)]
        for m, peer in enumerate(bpeers):
            cp = remote(piece, piece, s2.at[k, m], r2.at[k, m], peer)
            cp.start()
            second.append(cp)
    for cp in first:
        cp.wait_send()
    for cp in second + third:
        cp.wait()
    own.wait()
    ownq.wait()

def spread(q, kv, cols, ident):
    return pl.pallas_call(
        functools.partial(spread_kernel, cols),
        out_shape=[jax.ShapeDtypeStruct(q.shape, q.dtype), jax.ShapeDtypeStruct((8 * cols,) + kv.shape[1:], kv.dtype)],
        in_specs=[vmem()] * 2, out_specs=[vmem()] * 2,
        scratch_shapes=[DMA((7,))] * 4 + [DMA((8, max(cols - 1, 1)))] * 2 + [DMA((2,))],
        compiler_params=pltpu.CompilerParams(collective_id=ident, has_side_effects=True, vmem_limit_bytes=16 << 20),
        name="spread",
    )(q, kv)

def collect_kernel(cols, dq, dkv, dqo, dkvo, rbuf, total, sq, rq, sk, rk, s2, r2, here):
    a, b, c, f = place(cols)
    me, peers = octet(a, b, c, f, cols)
    bpeers = [(lax.rem(b + k, cols), device(a, lax.rem(b + k, cols), c, f, cols)) for k in range(1, cols)]
    meet([p for _, p in peers] + [p for _, p in bpeers])

    def slot(block, bb):
        return (block // 2 * cols + bb) * 2 + lax.rem(block, 2)

    order = [other for other, _ in peers] + [me]
    first = {}
    for n, block in enumerate(order):
        for k, (bb, peer) in enumerate(bpeers):
            cp = remote(dkv.at[slot(block, bb)], rbuf.at[k, n], s2.at[k, n], r2.at[k, n], peer)
            cp.start()
            first[k, n] = cp
    rest = []
    for k, (other, peer) in enumerate(peers):
        cp = remote(dq.at[other], dqo.at[me], sq.at[k], rq.at[k], peer)
        cp.start()
        rest.append(cp)
    own = pltpu.make_async_copy(dq.at[me], dqo.at[me], here.at[0])
    own.start()
    for n, block in enumerate(order):
        value = dkv[slot(block, b)].astype(F32)
        for k in range(cols - 1):
            first[k, n].wait_recv()
            value = value + rbuf[k, n].astype(F32)
        if n < 7:
            total[n] = value.astype(BF16)
            cp = remote(total.at[n], dkvo.at[me], sk.at[n], rk.at[n], peers[n][1])
            cp.start()
            rest.append(cp)
        else:
            dkvo[me] = value.astype(BF16)
    for cp in first.values():
        cp.wait_send()
    for cp in rest:
        cp.wait()
    own.wait()

def collect(dq, dkv, cols, ident):
    block = dkv.shape[1:]
    return pl.pallas_call(
        functools.partial(collect_kernel, cols),
        out_shape=[jax.ShapeDtypeStruct(dq.shape, dq.dtype), jax.ShapeDtypeStruct((8,) + block, dkv.dtype)],
        in_specs=[vmem()] * 2, out_specs=[vmem()] * 2,
        scratch_shapes=[pltpu.VMEM((max(cols - 1, 1), 8) + block, BF16), pltpu.VMEM((7,) + block, BF16)]
        + [DMA((7,))] * 4 + [DMA((max(cols - 1, 1), 8))] * 2 + [DMA((1,))],
        compiler_params=pltpu.CompilerParams(collective_id=ident, has_side_effects=True, vmem_limit_bytes=24 << 20),
        name="collect",
    )(dq, dkv)

def reduce_kernel(nf, cols, parts, grads, small, out, small_out, *refs):
    own, core_in, f_in, b_in, f_in2, b_in2, a_in, v_core, v_sum, v_f, v_b, v_a = refs[:12]
    load, sc, rc, s1, r1, s2, r2, s3, r3, s4, r4, s5, r5, s6, r6, sv, rv = refs[12:]
    a, b, c, f = place(cols)
    rows = grads.shape[5]
    fpeers = [(lax.rem(f + j, nf), device(a, b, c, lax.rem(f + j, nf), cols)) for j in range(1, nf)]
    bpeers = [(lax.rem(b + k, cols), device(a, lax.rem(b + k, cols), c, f, cols)) for k in range(1, cols)]
    apeers = [(lax.rem(a + k, 4), device(lax.rem(a + k, 4), b, c, f, cols)) for k in range(1, 4)]
    sibling = device(a, b, 1 - c, f, cols)
    meet([p for _, p in fpeers + bpeers + apeers] + [sibling])
    vector = remote(small, v_core, sv.at[0], rv.at[0], sibling)
    vector.start()
    order = [2, 1, 3, 0]
    dest = {k: lax.rem(a + k, 4) for k in range(4)}
    by_f = {k: k in (1, 2) for k in range(4)}
    loads, cores = {}, {}
    for k in order:
        for i in range(parts):
            cp = pltpu.make_async_copy(grads.at[c, dest[k], i], own.at[k, i], load.at[k, i])
            cp.start()
            loads[k, i] = cp
            cp = remote(grads.at[1 - c, dest[k], i], core_in.at[k, i], sc.at[k, i], rc.at[k, i], sibling)
            cp.start()
            cores[k, i] = cp
    one, two, three = {}, {}, {}
    vec = {}
    vector.wait_recv()
    v_sum[...] = small[...] + v_core[...]
    for j, (ff, peer) in enumerate(fpeers):
        vec[0, j] = remote(v_sum.at[ff], v_f.at[j], sv.at[1 + j], rv.at[1 + j], peer)
        vec[0, j].start()
    for k in order:
        for i in range(parts):
            loads[k, i].wait()
            cores[k, i].wait_recv()

            @pl.loop(0, nf * cols)
            def _(n):
                ff, bb = n // cols, lax.rem(n, cols)
                own[k, i, ff, bb] = (own[k, i, ff, bb].astype(F32) + core_in[k, i, ff, bb].astype(F32)).astype(BF16)

            if by_f[k]:
                for j, (ff, peer) in enumerate(fpeers):
                    cp = remote(own.at[k, i, ff], f_in.at[k, i, j], s1.at[k, i, j], r1.at[k, i, j], peer)
                    cp.start()
                    one[k, i, j] = cp
            else:
                for m, (bb, peer) in enumerate(bpeers):
                    for ff in range(nf):
                        cp = remote(own.at[k, i, ff, bb], b_in.at[k, i, m, ff], s1.at[k, i, m * nf + ff], r1.at[k, i, m * nf + ff], peer)
                        cp.start()
                        one[k, i, m * nf + ff] = cp
    value = v_sum[f]
    for j in range(nf - 1):
        vec[0, j].wait_recv()
        value = value + v_f[j]
    v_b[b] = value
    for m, (bb, peer) in enumerate(bpeers):
        vec[1, m] = remote(v_b.at[b], v_b.at[b], sv.at[nf + m], rv.at[nf + m], peer)
        vec[1, m].start()
    for k in order:
        for i in range(parts):
            if by_f[k]:
                for j in range(nf - 1):
                    one[k, i, j].wait_recv()

                @pl.loop(0, cols)
                def _(bb):
                    value = own[k, i, f, bb].astype(F32)
                    for j in range(nf - 1):
                        value = value + f_in[k, i, j, bb].astype(F32)
                    own[k, i, f, bb] = value.astype(BF16)

                for m, (bb, peer) in enumerate(bpeers):
                    cp = remote(own.at[k, i, f, bb], b_in2.at[k, i, m], s2.at[k, i, m], r2.at[k, i, m], peer)
                    cp.start()
                    two[k, i, m] = cp
            else:
                for m in range(cols - 1):
                    for ff in range(nf):
                        one[k, i, m * nf + ff].wait_recv()

                @pl.loop(0, nf)
                def _(ff):
                    value = own[k, i, ff, b].astype(F32)
                    for m in range(cols - 1):
                        value = value + b_in[k, i, m, ff].astype(F32)
                    own[k, i, ff, b] = value.astype(BF16)

                for j, (ff, peer) in enumerate(fpeers):
                    cp = remote(own.at[k, i, ff, b], f_in2.at[k, i, j], s2.at[k, i, j], r2.at[k, i, j], peer)
                    cp.start()
                    two[k, i, j] = cp
    for m in range(cols - 1):
        vec[1, m].wait_recv()
    value = v_b[0]
    for m in range(1, cols):
        value = value + v_b[m]
    v_a[a] = value
    for k in range(1, 4):
        vec[2, k] = remote(v_a.at[a], v_a.at[a], sv.at[nf + cols + k - 2], rv.at[nf + cols + k - 2], apeers[k - 1][1])
        vec[2, k].start()
    for k in order:
        for i in range(parts):
            value = own[k, i, f, b].astype(F32)
            if by_f[k]:
                for m in range(cols - 1):
                    two[k, i, m].wait_recv()
                    value = value + b_in2[k, i, m].astype(F32)
            else:
                for j in range(nf - 1):
                    two[k, i, j].wait_recv()
                    value = value + f_in2[k, i, j].astype(F32)
            if k != 0:
                own[k, i, f, b] = value.astype(BF16)
                cp = remote(own.at[k, i, f, b], a_in.at[k - 1, i], s3.at[k - 1, i], r3.at[k - 1, i], apeers[k - 1][1])
                cp.start()
                three[k, i] = cp
            else:
                own[k, i, f, b] = value.astype(BF16)
    for k in range(1, 4):
        vec[2, k].wait_recv()
    small_out[...] = v_a[0] + v_a[1] + v_a[2] + v_a[3]
    four, five, six = {}, {}, {}

    def piece(aa, bb, cc, i):
        return out.at[cc, aa, bb, i]

    pending = []
    for i in range(parts):
        value = own[0, i, f, b].astype(F32)
        for k in range(1, 4):
            three[k, i].wait_recv()
            value = value + a_in[k - 1, i].astype(F32)
        out[c, a, b, i] = value.astype(BF16)
        mine = piece(a, b, c, i)
        for k in (2, 1, 3):
            cp = remote(mine, mine, s4.at[k - 1, i], r4.at[k - 1, i], apeers[k - 1][1])
            cp.start()
            four[k, i] = cp
        for m, (bb, peer) in enumerate(bpeers):
            cp = remote(mine, mine, s5.at[0, i, m], r5.at[0, i, m], peer)
            cp.start()
            five[0, i, m] = cp
        cp = remote(mine, mine, s6.at[0, i, 0], r6.at[0, i, 0], sibling)
        cp.start()
        six[0, i, 0] = cp
    for i in range(parts):
        for k in (1, 3, 2):
            four[k, i].wait_recv()
            got = piece(lax.rem(a + 4 - k, 4), b, c, i)
            for m, (bb, peer) in enumerate(bpeers):
                cp = remote(got, got, s5.at[k, i, m], r5.at[k, i, m], peer)
                cp.start()
                five[k, i, m] = cp
            cp = remote(got, got, s6.at[k, i, 0], r6.at[k, i, 0], sibling)
            cp.start()
            six[k, i, 0] = cp
    for i in range(parts):
        for k in (0, 1, 3, 2):
            for m in range(cols - 1):
                five[k, i, m].wait_recv()
                got = piece(lax.rem(a + 4 - k, 4), lax.rem(b + cols - (m + 1), cols), c, i)
                cp = remote(got, got, s6.at[k, i, m + 1], r6.at[k, i, m + 1], sibling)
                cp.start()
                six[k, i, m + 1] = cp
    for cp in six.values():
        cp.wait_recv()
    vector.wait_send()
    for group in (cores, one, two, three, four, five, six, vec):
        for cp in group.values():
            cp.wait_send()

def reduce_grads(grads, small, nf, cols, ident):
    _, _, parts, _, _, rows, width = grads.shape
    block = (rows, width)
    m = max(cols - 1, 1)
    n = max((cols - 1) * nf, nf - 1)
    return pl.pallas_call(
        functools.partial(reduce_kernel, nf, cols, parts),
        out_shape=[jax.ShapeDtypeStruct((2, 4, cols, parts) + block, BF16), jax.ShapeDtypeStruct(small.shape[1:], F32)],
        in_specs=[pl.BlockSpec(memory_space=pl.ANY), vmem()], out_specs=[vmem()] * 2,
        scratch_shapes=[pltpu.VMEM((4, parts, nf, cols) + block, BF16), pltpu.VMEM((4, parts, nf, cols) + block, BF16),
                        pltpu.VMEM((4, parts, nf - 1, cols) + block, BF16), pltpu.VMEM((4, parts, m, nf) + block, BF16),
                        pltpu.VMEM((4, parts, nf - 1) + block, BF16), pltpu.VMEM((4, parts, m) + block, BF16),
                        pltpu.VMEM((3, parts) + block, BF16),
                        pltpu.VMEM(small.shape, F32), pltpu.VMEM(small.shape, F32), pltpu.VMEM((nf - 1,) + small.shape[1:], F32),
                        pltpu.VMEM((cols,) + small.shape[1:], F32), pltpu.VMEM((4,) + small.shape[1:], F32),
                        DMA((4, parts)), DMA((4, parts)), DMA((4, parts)), DMA((4, parts, n)), DMA((4, parts, n)),
                        DMA((4, parts, max(m, nf - 1))), DMA((4, parts, max(m, nf - 1))),
                        DMA((3, parts)), DMA((3, parts)), DMA((3, parts)), DMA((3, parts)),
                        DMA((4, parts, m)), DMA((4, parts, m)), DMA((4, parts, cols)), DMA((4, parts, cols)),
                        DMA((nf + cols + 2,)), DMA((nf + cols + 2,))],
        compiler_params=pltpu.CompilerParams(collective_id=ident, has_side_effects=True, vmem_limit_bytes=56 << 20),
        name="reduce_grads",
    )(grads, small)
KB = 256
SPAN = 256
MASKED = -1e30

def dot(x, y, dims):
    return lax.dot_general(x, y, (dims, ((), ())), preferred_element_type=F32)

NT = ((1,), (1,))
NN = ((1,), (0,))
TN = ((0,), (0,))

def bounds(lens, stream):
    ends, total = [], 0
    for j in range(4):
        total = total + lens[stream, j]
        ends.append(total)
    return ends

def doc_range(pos, ends):
    start = jnp.where(pos >= ends[0], ends[0], 0)
    stop = jnp.where(pos < ends[0], ends[0], ends[3])
    for j in (1, 2):
        start = jnp.where(pos >= ends[j], ends[j], start)
    for j in (2, 1, 0):
        stop = jnp.where(pos < ends[j], ends[j], stop)
    return start, stop

def block_range(base, ends):
    low, _ = doc_range(base, ends)
    _, high = doc_range(base + (SPAN - 1), ends)
    return low // KB, (high + (KB - 1)) // KB

def lane_head(shape, shift):
    lane = lax.broadcasted_iota(jnp.int32, shape, 1)
    return (lane - shift) // 64

def forward_kernel(cols, packed, lens, q_ref, kv_ref, o_ref, ot_ref, lse_ref, qm, vt, acc):
    index = lax.axis_index("ctx")
    b, c = lax.rem(index // 2, cols), lax.rem(index, 2)
    ends = bounds(lens, c)
    total = kv_ref.shape[0]

    @pl.loop(0, total // KB)
    def _(n):
        rows = pl.ds(pl.multiple_of(n * KB, KB), KB)
        vt[:, rows] = kv_ref[rows, 128:384].astype(F32).T.astype(BF16)

    @pl.loop(0, 4)
    def _(stripe):
        base = SPAN * (stripe * cols + b)
        rows = pl.ds(pl.multiple_of(stripe * SPAN, SPAN), SPAN)
        head = lane_head((SPAN, 256), 0)
        if packed:
            q = jnp.concatenate([unpack(q_ref[stripe * 2 + i].astype(F32), 0) for i in range(2)], axis=0) * 0.125
        else:
            q = q_ref[rows].astype(F32) * 0.125
        for h in range(3):
            qm[h] = jnp.where(head == h, q, 0.0).astype(BF16)
        qpos = base + lax.broadcasted_iota(jnp.int32, (1, SPAN), 1)
        start, stop = doc_range(qpos, ends)
        low, high = block_range(base, ends)
        acc[...] = jnp.zeros_like(acc)

        def step(n, state):
            krows = pl.ds(pl.multiple_of(n * KB, KB), KB)
            keys = kv_ref[krows, 0:256]
            kpos = n * KB + lax.broadcasted_iota(jnp.int32, (KB, 1), 0)
            allowed = (kpos >= start) & (kpos < stop)
            out = []
            for h in range(3):
                top, tot = state[h]
                s = jnp.where(allowed, dot(keys, qm[h], NT), MASKED)
                new = jnp.maximum(top, jnp.max(s, axis=0, keepdims=True))
                p = jnp.exp(s - new)
                scale = jnp.exp(top - new)
                hrows = pl.ds(64 * (h + 1), 64)
                acc[hrows] = acc[hrows] * scale + dot(vt[hrows, krows], p.astype(BF16), NN)
                out.append((new, tot * scale + jnp.sum(p, axis=0, keepdims=True)))
            return tuple(out)

        first = tuple((jnp.full((1, SPAN), MASKED, F32), jnp.zeros((1, SPAN), F32)) for _ in range(3))
        final = lax.fori_loop(low, high, step, first)
        for h in range(3):
            top, tot = final[h]
            hrows = pl.ds(64 * (h + 1), 64)
            acc[hrows] = acc[hrows] * (1.0 / tot)
            lse_ref[stripe, pl.ds(h, 1)] = top + jnp.log(tot)
        ot_ref[stripe] = acc[...]
        value = acc[...].T
        if packed:
            for i in range(2):
                o_ref[stripe * 2 + i] = pack(value[128 * i:128 * i + 128], 64).astype(BF16)
        else:
            o_ref[rows] = value.astype(BF16)

def vmem():
    return pl.BlockSpec(memory_space=pltpu.VMEM)

def attend_forward(lens, q, kv, cols, packed=False):
    total = kv.shape[0]
    return pl.pallas_call(
        functools.partial(forward_kernel, cols, packed),
        out_shape=[jax.ShapeDtypeStruct(q.shape, BF16), jax.ShapeDtypeStruct((4, 256, SPAN), F32),
                   jax.ShapeDtypeStruct((4, 8, SPAN), F32)],
        in_specs=[pl.BlockSpec(memory_space=pltpu.SMEM), vmem(), vmem()],
        out_specs=[vmem()] * 3,
        scratch_shapes=[pltpu.VMEM((3, SPAN, 256), BF16), pltpu.VMEM((256, total), BF16), pltpu.VMEM((256, SPAN), F32)],
        compiler_params=pltpu.CompilerParams(vmem_limit_bytes=62 << 20),
        name="attend_forward",
    )(lens, q, kv)

def backward_kernel(cols, lens, q_ref, kv_ref, do_ref, ot_ref, lse_ref, dq_ref, dkv_ref, qm, dm, kt, dk, dv, acc):
    index = lax.axis_index("ctx")
    b, c = lax.rem(index // 2, cols), lax.rem(index, 2)
    ends = bounds(lens, c)
    total = kv_ref.shape[0]

    @pl.loop(0, total // KB)
    def _(n):
        rows = pl.ds(pl.multiple_of(n * KB, KB), KB)
        kt[:, rows] = kv_ref[rows, 0:256].astype(F32).T.astype(BF16)
        dk[rows] = jnp.zeros((KB, 256), F32)
        dv[rows] = jnp.zeros((KB, 256), F32)

    @pl.loop(0, 4)
    def _(stripe):
        base = SPAN * (stripe * cols + b)
        rows = pl.ds(pl.multiple_of(stripe * SPAN, SPAN), SPAN)
        head = lane_head((SPAN, 256), 0)
        headv = lane_head((SPAN, 256), 64)
        q = q_ref[rows].astype(F32) * 0.125
        grad = do_ref[rows].astype(F32)
        for h in range(3):
            qm[h] = jnp.where(head == h, q, 0.0).astype(BF16)
            dm[h] = jnp.where(headv == h, grad, 0.0).astype(BF16)
        prod = grad.T * ot_ref[stripe]
        deltas = [jnp.sum(prod[64 * (h + 1):64 * (h + 2)], axis=0, keepdims=True) for h in range(3)]
        lses = [lse_ref[stripe, pl.ds(h, 1)] for h in range(3)]
        qpos = base + lax.broadcasted_iota(jnp.int32, (1, SPAN), 1)
        start, stop = doc_range(qpos, ends)
        low, high = block_range(base, ends)
        acc[...] = jnp.zeros_like(acc)

        @pl.loop(low, high)
        def _(n):
            krows = pl.ds(pl.multiple_of(n * KB, KB), KB)
            keys = kv_ref[krows, 0:256]
            vals = kv_ref[krows, 128:384]
            kpos = n * KB + lax.broadcasted_iota(jnp.int32, (KB, 1), 0)
            allowed = (kpos >= start) & (kpos < stop)
            newk, newv = dk[krows], dv[krows]
            for h in range(3):
                s = jnp.where(allowed, dot(keys, qm[h], NT), MASKED)
                p = jnp.exp(s - lses[h])
                gp = dot(vals, dm[h], NT)
                ds = (p * (gp - deltas[h])).astype(BF16)
                newv = newv + dot(p.astype(BF16), dm[h], NN)
                newk = newk + dot(ds, qm[h], NN)
                hrows = pl.ds(64 * h, 64)
                acc[hrows] = acc[hrows] + dot(kt[hrows, krows], ds, NN)
            dk[krows] = newk
            dv[krows] = newv

        dq_ref[rows] = (acc[...] * 0.125).T.astype(BF16)

    @pl.loop(0, total // KB)
    def _(n):
        rows = pl.ds(pl.multiple_of(n * KB, KB), KB)
        dkv_ref[rows, 0:128] = dk[rows, 0:128].astype(BF16)
        dkv_ref[rows, 128:256] = (dk[rows, 128:256] + dv[rows, 0:128]).astype(BF16)
        dkv_ref[rows, 256:384] = dv[rows, 128:256].astype(BF16)

def attend_backward(lens, q, kv, do, ot, lse, cols):
    total = kv.shape[0]
    return pl.pallas_call(
        functools.partial(backward_kernel, cols),
        out_shape=[jax.ShapeDtypeStruct(q.shape, BF16), jax.ShapeDtypeStruct(kv.shape, BF16)],
        in_specs=[pl.BlockSpec(memory_space=pltpu.SMEM)] + [vmem()] * 5,
        out_specs=[vmem()] * 2,
        scratch_shapes=[pltpu.VMEM((3, SPAN, 256), BF16), pltpu.VMEM((3, SPAN, 256), BF16), pltpu.VMEM((256, total), BF16),
                        pltpu.VMEM((total, 256), F32), pltpu.VMEM((total, 256), F32), pltpu.VMEM((256, SPAN), F32)],
        compiler_params=pltpu.CompilerParams(vmem_limit_bytes=40 << 20),
        name="attend_backward",
    )(lens, q, kv, do, ot, lse)


def pack(block, base):
    free = 0 if base else 192
    lane = lax.broadcasted_iota(jnp.int32, (32, 256), 1)
    tail = block[96:128]
    rows = []
    for k in range(3):
        moved = pltpu.roll(tail, (free - base - 64 * k) % 256, 1)
        rows.append(jnp.where((lane >= free) & (lane < free + 64), moved, block[32 * k:32 * k + 32]))
    return jnp.concatenate(rows, axis=0)


def unpack(packed, base):
    free = 0 if base else 192
    lane = lax.broadcasted_iota(jnp.int32, (32, 256), 1)
    tail = jnp.zeros((32, 256), F32)
    rows = []
    for k in range(3):
        part = packed[32 * k:32 * k + 32]
        rows.append(jnp.where((lane >= free) & (lane < free + 64), 0.0, part))
        spot = base + 64 * k
        tail = jnp.where((lane >= spot) & (lane < spot + 64), pltpu.roll(part, (spot - free) % 256, 1), tail)
    return jnp.concatenate(rows + [tail], axis=0)


STEPS = ((1, 0), (3, 0), (1, 1), (3, 1), (2, 0), (0, 1), (2, 1))


class Octet:
    def __init__(self, go):
        self.go = go
        self.a, self.b, self.c, self.f = a, b, c, f = place(2)
        self.me = a * 2 + c
        self.others = [lax.rem(a + da, 4) * 2 + lax.rem(c + dc, 2) for da, dc in STEPS]
        self.sources = [lax.rem(a + 4 - da, 4) * 2 + lax.rem(c + dc, 2) for da, dc in STEPS]
        self.devices = [device(lax.rem(a + da, 4), b, lax.rem(c + dc, 2), f, 2) for da, dc in STEPS]

    def send(self, n, source, target):
        return self.go(source, target(self.me), self.devices[n])


def project_kernel(tokens, *refs):
    shards, vectors = refs[:4], refs[4:13]
    q_held, kv_held, f_qkv, f_out, f_in, f_back, vec, turned = refs[13:21]
    own = refs[21:25]
    whole, acc, q_sent, kv_sent, v_own, token, held = refs[25:32]
    flat, (send, recv, here) = refs[32:41], refs[41:]
    fulls = (f_qkv, f_out, f_in, f_back)
    a, b, c, f = place(2)
    group = Octet(None)
    me = group.me
    odd_a = lax.rem(a, 2)
    xp, yp, sp = device(a, 1 - b, c, f, 2), device(a, b, c, 1 - f, 2), device(a, b, 1 - c, f, 2)
    pairs = [device(lax.rem(a + 5 - 2 * odd_a, 4), b, c, f, 2), device(lax.rem(a + 3 + 2 * odd_a, 4), b, c, f, 2)]
    loads = [pltpu.make_async_copy(shards[w], own[w], here.at[w]) for w in range(4)]
    flats = [pltpu.make_async_copy(ref, flat[n], here.at[12 + n]) for n, ref in enumerate(vectors)]
    flats.append(pltpu.make_async_copy(tokens, token, here.at[11]))
    for cp in flats + loads:
        cp.start()
    meet(group.devices + [xp, yp])
    wires = Wires(send, recv)
    go = group.go = wires.go

    def rows_of(w, which, chunk):
        size = shards[w].shape[0] // 4
        return pl.multiple_of(which * 2 * size + chunk * size, 16), size

    def cols_of(w, cc):
        half = shards[w].shape[1] // 2
        return pl.ds(pl.multiple_of(cc * half, 128), half)

    def region(target, w, owner, which, cc, chunk):
        start, size = rows_of(w, which, chunk)
        return target.at[pl.ds(owner * shards[w].shape[0] + start, size), cols_of(w, cc)]

    def source(w, which, chunk):
        start, size = rows_of(w, which, chunk)
        return shards[w].at[pl.ds(start, size), cols_of(w, c)]

    other_f = 1 - f

    class Fetch:
        def __init__(self, target, w, chunk, pair=None):
            self.target, self.w, self.chunk = target, w, chunk
            self.which = b if pair is None else odd_a
            self.peer = xp if pair is None else pairs[pair]
            self.first = go(source(w, self.which, chunk), region(target, w, f, self.which, c, chunk), yp)

        def second(self):
            self.first.wait_recv()
            got = region(self.target, self.w, other_f, self.which, c, self.chunk)
            self.cross = go(got, got, self.peer)
            self.side = go(got, got, sp)

        def third(self):
            self.cross.wait_recv()
            got = region(self.target, self.w, other_f, 1 - self.which, c, self.chunk)
            self.side2 = go(got, got, sp)

        def end(self):
            self.side.wait_recv()
            self.side2.wait_recv()

    class Straight:
        def __init__(self, target, w, chunk, which):
            self.place = (target, w, other_f, which, c, chunk)
            self.first = go(source(w, which, chunk), region(target, w, f, which, c, chunk), yp)

        def second(self):
            self.first.wait_recv()
            got = region(*self.place)
            self.side = go(got, got, sp)

        def third(self):
            pass

        def end(self):
            self.side.wait_recv()

    qkv = [Fetch(whole, 0, 0)]
    for cp in flats:
        cp.wait()

    def token_block(dc):
        return token.at[pl.ds(pl.multiple_of(lax.rem(c + dc, 2) * 128, 128), 128)]

    toks = [go(token_block(STEPS[n][1]), held.at[m], group.devices[n]) for m, n in enumerate((0, 1, 2, 3, 5))]
    held[5] = token[pl.ds(pl.multiple_of(c * 128, 128), 128)]
    for n in range(9):
        value = flat[n][...].astype(F32)
        if n == 3:
            for j in range(4):
                v_own[8 + j:9 + j] = value[384 * j:384 * j + 384].reshape(1, 384)
        else:
            row = n if n < 3 else n - 1
            v_own[row:row + 1] = value.reshape(1, 384)
    v_own[12:16] = jnp.zeros((4, 384), F32)
    vec[f] = v_own[...]
    small = go(v_own, vec.at[f], yp)
    loads[0].wait()
    mine = pl.ds(pl.multiple_of(f * 384, 128), 384)
    theirs = pl.ds(pl.multiple_of(other_f * 384, 128), 384)

    @pl.loop(0, 6)
    def _(n):
        cols = pl.ds(pl.multiple_of(n * 384, 128), 384)
        acc[:, cols] = dot(token[:, mine], own[0][:, cols], NN)

    qkv[0].second()
    qkv.append(Fetch(whole, 0, 1))
    qkv[1].second()
    outer = [Fetch(f_back, 3, chunk) for chunk in range(2)]
    rest = [Fetch(f_out, 1, chunk) for chunk in range(2)]
    inner = [Straight(f_in, 2, chunk, which) for chunk in range(2) for which in range(2)]
    qkv[0].third()
    qkv[1].third()
    stores = []
    for w in range(4):
        if w > 0:
            loads[w].wait()
        rows = shards[w].shape[0]
        cp = pltpu.make_async_copy(own[w], fulls[w].at[pl.ds(pl.multiple_of(f * rows, 16), rows)], here.at[4 + w])
        cp.start()
        stores.append(cp)
    small.wait_recv()
    qkv[0].end()
    qkv[1].end()
    cp = pltpu.make_async_copy(whole.at[pl.ds(pl.multiple_of(other_f * 384, 16), 384)],
                               f_qkv.at[pl.ds(pl.multiple_of(other_f * 384, 16), 384)], here.at[8])
    cp.start()
    stores.append(cp)

    def column(n):
        cols = slice(384 * n, 384 * n + 384)
        value = acc[:, cols] + dot(token[:, theirs], whole[pl.ds(pl.multiple_of(other_f * 384, 16), 384), cols], NN)
        if n < 2:
            value = value + vec[n, 0:1]
        if n >= 4:
            value = value + vec[n - 4, 1:2]
        return value

    lane = lax.broadcasted_iota(jnp.int32, (256, 384), 1)
    for p in range(2):
        k, v = column(2 + p), column(4 + p)
        turned_k, turned_v = pltpu.roll(k, 192, 1), pltpu.roll(v, 192, 1)
        even = jnp.where(lane < 192, k, turned_v).astype(BF16)
        odd = jnp.where(lane < 192, turned_k, v).astype(BF16)
        q = column(p)
        q_even, q_odd = q[:, :256], pltpu.roll(q, 192, 1)[:, :256]
        for s in range(2):
            rows = slice(128 * s, 128 * s + 128)
            kv_sent[4 * p + s], kv_sent[4 * p + 2 + s] = even[rows], odd[rows]
            q_sent[4 * p + s], q_sent[4 * p + 2 + s] = pack(q_even[rows], 0).astype(BF16), pack(q_odd[rows], 0).astype(BF16)

    def slot(block, bb):
        return (block // 2 * 2 + bb) * 2 + lax.rem(block, 2)

    kv_slot = lambda block: kv_held.at[slot(block, b)]
    q_slot = lambda block: q_held.at[block]
    first = [group.send(n, kv_sent.at[group.others[n]], kv_slot) for n in (6, 0, 1, 2, 3, 4, 5)]
    first = first[1:] + first[:1]
    own_kv = pltpu.make_async_copy(kv_sent.at[me], kv_held.at[slot(me, b)], here.at[9])
    own_kv.start()
    own_q = pltpu.make_async_copy(q_sent.at[me], q_held.at[me], here.at[10])
    own_q.start()
    crossed = [go(kv_sent.at[me], kv_held.at[slot(me, b)], xp)]
    third = [group.send(n, q_sent.at[group.others[n]], q_slot) for n in (6, 0, 1, 2, 3, 4, 5)]
    third = third[1:] + third[:1]

    def onward(n):
        first[n].wait_recv()
        piece = kv_slot(group.sources[n])
        crossed.append(go(piece, piece, xp))

    onward(5)
    onward(0)
    onward(1)
    for cp in outer:
        cp.second()
    for cp in rest:
        cp.second()
    onward(2)
    onward(3)
    onward(4)
    onward(6)
    for cp in toks:
        cp.wait_recv()

    @pl.loop(0, 6)
    def _(n):
        @pl.loop(0, 6)
        def _(m):
            lanes = pl.ds(pl.multiple_of(m * 128, 128), 128)
            turned[n, lanes] = held[n, :, lanes].astype(F32).T.astype(BF16)

    for cp in inner:
        cp.second()
    for cp in outer:
        cp.third()
    for cp in rest:
        cp.third()
    for cp in crossed + third:
        cp.wait_recv()
    for cp in rest + inner + outer:
        cp.end()
    for cp in wires.made:
        cp.wait_send()
    for cp in stores + [own_kv, own_q]:
        cp.wait()


def project(tokens, shards, vectors, ident):
    rows, width = tokens.shape
    anywhere = pl.BlockSpec(memory_space=pl.ANY)
    wires = 80
    return pl.pallas_call(
        project_kernel,
        out_shape=[jax.ShapeDtypeStruct((8, 96, 256), BF16), jax.ShapeDtypeStruct((16, 128, 384), BF16)]
        + [jax.ShapeDtypeStruct((2 * s.shape[0], s.shape[1]), BF16) for s in shards]
        + [jax.ShapeDtypeStruct((2, 16, 384), F32), jax.ShapeDtypeStruct((6, 768, 128), BF16)],
        in_specs=[pl.BlockSpec(memory_space=pltpu.HBM)] * 14,
        out_specs=[vmem()] * 2 + [anywhere] * 4 + [vmem()] * 2,
        scratch_shapes=[pltpu.VMEM(s.shape, BF16) for s in shards]
        + [pltpu.VMEM((768, 2304), BF16), pltpu.VMEM((256, 2304), F32), pltpu.VMEM((8, 96, 256), BF16),
           pltpu.VMEM((8, 128, 384), BF16), pltpu.VMEM((16, 384), F32), pltpu.VMEM(tokens.shape, BF16),
           pltpu.VMEM((6, 128, 768), BF16),
           *[pltpu.VMEM(v.shape, BF16) for v in vectors], DMA((wires,)), DMA((wires,)), DMA((21,))],
        compiler_params=pltpu.CompilerParams(collective_id=ident, has_side_effects=True, vmem_limit_bytes=62 << 20),
        name="project",
    )(tokens, *shards, *vectors)


BLK = 48
Z1, X1, Y1 = (0, 768), (768, 1920), (1920, 3456)
LATE = (0, 640)


class Wires:
    def __init__(self, send, recv):
        self.send, self.recv, self.made = send, recv, []

    def go(self, source, target, peer):
        n = len(self.made)
        cp = remote(source, target, self.send.at[n], self.recv.at[n], peer)
        cp.start()
        self.made.append(cp)
        return cp


def transpose_into(target, source, base):
    width = source.shape[1]

    @pl.loop(0, width // 128)
    def _(n):
        at = pl.multiple_of(n * 128, 128)
        target[pl.ds(base + at, 128)] = source[:, pl.ds(at, 128)].astype(F32).T.astype(BF16)


def pair_columns(even, odd, lane, second):
    if second:
        return jnp.where(lane < 192, pltpu.roll(even, 192, 1), odd)
    return jnp.where(lane < 192, even, pltpu.roll(odd, 192, 1))


def halves(span):
    tiles = (span[1] - span[0]) // 128
    mid = span[0] + tiles // 2 * 128
    return (span[0], mid), (mid, span[1])


def within(span, group):
    base = 0
    for member in group:
        if member == span:
            return slice(base, base + span[1] - span[0])
        base += member[1] - member[0]


def gradient_kernel(lens, wqkv, gfirst_hbm, near_hbm, far_hbm, q_hbm, kv_hbm, ot_hbm, xt, gbr, ghid, gsec, small, do_sent, lse_ref,
                    out, late_out, igrad, small_out,
                    joined, wqkv_held, gfirst, near, far, q_held, kv_ref, ot_ref, mine, sib, cin, y8, y4, x8, x4, z4, z1r, zyb, zxb,
                    do_held, qm, dm, kt, dk, dv, acc, rowsc, delta, dq_sent, dq_all, dkv_all, dqo, dkvo, xsend, rbuf,
                    l_sib, l_in, l_acc, l_mine, ly, lx,
                    v_own, v_core, v_f, v_b, v_a, send, recv, here):
    inputs = [pltpu.make_async_copy(s, t, here.at[5 + n]) for n, (s, t) in enumerate(
        ((kv_hbm, kv_ref), (q_hbm, q_held), (ot_hbm, ot_ref), (near_hbm, near), (far_hbm, far), (gfirst_hbm, gfirst), (wqkv, wqkv_held)))]
    for cp in inputs:
        cp.start()
    group = Octet(None)
    a, b, c, f, me = group.a, group.b, group.c, group.f, group.me
    xp, yp, sp = device(a, 1 - b, c, f, 2), device(a, b, c, 1 - f, 2), device(a, b, 1 - c, f, 2)
    up, down = lax.rem(a + 1, 4), lax.rem(a + 3, 4)
    upp, downp = device(up, b, c, f, 2), device(down, b, c, f, 2)
    ends = bounds(lens, c)
    total = kv_ref.shape[0]
    meet(group.devices + [xp, yp])
    wires = Wires(send, recv)
    go = group.go = wires.go
    pending = []

    do_slot = lambda block: do_held.at[block]
    swaps = {n: group.send(n, do_sent.at[group.others[n]], do_slot) for n in (6, 0, 1, 2, 3, 4, 5)}
    do_held[me] = do_sent[me]


    def produce(kind, first, count, part, finish):
        @pl.loop(0, 2 * count)
        def _(n):
            ff, j = lax.rem(n, 2), first + n // 2
            if kind == "out":
                left, right = xt[pl.ds(pl.multiple_of(ff * 384, 128), 384)], gbr[:, pl.ds(pl.multiple_of(part * 384, 128), 384)]
                col = 768
            elif kind == "in":
                left = xt[pl.ds(pl.multiple_of(768 + ff * 384, 128), 384)]
                right = ghid[:, pl.ds(pl.multiple_of(part * 1536 + j * 384, 128), 384)]
                col = pl.multiple_of(j * 384 + (384 if first else 0), 128)
            else:
                left = xt[pl.ds(pl.multiple_of(1536 + ff * 1536 + j * 384, 128), 384)]
                right = gsec[:, pl.ds(pl.multiple_of(part * 384, 128), 384)]
                col = pl.multiple_of(1920 + j * 384, 128)
            finish(pl.ds(ff * 2, 2), pl.ds(col, 384), dot(left, right, NN).reshape(2, 4, BLK, 384))

    def keep(rows, cols, value):
        sib[rows, :, :, cols] = value.astype(BF16)

    def join(rows, cols, value):
        mine[rows, :, :, cols] = (value + cin[rows, :, :, cols].astype(F32)).astype(BF16)

    core = {}

    def share(span):
        cols = slice(span[0], span[1])
        core[span] = go(sib.at[:, :, :, cols], cin.at[:, :, :, cols], sp)

    RS = (Y1, X1)

    def add(target, source):
        def step(n):
            t, s = target(n), source(n)
            t[...] = (t[...].astype(F32) + s[...].astype(F32)).astype(BF16)
        return step

    def accumulate(target, source, count):
        pl.loop(0, count)(add(target, source))

    ycols, xcols, zcols = slice(*Y1), slice(*X1), slice(*Z1)

    def start_y():
        return go(mine.at[pl.ds((1 - f) * 2, 2), :, :, ycols], y8, yp)

    def start_x():
        return [go(mine.at[ff * 2 + 1 - b, :, :, xcols], x8.at[ff], xp) for ff in range(2)]

    def next_y(cp):
        cp.wait_recv()
        accumulate(lambda n: mine.at[f * 2 + n // 4, lax.rem(n, 4), :, ycols], lambda n: y8.at[n // 4, lax.rem(n, 4)], 8)
        return go(mine.at[f * 2 + 1 - b, :, :, ycols], x4, xp)

    def next_x(cps):
        for cp in cps:
            cp.wait_recv()
        accumulate(lambda n: mine.at[n // 4 * 2 + b, lax.rem(n, 4), :, xcols], lambda n: x8.at[n // 4, lax.rem(n, 4)], 8)
        return go(mine.at[(1 - f) * 2 + b, :, :, xcols], y4, yp)

    def last_y(cp):
        cp.wait_recv()
        accumulate(lambda n: mine.at[f * 2 + b, n, :, ycols], lambda n: x4.at[n], 4)

    def last_x(cp):
        cp.wait_recv()
        accumulate(lambda n: mine.at[f * 2 + b, n, :, xcols], lambda n: y4.at[n], 4)

    def landing(span, step, part, single):
        if single:
            base = within(span, RS).start - span[0]
            return z1r.at[step, :, base + part[0]:base + part[1]]
        return z4.at[step, :, :, part[0]:part[1]]

    def ring_source(aa, part, single):
        cols = slice(part[0], part[1])
        return mine.at[f * 2 + b, aa, :, cols] if single else mine.at[:, aa, :, cols]

    def ring_send(span, step, single):
        lo, hi = halves(span)
        ud, dd = lax.rem(a + 3 - step, 4), lax.rem(a + 1 + step, 4)
        return (go(ring_source(ud, lo, single), landing(span, step, lo, single), upp),
                go(ring_source(dd, hi, single), landing(span, step, hi, single), downp))

    def ring_add(span, step, single, cps):
        lo, hi = halves(span)
        ud, dd = lax.rem(a + 6 - step, 4), lax.rem(a + 2 + step, 4)
        for cp, part, aa in zip(cps, (lo, hi), (ud, dd)):
            cp.wait_recv()
            got = landing(span, step, part, single)
            if single:
                add(lambda n: ring_source(aa, part, True), lambda n: got)(0)
            else:
                cols = slice(part[0], part[1])
                accumulate(lambda n: mine.at[n, aa, :, cols], lambda n: got.at[n], 4)

    def tail_z_y():
        return go(mine.at[pl.ds((1 - f) * 2, 2), a, :, zcols], zyb, yp)

    def tail_z_x(cp):
        cp.wait_recv()
        accumulate(lambda n: mine.at[f * 2 + n, a, :, zcols], lambda n: zyb.at[n], 2)
        return go(mine.at[f * 2 + 1 - b, a, :, zcols], zxb, xp)

    def tail_z_end(cp):
        cp.wait_recv()
        add(lambda n: mine.at[f * 2 + b, a, :, zcols], lambda n: zxb)(0)

    class Gather:
        def __init__(self, own, spot, span, first):
            self.span, self.first, self.spot = span, first, spot
            self.own = own
            self.copy = pltpu.make_async_copy(own, spot(b, a, span), here.at[len(locals_)])
            self.copy.start()
            locals_.append(self.copy)
            pending.append(go(own, spot(b, a, span), sp))
            self.ring = go(own, spot(b, a, span), upp), go(own, spot(b, a, span), downp)
            self.cross = go(own, spot(b, a, span), xp)

        def spread(self, bb, aa):
            p = self.spot(bb, aa, self.span)
            pending.append(go(p, p, sp))

        def passed(self, bb, ring):
            lo, hi = halves(self.span)
            ring[0].wait_recv()
            p = self.spot(bb, down, lo)
            first = go(p, p, upp)
            ring[1].wait_recv()
            p = self.spot(bb, up, hi)
            second = go(p, p, downp)
            for aa in (down, up):
                self.spread(bb, aa)
            return first, second

        def arrived(self, bb, ring):
            for cp in ring:
                cp.wait_recv()
            self.spread(bb, lax.rem(a + 2, 4))

        def second(self):
            self.ring2 = self.passed(b, self.ring)
            if self.first == "b":
                self.cross.wait_recv()
                self.spread(1 - b, a)
                p = self.spot(1 - b, a, self.span)
                self.other = go(p, p, upp), go(p, p, downp)
            else:
                spots = [self.spot(b, aa, self.span) for aa in (down, up)]
                self.more = [go(p, p, xp) for p in spots]

        def third(self):
            self.arrived(b, self.ring2)
            if self.first == "b":
                self.other2 = self.passed(1 - b, self.other)
            else:
                p = self.spot(b, lax.rem(a + 2, 4), self.span)
                self.more.append(go(p, p, xp))
                self.cross.wait_recv()
                self.spread(1 - b, a)

        def fourth(self):
            if self.first == "b":
                self.arrived(1 - b, self.other2)
            else:
                for cp, aa in zip(self.more, (down, up, lax.rem(a + 2, 4))):
                    cp.wait_recv()
                    self.spread(1 - b, aa)

    locals_ = []

    def early_spot(bb, aa, span):
        return out.at[c, bb * 4 + aa, :, span[0]:span[1]]

    def late_spot(bb, aa, span):
        return late_out.at[aa, bb * 2 + c, :, span[0]:span[1]]

    def early_gather(span, first):
        return Gather(mine.at[f * 2 + b, a, :, span[0]:span[1]], early_spot, span, first)

    def prepare():
        @pl.loop(0, total // KB)
        def _(n):
            rows = pl.ds(pl.multiple_of(n * KB, KB), KB)
            kt[:, rows] = kv_ref[rows, 0:256].astype(F32).T.astype(BF16)

        @pl.loop(0, 4)
        def _(stripe):
            head = lane_head((SPAN, 256), 0)
            headv = lane_head((SPAN, 256), 64)
            q = jnp.concatenate([unpack(q_held[stripe * 2 + i].astype(F32), 0) for i in range(2)], axis=0) * 0.125
            grad = jnp.concatenate([unpack(do_held[stripe * 2 + i].astype(F32), 64) for i in range(2)], axis=0)
            for h in range(3):
                qm[stripe, h] = jnp.where(head == h, q, 0.0).astype(BF16)
                dm[stripe, h] = jnp.where(headv == h, grad, 0.0).astype(BF16)
            prod = grad.T * ot_ref[stripe]
            for h in range(3):
                delta[stripe, h:h + 1] = jnp.sum(prod[64 * (h + 1):64 * (h + 2)], axis=0, keepdims=True)
            qpos = SPAN * (stripe * 2 + b) + lax.broadcasted_iota(jnp.int32, (1, SPAN), 1)
            start, stop = doc_range(qpos, ends)
            rowsc[stripe, 0:1] = start
            rowsc[stripe, 1:2] = stop
            acc[stripe] = jnp.zeros((256, SPAN), F32)

    reach = total * 5 // 8 // KB

    def attend(da, parity):
        block = lax.rem(a + da, 4) * 2 + parity
        krows = pl.ds(pl.multiple_of(block * KB, KB), KB)
        dk[...] = jnp.zeros((KB, 256), F32)
        dv[...] = jnp.zeros((KB, 256), F32)
        @pl.loop(0, 4)
        def _(stripe):
            away = stripe * 2 + b - block

            @pl.when((away <= reach) & (away >= -reach))
            def _():
                keys = kv_ref[krows, 0:256]
                vals = kv_ref[krows, 128:384]
                kpos = block * KB + lax.broadcasted_iota(jnp.int32, (KB, 1), 0)
                allowed = (kpos >= rowsc[stripe, 0:1]) & (kpos < rowsc[stripe, 1:2])
                newk, newv = dk[...], dv[...]
                for h in range(3):
                    s = jnp.where(allowed, dot(keys, qm[stripe, h], NT), MASKED)
                    p = jnp.exp(s - lse_ref[stripe, h:h + 1])
                    gp = dot(vals, dm[stripe, h], NT)
                    ds = (p * (gp - delta[stripe, h:h + 1])).astype(BF16)
                    newv = newv + dot(p.astype(BF16), dm[stripe, h], NN)
                    newk = newk + dot(ds, qm[stripe, h], NN)
                    hrows = pl.ds(64 * h, 64)
                    acc[stripe, hrows] = acc[stripe, hrows] + dot(kt[hrows, krows], ds, NN)
                dk[...] = newk
                dv[...] = newv

    def slot(block, bb):
        return (block // 2 * 2 + bb) * 2 + lax.rem(block, 2)

    def grads_of(dc):
        rows = pl.ds(pl.multiple_of(lax.rem(c + dc, 2) * 128, 128), 128)
        k, v = dk[rows], dv[rows]
        return jnp.concatenate([k[:, :128], k[:, 128:] + v[:, :128], v[:, 128:]], axis=1)

    FAR, NEXT = ((6, 1), (4, 0)), ((0, 0), (2, 1))
    BACK, HERE = ((1, 0), (3, 1)), ((5, 1), (7, 0))
    crossed = {}

    def cross(members):
        for n, dc in members:
            xsend[n] = grads_of(dc).astype(BF16)
            crossed[n] = go(xsend.at[n], rbuf.at[n], xp)

    dkv_slot = lambda block: dkvo.at[block]
    dkvs = {}

    def settle(members):
        for n, dc in members:
            crossed[n].wait_recv()
            value = (grads_of(dc) + rbuf[n].astype(F32)).astype(BF16)
            if n == 7:
                dkv_all[me] = value
                dkvo[me] = value
            else:
                dkv_all[group.others[n]] = value
                dkvs[n] = group.send(n, dkv_all.at[group.others[n]], dkv_slot)

    dq_slot = lambda block: dqo.at[block]
    dqs = {}

    produce("out", 0, 1, 1 - c, keep)
    produce("in", 2, 2, 1 - c, keep)
    share(X1)
    produce("back", 0, 4, 1 - c, keep)
    share(Y1)
    core[X1].wait_recv()
    produce("out", 0, 1, c, join)
    produce("in", 2, 2, c, join)
    x1 = start_x()
    core[Y1].wait_recv()
    produce("back", 0, 4, c, join)
    y1 = start_y()
    produce("in", 0, 2, 1 - c, keep)
    share(Z1)
    for cp in swaps.values():
        cp.wait_recv()
    for cp in inputs[:3]:
        cp.wait()
    prepare()
    core[Z1].wait_recv()
    produce("in", 0, 2, c, join)
    z1 = ring_send(Z1, 0, False)
    attend(2, 1 - b)
    cross(FAR)
    attend(1, 1 - b)
    cross(NEXT)
    ring_add(Z1, 0, False, z1)
    z1 = ring_send(Z1, 1, False)
    attend(3, 1 - b)
    cross(BACK)
    attend(0, 1 - b)
    cross(HERE)
    x1 = next_x(x1)
    ring_add(Z1, 1, False, z1)
    z1 = ring_send(Z1, 2, False)
    attend(2, b)
    settle(FAR)
    y1 = next_y(y1)
    attend(1, b)
    settle(NEXT)
    ring_add(Z1, 2, False, z1)
    z1 = tail_z_y()
    attend(3, b)
    settle(BACK)
    last_x(x1)
    x1 = ring_send(X1, 0, True)
    attend(0, b)

    @pl.loop(0, 4)
    def _(stripe):
        value = (acc[stripe] * 0.125).T
        dq_all[pl.ds(stripe * 2, 2)] = value.astype(BF16).reshape(2, 128, 256)
        for i in range(2):
            dq_sent[stripe * 2 + i] = pack(value[128 * i:128 * i + 128], 0).astype(BF16)

    def send_dq(*which):
        for n in which:
            dqs[n] = group.send(n, dq_sent.at[group.others[n]], dq_slot)

    dqo[me] = dq_sent[me]
    settle(HERE)
    z1 = tail_z_x(z1)
    ring_add(X1, 0, True, x1)
    x1 = ring_send(X1, 1, True)

    def project_back(n, right):
        rows = pl.ds(pl.multiple_of(n * 96, 32), 96)
        value = dot(near[5, rows], right[me], NN)
        for m, k in enumerate((0, 1, 2, 3, 5)):
            value = value + dot(near[m, rows], right[group.sources[k]], NN)
        for m, k in ((0, 4), (1, 6)):
            value = value + dot(far[m, rows], right[group.sources[k]], NN)
        return value

    for cp in inputs[3:]:
        cp.wait()

    @pl.loop(0, 4)
    def _(n):
        theirs, ours = n * 2 + 1 - c, n * 2 + c
        l_sib[n, :, 0:256] = project_back(theirs, dq_all).astype(BF16)
        l_sib[n, :, 256:640] = project_back(theirs, dkv_all).astype(BF16)
        l_acc[n, :, 0:256] = project_back(ours, dq_all)
        l_acc[n, :, 256:640] = project_back(ours, dkv_all)

    late = go(l_sib, l_in, sp)
    send_dq(6, 4)
    last_y(y1)
    y1 = ring_send(Y1, 0, True)
    ring_add(X1, 1, True, x1)
    x1 = ring_send(X1, 2, True)
    send_dq(0, 2)
    late.wait_recv()

    @pl.loop(0, 4)
    def _(n):
        l_mine[n] = (l_acc[n] + l_in[n].astype(F32)).astype(BF16)

    late = go(l_mine.at[pl.ds((1 - f) * 2, 2)], ly, yp)
    tail_z_end(z1)
    g_z1 = early_gather(Z1, "a")
    ring_add(Y1, 0, True, y1)
    y1 = ring_send(Y1, 1, True)
    send_dq(1, 3)
    late.wait_recv()
    accumulate(lambda n: l_mine.at[f * 2 + n], lambda n: ly.at[n], 2)
    late = go(l_mine.at[f * 2 + 1 - b], lx, xp)
    ring_add(X1, 2, True, x1)
    g_x1 = early_gather(X1, "a")
    send_dq(5)
    ring_add(Y1, 1, True, y1)
    y1 = ring_send(Y1, 2, True)
    late.wait_recv()
    add(lambda n: l_mine.at[f * 2 + b], lambda n: lx)(0)
    g_l = Gather(l_mine.at[f * 2 + b], late_spot, LATE, "a")
    g_z1.second()
    g_x1.second()
    ring_add(Y1, 2, True, y1)
    g_y1 = early_gather(Y1, "a")

    for cp in list(dqs.values()) + list(dkvs.values()):
        cp.wait_recv()
    lane = lax.broadcasted_iota(jnp.int32, (128, 384), 1)
    for s in range(2):
        rows = slice(s * 128, s * 128 + 128)
        for p in range(2):
            even, odd = 4 * p + s, 4 * p + 2 + s
            blank = jnp.zeros((128, 128), F32)
            qe = jnp.concatenate([unpack(dqo[even].astype(F32), 0), blank], axis=1)
            qo = jnp.concatenate([unpack(dqo[odd].astype(F32), 0), blank], axis=1)
            joined[rows, 384 * p:384 * p + 384] = pair_columns(qe, qo, lane, False).astype(BF16)
            ke, ko = dkvo[even].astype(F32), dkvo[odd].astype(F32)
            joined[rows, 768 + 384 * p:1152 + 384 * p] = pair_columns(ke, ko, lane, False).astype(BF16)
            joined[rows, 1536 + 384 * p:1920 + 384 * p] = pair_columns(ke, ko, lane, True).astype(BF16)
    v_own[...] = small[...]
    v_own[0:1] = jnp.sum(joined[:, 0:768].astype(F32), axis=0, keepdims=True)
    v_own[1:2] = jnp.sum(joined[:, 1536:2304].astype(F32), axis=0, keepdims=True)
    vec = go(v_own, v_core, sp)

    g_l.second()
    vec.wait_recv()
    v_core[...] = v_own[...] + v_core[...]
    vec = go(v_core.at[:, pl.ds(pl.multiple_of((1 - f) * 384, 128), 384)], v_f, yp)
    g_z1.third()
    g_x1.third()
    vec.wait_recv()
    v_b[b] = v_core[:, pl.ds(pl.multiple_of(f * 384, 128), 384)] + v_f[...]
    vec = go(v_b.at[b], v_b.at[b], xp)

    @pl.loop(0, 3)
    def _(n):
        rows = pl.ds(pl.multiple_of(n * 256, 256), 256)
        igrad[:, rows] = gfirst[:, rows] + dot(joined[...], wqkv_held[rows], NT)

    g_y1.second()
    g_l.third()
    g_z1.fourth()
    g_x1.fourth()
    vec.wait_recv()
    v_a[a] = v_b[0] + v_b[1]
    vec = [go(v_a.at[a], v_a.at[a], device(lax.rem(a + k, 4), b, c, f, 2)) for k in range(1, 4)]
    g_y1.third()
    g_l.fourth()
    g_y1.fourth()
    for cp in vec + pending:
        cp.wait_recv()
    small_out[...] = v_a[0] + v_a[1] + v_a[2] + v_a[3]
    for cp in locals_:
        cp.wait()
    for cp in wires.made:
        cp.wait_send()


def reduce_all(lens, wqkv, gfirst, near, far, xt, gbr, ghid, gsec, small, do_sent, q, kv, ot, lse, ident):
    wires = 192
    total = kv.shape[0]
    bf = lambda *shape: pltpu.VMEM(shape, BF16)
    fl = lambda *shape: pltpu.VMEM(shape, F32)
    anywhere = pl.BlockSpec(memory_space=pl.ANY)
    return pl.pallas_call(
        gradient_kernel,
        out_shape=[jax.ShapeDtypeStruct((2, 8, BLK, 3456), BF16), jax.ShapeDtypeStruct((4, 4, 96, 640), BF16),
                   jax.ShapeDtypeStruct((256, 768), F32), jax.ShapeDtypeStruct((16, 384), F32)],
        in_specs=[pl.BlockSpec(memory_space=pltpu.SMEM)] + [anywhere] * 7 + [vmem()] * 7, out_specs=[anywhere] * 2 + [vmem()] * 2,
        scratch_shapes=[
            bf(256, 2304), bf(768, 2304), fl(256, 768), bf(6, 768, 128), bf(2, 768, 128), bf(8, 96, 256), bf(total, 384), fl(4, 256, SPAN),
            bf(4, 4, BLK, 3456), bf(4, 4, BLK, 3456), bf(4, 4, BLK, 3456),
            bf(2, 4, BLK, 1536), bf(4, BLK, 1152), bf(2, 4, BLK, 1152), bf(4, BLK, 1536),
            bf(3, 4, BLK, 768), bf(3, BLK, 2688), bf(2, BLK, 768), bf(BLK, 768),
            bf(8, 96, 256), bf(4, 3, SPAN, 256), bf(4, 3, SPAN, 256), bf(256, total), fl(KB, 256), fl(KB, 256), fl(4, 256, SPAN),
            pltpu.VMEM((4, 8, SPAN), jnp.int32), fl(4, 8, SPAN),
            bf(8, 96, 256), bf(8, 128, 256), bf(8, 128, 384), bf(8, 96, 256), bf(8, 128, 384), bf(8, 128, 384), bf(8, 128, 384),
            bf(4, 96, 640), bf(4, 96, 640), fl(4, 96, 640), bf(4, 96, 640), bf(2, 96, 640), bf(96, 640),
            fl(16, 768), fl(16, 768), fl(16, 384), fl(2, 16, 384), fl(4, 16, 384),
            DMA((wires,)), DMA((wires,)), DMA((12,))],
        compiler_params=pltpu.CompilerParams(collective_id=ident, has_side_effects=True, vmem_limit_bytes=62 << 20),
        name="reduce_all",
    )(lens, wqkv, gfirst, near, far, q, kv, ot, xt, gbr, ghid, gsec, small, do_sent, lse)


def widen_kernel(grads, late, low, igrad, sums, g_qkv, g_out, g_in, g_back, low_out, igrad_out, *vectors):
    for core in range(2):
        part = grads.at[core]
        g_out[:, core * 384:core * 384 + 384] = part[:, 768:1152].astype(F32)
        g_in[:, core * 1536:core * 1536 + 768] = part[:, 0:768].astype(F32)
        g_in[:, core * 1536 + 768:core * 1536 + 1536] = part[:, 1152:1920].astype(F32)
        for j in range(4):
            g_back[j, :, core * 384:core * 384 + 384] = part[:, 1920 + 384 * j:2304 + 384 * j].astype(F32)
    lane = lax.broadcasted_iota(jnp.int32, (192, 384), 1)
    for p in range(2):
        even, odd = late[2 * p].astype(F32), late[2 * p + 1].astype(F32)
        g_qkv[:, 384 * p:384 * p + 384] = pair_columns(even[:, :384], odd[:, :384], lane, False)
        ke, ko = even[:, 256:], odd[:, 256:]
        g_qkv[:, 768 + 384 * p:1152 + 384 * p] = pair_columns(ke, ko, lane, False)
        g_qkv[:, 1536 + 384 * p:1920 + 384 * p] = pair_columns(ke, ko, lane, True)
    low_out[...] = low[...]
    igrad_out[...] = igrad[...]

    @pl.when(pl.program_id(0) == 0)
    def _():
        for n, ref in enumerate(vectors):
            if n == 3:
                for j in range(4):
                    ref[384 * j:384 * j + 384] = sums[8 + j:9 + j].reshape(384)
            else:
                row = n if n < 3 else n - 1
                ref[...] = sums[row:row + 1].reshape(384)


def widen(grads, late, low, igrad, sums):
    rows, step = 384, 192
    spec = lambda tall, wide: pl.BlockSpec((tall, wide), lambda n: (n, 0))
    flat = lambda size: pl.BlockSpec((size,), lambda n: (0,))
    sizes = [384] * 3 + [1536] + [384] * 5
    return pl.pallas_call(
        widen_kernel,
        grid=(rows // step,),
        out_shape=[jax.ShapeDtypeStruct((rows, 2304), F32), jax.ShapeDtypeStruct((rows, 768), F32),
                   jax.ShapeDtypeStruct((rows, 3072), F32), jax.ShapeDtypeStruct((4, rows, 768), F32),
                   jax.ShapeDtypeStruct(low.shape, BF16), jax.ShapeDtypeStruct(igrad.shape, F32)]
        + [jax.ShapeDtypeStruct((size,), F32) for size in sizes],
        in_specs=[pl.BlockSpec((2, step, 3456), lambda n: (0, n, 0)), pl.BlockSpec((4, step, 640), lambda n: (0, n, 0)),
                  spec(128, 768), spec(128, 768), pl.BlockSpec((16, 384), lambda n: (0, 0))],
        out_specs=[spec(step, 2304), spec(step, 768), spec(step, 3072), pl.BlockSpec((4, step, 768), lambda n: (0, n, 0)),
                   spec(128, 768), spec(128, 768)] + [flat(size) for size in sizes],
        compiler_params=pltpu.CompilerParams(vmem_limit_bytes=62 << 20),
        name="widen",
    )(grads, late.reshape(4, rows, 640), low, igrad, sums)


def middle_kernel(o_sent, tokens, cotangent, w_out, w_in, w_back, vec,
                  output, gfirst, xt, gbr, ghid, gsec, do_sent, small, far,
                  o_held, f_held, v_out, v_in, v_back, normed, xhat1, final, slope, act, send, recv, here):
    group = Octet(None)
    a, b, c, f, me = group.a, group.b, group.c, group.f, group.me
    loads = [pltpu.make_async_copy(s, t, here.at[n]) for n, (s, t) in enumerate(((w_out, v_out), (w_in, v_in), (w_back, v_back)))]
    for cp in loads:
        cp.start()
    meet(group.devices)
    wires = Wires(send, recv)
    go = group.go = wires.go
    o_slot = lambda block: o_held.at[block]
    swaps = {n: group.send(n, o_sent.at[group.others[n]], o_slot) for n in (6, 0, 1, 2, 3, 4, 5)}
    o_held[me] = o_sent[me]

    def token_block(dc):
        return tokens.at[pl.ds(pl.multiple_of(lax.rem(c + dc, 2) * 128, 128), 128)]


    def row(n):
        return jnp.concatenate([vec[0, n:n + 1], vec[1, n:n + 1]], axis=1)

    def sums(n, value):
        small[n:n + 1] = jnp.sum(value, axis=0, keepdims=True)

    for cp in swaps.values():
        cp.wait_recv()
    beyond = [go(token_block(dc), f_held.at[dc], group.devices[n]) for dc, n in ((0, 4), (1, 6))]
    lane = lax.broadcasted_iota(jnp.int32, (128, 384), 1)
    blank = jnp.zeros((128, 128), F32)
    att = act
    for s in range(2):
        rows = slice(s * 128, s * 128 + 128)
        for p in range(2):
            sides = [jnp.concatenate([pltpu.roll(unpack(o_held[4 * p + 2 * k + s].astype(F32), 64), 192, 1), blank], axis=1) for k in range(2)]
            att[rows, 384 * p:384 * p + 384] = pair_columns(sides[0], sides[1], lane, False).astype(BF16)
    transpose_into(xt, att.at[:, 0:768], 0)

    def norm(value):
        mean = jnp.sum(value, axis=1, keepdims=True) * (1.0 / 768)
        centered = value - mean
        variance = jnp.sum(centered * centered, axis=1, keepdims=True) * (1.0 / 768)
        inverse = lax.rsqrt(variance + EPSILON)
        return centered * inverse, inverse

    def norm_back(upstream, gain, hat, inverse):
        scaled = upstream * gain
        first = jnp.sum(scaled, axis=1, keepdims=True) * (1.0 / 768)
        second = jnp.sum(scaled * hat, axis=1, keepdims=True) * (1.0 / 768)
        return inverse * (scaled - first - hat * second)

    loads[0].wait()
    hat, inverse1 = norm(tokens[...].astype(F32) + (dot(att[:, 0:768], v_out[...], NN) + row(2)))
    xhat1[...] = hat
    value = hat * row(4) + row(5)
    normed[...] = value
    output[...] = value.astype(BF16)
    transpose_into(xt, output, 768)
    loads[1].wait()

    @pl.loop(0, 4)
    def _(n):
        cols = pl.ds(pl.multiple_of(n * 768, 128), 768)
        ff, j = n // 2, lax.rem(n, 2) * 2
        bias = jnp.concatenate([vec[ff, pl.ds(8 + j, 1)], vec[ff, pl.ds(9 + j, 1)]], axis=1)
        hidden = dot(output[...], v_in[:, cols], NN) + bias
        half = 0.5 * (1.0 + lax.erf(hidden * 0.7071067811865476))
        slope[:, cols] = half + hidden * (jnp.exp(-0.5 * hidden * hidden) * 0.3989422804014327)
        value = hidden * half
        act[:, cols] = value.astype(BF16)
        xt[pl.ds(pl.multiple_of(1536 + n * 768, 128), 768)] = value.T.astype(BF16)

    loads[2].wait()
    final[...] = normed[...] + (dot(act[...], v_back[...], NN) + row(3))
    hat2, inverse2 = norm(final[...])
    output[...] = (hat2 * row(6) + row(7)).astype(BF16)
    upstream = cotangent[...].astype(F32)
    sums(6, upstream * hat2)
    sums(7, upstream)
    gfinal = norm_back(upstream, row(6), hat2, inverse2)
    final[...] = gfinal
    gsec[...] = gfinal.astype(BF16)
    sums(3, gsec[...].astype(F32))

    @pl.loop(0, 4)
    def _(n):
        cols = pl.ds(pl.multiple_of(n * 768, 128), 768)
        ff, j = n // 2, lax.rem(n, 2) * 2
        value = (dot(gsec[...], v_back[cols], NT) * slope[:, cols]).astype(BF16)
        ghid[:, cols] = value
        total = jnp.sum(value.astype(F32), axis=0, keepdims=True)
        lanes = pl.ds(pl.multiple_of(ff * 384, 128), 384)
        small[pl.ds(8 + j, 1), lanes] = total[:, :384]
        small[pl.ds(9 + j, 1), lanes] = total[:, 384:]

    small[0:2] = jnp.zeros((2, 768), F32)
    small[12:16] = jnp.zeros((4, 768), F32)

    @pl.loop(0, 3)
    def _(n):
        cols = pl.ds(pl.multiple_of(n * 256, 128), 256)
        final[:, cols] = final[:, cols] + dot(ghid[...], v_in[cols], NT)

    hat = xhat1[...]
    upstream = final[...]
    sums(4, upstream * hat)
    sums(5, upstream)
    value = norm_back(upstream, row(4), hat, inverse1)
    gfirst[...] = value
    gbr[...] = value.astype(BF16)
    sums(2, gbr[...].astype(F32))
    normed[...] = dot(gbr[...], v_out[...], NT)
    wide = lax.broadcasted_iota(jnp.int32, (256, 256), 1)
    for p in range(2):
        part = normed[:, 384 * p:384 * p + 384]
        for k in range(2):
            turned = part if k == 0 else pltpu.roll(part, 192, 1)
            block = pltpu.roll(jnp.where(wide < 192, turned[:, :256], 0.0), 64, 1)
            for s in range(2):
                do_sent[4 * p + 2 * k + s] = pack(block[128 * s:128 * s + 128], 64).astype(BF16)
    for cp in beyond:
        cp.wait_recv()
    for n in range(2):
        @pl.loop(0, 6)
        def _(m):
            lanes = pl.ds(pl.multiple_of(m * 128, 128), 128)
            far[n, lanes] = f_held[n, :, lanes].astype(F32).T.astype(BF16)
    for cp in wires.made:
        cp.wait_send()


def middle(o_sent, tokens, cotangent, w_out, w_in, w_back, vec, ident):
    bf = lambda *shape: pltpu.VMEM(shape, BF16)
    fl = lambda *shape: pltpu.VMEM(shape, F32)
    out = lambda d, *shape: jax.ShapeDtypeStruct(shape, d)
    anywhere = pl.BlockSpec(memory_space=pl.ANY)
    wires = 16
    return pl.pallas_call(
        middle_kernel,
        out_shape=[out(BF16, 256, 768), out(F32, 256, 768), out(BF16, 4608, 256), out(BF16, 256, 768), out(BF16, 256, 3072),
                   out(BF16, 256, 768), out(BF16, 8, 96, 256), out(F32, 16, 768), out(BF16, 2, 768, 128)],
        in_specs=[vmem()] * 3 + [anywhere] * 3 + [vmem()], out_specs=[vmem()] * 9,
        scratch_shapes=[bf(8, 96, 256), bf(2, 128, 768), bf(768, 768), bf(768, 3072), bf(3072, 768),
                        fl(256, 768), fl(256, 768), fl(256, 768), fl(256, 3072), bf(256, 3072),
                        DMA((wires,)), DMA((wires,)), DMA((3,))],
        compiler_params=pltpu.CompilerParams(collective_id=ident, has_side_effects=True, vmem_limit_bytes=60 << 20),
        name="middle",
    )(o_sent, tokens, cotangent, w_out, w_in, w_back, vec)


def layer_norm(values, gain_row, shift_row):
    average = jnp.mean(values, axis=-1, keepdims=True)
    centered = values - average
    variance = jnp.mean(centered * centered, axis=-1, keepdims=True)
    return centered * lax.rsqrt(variance + EPSILON) * gain_row + shift_row


def exact_gelu(values):
    return jax.nn.gelu(values, approximate=False)


def by_group(rows, micro, front, back):
    parts = rows.reshape(micro, -1, 4, 192).transpose(2, 0, 1, 3)
    parts = jnp.pad(parts, ((0, 0), (0, 0), (0, 0), (front, back)))
    return parts.reshape((-1,) + parts.shape[2:])


def from_group(blocks, micro, front):
    rows = blocks.shape[1]
    parts = blocks.reshape(4, micro, rows, -1)[..., front:front + 192]
    return parts.transpose(1, 2, 0, 3).reshape(micro * rows, 768)


def shards(tokens, cotangent, doc_lengths, w_qkv, w_out, w_in, w_back, *vectors):
    micro, per, width = tokens.shape
    nf, cols = lax.axis_size("fsdp"), lax.axis_size("ctx") // 8
    share = width // nf
    inputs = tokens.reshape(micro * per, width)
    cube = nf == 2 and cols == 2
    if cube:
        q_held, kv_held, full_qkv, full_out, full_in, full_back, sides, near = project(inputs, (w_qkv, w_out, w_in, w_back), vectors, 1)
        kv_held = kv_held.reshape(-1, 384)
        mixed, mixed_t, log_total = attend_forward(doc_lengths, q_held, kv_held, cols, True)
        output, grad_first, xt, grad_branch, grad_hidden, grad_second, do_sent, small, far = middle(
            mixed, inputs, cotangent.reshape(inputs.shape), full_out, full_in, full_back, sides, 3)
        grads, late, input_grad, sums = reduce_all(
            doc_lengths, full_qkv, grad_first, near, far, xt, grad_branch, grad_hidden, grad_second, small, do_sent, q_held, kv_held,
            mixed_t, log_total, 5)
        g_qkv, g_out, g_in, g_back, output, input_grad, *rows = widen(grads.reshape(2, share, 3456), late, output, input_grad, sums)
        return (output.reshape(tokens.shape), input_grad.reshape(tokens.shape), g_qkv, g_out, g_in, g_back.reshape(4 * share, width)) + tuple(rows)
    tiny = jnp.concatenate(vectors).reshape(8, -1)
    full_qkv, full_out, full_in, full_back, tinies = gather_weights((w_qkv, w_out, w_in, w_back), tiny, nf, cols)
    tinies = tinies.reshape(nf, -1).astype(F32)
    named, at = [], 0
    for vector in vectors:
        size = vector.shape[0]
        named.append(tinies[:, at:at + size].reshape(-1))
        at += size
    b_query, b_value, b_out, b_in, b_back, gain_one, shift_one, gain_two, shift_two = named
    joined = jnp.dot(inputs, full_qkv, preferred_element_type=F32)
    bias = jnp.concatenate([b_query, jnp.zeros_like(b_query), b_value])
    joined = (joined + bias).astype(BF16)
    q_sent = by_group(joined[:, :width], micro, 0, 64)
    kv_sent = jnp.concatenate([by_group(joined[:, width:2 * width], micro, 0, 0), by_group(joined[:, 2 * width:], micro, 0, 0)], axis=2)
    q_held, kv_held = spread(q_sent, kv_sent, cols, 2)
    q_held = q_held.reshape(8 * per, 256)
    kv_held = kv_held.reshape(-1, 384)
    mixed, mixed_t, log_total = attend_forward(doc_lengths, q_held, kv_held, cols)
    (back,) = swap([mixed.reshape(8, per, 256)], cols, 3)
    attended = from_group(back, micro, 64)
    first_sum = inputs.astype(F32) + (jnp.dot(attended, full_out, preferred_element_type=F32) + b_out)
    normed = layer_norm(first_sum, gain_one, shift_one)
    normed_low = normed.astype(BF16)
    hidden = jnp.dot(normed_low, full_in, preferred_element_type=F32) + b_in
    activated = exact_gelu(hidden).astype(BF16)
    final_sum = normed + (jnp.dot(activated, full_back, preferred_element_type=F32) + b_back)
    output = layer_norm(final_sum, gain_two, shift_two).astype(BF16)

    upstream = cotangent.reshape(micro * per, width).astype(F32)
    grad_final, g_gain_two, g_shift_two = jax.vjp(layer_norm, final_sum, gain_two, shift_two)[1](upstream)
    grad_second = grad_final.astype(BF16)
    g_back_bias = jnp.sum(grad_second.astype(F32), axis=0)
    grad_activated = jnp.einsum("rm,km->rk", grad_second, full_back, preferred_element_type=F32)
    grad_hidden = jax.vjp(exact_gelu, hidden)[1](grad_activated)[0].astype(BF16)
    g_in_bias = jnp.sum(grad_hidden.astype(F32), axis=0)
    grad_normed = grad_final + jnp.einsum("rf,mf->rm", grad_hidden, full_in, preferred_element_type=F32)
    grad_first, g_gain_one, g_shift_one = jax.vjp(layer_norm, first_sum, gain_one, shift_one)[1](grad_normed)
    grad_branch = grad_first.astype(BF16)
    g_out_bias = jnp.sum(grad_branch.astype(F32), axis=0)
    grad_attended = jnp.einsum("rm,km->rk", grad_branch, full_out, preferred_element_type=F32).astype(BF16)
    (do_held,) = swap([by_group(grad_attended, micro, 64, 0)], cols, 4)
    dq, dkv = attend_backward(doc_lengths, q_held, kv_held, do_held.reshape(8 * per, 256), mixed_t, log_total, cols)
    dq_own, dkv_own = collect(dq.reshape(8, per, 256), dkv.reshape(8 * cols, per, 384), cols, 5)
    grad_joined = jnp.concatenate(
        [from_group(dq_own, micro, 0), from_group(dkv_own, micro, 0), from_group(dkv_own, micro, 192)], axis=1)
    g_query_bias = jnp.sum(grad_joined[:, :width].astype(F32), axis=0)
    g_value_bias = jnp.sum(grad_joined[:, 2 * width:].astype(F32), axis=0)
    input_grad = grad_first + jnp.einsum("rc,mc->rm", grad_joined, full_qkv, preferred_element_type=F32)

    def halves(left, right):
        blocks = right.shape[1] // 384
        return jnp.einsum("rm,rhc->hmc", left, right.reshape(-1, blocks, 384), preferred_element_type=F32).astype(BF16)

    back_grads = jnp.einsum("rk,rm->km", activated, grad_second, preferred_element_type=F32).astype(BF16)
    back_grads = back_grads.reshape(nf, 4, share, 2, 384).transpose(1, 3, 0, 2, 4).reshape(8, width, 384)
    grads = jnp.concatenate(
        [halves(inputs, grad_joined), halves(attended, grad_branch), halves(normed_low, grad_hidden), back_grads])
    grads = grads.reshape(2, 4, 3, nf, cols, share // cols, 384)
    small = (g_query_bias, g_value_bias, g_out_bias, g_in_bias, g_back_bias, g_gain_one, g_shift_one, g_gain_two, g_shift_two)
    small = jnp.concatenate([x.reshape(nf, -1) for x in small], axis=1).reshape(nf, 8, -1)
    owned, small_owned = reduce_grads(grads, small, nf, cols, 6)
    owned = owned.transpose(0, 1, 3, 2, 4, 5).reshape(24, share, 384)

    def columns(first, last):
        return owned[first:last].transpose(1, 0, 2).reshape(share, -1).astype(F32)

    g_back = owned[16:].reshape(4, 2, share, 384).transpose(0, 2, 1, 3).reshape(4 * share, width).astype(F32)
    small_owned = small_owned.reshape(-1)
    small_grads, at = [], 0
    for vector in vectors:
        small_grads.append(small_owned[at:at + vector.shape[0]])
        at += vector.shape[0]
    return (output.reshape(tokens.shape), input_grad.reshape(tokens.shape), columns(0, 6), columns(6, 8), columns(8, 16), g_back) + tuple(small_grads)


def solution(mesh):
    rows, flat = P("fsdp", "ctx", None), P("fsdp", None)
    return jax.shard_map(
        shards,
        mesh=mesh,
        in_specs=(rows, rows, flat) + (flat,) * 4 + (P("fsdp"),) * 9,
        out_specs=(rows, rows) + (flat,) * 4 + (P("fsdp"),) * 9,
        check_vma=False,
    )
```
